32 devices in a mesh: dp: 8 (over z, core), tensor: 4 (over y, x).
Axes of the slice: x: 2, y: 2, z: 4, core: 2. Of those that a mesh axis runs over, the one named last changes fastest.
Arguments:
- block_input: float32 [16384, 768], P(('dp', 'tensor')), may hold values from -6 to 6
- segment_ids: int32 [8, 2048], P('dp'), may hold values from 0 to 3, never falling along the last dimension, each value on 1 to 1024 neighbouring positions
- norm_gain: float32 [768], replicated, may hold values from 0.5 to 1.5
- gate_proj: bfloat16 [768, 1536], P('dp', 'tensor'), may hold values from -0.21875 to 0.21875
- value_proj: bfloat16 [768, 1536], P('dp', 'tensor'), may hold values from -0.21875 to 0.21875
- shared_proj: bfloat16 [768, 256], P('dp'), may hold values from -0.21875 to 0.21875
- step_proj: bfloat16 [768, 24], P('dp', 'tensor'), may hold values from -0.21875 to 0.21875
- conv_value_weight: float32 [4, 1536], P(None, 'tensor'), may hold values from -2 to 2
- conv_value_bias: float32 [1536], P('tensor'), may hold values from -0.5 to 0.5
- conv_shared_weight: float32 [4, 256], replicated, may hold values from -2 to 2
- conv_shared_bias: float32 [256], replicated, may hold values from -0.5 to 0.5
- step_bias: float32 [24], P('tensor'), may hold values from -5 to -2
- decay_log: float32 [24], P('tensor'), may hold values from -2 to 2
- skip_weight: float32 [24], P('tensor'), may hold values from 0.5 to 1.5
- gate_gain: float32 [1536], P('tensor'), may hold values from 0.5 to 1.5
- output_proj: bfloat16 [1536, 768], P('tensor', 'dp'), may hold values from -0.15625 to 0.15625
- out_cotangent: bfloat16 [16384, 768], P(('dp', 'tensor')), may hold values from -6 to 6
Outputs:
- block_output: float32 [16384, 768], P(('dp', 'tensor'))
- input_grad: float32 [16384, 768], P(('dp', 'tensor'))
- norm_gain_grad: float32 [768], replicated
- gate_proj_grad: float32 [768, 1536], P('dp', 'tensor')
- value_proj_grad: float32 [768, 1536], P('dp', 'tensor')
- shared_proj_grad: float32 [768, 256], P('dp')
- step_proj_grad: float32 [768, 24], P('dp', 'tensor')
- conv_value_weight_grad: float32 [4, 1536], P(None, 'tensor')
- conv_value_bias_grad: float32 [1536], P('tensor')
- conv_shared_weight_grad: float32 [4, 256], replicated
- conv_shared_bias_grad: float32 [256], replicated
- step_bias_grad: float32 [24], P('tensor')
- decay_log_grad: float32 [24], P('tensor')
- skip_weight_grad: float32 [24], P('tensor')
- gate_gain_grad: float32 [1536], P('tensor')
- output_proj_grad: float32 [1536, 768], P('tensor', 'dp')
The draws below stay inside these ranges and needn't reach their ends.
Inputs may be any that keep to these rules, and one draw needn't show every extreme that they name: `segment_ids`: along each sequence the segment numbers never fall and every number from 0 to 3 occurs; a document holds at most 1024 tokens, and one document of each sequence holds exactly that many.
All inputs are finite; a program needn't handle non-finite values.
Results may differ from the reference program's by a relative error of at most 0.019.
Values may be sent and summed in bfloat16 or wider, within the bound.
No kernel may reach another device: no remote copies, remote signals or barrier semaphores. Data moves between devices by JAX's collectives and lax.ppermute only.
A program may use at most 192 MiB of HBM per device.

```python
import math
import jax
import jax.numpy as jnp
import numpy as np
from jax import lax

D = 768
INNER = 1536
HEADS = 24
STATE = 128
CONV = 4
SPAN = 256
SEQ_LEN = 2048
SEGS = 4
SEQS = 8
TOKENS = 16384


def level_of(own_key, shape, shards, smallest, high):
    gain, own = 1.0, jax.random.fold_in(own_key, 6)
    for dim, shards_of in shards:
        draws = jnp.exp(jax.random.uniform(jax.random.fold_in(own, dim), (shards_of,), jnp.float32, smallest / len(shards), high / len(shards)))
        gain = gain * jnp.repeat(draws, shape[dim] // shards_of).reshape([-1 if axis == dim else 1 for axis in range(len(shape))])
    return gain


def split_up(number_of, total, limit, lean):
    weights = [(1 << 20) // math.isqrt(rank ** lean) + 1 for rank in range(2, number_of + 1)]
    surplus, holding = total - limit - (number_of - 1), [1] * (number_of - 1)
    while surplus > 0:
        candidates = [i for i in range(number_of - 1) if holding[i] < limit]
        mass, budget = sum([weights[i] for i in candidates]), surplus
        for i in candidates:
            more = min(limit - holding[i], max(1, budget * weights[i] // mass), surplus)
            holding[i] = holding[i] + more
            surplus = surplus - more
    return np.array([limit] + holding)


def uneven_parts(stream_key, count, total, bound, slope):
    if count == 2:
        one = jax.random.randint(stream_key, (), max(1, total - bound), min(bound, total - 1) + 1)
        return jnp.stack([one, total - one])
    lengths = jnp.asarray(split_up(count, total, bound, slope), jnp.int32)
    pairs = (count - 1) // 2
    donor, receiver = lengths[1:1 + 2 * pairs:2], lengths[2:2 + 2 * pairs:2]
    margin = jnp.minimum(donor - 1, bound - receiver)
    passed = jax.random.randint(jax.random.fold_in(stream_key, 1), (pairs,), 0, 1 << 20) % (margin + 1)
    lengths = lengths.at[1:1 + 2 * pairs:2].set(donor - passed).at[2:2 + 2 * pairs:2].set(receiver + passed)
    return lengths[jax.random.permutation(jax.random.fold_in(stream_key, 2), count)]


def normal_values(own_key, extent, deviation, bound, shards=(), dtype=jnp.bfloat16):
    entries = deviation * jax.random.normal(own_key, extent, jnp.float32)
    if shards:
        entries = entries * level_of(own_key, extent, shards, -0.22, 0.18)
    return jnp.clip(entries, -bound, bound).astype(dtype)


def setup_inputs(seed: int = 0) -> dict:
    key_of = jax.random.split(jax.random.key(seed), 18)
    block_input = normal_values(key_of[0], (TOKENS, D), 1.0, 6.0, ((0, 32),), jnp.float32)
    segment_ids = jax.vmap(lambda own: jnp.searchsorted(jnp.cumsum(uneven_parts(own, SEGS, SEQ_LEN, SEQ_LEN // 2, 0)), jnp.arange(SEQ_LEN), side="right"))(jax.random.split(key_of[1], SEQS)).reshape((SEQS, SEQ_LEN)).astype(jnp.int32)
    norm_gain = jnp.clip(1.0 + 0.1 * jax.random.normal(key_of[2], (D,), jnp.float32), 0.5, 1.5)
    gate_proj = normal_values(key_of[3], (D, INNER), D ** -0.5, 0.21875, ((0, 8), (1, 4)))
    value_proj = normal_values(key_of[4], (D, INNER), D ** -0.5, 0.21875, ((0, 8), (1, 4)))
    shared_proj = normal_values(key_of[5], (D, 2 * STATE), D ** -0.5, 0.21875, ((0, 8),))
    step_proj = normal_values(key_of[6], (D, HEADS), D ** -0.5, 0.21875, ((0, 8), (1, 4)))
    conv_value_weight = normal_values(key_of[7], (CONV, INNER), 0.5, 2.0, ((1, 4),), jnp.float32)
    conv_value_bias = jnp.clip(jax.random.uniform(key_of[8], (INNER,), jnp.float32, -0.5, 0.5) * level_of(key_of[8], (INNER,), ((0, 4),), -0.4, 0.0), -0.5, 0.5)
    conv_shared_weight = normal_values(key_of[9], (CONV, 2 * STATE), 0.5, 2.0, (), jnp.float32)
    conv_shared_bias = jnp.clip(jax.random.uniform(key_of[10], (2 * STATE,), jnp.float32, -0.5, 0.5), -0.5, 0.5)
    step_bias = jnp.clip(-5.0 + 3.0 * jax.random.uniform(key_of[11], (HEADS,), jnp.float32) ** level_of(key_of[11], (HEADS,), ((0, 4),), -0.2, 0.2), -5.0, -2.0)
    decay_log = jnp.clip(jax.random.uniform(key_of[12], (HEADS,), jnp.float32, -2.0, 2.0) * level_of(key_of[12], (HEADS,), ((0, 4),), -0.4, 0.0), -2.0, 2.0)
    skip_weight = jnp.clip(0.5 + 1.0 * jax.random.uniform(key_of[13], (HEADS,), jnp.float32) ** level_of(key_of[13], (HEADS,), ((0, 4),), -0.2, 0.2), 0.5, 1.5)
    gate_gain = jnp.clip(1.0 + 0.1 * jax.random.normal(key_of[14], (INNER,), jnp.float32), 0.5, 1.5)
    output_proj = normal_values(key_of[15], (INNER, D), INNER ** -0.5, 0.15625, ((0, 4), (1, 8)))
    out_cotangent = normal_values(key_of[16], (TOKENS, D), 1.0, 6.0, ((0, 32),))
    return dict(block_input=block_input, segment_ids=segment_ids, norm_gain=norm_gain, gate_proj=gate_proj, value_proj=value_proj, shared_proj=shared_proj, step_proj=step_proj, conv_value_weight=conv_value_weight, conv_value_bias=conv_value_bias, conv_shared_weight=conv_shared_weight, conv_shared_bias=conv_shared_bias, step_bias=step_bias, decay_log=decay_log, skip_weight=skip_weight, gate_gain=gate_gain, output_proj=output_proj, out_cotangent=out_cotangent)


epsilon = 1e-05
HIGHEST = lax.Precision.HIGHEST

def causal_conv(values, kernel, offset, segment):
    length = values.shape[0]
    taps_count = kernel.shape[0]
    padded = jnp.concatenate([jnp.zeros((taps_count - 1, values.shape[1]), jnp.float32), values], 0)
    segment_pad = jnp.concatenate([jnp.full((taps_count - 1,), -1, jnp.int32), segment.astype(jnp.int32)])
    result = jnp.zeros(values.shape, jnp.float32) + offset
    for tap_index in range(taps_count):
        linked = (segment_pad[tap_index:tap_index + length] == segment).astype(jnp.float32)
        result = result + kernel[tap_index] * padded[tap_index:tap_index + length] * linked[:, None]
    return result

def span_scan(inputs, step_sizes, decay_rate, input_map, output_map, segment):
    length, head_count, head_size = inputs.shape
    blocks = length // SPAN
    values = inputs.reshape(blocks, SPAN, head_count, head_size)
    deltas = step_sizes.reshape(blocks, SPAN, head_count)
    in_block = input_map.reshape(blocks, SPAN, -1)
    out_block = output_map.reshape(blocks, SPAN, -1)
    segment_block = segment.reshape(blocks, SPAN)
    log_decay = jnp.cumsum(deltas * decay_rate, axis=1)
    scores = jnp.einsum('cqn,csn->cqs', out_block, in_block, precision=HIGHEST)
    position = jnp.arange(SPAN)
    causal = position[:, None] >= position[None, :]
    inside = (causal[None] & (segment_block[:, :, None] == segment_block[:, None, :]))[..., None]
    gap_logs = log_decay[:, :, None, :] - log_decay[:, None, :, :]
    mixing = jnp.where(inside, jnp.exp(jnp.where(inside, gap_logs, 0.0)), 0.0) * scores[..., None] * deltas[:, None, :, :]
    local_out = jnp.einsum('cqsh,cshp->cqhp', mixing, values, precision=HIGHEST)
    last_seg = segment_block[:, -1]
    same_end = (segment_block == last_seg[:, None]).astype(jnp.float32)
    to_end = jnp.exp(log_decay[:, -1:, :] - log_decay) * same_end[..., None] * deltas
    states = jnp.einsum('csn,csh,cshp->chnp', in_block, to_end, values, precision=HIGHEST)
    prev_last = jnp.concatenate([jnp.full((1,), -1, jnp.int32), last_seg[:-1]])
    survive = (last_seg == prev_last).astype(jnp.float32)
    span_totals = jnp.exp(log_decay[:, -1, :])

    def advance(carried, span_items):
        fresh_state, span_total, kept_flag = span_items
        return (fresh_state + kept_flag * span_total[:, None, None] * carried, carried)
    _, previous = lax.scan(advance, jnp.zeros_like(states[0]), (states, span_totals, survive))
    entering = jnp.exp(log_decay) * (segment_block == prev_last[:, None]).astype(jnp.float32)[..., None]
    carry_out = jnp.einsum('cqn,chnp->cqhp', out_block, previous, precision=HIGHEST) * entering[..., None]
    return (local_out + carry_out).reshape(length, head_count, head_size)

def mixer_split(projected, params, segment):
    conv_value_weight, conv_value_bias, conv_shared_weight, conv_shared_bias, step_bias, decay_log, skip_weight = params
    inner_count = conv_value_weight.shape[1]
    head_count = step_bias.shape[0]
    length = projected.shape[0]
    gate_rows = projected[:, :inner_count]
    value_rows = projected[:, inner_count:2 * inner_count]
    step_rows = projected[:, 2 * inner_count:2 * inner_count + head_count]
    shared_rows = projected[:, 2 * inner_count + head_count:]
    activated = jax.nn.silu(causal_conv(value_rows, conv_value_weight, conv_value_bias, segment))
    shared = jax.nn.silu(causal_conv(shared_rows, conv_shared_weight, conv_shared_bias, segment))
    step_sizes = jax.nn.softplus(step_rows + step_bias)
    decay_rate = -jnp.exp(decay_log)
    inputs = activated.reshape(length, head_count, -1)
    scanned = span_scan(inputs, step_sizes, decay_rate, shared[:, :STATE], shared[:, STATE:], segment)
    scanned = scanned + skip_weight[:, None] * inputs
    return scanned.reshape(length, -1) * jax.nn.silu(gate_rows)

def reference(block_input, segment_ids, norm_gain, gate_proj, value_proj, shared_proj, step_proj, conv_value_weight, conv_value_bias, conv_shared_weight, conv_shared_bias, step_bias, decay_log, skip_weight, gate_gain, output_proj, out_cotangent):
    joined = jnp.concatenate([gate_proj, value_proj, step_proj, shared_proj], axis=1)
    small_params = (conv_value_weight, conv_value_bias, conv_shared_weight, conv_shared_bias, step_bias, decay_log, skip_weight)
    contract_rows = (((0,), (0,)), ((), ()))
    contract_cols = (((1,), (1,)), ((), ()))

    def one_sequence(accum, seq_items):
        inputs_seq, cot_seq, segment = seq_items
        inv_root = lax.rsqrt(lax.optimization_barrier(jnp.mean(inputs_seq * inputs_seq, axis=1, keepdims=True)) + epsilon)
        normed = (inputs_seq * inv_root * norm_gain).astype(jnp.bfloat16)
        projected = jnp.dot(normed, joined, preferred_element_type=jnp.float32)
        gated = mixer_split(projected, small_params, segment)
        gate_root = lax.rsqrt(lax.optimization_barrier(jnp.mean(gated * gated, axis=1, keepdims=True)) + epsilon)
        scaled = (gated * gate_root * gate_gain).astype(jnp.bfloat16)
        output_seq = inputs_seq + jnp.dot(scaled, output_proj, preferred_element_type=jnp.float32)
        scaled_cot = lax.dot_general(cot_seq, output_proj, contract_cols, preferred_element_type=jnp.float32)
        out_grad = lax.dot_general(scaled, cot_seq, contract_rows, preferred_element_type=jnp.float32)
        gain_grad = lax.optimization_barrier(jnp.sum(scaled_cot * gated * gate_root, axis=0))
        gate_dots = lax.optimization_barrier(jnp.sum(scaled_cot * gate_gain * gated, axis=1, keepdims=True))
        gated_cot = gate_root * gate_gain * scaled_cot - gated * (gate_root * gate_root * gate_root) * (gate_dots / INNER)
        _, pullback = jax.vjp(lambda first, second: mixer_split(first, second, segment), projected, small_params)
        raw_cot, param_cot = pullback(gated_cot)
        proj_cot = raw_cot.astype(jnp.bfloat16)
        joined_grad = lax.dot_general(normed, proj_cot, contract_rows, preferred_element_type=jnp.float32)
        normed_cot = lax.dot_general(proj_cot, joined, contract_cols, preferred_element_type=jnp.float32)
        norm_grad = lax.optimization_barrier(jnp.sum(normed_cot * inputs_seq * inv_root, axis=0))
        hat_cot = normed_cot * norm_gain
        input_seq_grad = cot_seq.astype(jnp.float32) + inv_root * hat_cot - inputs_seq * (inv_root * inv_root * inv_root) * lax.optimization_barrier(jnp.mean(hat_cot * inputs_seq, axis=1, keepdims=True))
        terms = (norm_grad, joined_grad, param_cot, gain_grad, out_grad)
        return (jax.tree.map(jnp.add, accum, terms), (output_seq, input_seq_grad))
    start_accum = (jnp.zeros((D,), jnp.float32), jnp.zeros(joined.shape, jnp.float32), jax.tree.map(lambda leaf: jnp.zeros(leaf.shape, jnp.float32), small_params), jnp.zeros((INNER,), jnp.float32), jnp.zeros((INNER, D), jnp.float32))
    seq_inputs = block_input.reshape(SEQS, SEQ_LEN, D)
    seq_cots = out_cotangent.reshape(SEQS, SEQ_LEN, D)
    totals, stacked = lax.scan(one_sequence, start_accum, (seq_inputs, seq_cots, segment_ids))
    norm_grad, joined_grad, param_grads, gain_grad, out_grad = totals
    block_output = stacked[0].reshape(TOKENS, D)
    input_grad = stacked[1].reshape(TOKENS, D)
    cut_one = INNER
    cut_two = 2 * INNER
    cut_three = 2 * INNER + HEADS
    return (block_output, input_grad, norm_grad, joined_grad[:, :cut_one], joined_grad[:, cut_one:cut_two], joined_grad[:, cut_three:], joined_grad[:, cut_two:cut_three], param_grads[0], param_grads[1], param_grads[2], param_grads[3], param_grads[4], param_grads[5], param_grads[6], gain_grad, out_grad)
```

```python
import functools
import math

import jax
import jax.numpy as jnp
from jax import lax
from jax.experimental import pallas as pl
from jax.experimental.pallas import tpu as pltpu
from jax.sharding import PartitionSpec as P

BLOCK = 256
LANES = 128
EPS = 1e-05
LOG2E = math.log2(math.e)
FAR = -1e30
F32 = jnp.float32
BF16 = jnp.bfloat16

MM = (((1,), (0,)), ((), ()))
MT = (((1,), (1,)), ((), ()))
TM = (((0,), (0,)), ((), ()))


def dot(a, b, dims=MM):
    return lax.dot_general(a, b, dims, preferred_element_type=F32)


def dot_split(exact, values, dims=MM):
    high = values.astype(BF16)
    low = (values - high.astype(F32)).astype(BF16)
    return dot(exact, high, dims) + dot(exact, low, dims)


def split_dot(values, exact, dims=MM):
    high = values.astype(BF16)
    low = (values - high.astype(F32)).astype(BF16)
    return dot(high, exact, dims) + dot(low, exact, dims)


def up(n, to=LANES):
    return -(-n // to) * to


def softplus(v):
    return jnp.maximum(v, 0.0) + jnp.log1p(jnp.exp(-jnp.abs(v)))


def sigmoid(v):
    return 1.0 / (1.0 + jnp.exp(-v))


def colsum(v):
    return jnp.sum(v.reshape(v.shape[0] // 8, 8, v.shape[1]), axis=0)


def spread(cols, pair, hd):
    per = LANES // hd
    lane = lax.broadcasted_iota(jnp.int32, (cols.shape[0], LANES), 1)
    out = jnp.broadcast_to(cols[:, pair * per : pair * per + 1], lane.shape)
    for j in range(1, per):
        col = cols[:, pair * per + j : pair * per + j + 1]
        out = jnp.where(lane >= j * hd, jnp.broadcast_to(col, lane.shape), out)
    return out


def columns_of(rows):
    pad = jnp.zeros((LANES - rows.shape[0], rows.shape[1]), F32)
    return jnp.concatenate([rows, pad], axis=0).T


class Dims:
    def __init__(self, length, width, inner, hd, state, parts, part_rows, chunks, chunk_rows):
        self.length, self.width, self.state, self.hd = length, width, state, hd
        self.ip = up(inner)
        self.vs = self.ip + 2 * state
        self.np = self.ip + self.vs + LANES
        self.wc = self.np + self.ip
        self.blocks = length // BLOCK
        self.parts, self.part_rows = parts, part_rows
        self.chunks, self.chunk_rows = chunks, chunk_rows
        self.pairs = self.ip // LANES
        self.per = LANES // hd


def load_parts(refs, target, sems, scalars, first, rows):
    return [
        pltpu.make_async_copy(
            ref, target.at[pl.ds(pl.multiple_of(scalars[first + k], rows), rows), :], sems.at[k]
        )
        for k, ref in enumerate(refs)
    ]


def decay_parts(dm, raw, hp_ref, cols, tri):
    delta = softplus(raw + hp_ref[0:1, :])
    logs = dot_split(tri, delta * (hp_ref[1:2, :] * LOG2E))
    enter = jnp.exp2(logs) * cols[:, 7:8]
    ending = jnp.exp2(logs[BLOCK - 1 :, :] - logs) * cols[:, 8:9]
    return delta, logs, enter, ending


def forward_kernel(dm, scalars, *refs):
    q, ip, vs, st, hd = BLOCK, dm.ip, dm.vs, dm.state, dm.hd
    w_parts = refs[: dm.parts]
    n_parts = refs[dm.parts : dm.parts + dm.chunks]
    c_parts = refs[dm.parts + dm.chunks : dm.parts + 2 * dm.chunks]
    rest = refs[dm.parts + 2 * dm.chunks :]
    rows_ref, conv_ref, hp_ref, lane_ref = rest[:4]
    (g_out, v_out, cv_out, ys_out, st_out, sc_out, h_out, sum_out, br_out, nm_out, ct_out, sg_out) = rest[4:16]
    (w_v, nm_v, ct_v, h_ref, vbuf, tri_ref, bias_ref, w_sem, n_sem, c_sem) = rest[16:]
    i = pl.program_id(0)
    at = pl.ds(pl.multiple_of(i * q, q), q)

    @pl.when(i == 0)
    def _():
        copies = (
            load_parts(w_parts, w_v, w_sem, scalars, 0, dm.part_rows)
            + load_parts(n_parts, nm_v, n_sem, scalars, dm.parts, dm.chunk_rows)
            + load_parts(c_parts, ct_v, c_sem, scalars, dm.parts, dm.chunk_rows)
        )
        for copy in copies:
            copy.start()
        h_ref[...] = jnp.zeros_like(h_ref)
        vbuf[...] = jnp.zeros_like(vbuf)
        r = lax.broadcasted_iota(jnp.int32, (q, q), 0)
        c = lax.broadcasted_iota(jnp.int32, (q, q), 1)
        tri_ref[...] = jnp.where(r >= c, 1.0, 0.0).astype(BF16)
        for copy in copies:
            copy.wait()

    rows = rows_ref[...]
    cols = columns_of(rows)
    normed = nm_v[at, :]
    cot = ct_v[at, :]
    nm_out[...] = normed
    ct_out[...] = cot
    projected = dot(normed, w_v[:, : dm.np])
    g_out[...] = projected[:, :ip]
    vbuf[0:8, :] = vbuf[q : q + 8, :]
    vbuf[8 : 8 + q, :] = projected[:, ip : ip + vs]
    v_out[...] = projected[:, ip : ip + vs]
    raw = projected[:, ip + vs :]
    st_out[...] = raw

    acts = []
    for c in range(vs // LANES):
        g = slice(c * LANES, (c + 1) * LANES)
        acc = conv_ref[4:5, g] + conv_ref[3:4, g] * vbuf[8 : 8 + q, g]
        for lag in range(1, 4):
            acc = acc + conv_ref[3 - lag : 4 - lag, g] * (
                vbuf[8 - lag : 8 - lag + q, g] * cols[:, lag : lag + 1]
            )
        cv_out[:, g] = acc
        acts.append(acc * sigmoid(acc))
    in_map = jnp.concatenate(acts[dm.pairs : dm.pairs + st // LANES], axis=1).astype(BF16)
    out_map = jnp.concatenate(acts[dm.pairs + st // LANES :], axis=1).astype(BF16)

    delta, logs, enter, ending = decay_parts(dm, raw, hp_ref, cols, tri_ref[...])
    logs_t = logs.T
    r = lax.broadcasted_iota(jnp.int32, (q, q), 0)
    c = lax.broadcasted_iota(jnp.int32, (q, q), 1)
    bias_ref[...] = jnp.where((r >= c) & (cols[:, 0:1] == rows[0:1, :]), 0.0, FAR)
    scores = dot(out_map, in_map, MT)
    keep = scalars[dm.parts + dm.chunks + i].astype(F32)
    total = jnp.exp2(logs[q - 1 :, :]) * keep
    lane = lax.broadcasted_iota(jnp.int32, (q, LANES), 1)
    h_out[...] = h_ref[...]
    in_map_t = in_map.T
    squares = jnp.zeros((q, 1), F32)
    dots = jnp.zeros((q, 1), F32)
    for p in range(dm.pairs):
        g = slice(p * LANES, (p + 1) * LANES)
        x = acts[p]
        u = x * spread(delta, p, hd)
        ub = u.astype(BF16)
        y = None
        for j in range(dm.per):
            h = p * dm.per + j
            decay = jnp.exp2(logs[:, h : h + 1] - logs_t[h : h + 1, :] + bias_ref[...])
            part = dot((decay * scores).astype(BF16), ub)
            y = part if y is None else jnp.where(lane >= j * hd, part, y)
        held = h_ref[:, g]
        y = y + dot(out_map, held.astype(BF16)) * spread(enter, p, hd)
        wu = (u * spread(ending, p, hd)).astype(BF16)
        h_ref[:, g] = held * spread(total, p, hd) + dot(in_map_t, wu)
        ys_out[:, g] = y
        gate = g_out[:, g]
        gated = (y + lane_ref[0:1, g] * x) * (gate * sigmoid(gate))
        sc = dot(cot, w_v[:, dm.np + p * LANES : dm.np + (p + 1) * LANES])
        sc_out[:, g] = sc
        scaled = gated * lane_ref[1:2, g]
        sg_out[:, g] = scaled.astype(BF16)
        squares = squares + jnp.sum(gated * gated, axis=1, keepdims=True)
        dots = dots + jnp.sum(sc * scaled, axis=1, keepdims=True)
    two = jnp.where(lane == 0, squares, jnp.where(lane == 1, dots, 0.0)).T
    sum_out[...] = two[0:2, :]
    br_out[...] = dot(sg_out[...], w_v[:, dm.np :], MT).astype(BF16)


def backward_kernel(dm, scalars, *refs):
    q, ip, vs, st, hd = BLOCK, dm.ip, dm.vs, dm.state, dm.hd
    w_parts = refs[: dm.parts]
    rest = refs[dm.parts :]
    (rows_ref, conv_ref, hp_ref, lane_ref, rk_ref, g_in, v_in, cv_in, ys_in, st_in, sc_in, h_in) = rest[:12]
    (pj_out, nc_out, tap_out, lane_out, head_out) = rest[12:17]
    (w_v, dh_ref, dbuf, tri_ref, bias_ref, ds_ref, dy_s, u_s, du_s, dx_s, act_s, t1_s, t2_s, w_sem) = rest[17:]
    i = pl.program_id(0)
    blk = dm.blocks - 1 - i

    @pl.when(i == 0)
    def _():
        copies = load_parts(w_parts, w_v, w_sem, scalars, 0, dm.part_rows)
        for copy in copies:
            copy.start()
        dh_ref[...] = jnp.zeros_like(dh_ref)
        dbuf[...] = jnp.zeros_like(dbuf)
        tap_out[...] = jnp.zeros_like(tap_out)
        lane_out[...] = jnp.zeros_like(lane_out)
        head_out[...] = jnp.zeros_like(head_out)
        r = lax.broadcasted_iota(jnp.int32, (q, q), 0)
        c = lax.broadcasted_iota(jnp.int32, (q, q), 1)
        tri_ref[...] = jnp.where(r >= c, 1.0, 0.0).astype(BF16)
        for copy in copies:
            copy.wait()

    rows = rows_ref[...]
    cols = columns_of(jnp.concatenate([rows, rk_ref[...]], axis=0))
    root, pull = cols[:, 16:17], cols[:, 17:18]
    raw = st_in[...]
    tri = tri_ref[...]
    delta, logs, enter, ending = decay_parts(dm, raw, hp_ref, cols, tri)
    logs_t = logs.T
    lane = lax.broadcasted_iota(jnp.int32, (q, LANES), 1)

    acts, slopes = [], []
    for c in range(vs // LANES):
        g = slice(c * LANES, (c + 1) * LANES)
        cv = cv_in[:, g]
        sig = sigmoid(cv)
        act = cv * sig
        acts.append(act)
        slopes.append(sig + act * (1.0 - sig))
    in_map = jnp.concatenate(acts[dm.pairs : dm.pairs + st // LANES], axis=1).astype(BF16)
    out_map = jnp.concatenate(acts[dm.pairs + st // LANES :], axis=1).astype(BF16)

    for p in range(dm.pairs):
        g = slice(p * LANES, (p + 1) * LANES)
        gate, sc, x, ys = g_in[:, g], sc_in[:, g], acts[p], ys_in[:, g]
        sig = sigmoid(gate)
        z = gate * sig
        y = ys + lane_ref[0:1, g] * x
        gated = y * z
        cot = root * (lane_ref[1:2, g] * sc) - pull * gated
        lane_out[0:8, g] += colsum(sc * gated * root)
        dy = cot * z
        dy_s[:, g] = dy
        pj_out[:, g] = (cot * y * (sig + z * (1.0 - sig))).astype(BF16)
        lane_out[8:16, g] += colsum(dy * x)
        u_s[:, g] = x * spread(delta, p, hd)

    r = lax.broadcasted_iota(jnp.int32, (q, q), 0)
    c = lax.broadcasted_iota(jnp.int32, (q, q), 1)
    bias_ref[...] = jnp.where((r <= c) & (cols[:, 0:1] == rows[0:1, :]), 0.0, FAR)
    scores = dot(in_map, out_map, MT)
    dh_b = dh_ref[...].astype(BF16)
    h_b = h_in[...].astype(BF16)
    out_map_t = out_map.T
    keep = scalars[dm.parts + dm.chunks + blk].astype(F32)
    total = jnp.exp2(logs[q - 1 :, :]) * keep
    d_in = jnp.zeros((q, st), F32)
    d_out = jnp.zeros((q, st), F32)
    for p in range(dm.pairs):
        g = slice(p * LANES, (p + 1) * LANES)
        u, dy = u_s[:, g], dy_s[:, g]
        ub, dyb = u.astype(BF16), dy.astype(BF16)
        du = None
        for j in range(dm.per):
            h = p * dm.per + j
            mine = (lane >= j * hd) & (lane < (j + 1) * hd)
            decay = jnp.exp2(logs_t[h : h + 1, :] - logs[:, h : h + 1] + bias_ref[...])
            part = dot((decay * scores).astype(BF16), dyb)
            du = part if du is None else jnp.where(lane >= j * hd, part, du)
            dm_t = dot(jnp.where(mine, u, 0.0).astype(BF16), dyb, MT)
            if p == 0 and j == 0:
                ds_ref[...] = dm_t * decay
            else:
                ds_ref[...] += dm_t * decay
        end_e = spread(ending, p, hd)
        late = end_e * dot(in_map, dh_b[:, g])
        du = du + late
        wu = (u * end_e).astype(BF16)
        edy = (dy * spread(enter, p, hd)).astype(BF16)
        d_in = d_in + dot(wu, dh_b[:, g], MT)
        d_out = d_out + dot(edy, h_b[:, g], MT)
        u32 = ub.astype(F32)
        t1_s[:, g] = dyb.astype(F32) * ys_in[:, g] - u32 * du
        t2_s[:, g] = du * acts[p]
        kept = dh_ref[:, g] * spread(total, p, hd)
        act_s[:, g] = colsum(u32 * late) + colsum(h_in[:, g] * kept)
        dh_ref[:, g] = kept + dot(out_map_t, edy)
        dx_s[:, g] = (spread(delta, p, hd) * du + lane_ref[0:1, g] * dy) * slopes[p]
    ds_b = ds_ref[...].astype(BF16)
    d_in = d_in + dot(ds_b, out_map)
    d_out = d_out + dot(ds_b, in_map, TM)

    hr = lax.broadcasted_iota(jnp.int32, (ip, LANES), 0)
    hc = lax.broadcasted_iota(jnp.int32, (ip, LANES), 1)
    pick = jnp.where(hr // hd == hc, 1.0, 0.0).astype(BF16)
    d_log = split_dot(t1_s[...], pick)
    last = split_dot(jnp.sum(act_s[...], axis=0, keepdims=True), pick)
    row = lax.broadcasted_iota(jnp.int32, (q, LANES), 0)
    d_log = d_log + jnp.where(row == q - 1, last, 0.0)
    d_step = dot_split(tri, d_log, TM)
    head_out[8:16, :] += colsum(d_step * delta)
    d_delta = hp_ref[1:2, :] * d_step + split_dot(t2_s[...], pick)
    d_raw = d_delta * sigmoid(raw + hp_ref[0:1, :])
    head_out[0:8, :] += colsum(d_raw)
    pj_out[:, ip + vs :] = d_raw.astype(BF16)

    dbuf[q : q + 8, :] = dbuf[0:8, :]
    for c in range(vs // LANES):
        g = slice(c * LANES, (c + 1) * LANES)
        if c < dm.pairs:
            dbuf[0:q, g] = dx_s[:, g]
        else:
            k = (c - dm.pairs) * LANES
            source = d_in[:, k : k + LANES] if k < st else d_out[:, k - st : k - st + LANES]
            dbuf[0:q, g] = source * slopes[c]
    for c in range(vs // LANES):
        g = slice(c * LANES, (c + 1) * LANES)
        v = v_in[:, g]
        shifted = dbuf[0:q, g]
        tap_out[32:40, g] += colsum(shifted)
        tap_out[24:32, g] += colsum(shifted * v)
        dv = conv_ref[3:4, g] * shifted
        for lag in range(1, 4):
            shifted = dbuf[lag : lag + q, g] * cols[:, 3 + lag : 4 + lag]
            tap_out[24 - 8 * lag : 32 - 8 * lag, g] += colsum(shifted * v)
            dv = dv + conv_ref[3 - lag : 4 - lag, g] * shifted
        pj_out[:, ip + c * LANES : ip + (c + 1) * LANES] = dv.astype(BF16)
    nc_out[...] = dot(pj_out[...], w_v[:, : dm.np], MT).astype(BF16)


def shift_hi(n, k):
    return [(i, ((i // 2 + k) % (n // 2)) * 2 + i % 2) for i in range(n)]


def swap(n, k):
    return [(i, i ^ k) for i in range(n)]


def all_sum(v, axis, n):
    k = 1
    while k < n:
        v = v + lax.ppermute(v, axis, swap(n, k))
        k *= 2
    return v


def pad_cols(v, to):
    return jnp.pad(v, ((0, 0), (0, to - v.shape[1])))


def pad_vec(v, to):
    return jnp.pad(v, (0, to - v.shape[0]))


def body(
    n_dp,
    n_t,
    block_input,
    segment_ids,
    norm_gain,
    gate_proj,
    value_proj,
    shared_proj,
    step_proj,
    conv_value_weight,
    conv_value_bias,
    conv_shared_weight,
    conv_shared_bias,
    step_bias,
    decay_log,
    skip_weight,
    gate_gain,
    output_proj,
    out_cotangent,
):
    q = BLOCK
    chunk_rows, width = block_input.shape
    length = segment_ids.shape[1]
    inner, heads = gate_proj.shape[1], step_proj.shape[1]
    part_rows = gate_proj.shape[0]
    state = shared_proj.shape[1] // 2
    hd = inner // heads
    dm = Dims(length, width, inner, hd, state, n_dp, part_rows, n_t, chunk_rows)
    ip, vs, nb = dm.ip, dm.vs, dm.blocks
    me_t = lax.axis_index("tensor")
    me_dp = lax.axis_index("dp")
    hi, core, n_hi = me_dp // 2, me_dp % 2, n_dp // 2

    packed = jnp.concatenate(
        [
            pad_cols(gate_proj, ip),
            pad_cols(value_proj, ip),
            shared_proj,
            pad_cols(step_proj, LANES),
            pad_cols(output_proj.T, ip),
        ],
        axis=1,
    )
    inv_root = lax.rsqrt(jnp.mean(block_input * block_input, axis=1, keepdims=True) + EPS)
    normed = (block_input * inv_root * norm_gain).astype(BF16)
    n_list = [normed] + [lax.ppermute(normed, "tensor", swap(n_t, k)) for k in range(1, n_t)]
    w_list = [packed] + [lax.ppermute(packed, "dp", shift_hi(n_dp, k)) for k in range(1, n_hi)]
    w_list = w_list + [lax.ppermute(part, "dp", swap(n_dp, 1)) for part in w_list]
    c_list = [out_cotangent] + [
        lax.ppermute(out_cotangent, "tensor", swap(n_t, k)) for k in range(1, n_t)
    ]

    seg = segment_ids[0]
    segb = seg.reshape(nb, q)
    last = segb[:, -1]
    prev_last = jnp.concatenate([jnp.full((1,), -1, jnp.int32), last[:-1]])
    gap = jnp.full((3,), -1, jnp.int32)
    wide = jnp.concatenate([gap, seg, gap])
    rows = [seg.astype(F32)]
    rows += [(wide[3 - k : 3 - k + length] == seg).astype(F32) for k in range(1, 4)]
    rows += [(wide[3 + k : 3 + k + length] == seg).astype(F32) for k in range(1, 4)]
    rows += [
        (segb == prev_last[:, None]).astype(F32).reshape(-1),
        (segb == last[:, None]).astype(F32).reshape(-1),
    ]
    rows = jnp.concatenate(
        [jnp.stack(rows), jnp.zeros((16 - len(rows), length), F32)], axis=0
    )
    keep = (last == prev_last).astype(jnp.int32)
    ks = jnp.arange(n_hi)
    other = (hi - ks) % n_hi
    block_chunk = jnp.arange(nb) * q // chunk_rows
    scalars = jnp.concatenate(
        [
            (other * 2 + core) * part_rows,
            (other * 2 + 1 - core) * part_rows,
            (me_t ^ jnp.arange(n_t)) * chunk_rows,
            keep,
            block_chunk ^ me_t,
        ]
    ).astype(jnp.int32)
    rel_at = n_dp + n_t + nb

    conv = jnp.concatenate(
        [
            pad_cols(jnp.concatenate([conv_value_weight, conv_value_bias[None]]), ip),
            jnp.concatenate([conv_shared_weight, conv_shared_bias[None]]),
        ],
        axis=1,
    )
    conv = jnp.pad(conv, ((0, 3), (0, 0)))
    rate = -jnp.exp(decay_log)
    per_head = jnp.stack([pad_vec(step_bias, LANES), pad_vec(rate, LANES)])
    per_head = jnp.pad(per_head, ((0, 6), (0, 0)))
    per_lane = jnp.stack([pad_vec(jnp.repeat(skip_weight, hd), ip), pad_vec(gate_gain, ip)])
    per_lane = jnp.pad(per_lane, ((0, 6), (0, 0)))

    hbm = pl.BlockSpec(memory_space=pl.ANY)

    def const(shape):
        return pl.BlockSpec(shape, lambda i, s: (0, 0))

    def fblock(cols):
        return pl.BlockSpec((q, cols), lambda i, s: (i, 0))

    per = chunk_rows // q
    out_shapes = [
        ((length, ip), F32, fblock(ip)),
        ((length, vs), F32, fblock(vs)),
        ((length, vs), F32, fblock(vs)),
        ((length, ip), F32, fblock(ip)),
        ((length, LANES), F32, fblock(LANES)),
        ((length, ip), F32, fblock(ip)),
        ((nb * state, ip), F32, pl.BlockSpec((state, ip), lambda i, s: (i, 0))),
        ((nb, 2, q), F32, pl.BlockSpec((None, 2, q), lambda i, s: (i, 0, 0))),
        (
            (n_t, chunk_rows, width),
            BF16,
            pl.BlockSpec((None, q, width), lambda i, s: (s[rel_at + i], i % per, 0)),
        ),
        ((length, width), BF16, fblock(width)),
        ((length, width), BF16, fblock(width)),
        ((length, ip), BF16, fblock(ip)),
    ]
    limit = 60 * 1024 * 1024
    forward = pl.pallas_call(
        functools.partial(forward_kernel, dm),
        out_shape=[jax.ShapeDtypeStruct(s, t) for s, t, _ in out_shapes],
        grid_spec=pltpu.PrefetchScalarGridSpec(
            num_scalar_prefetch=1,
            grid=(nb,),
            in_specs=[hbm] * (n_dp + 2 * n_t)
            + [
                pl.BlockSpec((16, q), lambda i, s: (0, i)),
                const((8, vs)),
                const((8, LANES)),
                const((8, ip)),
            ],
            out_specs=[spec for _, _, spec in out_shapes],
            scratch_shapes=[
                pltpu.VMEM((width, dm.wc), BF16),
                pltpu.VMEM((length, width), BF16),
                pltpu.VMEM((length, width), BF16),
                pltpu.VMEM((state, ip), F32),
                pltpu.VMEM((q + 8, vs), F32),
                pltpu.VMEM((q, q), BF16),
                pltpu.VMEM((q, q), F32),
                pltpu.SemaphoreType.DMA((n_dp,)),
                pltpu.SemaphoreType.DMA((n_t,)),
                pltpu.SemaphoreType.DMA((n_t,)),
            ],
        ),
        compiler_params=pltpu.CompilerParams(
            dimension_semantics=("arbitrary",), vmem_limit_bytes=limit
        ),
        name="block_forward",
    )
    (gate, value, conved, scan, steps, sc, held, sums, branch, normed_all, cot_all, scaled) = forward(
        scalars, *w_list, *n_list, *c_list, rows, conv, per_head, per_lane
    )

    sums = all_sum(sums, "tensor", n_t)
    root = lax.rsqrt(sums[:, 0] / (inner * n_t) + EPS)
    pull = root * root * root * (sums[:, 1] / (inner * n_t))
    rk = jnp.stack([root, pull], axis=1)

    def swap_sum(pieces):
        total = pieces[0].astype(F32)
        for k in range(1, n_t):
            total = total + lax.ppermute(pieces[k], "tensor", swap(n_t, k)).astype(F32)
        return total

    own_root = lax.dynamic_slice_in_dim(root.reshape(length), me_t * chunk_rows, chunk_rows)
    block_output = block_input + own_root[:, None] * swap_sum(branch)

    def bblock(cols):
        return pl.BlockSpec((q, cols), lambda i, s: (nb - 1 - i, 0))

    backward = pl.pallas_call(
        functools.partial(backward_kernel, dm),
        out_shape=[
            jax.ShapeDtypeStruct((length, dm.np), BF16),
            jax.ShapeDtypeStruct((n_t, chunk_rows, width), BF16),
            jax.ShapeDtypeStruct((40, vs), F32),
            jax.ShapeDtypeStruct((16, ip), F32),
            jax.ShapeDtypeStruct((16, LANES), F32),
        ],
        grid_spec=pltpu.PrefetchScalarGridSpec(
            num_scalar_prefetch=1,
            grid=(nb,),
            in_specs=[hbm] * n_dp
            + [
                pl.BlockSpec((16, q), lambda i, s: (0, nb - 1 - i)),
                const((8, vs)),
                const((8, LANES)),
                const((8, ip)),
                pl.BlockSpec((None, 2, q), lambda i, s: (nb - 1 - i, 0, 0)),
                bblock(ip),
                bblock(vs),
                bblock(vs),
                bblock(ip),
                bblock(LANES),
                bblock(ip),
                pl.BlockSpec((state, ip), lambda i, s: (nb - 1 - i, 0)),
            ],
            out_specs=[
                bblock(dm.np),
                pl.BlockSpec(
                    (None, q, width),
                    lambda i, s: (s[rel_at + nb - 1 - i], (nb - 1 - i) % per, 0),
                ),
                const((40, vs)),
                const((16, ip)),
                const((16, LANES)),
            ],
            scratch_shapes=[
                pltpu.VMEM((width, dm.wc), BF16),
                pltpu.VMEM((state, ip), F32),
                pltpu.VMEM((q + 8, vs), F32),
                pltpu.VMEM((q, q), BF16),
                pltpu.VMEM((q, q), F32),
                pltpu.VMEM((q, q), F32),
                pltpu.VMEM((q, ip), F32),
                pltpu.VMEM((q, ip), F32),
                pltpu.VMEM((q, ip), F32),
                pltpu.VMEM((q, ip), F32),
                pltpu.VMEM((8, ip), F32),
                pltpu.VMEM((q, ip), F32),
                pltpu.VMEM((q, ip), F32),
                pltpu.SemaphoreType.DMA((n_dp,)),
            ],
        ),
        compiler_params=pltpu.CompilerParams(
            dimension_semantics=("arbitrary",), vmem_limit_bytes=limit
        ),
        name="block_backward",
    )
    proj_cot, normed_cot, taps, lanes, head_sums = backward(
        scalars,
        *w_list,
        rows,
        conv,
        per_head,
        per_lane,
        rk,
        gate,
        value,
        conved,
        scan,
        steps,
        sc,
        held,
    )
    nc = swap_sum(normed_cot)

    scaled = (scaled.astype(F32) * root.reshape(length, 1)).astype(BF16)
    out_grad = dot(cot_all, scaled, TM)
    joined = jnp.concatenate([dot(normed_all, proj_cot, TM), out_grad], axis=1)
    weight_rows = jnp.concatenate(w_list, axis=0)
    order = jnp.concatenate([other * 2 + core, other * 2 + 1 - core])
    joined_parts = joined.reshape(n_dp, part_rows, dm.wc)
    rel_joined = joined_parts[order].reshape(width, dm.wc)
    gain_rows = jnp.sum(weight_rows[:, : dm.np].astype(F32) * rel_joined[:, : dm.np], axis=1)
    gain_grad = jnp.zeros((n_dp, part_rows), F32).at[order].set(gain_rows.reshape(n_dp, part_rows))
    gain_grad = gain_grad.reshape(width) / norm_gain

    parts = joined_parts.reshape(n_hi, 2, part_rows, dm.wc)
    mine = lax.dynamic_index_in_dim(parts, core, 1, False)
    theirs = lax.dynamic_index_in_dim(parts, 1 - core, 1, False).astype(BF16)
    both = mine + lax.ppermute(theirs, "dp", swap(n_dp, 1)).astype(F32)
    total = lax.dynamic_index_in_dim(both, hi, 0, False)
    for k in range(1, n_hi):
        piece = lax.dynamic_index_in_dim(both, (hi + k) % n_hi, 0, False).astype(BF16)
        total = total + lax.ppermute(piece, "dp", shift_hi(n_dp, k)).astype(F32)
    gate_proj_grad = total[:, :inner]
    value_proj_grad = total[:, ip : ip + inner]
    step_proj_grad = total[:, ip + vs : ip + vs + heads]
    output_proj_grad = total[:, dm.np : dm.np + inner].T
    shared = total[:, 2 * ip : ip + vs]
    shared_proj_grad = shared
    for k in range(1, n_t):
        shared_proj_grad = shared_proj_grad + lax.ppermute(
            shared.astype(BF16), "tensor", swap(n_t, k)
        ).astype(F32)

    taps = jnp.sum(taps.reshape(5, 8, vs), axis=1)
    lanes = jnp.sum(lanes.reshape(2, 8, ip), axis=1)
    head_sums = jnp.sum(head_sums.reshape(2, 8, LANES), axis=1)
    local = jnp.concatenate([taps[:, :ip].reshape(-1), lanes.reshape(-1), head_sums.reshape(-1)])
    common = jnp.concatenate([taps[:, ip:].reshape(-1), gain_grad])
    split_at = local.shape[0]
    small = all_sum(jnp.concatenate([local, common]).reshape(-1, LANES), "dp", n_dp).reshape(-1)
    local = small[:split_at]
    common = all_sum(small[split_at:].reshape(-1, LANES), "tensor", n_t).reshape(-1)
    taps = local[: 5 * ip].reshape(5, ip)
    lanes = local[5 * ip : 7 * ip].reshape(2, ip)
    head_sums = local[7 * ip :].reshape(2, LANES)
    shared_taps = common[: 10 * state].reshape(5, 2 * state)
    norm_gain_grad = common[10 * state :]

    hat = nc * norm_gain
    input_grad = (
        out_cotangent.astype(F32)
        + inv_root * hat
        - block_input
        * (inv_root * inv_root * inv_root)
        * jnp.mean(hat * block_input, axis=1, keepdims=True)
    )
    return (
        block_output,
        input_grad,
        norm_gain_grad,
        gate_proj_grad,
        value_proj_grad,
        shared_proj_grad,
        step_proj_grad,
        taps[:4, :inner],
        taps[4, :inner],
        shared_taps[:4],
        shared_taps[4],
        head_sums[0, :heads],
        head_sums[1, :heads] * rate,
        jnp.sum(lanes[1, :inner].reshape(heads, hd), axis=1),
        lanes[0, :inner],
        output_proj_grad,
    )


def solution(mesh):
    n_dp, n_t = mesh.shape["dp"], mesh.shape["tensor"]
    both = ("dp", "tensor")
    return jax.shard_map(
        functools.partial(body, n_dp, n_t),
        mesh=mesh,
        in_specs=(
            P(both, None),
            P("dp", None),
            P(),
            P("dp", "tensor"),
            P("dp", "tensor"),
            P("dp", None),
            P("dp", "tensor"),
            P(None, "tensor"),
            P("tensor"),
            P(),
            P(),
            P("tensor"),
            P("tensor"),
            P("tensor"),
            P("tensor"),
            P("tensor", "dp"),
            P(both, None),
        ),
        out_specs=(
            P(both, None),
            P(both, None),
            P(),
            P("dp", "tensor"),
            P("dp", "tensor"),
            P("dp", None),
            P("dp", "tensor"),
            P(None, "tensor"),
            P("tensor"),
            P(),
            P(),
            P("tensor"),
            P("tensor"),
            P("tensor"),
            P("tensor"),
            P("tensor", "dp"),
        ),
        check_vma=False,
    )
```

```python
import functools
import math

import jax
import jax.numpy as jnp
from jax import lax
from jax.experimental import pallas as pl
from jax.experimental.pallas import tpu as pltpu
from jax.sharding import PartitionSpec as P


BLOCK = 256
LANES = 128
EPS = 1e-05
LOG2E = math.log2(math.e)
FAR = -1e30
F32 = jnp.float32
BF16 = jnp.bfloat16

MM = (((1,), (0,)), ((), ()))
MT = (((1,), (1,)), ((), ()))
TM = (((0,), (0,)), ((), ()))


def dot(a, b, dims=MM):
    return lax.dot_general(a, b, dims, preferred_element_type=F32)


def dot_split(exact, values, dims=MM):
    high = values.astype(BF16)
    low = (values - high.astype(F32)).astype(BF16)
    return dot(exact, high, dims) + dot(exact, low, dims)


def split_dot(values, exact, dims=MM):
    high = values.astype(BF16)
    low = (values - high.astype(F32)).astype(BF16)
    return dot(high, exact, dims) + dot(low, exact, dims)


def up(n, to=LANES):
    return -(-n // to) * to


def softplus(v):
    return jnp.maximum(v, 0.0) + jnp.log1p(jnp.exp(-jnp.abs(v)))


def sigmoid(v):
    return 1.0 / (1.0 + jnp.exp(-v))


def colsum(v):
    return jnp.sum(v.reshape(v.shape[0] // 8, 8, v.shape[1]), axis=0)


def spread(cols, pair, hd):
    per = LANES // hd
    lane = lax.broadcasted_iota(jnp.int32, (cols.shape[0], LANES), 1)
    out = jnp.broadcast_to(cols[:, pair * per : pair * per + 1], lane.shape)
    for j in range(1, per):
        col = cols[:, pair * per + j : pair * per + j + 1]
        out = jnp.where(lane >= j * hd, jnp.broadcast_to(col, lane.shape), out)
    return out


def columns_of(rows):
    pad = jnp.zeros((LANES - rows.shape[0], rows.shape[1]), F32)
    return jnp.concatenate([rows, pad], axis=0).T


class Dims:
    def __init__(self, n_dp, n_t, length, width, inner, hd, state, part_rows, chunk_rows):
        self.length, self.width, self.state, self.hd = length, width, state, hd
        self.n_dp, self.n_t, self.n_hi = n_dp, n_t, n_dp // 2
        self.ip = up(inner)
        self.vs = self.ip + 2 * state
        self.np = self.ip + self.vs + LANES
        self.wc = self.np + self.ip
        self.blocks = length // BLOCK
        self.part_rows, self.chunk_rows = part_rows, chunk_rows
        self.pairs = self.ip // LANES
        self.per = LANES // hd
        self.halves = 2 if n_t == 4 and chunk_rows == 2 * BLOCK else 1
        self.piece_rows = chunk_rows // self.halves
        self.pieces = n_t * self.halves
        self.at_n = n_dp
        self.at_c = self.at_n + self.pieces
        self.at_keep = self.at_c + n_t
        self.at_rel = self.at_keep + self.blocks
        self.at_group = self.at_rel + self.blocks
        self.at_slot = self.at_group + self.blocks
        self.at_hi = self.at_slot + self.blocks
        self.at_core = self.at_hi + self.n_hi


def load_parts(refs, target, sems, scalars, first, rows):
    return [
        pltpu.make_async_copy(
            ref, target.at[pl.ds(pl.multiple_of(scalars[first + k], rows), rows), :], sems.at[k]
        )
        for k, ref in enumerate(refs)
    ]


def decay_parts(raw, hp_ref, cols, tri):
    delta = softplus(raw + hp_ref[0:1, :])
    logs = dot_split(tri, delta * (hp_ref[1:2, :] * LOG2E))
    enter = jnp.exp2(logs) * cols[:, 7:8]
    ending = jnp.exp2(logs[BLOCK - 1 :, :] - logs) * cols[:, 8:9]
    return delta, logs, enter, ending


def norm_kernel(steps, x_ref, gain_ref, *outs):
    x = x_ref[...]
    root = lax.rsqrt(jnp.mean(x * x, axis=1, keepdims=True) + EPS)
    normed = (x * root * gain_ref[...]).astype(BF16)
    for k, out in enumerate(outs):

        @pl.when(pl.program_id(0) // steps == k)
        def _():
            out[...] = normed


def pack_kernel(dm, gate_ref, value_ref, shared_ref, step_ref, outp_ref, out_ref):
    out_ref[...] = jnp.zeros_like(out_ref)
    inner, heads, r = gate_ref.shape[1], step_ref.shape[0], step_ref.shape[1]
    row = lax.broadcasted_iota(jnp.int32, (r, r), 0)
    col = lax.broadcasted_iota(jnp.int32, (r, r), 1)
    eye = jnp.where(row == col, 1.0, 0.0).astype(BF16)
    out_ref[:, :inner] = gate_ref[...]
    out_ref[:, dm.ip : dm.ip + inner] = value_ref[...]
    out_ref[:, 2 * dm.ip : dm.ip + dm.vs] = shared_ref[...]
    out_ref[:, dm.ip + dm.vs : dm.ip + dm.vs + heads] = dot(eye, step_ref[...], MT).astype(BF16)
    out_ref[:, dm.np : dm.np + inner] = outp_ref[...]


def forward_kernel(dm, scalars, *refs):
    q, ip, vs, st, hd = BLOCK, dm.ip, dm.vs, dm.state, dm.hd
    w_parts = refs[: dm.n_dp]
    n_parts = refs[dm.n_dp : dm.n_dp + dm.pieces]
    rest = refs[dm.n_dp + dm.pieces :]
    rows_ref, conv_ref, hp_ref, lane_ref = rest[:4]
    (g_out, v_out, cv_out, ys_out, st_out, h_out, sum_out, nt_out, sg_out, w_out) = rest[4:14]
    (w_v, nm_v, h_ref, vbuf, tri_ref, bias_ref, w_sem, n_sem, o_sem) = rest[14:]
    i = pl.program_id(0)
    at = pl.ds(pl.multiple_of(i * q, q), q)
    save = pltpu.make_async_copy(w_v, w_out, o_sem)

    @pl.when(i == 0)
    def _():
        copies = load_parts(w_parts, w_v, w_sem, scalars, 0, dm.part_rows)
        copies += load_parts(n_parts, nm_v, n_sem, scalars, dm.at_n, dm.piece_rows)
        for copy in copies:
            copy.start()
        h_ref[...] = jnp.zeros_like(h_ref)
        vbuf[...] = jnp.zeros_like(vbuf)
        r = lax.broadcasted_iota(jnp.int32, (q, q), 0)
        c = lax.broadcasted_iota(jnp.int32, (q, q), 1)
        tri_ref[...] = jnp.where(r >= c, 1.0, 0.0).astype(BF16)
        for copy in copies:
            copy.wait()
        save.start()

    rows = rows_ref[...]
    cols = columns_of(rows)
    normed = nm_v[at, :]
    nt_out[...] = normed
    projected = dot(normed, w_v[:, : dm.np])
    g_out[...] = projected[:, :ip]
    vbuf[0:8, :] = vbuf[q : q + 8, :]
    vbuf[8 : 8 + q, :] = projected[:, ip : ip + vs]
    v_out[...] = projected[:, ip : ip + vs]
    raw = projected[:, ip + vs :]
    st_out[...] = raw

    acts = []
    for c in range(vs // LANES):
        g = slice(c * LANES, (c + 1) * LANES)
        acc = conv_ref[4:5, g] + conv_ref[3:4, g] * vbuf[8 : 8 + q, g]
        for lag in range(1, 4):
            acc = acc + conv_ref[3 - lag : 4 - lag, g] * (
                vbuf[8 - lag : 8 - lag + q, g] * cols[:, lag : lag + 1]
            )
        cv_out[:, g] = acc
        acts.append(acc * sigmoid(acc))
    in_map = jnp.concatenate(acts[dm.pairs : dm.pairs + st // LANES], axis=1).astype(BF16)
    out_map = jnp.concatenate(acts[dm.pairs + st // LANES :], axis=1).astype(BF16)

    delta, logs, enter, ending = decay_parts(raw, hp_ref, cols, tri_ref[...])
    logs_t = logs.T
    r = lax.broadcasted_iota(jnp.int32, (q, q), 0)
    c = lax.broadcasted_iota(jnp.int32, (q, q), 1)
    bias_ref[...] = jnp.where((r >= c) & (cols[:, 0:1] == rows[0:1, :]), 0.0, FAR)
    scores = dot(out_map, in_map, MT)
    keep = scalars[dm.at_keep + i].astype(F32)
    total = jnp.exp2(logs[q - 1 :, :]) * keep
    lane = lax.broadcasted_iota(jnp.int32, (q, LANES), 1)
    h_out[...] = h_ref[...]
    in_map_t = in_map.T
    squares = jnp.zeros((q, LANES), F32)
    for p in range(dm.pairs):
        g = slice(p * LANES, (p + 1) * LANES)
        x = acts[p]
        u = x * spread(delta, p, hd)
        ub = u.astype(BF16)
        y = None
        for j in range(dm.per):
            h = p * dm.per + j
            decay = jnp.exp2(logs[:, h : h + 1] - logs_t[h : h + 1, :] + bias_ref[...])
            part = dot((decay * scores).astype(BF16), ub)
            y = part if y is None else jnp.where(lane >= j * hd, part, y)
        held = h_ref[:, g]
        y = y + dot(out_map, held.astype(BF16)) * spread(enter, p, hd)
        wu = (u * spread(ending, p, hd)).astype(BF16)
        h_ref[:, g] = held * spread(total, p, hd) + dot(in_map_t, wu)
        ys_out[:, g] = y
        gate = g_out[:, g]
        gated = (y + lane_ref[0:1, g] * x) * (gate * sigmoid(gate))
        sg_out[:, g] = (gated * lane_ref[1:2, g]).astype(BF16)
        squares = squares + gated * gated
    sum_out[...] = jnp.sum(squares.T, axis=0, keepdims=True)

    @pl.when(i == dm.blocks - 1)
    def _():
        save.wait()


def cotangent_kernel(dm, scalars, *refs):
    q = BLOCK
    c_parts = refs[: dm.n_t]
    w_ref, sg_ref, sq_ref = refs[dm.n_t : dm.n_t + 3]
    sc_out, sum_out, ct_out = refs[dm.n_t + 3 : dm.n_t + 6]
    ct_v, c_sem = refs[dm.n_t + 6 :]
    i = pl.program_id(0)

    @pl.when(i == 0)
    def _():
        copies = load_parts(c_parts, ct_v, c_sem, scalars, dm.at_c, dm.chunk_rows)
        for copy in copies:
            copy.start()
        for copy in copies:
            copy.wait()

    cot = ct_v[pl.ds(pl.multiple_of(i * q, q), q), :]
    ct_out[...] = cot
    sc = dot(cot, w_ref[...])
    sc_out[...] = sc.astype(BF16)
    prod = sc * sg_ref[...].astype(F32)
    dots = prod[:, :LANES]
    for p in range(1, dm.pairs):
        dots = dots + prod[:, p * LANES : (p + 1) * LANES]
    sum_out[0:1, :] = sq_ref[...]
    sum_out[1:2, :] = jnp.sum(dots.T, axis=0, keepdims=True)


def branch_kernel(dm, scalars, w_ref, sg_ref, *refs):
    outs, (buf, sem) = refs[: dm.n_t], refs[dm.n_t :]
    i = pl.program_id(0)
    slot = lax.rem(i, 2)
    per = dm.chunk_rows // BLOCK

    def copy(k, at, row):
        return pltpu.make_async_copy(buf.at[at], outs[k].at[row], sem.at[at])

    @pl.when(i >= 2)
    def _():
        copy(0, slot, 0).wait()

    buf[slot] = dot(sg_ref[...], w_ref[...], MT).astype(BF16)
    for k in range(dm.n_t):

        @pl.when(scalars[dm.at_rel + i] == k)
        def _():
            copy(k, slot, lax.rem(i, per)).start()

    @pl.when(i == dm.blocks - 1)
    def _():
        copy(0, 1 - slot, 0).wait()
        copy(0, slot, 0).wait()


def gate_kernel(dm, scalars, *refs):
    q, ip, r = BLOCK, dm.ip, dm.part_rows
    (w_ref, rk_ref, lane_ref, g_in, cv_in, ys_in, sc_in, nm_in, ct_in) = refs[:9]
    dg_out, dy_out, lane_out, rows_out, own_out = refs[9:14]
    z_outs = refs[14 : 13 + dm.n_hi]
    acc, both = refs[13 + dm.n_hi :]
    i = pl.program_id(0)

    @pl.when(i == 0)
    def _():
        lane_out[...] = jnp.zeros_like(lane_out)
        acc[...] = jnp.zeros_like(acc)

    pad = jnp.zeros((LANES - 2, q), F32)
    cols = jnp.concatenate([rk_ref[...], pad], axis=0).T
    root, pull = cols[:, 0:1], cols[:, 1:2]
    for p in range(dm.pairs):
        g = slice(p * LANES, (p + 1) * LANES)
        gate, sc, ys, cv = g_in[:, g], sc_in[:, g].astype(F32), ys_in[:, g], cv_in[:, g]
        x = cv * sigmoid(cv)
        sig = sigmoid(gate)
        z = gate * sig
        y = ys + lane_ref[0:1, g] * x
        gated = y * z
        cot = root * (lane_ref[1:2, g] * sc) - pull * gated
        lane_out[0:8, g] += colsum(sc * gated * root)
        dy = cot * z
        dy_out[:, g] = dy
        dg_out[:, g] = (cot * y * (sig + z * (1.0 - sig))).astype(BF16)
        lane_out[8:16, g] += colsum(dy * x)
        both[:, g] = (gated * lane_ref[1:2, g] * root).astype(BF16)
    acc[:, :ip] += dot(nm_in[...], dg_out[...], TM)
    acc[:, ip:] += dot(ct_in[...], both[...], TM)

    @pl.when(i == dm.blocks - 1)
    def _():
        prod = acc[:, :LANES] * w_ref[:, :LANES].astype(F32)
        for p in range(1, dm.pairs):
            g = slice(p * LANES, (p + 1) * LANES)
            prod = prod + acc[:, g] * w_ref[:, g].astype(F32)
        rows_out[...] = gain_rows(prod)
        hi = scalars[dm.at_hi]
        own_out[...] = acc[pl.ds(pl.multiple_of(hi * 2 * r, 8), 2 * r), :]
        for k, z_out in enumerate(z_outs):
            at = pl.multiple_of(scalars[dm.at_hi + k + 1] * 2 * r, 8)
            z_out[...] = acc[pl.ds(at, 2 * r), :].astype(BF16)


def backward_kernel(dm, scalars, *refs):
    q, ip, vs, st, hd = BLOCK, dm.ip, dm.vs, dm.state, dm.hd
    groups = dm.group_sizes
    w_ref, rows_ref, conv_ref, hp_ref, lane_ref = refs[:5]
    dg_in, dy_in, v_in, cv_in, ys_in, st_in, h_in = refs[5:12]
    pj_out, tap_out, head_out = refs[12:15]
    nc_outs = refs[15 : 15 + len(groups)]
    (w_v, dh_ref, dbuf, tri_ref, bias_ref, ds_ref, u_s, dx_s, act_s, t1_s, t2_s, nc_buf, w_sem, nc_sem) = refs[
        15 + len(groups) :
    ]
    i = pl.program_id(0)
    blk = dm.blocks - 1 - i
    load = pltpu.make_async_copy(w_ref, w_v, w_sem)

    def send(k, at, row):
        return pltpu.make_async_copy(nc_buf.at[at], nc_outs[k].at[row], nc_sem.at[at])

    @pl.when(i == 0)
    def _():
        load.start()
        dh_ref[...] = jnp.zeros_like(dh_ref)
        dbuf[...] = jnp.zeros_like(dbuf)
        tap_out[...] = jnp.zeros_like(tap_out)
        head_out[...] = jnp.zeros_like(head_out)
        r = lax.broadcasted_iota(jnp.int32, (q, q), 0)
        c = lax.broadcasted_iota(jnp.int32, (q, q), 1)
        tri_ref[...] = jnp.where(r >= c, 1.0, 0.0).astype(BF16)

    rows = rows_ref[...]
    cols = columns_of(rows)
    raw = st_in[...]
    tri = tri_ref[...]
    delta, logs, enter, ending = decay_parts(raw, hp_ref, cols, tri)
    logs_t = logs.T
    lane = lax.broadcasted_iota(jnp.int32, (q, LANES), 1)

    acts, slopes = [], []
    for c in range(vs // LANES):
        g = slice(c * LANES, (c + 1) * LANES)
        cv = cv_in[:, g]
        sig = sigmoid(cv)
        act = cv * sig
        acts.append(act)
        slopes.append(sig + act * (1.0 - sig))
    in_map = jnp.concatenate(acts[dm.pairs : dm.pairs + st // LANES], axis=1).astype(BF16)
    out_map = jnp.concatenate(acts[dm.pairs + st // LANES :], axis=1).astype(BF16)

    for p in range(dm.pairs):
        g = slice(p * LANES, (p + 1) * LANES)
        u_s[:, g] = acts[p] * spread(delta, p, hd)

    r = lax.broadcasted_iota(jnp.int32, (q, q), 0)
    c = lax.broadcasted_iota(jnp.int32, (q, q), 1)
    bias_ref[...] = jnp.where((r <= c) & (cols[:, 0:1] == rows[0:1, :]), 0.0, FAR)
    scores = dot(in_map, out_map, MT)
    dh_b = dh_ref[...].astype(BF16)
    h_b = h_in[...].astype(BF16)
    out_map_t = out_map.T
    keep = scalars[dm.at_keep + blk].astype(F32)
    total = jnp.exp2(logs[q - 1 :, :]) * keep
    d_in = jnp.zeros((q, st), F32)
    d_out = jnp.zeros((q, st), F32)
    for p in range(dm.pairs):
        g = slice(p * LANES, (p + 1) * LANES)
        u, dy = u_s[:, g], dy_in[:, g]
        ub, dyb = u.astype(BF16), dy.astype(BF16)
        du = None
        for j in range(dm.per):
            h = p * dm.per + j
            mine = (lane >= j * hd) & (lane < (j + 1) * hd)
            decay = jnp.exp2(logs_t[h : h + 1, :] - logs[:, h : h + 1] + bias_ref[...])
            part = dot((decay * scores).astype(BF16), dyb)
            du = part if du is None else jnp.where(lane >= j * hd, part, du)
            dm_t = dot(jnp.where(mine, u, 0.0).astype(BF16), dyb, MT)
            if p == 0 and j == 0:
                ds_ref[...] = dm_t * decay
            else:
                ds_ref[...] += dm_t * decay
        end_e = spread(ending, p, hd)
        late = end_e * dot(in_map, dh_b[:, g])
        du = du + late
        wu = (u * end_e).astype(BF16)
        edy = (dy * spread(enter, p, hd)).astype(BF16)
        d_in = d_in + dot(wu, dh_b[:, g], MT)
        d_out = d_out + dot(edy, h_b[:, g], MT)
        u32 = ub.astype(F32)
        t1_s[:, g] = dyb.astype(F32) * ys_in[:, g] - u32 * du
        t2_s[:, g] = du * acts[p]
        kept = dh_ref[:, g] * spread(total, p, hd)
        act_s[:, g] = colsum(u32 * late) + colsum(h_in[:, g] * kept)
        dh_ref[:, g] = kept + dot(out_map_t, edy)
        dx_s[:, g] = (spread(delta, p, hd) * du + lane_ref[0:1, g] * dy) * slopes[p]
    ds_b = ds_ref[...].astype(BF16)
    d_in = d_in + dot(ds_b, out_map)
    d_out = d_out + dot(ds_b, in_map, TM)

    hr = lax.broadcasted_iota(jnp.int32, (ip, LANES), 0)
    hc = lax.broadcasted_iota(jnp.int32, (ip, LANES), 1)
    pick = jnp.where(hr // hd == hc, 1.0, 0.0).astype(BF16)
    d_log = split_dot(t1_s[...], pick)
    last = split_dot(jnp.sum(act_s[...], axis=0, keepdims=True), pick)
    row = lax.broadcasted_iota(jnp.int32, (q, LANES), 0)
    d_log = d_log + jnp.where(row == q - 1, last, 0.0)
    d_step = dot_split(tri, d_log, TM)
    head_out[8:16, :] += colsum(d_step * delta)
    d_delta = hp_ref[1:2, :] * d_step + split_dot(t2_s[...], pick)
    d_raw = d_delta * sigmoid(raw + hp_ref[0:1, :])
    head_out[0:8, :] += colsum(d_raw)
    pj_out[:, vs:] = d_raw.astype(BF16)

    dbuf[q : q + 8, :] = dbuf[0:8, :]
    for c in range(vs // LANES):
        g = slice(c * LANES, (c + 1) * LANES)
        if c < dm.pairs:
            dbuf[0:q, g] = dx_s[:, g]
        else:
            k = (c - dm.pairs) * LANES
            source = d_in[:, k : k + LANES] if k < st else d_out[:, k - st : k - st + LANES]
            dbuf[0:q, g] = source * slopes[c]
    for c in range(vs // LANES):
        g = slice(c * LANES, (c + 1) * LANES)
        v = v_in[:, g]
        shifted = dbuf[0:q, g]
        tap_out[32:40, g] += colsum(shifted)
        tap_out[24:32, g] += colsum(shifted * v)
        dv = conv_ref[3:4, g] * shifted
        for lag in range(1, 4):
            shifted = dbuf[lag : lag + q, g] * cols[:, 3 + lag : 4 + lag]
            tap_out[24 - 8 * lag : 32 - 8 * lag, g] += colsum(shifted * v)
            dv = dv + conv_ref[3 - lag : 4 - lag, g] * shifted
        pj_out[:, g] = dv.astype(BF16)

    @pl.when(i == 0)
    def _():
        load.wait()

    slot = lax.rem(i, 2)

    @pl.when(i >= 2)
    def _():
        send(0, slot, 0).wait()

    nc = dot(dg_in[...], w_v[:, :ip], MT) + dot(pj_out[...], w_v[:, ip : dm.np], MT)
    nc_buf[slot] = nc.astype(BF16)
    for k in range(len(groups)):

        @pl.when(scalars[dm.at_group + blk] == k)
        def _():
            send(k, slot, scalars[dm.at_slot + blk]).start()

    @pl.when(i == dm.blocks - 1)
    def _():
        send(0, 1 - slot, 0).wait()
        send(0, slot, 0).wait()


def joined_kernel(dm, scalars, nm_ref, pj_ref, w_ref, taps_ref, lanes_ref, heads_ref, rows_ref, *refs):
    mine_out, theirs_out, small_out, acc = refs
    n = pl.program_id(0)
    r = dm.part_rows

    @pl.when(n == 0)
    def _():
        acc[...] = jnp.zeros_like(acc)

    acc[...] += dot(nm_ref[...], pj_ref[...], TM)

    @pl.when(n == pl.num_programs(0) - 1)
    def _():
        core = scalars[dm.at_core]
        for h in range(dm.n_hi):
            at = pl.multiple_of((2 * h + core) * r, 8)
            mine_out[h] = acc[pl.ds(at, r), :]
            at = pl.multiple_of((2 * h + 1 - core) * r, 8)
            theirs_out[h] = acc[pl.ds(at, r), :].astype(BF16)
        small_out[...] = jnp.zeros_like(small_out)
        row = 0

        def put(v):
            nonlocal row
            for c in range(v.shape[1] // LANES):
                small_out[row : row + 1, :] = jnp.sum(
                    v[:, c * LANES : (c + 1) * LANES], axis=0, keepdims=True
                )
                row += 1

        for k in range(5):
            put(taps_ref[8 * k : 8 * k + 8, : dm.ip])
        for k in range(2):
            put(lanes_ref[8 * k : 8 * k + 8, :])
        for k in range(2):
            put(heads_ref[8 * k : 8 * k + 8, :])
        row = dm.local_rows
        for k in range(5):
            put(taps_ref[8 * k : 8 * k + 8, dm.ip :])
        prod = acc[:, :LANES] * w_ref[:, dm.ip : dm.ip + LANES].astype(F32)
        for p in range(1, (dm.vs + LANES) // LANES):
            g = slice(p * LANES, (p + 1) * LANES)
            o = slice(dm.ip + p * LANES, dm.ip + (p + 1) * LANES)
            prod = prod + acc[:, g] * w_ref[:, o].astype(F32)
        put(gain_rows(prod) + rows_ref[...])


def gain_rows(acc):
    high = acc.astype(BF16)
    rest = acc - high.astype(F32)
    mid = rest.astype(BF16)
    low = (rest - mid.astype(F32)).astype(BF16)
    one = jnp.ones((8, LANES), BF16)
    return (dot(one, high, MT) + dot(one, mid, MT) + dot(one, low, MT)) * 0.125


def pair_kernel(scalars, mine_ref, theirs_ref, own_out, *outs):
    k = pl.program_id(0)
    both = mine_ref[...] + theirs_ref[...].astype(F32)

    @pl.when(k == 0)
    def _():
        own_out[...] = both

    for j, out in enumerate(outs):

        @pl.when(k == j + 1)
        def _():
            out[...] = both.astype(BF16)


def early_kernel(dm, scalars, own_ref, *refs):
    parts, (mine_out, theirs_out, total) = refs[: dm.n_hi - 1], refs[dm.n_hi - 1 :]
    r = dm.part_rows
    both = own_ref[...]
    for part in parts:
        both = both + part[...].astype(F32)
    total[...] = both
    core = scalars[dm.at_core]
    mine_out[...] = total[pl.ds(pl.multiple_of(core * r, 8), r), :]
    theirs_out[...] = total[pl.ds(pl.multiple_of((1 - core) * r, 8), r), :].astype(BF16)


def grads_kernel(dm, own_ref, mine_ref, theirs_ref, *refs):
    parts, outs = refs[: dm.n_hi - 1], refs[dm.n_hi - 1 :]
    gate_out, value_out, step_out, outp_out, shared_out = outs
    total = own_ref[...]
    for part in parts:
        total = total + part[...].astype(F32)
    early = mine_ref[...] + theirs_ref[...].astype(F32)
    inner, heads = gate_out.shape[1], step_out.shape[1]
    gate_out[...] = early[:, :inner]
    outp_out[...] = early[:, dm.ip : dm.ip + inner]
    value_out[...] = total[:, :inner]
    shared_out[...] = total[:, dm.ip : dm.vs]
    step_out[...] = total[:, dm.vs : dm.vs + heads]


def input_kernel(sets, steps, x_ref, cot_ref, gain_ref, *refs):
    out = refs[-1]
    x = x_ref[...]
    root = lax.rsqrt(jnp.mean(x * x, axis=1, keepdims=True) + EPS)
    first = 0
    for k, count in enumerate(sets):
        parts = refs[first : first + count]
        first += count

        @pl.when(pl.program_id(0) // steps == k)
        def _():
            nc = parts[0][...].astype(F32)
            for part in parts[1:]:
                nc = nc + part[...].astype(F32)
            hat = nc * gain_ref[...]
            mean = jnp.mean(hat * x, axis=1, keepdims=True)
            out[...] = cot_ref[...].astype(F32) + root * hat - x * (root * root * root * mean)


def shift_hi(n, k):
    return [(i, ((i // 2 + k) % (n // 2)) * 2 + i % 2) for i in range(n)]


def swap(n, k):
    return [(i, i ^ k) for i in range(n)]


def all_sum(v, axis, n):
    k = 1
    while k < n:
        v = v + lax.ppermute(v, axis, swap(n, k))
        k *= 2
    return v


def pad_cols(v, to):
    return jnp.pad(v, ((0, 0), (0, to - v.shape[1])))


def pad_vec(v, to):
    return jnp.pad(v, (0, to - v.shape[0]))


def body(
    n_dp,
    n_t,
    block_input,
    segment_ids,
    norm_gain,
    gate_proj,
    value_proj,
    shared_proj,
    step_proj,
    conv_value_weight,
    conv_value_bias,
    conv_shared_weight,
    conv_shared_bias,
    step_bias,
    decay_log,
    skip_weight,
    gate_gain,
    output_proj,
    out_cotangent,
):
    q = BLOCK
    chunk_rows, width = block_input.shape
    length = segment_ids.shape[1]
    inner, heads = gate_proj.shape[1], step_proj.shape[1]
    part_rows = gate_proj.shape[0]
    state = shared_proj.shape[1] // 2
    hd = inner // heads
    dm = Dims(n_dp, n_t, length, width, inner, hd, state, part_rows, chunk_rows)
    ip, vs, nb, n_hi = dm.ip, dm.vs, dm.blocks, dm.n_hi
    dm.local_rows = up(7 * dm.pairs + 2, 8)
    dm.small_rows = up(dm.local_rows + 10 * state // LANES + width // LANES, 8)
    me_t = lax.axis_index("tensor")
    me_dp = lax.axis_index("dp")
    hi, core = me_dp // 2, me_dp % 2

    def across(v, k):
        return lax.ppermute(v, "tensor", swap(n_t, k))

    def along(v, k):
        return lax.ppermute(v, "dp", shift_hi(n_dp, k))

    def partner(v):
        return lax.ppermute(v, "dp", swap(n_dp, 1))

    def vmem(shape, dtype):
        return pltpu.VMEM(shape, dtype)

    limit = 60 * 1024 * 1024
    params = pltpu.CompilerParams(dimension_semantics=("arbitrary",), vmem_limit_bytes=limit)
    hbm = pl.BlockSpec(memory_space=pl.ANY)

    def out(*shape, dtype=F32):
        return jax.ShapeDtypeStruct(shape, dtype)

    gain = norm_gain.reshape(1, width)
    part = min(LANES, dm.piece_rows)
    steps = dm.piece_rows // part

    def turn(k, rows=part):
        return pl.BlockSpec(
            (rows, width), lambda i: (jnp.clip(i - k * steps, 0, steps - 1), 0)
        )

    normed = pl.pallas_call(
        functools.partial(norm_kernel, steps),
        out_shape=[out(dm.piece_rows, width, dtype=BF16)] * dm.halves,
        grid=(dm.halves * steps,),
        in_specs=[
            pl.BlockSpec((part, width), lambda i: (i, 0)),
            pl.BlockSpec((1, width), lambda i: (0, 0)),
        ],
        out_specs=[turn(k) for k in range(dm.halves)],
        compiler_params=params,
        name="normalize",
    )(block_input, gain)
    if dm.halves == 2:
        a, b = normed
        xa, yb = across(a, 1), across(b, 2)
        ya, xb = across(a, 2), across(b, 1)
        n_list = [a, b, xa, xb, ya, yb, across(xa, 2), across(yb, 1)]
        n_rows = jnp.concatenate(
            [(me_t ^ k) * chunk_rows + jnp.arange(2) * dm.piece_rows for k in range(4)]
        )
    else:
        n_list = [normed[0]] + [across(normed[0], k) for k in range(1, n_t)]
        n_rows = (me_t ^ jnp.arange(n_t)) * chunk_rows
    packed = pl.pallas_call(
        functools.partial(pack_kernel, dm),
        out_shape=out(part_rows, dm.wc, dtype=BF16),
        name="pack_weights",
    )(gate_proj, value_proj, shared_proj, step_proj.T, output_proj.T)
    w_list = [packed] + [along(packed, k) for k in range(1, n_hi)]
    w_list = w_list + [partner(part) for part in w_list]

    seg = segment_ids[0]
    segb = seg.reshape(nb, q)
    last = segb[:, -1]
    prev_last = jnp.concatenate([jnp.full((1,), -1, jnp.int32), last[:-1]])
    gap = jnp.full((3,), -1, jnp.int32)
    wide = jnp.concatenate([gap, seg, gap])
    rows = [seg.astype(F32)]
    rows += [(wide[3 - k : 3 - k + length] == seg).astype(F32) for k in range(1, 4)]
    rows += [(wide[3 + k : 3 + k + length] == seg).astype(F32) for k in range(1, 4)]
    rows += [
        (segb == prev_last[:, None]).astype(F32).reshape(-1),
        (segb == last[:, None]).astype(F32).reshape(-1),
    ]
    rows = jnp.concatenate([jnp.stack(rows), jnp.zeros((16 - len(rows), length), F32)], axis=0)
    keep = (last == prev_last).astype(jnp.int32)
    other = (hi - jnp.arange(n_hi)) % n_hi
    rel = (jnp.arange(nb) * q // chunk_rows) ^ me_t
    half = jnp.arange(nb) % (chunk_rows // q)
    if dm.halves == 2:
        group_of = jnp.array([[2, 2], [0, 2], [2, 1], [0, 1]])
        slot_of = jnp.array([[0, 2], [0, 3], [1, 0], [1, 1]])
        group, slot = group_of[rel, half], slot_of[rel, half]
        dm.group_sizes = (2, 2, 4)
    else:
        group, slot = rel, half
        dm.group_sizes = (chunk_rows // q,) * n_t
    scalars = jnp.concatenate(
        [
            (other * 2 + core) * part_rows,
            (other * 2 + 1 - core) * part_rows,
            n_rows,
            (me_t ^ jnp.arange(n_t)) * chunk_rows,
            keep,
            rel,
            group,
            slot,
            (hi + jnp.arange(n_hi)) % n_hi,
            core[None],
        ]
    ).astype(jnp.int32)

    conv = jnp.concatenate(
        [
            pad_cols(jnp.concatenate([conv_value_weight, conv_value_bias[None]]), ip),
            jnp.concatenate([conv_shared_weight, conv_shared_bias[None]]),
        ],
        axis=1,
    )
    conv = jnp.pad(conv, ((0, 3), (0, 0)))
    rate = -jnp.exp(decay_log)
    per_head = jnp.stack([pad_vec(step_bias, LANES), pad_vec(rate, LANES)])
    per_head = jnp.pad(per_head, ((0, 6), (0, 0)))
    per_lane = jnp.stack([pad_vec(jnp.repeat(skip_weight, hd), ip), pad_vec(gate_gain, ip)])
    per_lane = jnp.pad(per_lane, ((0, 6), (0, 0)))

    def const(*shape):
        return pl.BlockSpec(shape, lambda i, s: (0,) * len(shape))

    def fblock(cols):
        return pl.BlockSpec((q, cols), lambda i, s: (i, 0))

    def fsum(k):
        return pl.BlockSpec((None, k, q), lambda i, s: (i, 0, 0))

    def grid(steps, in_specs, out_specs, scratch):
        return pltpu.PrefetchScalarGridSpec(
            num_scalar_prefetch=1,
            grid=(steps,),
            in_specs=in_specs,
            out_specs=out_specs,
            scratch_shapes=scratch,
        )

    (gate, value, conved, scan, steps_raw, held, squares, normed_all, scaled, weights) = pl.pallas_call(
        functools.partial(forward_kernel, dm),
        out_shape=[
            out(length, ip),
            out(length, vs),
            out(length, vs),
            out(length, ip),
            out(length, LANES),
            out(nb * state, ip),
            out(nb, 1, q),
            out(length, width, dtype=BF16),
            out(length, ip, dtype=BF16),
            out(width, dm.wc, dtype=BF16),
        ],
        grid_spec=grid(
            nb,
            [hbm] * (n_dp + dm.pieces)
            + [
                pl.BlockSpec((16, q), lambda i, s: (0, i)),
                const(8, vs),
                const(8, LANES),
                const(8, ip),
            ],
            [
                fblock(ip),
                fblock(vs),
                fblock(vs),
                fblock(ip),
                fblock(LANES),
                pl.BlockSpec((state, ip), lambda i, s: (i, 0)),
                fsum(1),
                fblock(width),
                fblock(ip),
                hbm,
            ],
            [
                vmem((width, dm.wc), BF16),
                vmem((length, width), BF16),
                vmem((state, ip), F32),
                vmem((q + 8, vs), F32),
                vmem((q, q), BF16),
                vmem((q, q), F32),
                pltpu.SemaphoreType.DMA((n_dp,)),
                pltpu.SemaphoreType.DMA((dm.pieces,)),
                pltpu.SemaphoreType.DMA,
            ],
        ),
        compiler_params=params,
        cost_estimate=pl.CostEstimate(
            flops=30_000_000_000, bytes_accessed=30_000_000, transcendentals=0
        ),
        name="block_forward",
    )(scalars, *w_list, *n_list, rows, conv, per_head, per_lane)

    c_list = [out_cotangent] + [across(out_cotangent, k) for k in range(1, n_t)]
    w_cols = pl.BlockSpec((width, ip), lambda i, s: (0, dm.np // ip))
    sc, sums, cot_all = pl.pallas_call(
        functools.partial(cotangent_kernel, dm),
        out_shape=[
            out(length, ip, dtype=BF16),
            out(nb, 2, q),
            out(length, width, dtype=BF16),
        ],
        grid_spec=grid(
            nb,
            [hbm] * n_t + [w_cols, fblock(ip), fsum(1)],
            [fblock(ip), fsum(2), fblock(width)],
            [vmem((length, width), BF16), pltpu.SemaphoreType.DMA((n_t,))],
        ),
        compiler_params=params,
        cost_estimate=pl.CostEstimate(
            flops=3_000_000_000, bytes_accessed=10_000_000, transcendentals=0
        ),
        name="branch_cotangent",
    )(scalars, *c_list, weights, scaled, squares)
    total = sums
    for k in range(1, n_t):
        total = total + across(sums, k)
    branch = pl.pallas_call(
        functools.partial(branch_kernel, dm),
        out_shape=[out(chunk_rows // q, q, width, dtype=BF16)] * n_t,
        grid_spec=grid(
            nb,
            [w_cols, fblock(ip)],
            [hbm] * n_t,
            [vmem((2, q, width), BF16), pltpu.SemaphoreType.DMA((2,))],
        ),
        compiler_params=params,
        cost_estimate=pl.CostEstimate(
            flops=3_000_000_000, bytes_accessed=10_000_000, transcendentals=0
        ),
        name="branch_output",
    )(scalars, weights, scaled)
    root = lax.rsqrt(total[:, 0] / (inner * n_t) + EPS)
    pull = root * root * root * (total[:, 1] / (inner * n_t))
    rk = jnp.stack([root, pull], axis=1)
    branch_sum = branch[0].astype(F32)
    for k in range(1, n_t):
        branch_sum = branch_sum + across(branch[k], k).astype(F32)
    own_root = lax.dynamic_slice_in_dim(root.reshape(length), me_t * chunk_rows, chunk_rows)
    block_output = block_input + own_root[:, None] * branch_sum.reshape(chunk_rows, width)

    def bblock(cols):
        return pl.BlockSpec((q, cols), lambda i, s: (nb - 1 - i, 0))

    dgate, dscan, lanes, gate_rows, own_early, *early = pl.pallas_call(
        functools.partial(gate_kernel, dm),
        out_shape=[
            out(length, ip, dtype=BF16),
            out(length, ip),
            out(16, ip),
            out(8, width),
            out(2 * part_rows, 2 * ip),
        ]
        + [out(2 * part_rows, 2 * ip, dtype=BF16)] * (n_hi - 1),
        grid_spec=grid(
            nb,
            [
                const(width, ip),
                fsum(2),
                const(8, ip),
                fblock(ip),
                fblock(ip),
                fblock(ip),
                fblock(ip),
                fblock(width),
                fblock(width),
            ],
            [fblock(ip), fblock(ip), const(16, ip), const(8, width)]
            + [const(2 * part_rows, 2 * ip)] * n_hi,
            [vmem((width, 2 * ip), F32), vmem((q, ip), BF16)],
        ),
        compiler_params=params,
        cost_estimate=pl.CostEstimate(
            flops=6_000_000_000, bytes_accessed=20_000_000, transcendentals=0
        ),
        name="gate_backward",
    )(scalars, weights, rk, per_lane, gate, conved, scan, sc, normed_all, cot_all)
    early = [along(v, k + 1) for k, v in enumerate(early)]

    proj_cot, taps, head_sums, *nc = pl.pallas_call(
        functools.partial(backward_kernel, dm),
        out_shape=[out(length, vs + LANES, dtype=BF16), out(40, vs), out(16, LANES)]
        + [out(k, q, width, dtype=BF16) for k in dm.group_sizes],
        grid_spec=grid(
            nb,
            [
                hbm,
                pl.BlockSpec((16, q), lambda i, s: (0, nb - 1 - i)),
                const(8, vs),
                const(8, LANES),
                const(8, ip),
                bblock(ip),
                bblock(ip),
                bblock(vs),
                bblock(vs),
                bblock(ip),
                bblock(LANES),
                pl.BlockSpec((state, ip), lambda i, s: (nb - 1 - i, 0)),
            ],
            [bblock(vs + LANES), const(40, vs), const(16, LANES)] + [hbm] * len(dm.group_sizes),
            [
                vmem((width, dm.wc), BF16),
                vmem((state, ip), F32),
                vmem((q + 8, vs), F32),
                vmem((q, q), BF16),
                vmem((q, q), F32),
                vmem((q, q), F32),
                vmem((q, ip), F32),
                vmem((q, ip), F32),
                vmem((8, ip), F32),
                vmem((q, ip), F32),
                vmem((q, ip), F32),
                vmem((2, q, width), BF16),
                pltpu.SemaphoreType.DMA,
                pltpu.SemaphoreType.DMA((2,)),
            ],
        ),
        compiler_params=params,
        cost_estimate=pl.CostEstimate(
            flops=40_000_000_000, bytes_accessed=30_000_000, transcendentals=0
        ),
        name="block_backward",
    )(scalars, weights, rows, conv, per_head, per_lane, dgate, dscan, value, conved, scan, steps_raw, held)

    def slot_of_piece(k, at):
        return pl.BlockSpec(
            (None, part, width), lambda i: (at, jnp.clip(i - k * steps, 0, steps - 1), 0)
        )

    if dm.halves == 2:
        from_x, from_y, stay = across(nc[0], 1), across(nc[1], 2), nc[2]
        pass_y = (stay[1].astype(F32) + from_x[1].astype(F32)).astype(BF16)
        pass_x = (stay[3].astype(F32) + from_y[1].astype(F32)).astype(BF16)
        got_y, got_x = across(pass_y, 2), across(pass_x, 1)
        sets = (3, 3)
        terms = [stay, from_x, got_y, stay, from_y, got_x]
        specs = [slot_of_piece(0, 0), slot_of_piece(0, 0), turn(0)]
        specs += [slot_of_piece(1, 2), slot_of_piece(1, 0), turn(1)]
    else:
        sets = (n_t,)
        terms = [nc[0]] + [across(nc[k], k) for k in range(1, n_t)]
        terms = [v.reshape(chunk_rows, width) for v in terms]
        specs = [turn(0)] * n_t
    in_turn = pl.BlockSpec((part, width), lambda i: (i, 0))
    input_grad = pl.pallas_call(
        functools.partial(input_kernel, sets, steps),
        out_shape=out(chunk_rows, width),
        grid=(len(sets) * steps,),
        in_specs=[in_turn, in_turn, pl.BlockSpec((1, width), lambda i: (0, 0))] + specs,
        out_specs=in_turn,
        compiler_params=params,
        name="input_gradient",
    )(block_input, out_cotangent, gain, *terms)

    late = vs + LANES
    k_rows = 2 * q
    mine, theirs, small = pl.pallas_call(
        functools.partial(joined_kernel, dm),
        out_shape=[
            out(n_hi, part_rows, late),
            out(n_hi, part_rows, late, dtype=BF16),
            out(dm.small_rows, LANES),
        ],
        grid_spec=grid(
            length // k_rows,
            [
                pl.BlockSpec((k_rows, width), lambda i, s: (i, 0)),
                pl.BlockSpec((k_rows, late), lambda i, s: (i, 0)),
                const(width, dm.wc),
                const(40, vs),
                const(16, ip),
                const(16, LANES),
                const(8, width),
            ],
            [
                const(n_hi, part_rows, late),
                const(n_hi, part_rows, late),
                const(dm.small_rows, LANES),
            ],
            [vmem((width, late), F32)],
        ),
        compiler_params=params,
        cost_estimate=pl.CostEstimate(
            flops=6_000_000_000, bytes_accessed=20_000_000, transcendentals=0
        ),
        name="weight_gradients",
    )(scalars, normed_all, proj_cot, weights, taps, lanes, head_sums, gate_rows)

    theirs = partner(theirs)
    by_hi = pl.BlockSpec((None, part_rows, late), lambda i, s: (s[dm.at_hi + i], 0, 0))
    own, *others = pl.pallas_call(
        pair_kernel,
        out_shape=[out(part_rows, late)] + [out(part_rows, late, dtype=BF16)] * (n_hi - 1),
        grid_spec=grid(n_hi, [by_hi, by_hi], [const(part_rows, late)] * n_hi, []),
        compiler_params=params,
        name="core_sum",
    )(scalars, mine, theirs)
    others = [along(v, k + 1) for k, v in enumerate(others)]
    early_spec = const(2 * part_rows, 2 * ip)
    mine, theirs = pl.pallas_call(
        functools.partial(early_kernel, dm),
        out_shape=[out(part_rows, 2 * ip), out(part_rows, 2 * ip, dtype=BF16)],
        grid_spec=grid(
            1,
            [early_spec] * n_hi,
            [const(part_rows, 2 * ip)] * 2,
            [vmem((2 * part_rows, 2 * ip), F32)],
        ),
        compiler_params=params,
        name="early_sum",
    )(scalars, own_early, *early)
    theirs = partner(theirs)
    gate_proj_grad, value_proj_grad, step_proj_grad, outp_t, shared = pl.pallas_call(
        functools.partial(grads_kernel, dm),
        out_shape=[
            out(part_rows, inner),
            out(part_rows, inner),
            out(part_rows, heads),
            out(part_rows, inner),
            out(part_rows, 2 * state),
        ],
        name="gradient_sum",
    )(own, mine, theirs, *others)
    output_proj_grad = outp_t.T

    small = all_sum(small, "dp", n_dp)
    common = all_sum(small[dm.local_rows :], "tensor", n_t)
    shared_b = shared.astype(BF16)
    shared_proj_grad = shared
    for k in range(1, n_t):
        shared_proj_grad = shared_proj_grad + across(shared_b, k).astype(F32)

    flat = small[: dm.local_rows].reshape(-1)
    taps = flat[: 5 * ip].reshape(5, ip)
    lanes = flat[5 * ip : 7 * ip].reshape(2, ip)
    head_sums = flat[7 * ip : 7 * ip + 2 * LANES].reshape(2, LANES)
    flat = common.reshape(-1)
    shared_taps = flat[: 10 * state].reshape(5, 2 * state)
    norm_gain_grad = flat[10 * state : 10 * state + width] / norm_gain
    return (
        block_output,
        input_grad,
        norm_gain_grad,
        gate_proj_grad,
        value_proj_grad,
        shared_proj_grad,
        step_proj_grad,
        taps[:4, :inner],
        taps[4, :inner],
        shared_taps[:4],
        shared_taps[4],
        head_sums[0, :heads],
        head_sums[1, :heads] * rate,
        jnp.sum(lanes[1, :inner].reshape(heads, hd), axis=1),
        lanes[0, :inner],
        output_proj_grad,
    )


def solution(mesh):
    n_dp, n_t = mesh.shape["dp"], mesh.shape["tensor"]
    both = ("dp", "tensor")
    return jax.shard_map(
        functools.partial(body, n_dp, n_t),
        mesh=mesh,
        in_specs=(
            P(both, None),
            P("dp", None),
            P(),
            P("dp", "tensor"),
            P("dp", "tensor"),
            P("dp", None),
            P("dp", "tensor"),
            P(None, "tensor"),
            P("tensor"),
            P(),
            P(),
            P("tensor"),
            P("tensor"),
            P("tensor"),
            P("tensor"),
            P("tensor", "dp"),
            P(both, None),
        ),
        out_specs=(
            P(both, None),
            P(both, None),
            P(),
            P("dp", "tensor"),
            P("dp", "tensor"),
            P("dp", None),
            P("dp", "tensor"),
            P(None, "tensor"),
            P("tensor"),
            P(),
            P(),
            P("tensor"),
            P("tensor"),
            P("tensor"),
            P("tensor"),
            P("tensor", "dp"),
        ),
        check_vma=False,
    )
```

```python
import functools
import math

import jax
import jax.numpy as jnp
from jax import lax
from jax.experimental import pallas as pl
from jax.experimental.pallas import tpu as pltpu
from jax.sharding import PartitionSpec as P


BLOCK = 256
LANES = 128
EPS = 1e-05
LOG2E = math.log2(math.e)
FAR = -1e30
F32 = jnp.float32
BF16 = jnp.bfloat16

MM = (((1,), (0,)), ((), ()))
MT = (((1,), (1,)), ((), ()))
TM = (((0,), (0,)), ((), ()))


def dot(a, b, dims=MM):
    return lax.dot_general(a, b, dims, preferred_element_type=F32)


def dot_split(exact, values, dims=MM):
    high = values.astype(BF16)
    low = (values - high.astype(F32)).astype(BF16)
    return dot(exact, high, dims) + dot(exact, low, dims)


def split_dot(values, exact, dims=MM):
    high = values.astype(BF16)
    low = (values - high.astype(F32)).astype(BF16)
    return dot(high, exact, dims) + dot(low, exact, dims)


def up(n, to=LANES):
    return -(-n // to) * to


def softplus(v):
    return jnp.maximum(v, 0.0) + jnp.log1p(jnp.exp(-jnp.abs(v)))


def sigmoid(v):
    return 0.5 + 0.5 * jnp.tanh(0.5 * v)


def colsum(v):
    return jnp.sum(v.reshape(v.shape[0] // 8, 8, v.shape[1]), axis=0)


def spread(cols, pair, hd):
    per = LANES // hd
    lane = lax.broadcasted_iota(jnp.int32, (cols.shape[0], LANES), 1)
    out = jnp.broadcast_to(cols[:, pair * per : pair * per + 1], lane.shape)
    for j in range(1, per):
        col = cols[:, pair * per + j : pair * per + j + 1]
        out = jnp.where(lane >= j * hd, jnp.broadcast_to(col, lane.shape), out)
    return out


def columns_of(rows):
    pad = jnp.zeros((LANES - rows.shape[0], rows.shape[1]), F32)
    return jnp.concatenate([rows, pad], axis=0).T


class Dims:
    def __init__(self, n_dp, n_t, length, width, inner, hd, state, part_rows, chunk_rows):
        self.length, self.width, self.state, self.hd = length, width, state, hd
        self.n_dp, self.n_t, self.n_hi = n_dp, n_t, n_dp // 2
        self.ip = up(inner)
        self.vs = self.ip + 2 * state
        self.np = self.ip + self.vs + LANES
        self.blocks = length // BLOCK
        self.part_rows, self.chunk_rows = part_rows, chunk_rows
        self.pairs = self.ip // LANES
        self.per = LANES // hd
        self.halves = 2 if n_t == 4 and chunk_rows == 2 * BLOCK else 1
        self.piece_rows = chunk_rows // self.halves
        self.pieces = n_t * self.halves
        self.at_n = n_dp
        self.at_c = self.at_n + self.pieces
        self.at_keep = self.at_c + n_t
        self.at_rel = self.at_keep + self.blocks
        self.at_group = self.at_rel + self.blocks
        self.at_slot = self.at_group + self.blocks
        self.at_hi = self.at_slot + self.blocks
        self.at_core = self.at_hi + self.n_hi
        self.at_from = self.at_core + 1
        self.at_side = self.at_from + self.n_hi
        self.late = self.vs + LANES
        self.local_rows = up(7 * self.pairs + 2, 8)


def load_parts(refs, target, sems, scalars, first, rows):
    return [
        pltpu.make_async_copy(
            ref, target.at[pl.ds(pl.multiple_of(scalars[first + k], rows), rows), :], sems.at[k]
        )
        for k, ref in enumerate(refs)
    ]


def decay_parts(raw, hp_ref, cols, tri):
    delta = softplus(raw + hp_ref[0:1, :])
    logs = dot_split(tri, delta * (hp_ref[1:2, :] * LOG2E))
    enter = jnp.exp2(logs) * cols[:, 7:8]
    ending = jnp.exp2(logs[BLOCK - 1 :, :] - logs) * cols[:, 8:9]
    return delta, logs, enter, ending


def norm_kernel(part, x_hbm, gain_ref, *refs):
    outs, (x_v, sem) = refs[:-2], refs[-2:]
    count = x_v.shape[0] // part
    copies = [
        pltpu.make_async_copy(
            x_hbm.at[pl.ds(k * part, part), :], x_v.at[pl.ds(k * part, part), :], sem.at[k]
        )
        for k in range(count)
    ]
    for copy in copies:
        copy.start()
    rows = outs[0].shape[0]
    for k, copy in enumerate(copies):
        copy.wait()
        x = x_v[k * part : (k + 1) * part]
        root = lax.rsqrt(jnp.mean(x * x, axis=1, keepdims=True) + EPS)
        first = k * part % rows
        outs[k * part // rows][first : first + part] = (x * root * gain_ref[...]).astype(BF16)


def pack_kernel(dm, gate_ref, value_ref, shared_ref, step_ref, out_ref):
    inner, heads, r = gate_ref.shape[1], step_ref.shape[0], step_ref.shape[1]
    if inner != dm.ip:
        out_ref[...] = jnp.zeros_like(out_ref)
    row = lax.broadcasted_iota(jnp.int32, (r, r), 0)
    col = lax.broadcasted_iota(jnp.int32, (r, r), 1)
    eye = jnp.where(row == col, 1.0, 0.0).astype(BF16)
    out_ref[:, :inner] = gate_ref[...]
    out_ref[:, dm.ip : dm.ip + inner] = value_ref[...]
    out_ref[:, 2 * dm.ip : dm.ip + dm.vs] = shared_ref[...]
    out_ref[:, dm.ip + dm.vs :] = jnp.zeros((r, LANES), BF16)
    out_ref[:, dm.ip + dm.vs : dm.ip + dm.vs + heads] = dot(eye, step_ref[...], MT).astype(BF16)


def forward_kernel(dm, scalars, *refs):
    q, ip, vs, st, hd = BLOCK, dm.ip, dm.vs, dm.state, dm.hd
    w_parts = refs[: dm.n_dp]
    n_parts = refs[dm.n_dp : dm.n_dp + dm.pieces]
    rest = refs[dm.n_dp + dm.pieces :]
    rows_ref, conv_ref, hp_ref, lane_ref = rest[:4]
    (g_out, v_out, cv_out, ys_out, st_out, h_out, sum_out, nm_out, sg_out, w_out) = rest[4:14]
    (w_v, nm_v, h_ref, vbuf, tri_ref, bias_ref, pbuf, w_sem, n_sem, o_sem) = rest[14:]
    i = pl.program_id(0)
    save = pltpu.make_async_copy(w_v, w_out, o_sem)

    def rows_at(k):
        return nm_v[pl.ds(pl.multiple_of(k * q, q), q), :]

    @pl.when(i == 0)
    def _():
        copies = load_parts(w_parts, w_v, w_sem, scalars, 0, dm.part_rows)
        copies += load_parts(n_parts, nm_v, n_sem, scalars, dm.at_n, dm.piece_rows)
        for copy in copies:
            copy.start()
        h_ref[...] = jnp.zeros_like(h_ref)
        vbuf[...] = jnp.zeros_like(vbuf)
        r = lax.broadcasted_iota(jnp.int32, (q, q), 0)
        c = lax.broadcasted_iota(jnp.int32, (q, q), 1)
        tri_ref[...] = jnp.where(r >= c, 1.0, 0.0).astype(BF16)
        for copy in copies:
            copy.wait()
        save.start()
        pbuf[...] = dot(nm_v[0:q, :], w_v[...])

    rows = rows_ref[...]
    cols = columns_of(rows)
    nm_out[...] = rows_at(i)
    vbuf[0:8, :] = vbuf[q : q + 8, :]
    vbuf[8 : 8 + q, :] = pbuf[:, ip : ip + vs]
    v_out[...] = pbuf[:, ip : ip + vs].astype(BF16)
    raw = pbuf[:, ip + vs :]
    gates = pbuf[:, :ip].astype(BF16)
    g_out[...] = gates
    st_out[...] = raw
    pbuf[...] = dot(rows_at(jnp.minimum(i + 1, dm.blocks - 1)), w_v[...])

    acts = []
    for c in range(vs // LANES):
        g = slice(c * LANES, (c + 1) * LANES)
        acc = conv_ref[4:5, g] + conv_ref[3:4, g] * vbuf[8 : 8 + q, g]
        for lag in range(1, 4):
            acc = acc + conv_ref[3 - lag : 4 - lag, g] * (
                vbuf[8 - lag : 8 - lag + q, g] * cols[:, lag : lag + 1]
            )
        rounded = acc.astype(BF16)
        cv_out[:, g] = rounded
        acc = rounded.astype(F32)
        acts.append(acc * sigmoid(acc))
    in_map = jnp.concatenate(acts[dm.pairs : dm.pairs + st // LANES], axis=1).astype(BF16)
    out_map = jnp.concatenate(acts[dm.pairs + st // LANES :], axis=1).astype(BF16)

    delta, logs, enter, ending = decay_parts(raw, hp_ref, cols, tri_ref[...])
    logs_t = logs.T
    r = lax.broadcasted_iota(jnp.int32, (q, q), 0)
    c = lax.broadcasted_iota(jnp.int32, (q, q), 1)
    bias_ref[...] = jnp.where((r >= c) & (cols[:, 0:1] == rows[0:1, :]), 0.0, FAR)
    scores = dot(out_map, in_map, MT)
    keep = scalars[dm.at_keep + i].astype(F32)
    total = jnp.exp2(logs[q - 1 :, :]) * keep
    lane = lax.broadcasted_iota(jnp.int32, (q, LANES), 1)
    h_out[...] = h_ref[...]
    in_map_t = in_map.T
    squares = jnp.zeros((q, LANES), F32)
    for p in range(dm.pairs):
        g = slice(p * LANES, (p + 1) * LANES)
        x = acts[p]
        u = x * spread(delta, p, hd)
        ub = u.astype(BF16)
        y = None
        for j in range(dm.per):
            h = p * dm.per + j
            decay = jnp.exp2(logs[:, h : h + 1] - logs_t[h : h + 1, :] + bias_ref[...])
            part = dot((decay * scores).astype(BF16), ub)
            y = part if y is None else jnp.where(lane >= j * hd, part, y)
        held = h_ref[:, g]
        y = y + dot(out_map, held.astype(BF16)) * spread(enter, p, hd)
        wu = (u * spread(ending, p, hd)).astype(BF16)
        h_ref[:, g] = held * spread(total, p, hd) + dot(in_map_t, wu)
        ys_out[:, g] = y
        gate = gates[:, g].astype(F32)
        gated = (y + lane_ref[0:1, g] * x) * (gate * sigmoid(gate))
        sg_out[:, g] = (gated * lane_ref[1:2, g]).astype(BF16)
        squares = squares + gated * gated
    sum_out[...] = jnp.sum(squares.T, axis=0, keepdims=True)

    @pl.when(i == dm.blocks - 1)
    def _():
        save.wait()


def cotangent_kernel(dm, scalars, *refs):
    q, n_dp, n_t = BLOCK, dm.n_dp, dm.n_t
    c_parts, w_parts = refs[:n_t], refs[n_t : n_t + n_dp]
    sg_hbm, sq_ref, sc_hbm, sum_out, ct_hbm, wo_out = refs[n_t + n_dp : n_t + n_dp + 6]
    ct_v, sg_v, sc_v, c_sem, w_sem, g_sem, o_sem, t_sem = refs[n_t + n_dp + 6 :]
    loads = load_parts(w_parts, wo_out, w_sem, scalars, 0, dm.part_rows)
    takes = load_parts(c_parts, ct_v, c_sem, scalars, dm.at_c, dm.chunk_rows)
    whole = pltpu.make_async_copy(sg_hbm, sg_v, g_sem)
    for copy in loads:
        copy.start()
    whole.start()
    for copy in takes:
        copy.start()
    for copy in loads:
        copy.wait()
    whole.wait()
    gives = []
    for k in range(n_t):
        takes[k].wait()
        chunk = pl.multiple_of(scalars[dm.at_c + k], dm.chunk_rows)
        for h in range(dm.chunk_rows // q):
            at = pl.ds(pl.multiple_of(chunk + h * q, q), q)
            sc = dot(ct_v[at, :], wo_out[...])
            sc_v[at, :] = sc.astype(BF16)
            prod = sc * sg_v[at, :].astype(F32)
            dots = prod[:, :LANES]
            for p in range(1, dm.pairs):
                dots = dots + prod[:, p * LANES : (p + 1) * LANES]
            blk = chunk // q + h
            sum_out[blk, 0:1, :] = sq_ref[blk]
            sum_out[blk, 1:2, :] = jnp.sum(dots.T, axis=0, keepdims=True)
        at = pl.ds(chunk, dm.chunk_rows)
        gives.append(pltpu.make_async_copy(sc_v.at[at, :], sc_hbm.at[at, :], o_sem.at[k]))
        gives.append(pltpu.make_async_copy(ct_v.at[at, :], ct_hbm.at[at, :], t_sem.at[k]))
        gives[-1].start()
        gives[-2].start()
    for copy in gives:
        copy.wait()


def branch_kernel(dm, scalars, w_ref, sg_ref, *refs):
    outs, (buf, sem) = refs[: dm.n_t], refs[dm.n_t :]
    per = dm.chunk_rows // BLOCK
    for i in range(dm.blocks):
        at = slice(i * BLOCK, (i + 1) * BLOCK)
        buf[i] = dot(sg_ref[at, :], w_ref[...], MT).astype(BF16)
        for k in range(dm.n_t):

            @pl.when(scalars[dm.at_rel + i] == k)
            def _():
                pltpu.make_async_copy(buf.at[i], outs[k].at[i % per], sem.at[i]).start()

    for i in range(dm.blocks):
        pltpu.make_async_copy(buf.at[i], outs[0].at[0], sem.at[i]).wait()


def gate_kernel(dm, scalars, *refs):
    q, ip, r = BLOCK, dm.ip, dm.part_rows
    (w_ref, rk_ref, lane_ref, g_in, cv_in, ys_in, sc_in, nm_in, ct_in) = refs[:9]
    dg_out, dy_out, lane_out, rows_out, own_out = refs[9:14]
    z_outs = refs[14 : 13 + dm.n_hi]
    acc, dg_s, both = refs[13 + dm.n_hi :]
    i = pl.program_id(0)

    @pl.when(i == 0)
    def _():
        lane_out[...] = jnp.zeros_like(lane_out)
        acc[...] = jnp.zeros_like(acc)

    def gather():
        acc[:, :ip] += dot(nm_in[...], dg_s[...], TM)
        acc[:, ip:] += dot(ct_in[...], both[...], TM)

    def gating():
        pad = jnp.zeros((LANES - 2, q), F32)
        cols = jnp.concatenate([rk_ref[...], pad], axis=0).T
        root, pull = cols[:, 0:1], cols[:, 1:2]
        for p in range(dm.pairs):
            g = slice(p * LANES, (p + 1) * LANES)
            gate, sc = g_in[:, g].astype(F32), sc_in[:, g].astype(F32)
            cv = cv_in[:, g].astype(F32)
            x = cv * sigmoid(cv)
            sig = sigmoid(gate)
            z = gate * sig
            y = ys_in[:, g] + lane_ref[0:1, g] * x
            gated = y * z
            scaled = gated * root
            cot = root * (lane_ref[1:2, g] * sc) - pull * gated
            lane_out[0:8, g] += colsum(sc * scaled)
            dy = cot * z
            dy_out[:, g] = dy.astype(BF16)
            dg = (cot * y * (sig + z * (1.0 - sig))).astype(BF16)
            dg_out[:, g] = dg
            dg_s[:, g] = dg
            lane_out[8:16, g] += colsum(dy * x)
            both[:, g] = (scaled * lane_ref[1:2, g]).astype(BF16)

    @pl.when(i == 0)
    def _():
        gating()

    @pl.when((i > 0) & (i < dm.blocks))
    def _():
        gather()
        gating()

    @pl.when(i == dm.blocks)
    def _():
        gather()
        prod = acc[:, :LANES] * w_ref[:, :LANES].astype(F32)
        for p in range(1, dm.pairs):
            g = slice(p * LANES, (p + 1) * LANES)
            prod = prod + acc[:, g] * w_ref[:, g].astype(F32)
        rows_out[...] = gain_rows(prod)
        hi = scalars[dm.at_hi]
        own_out[...] = acc[pl.ds(pl.multiple_of(hi * 2 * r, 8), 2 * r), :]
        for k, z_out in enumerate(z_outs):
            at = pl.multiple_of(scalars[dm.at_hi + k + 1] * 2 * r, 8)
            z_out[...] = acc[pl.ds(at, 2 * r), :].astype(BF16)


def backward_kernel(dm, scalars, *refs):
    q, ip, vs, st, hd, late_cols = BLOCK, dm.ip, dm.vs, dm.state, dm.hd, dm.late
    groups = dm.group_sizes
    w_ref, rows_ref, conv_ref, hp_ref, lane_ref, lanes_ref, gain_ref = refs[:7]
    dg_in, nm_in, dy_in, v_in, cv_in, ys_in, st_in, h_in = refs[7:15]
    mine_out, theirs_out = refs[15:17]
    nc_outs = refs[17 : 17 + len(groups)]
    (dh_ref, dbuf, tri_ref, bias_ref, ds_ref, u_s, dx_s, act_s, t1_s, t2_s) = refs[
        17 + len(groups) : 27 + len(groups)
    ]
    (pj_s, acc, tap_out, head_out, nc_buf, nc_sem) = refs[27 + len(groups) :]
    i = pl.program_id(0)
    blk = jnp.maximum(dm.blocks - 1 - i, 0)

    def send(k, at, row):
        return pltpu.make_async_copy(nc_buf.at[at], nc_outs[k].at[row], nc_sem.at[at])

    @pl.when(i == 0)
    def _():
        dh_ref[...] = jnp.zeros_like(dh_ref)
        dbuf[...] = jnp.zeros_like(dbuf)
        tap_out[...] = jnp.zeros_like(tap_out)
        head_out[...] = jnp.zeros_like(head_out)
        acc[...] = jnp.zeros_like(acc)
        r = lax.broadcasted_iota(jnp.int32, (q, q), 0)
        c = lax.broadcasted_iota(jnp.int32, (q, q), 1)
        tri_ref[...] = jnp.where(r >= c, 1.0, 0.0).astype(BF16)

    slot = lax.rem(i, 2)

    @pl.when(i >= 3)
    def _():
        send(0, slot, 0).wait()

    def project():
        nc = dot(dg_in[...], w_ref[:, :ip], MT) + dot(pj_s[...], w_ref[:, ip:], MT)
        nc_buf[slot] = nc.astype(BF16)
        acc[...] += dot(nm_in[...], pj_s[...], TM)

    def scan():
        rows = rows_ref[...]
        cols = columns_of(rows)
        raw = st_in[...]
        tri = tri_ref[...]
        delta, logs, enter, ending = decay_parts(raw, hp_ref, cols, tri)
        logs_t = logs.T
        lane = lax.broadcasted_iota(jnp.int32, (q, LANES), 1)

        acts, slopes = [], []
        for c in range(vs // LANES):
            g = slice(c * LANES, (c + 1) * LANES)
            cv = cv_in[:, g].astype(F32)
            sig = sigmoid(cv)
            act = cv * sig
            acts.append(act)
            slopes.append(sig + act * (1.0 - sig))
        in_map = jnp.concatenate(acts[dm.pairs : dm.pairs + st // LANES], axis=1).astype(BF16)
        out_map = jnp.concatenate(acts[dm.pairs + st // LANES :], axis=1).astype(BF16)

        for p in range(dm.pairs):
            g = slice(p * LANES, (p + 1) * LANES)
            u_s[:, g] = acts[p] * spread(delta, p, hd)

        r = lax.broadcasted_iota(jnp.int32, (q, q), 0)
        c = lax.broadcasted_iota(jnp.int32, (q, q), 1)
        bias_ref[...] = jnp.where((r <= c) & (cols[:, 0:1] == rows[0:1, :]), 0.0, FAR)
        scores = dot(in_map, out_map, MT)
        dh_b = dh_ref[...].astype(BF16)
        h_b = h_in[...].astype(BF16)
        out_map_t = out_map.T
        keep = scalars[dm.at_keep + blk].astype(F32)
        total = jnp.exp2(logs[q - 1 :, :]) * keep
        d_in = jnp.zeros((q, st), F32)
        d_out = jnp.zeros((q, st), F32)
        for p in range(dm.pairs):
            g = slice(p * LANES, (p + 1) * LANES)
            u, dyb = u_s[:, g], dy_in[:, g]
            ub, dy = u.astype(BF16), dyb.astype(F32)
            du = None
            for j in range(dm.per):
                h = p * dm.per + j
                mine = (lane >= j * hd) & (lane < (j + 1) * hd)
                decay = jnp.exp2(logs_t[h : h + 1, :] - logs[:, h : h + 1] + bias_ref[...])
                part = dot((decay * scores).astype(BF16), dyb)
                du = part if du is None else jnp.where(lane >= j * hd, part, du)
                dm_t = dot(jnp.where(mine, u, 0.0).astype(BF16), dyb, MT)
                if p == 0 and j == 0:
                    ds_ref[...] = dm_t * decay
                else:
                    ds_ref[...] += dm_t * decay
            end_e = spread(ending, p, hd)
            late = end_e * dot(in_map, dh_b[:, g])
            du = du + late
            wu = (u * end_e).astype(BF16)
            edy = (dy * spread(enter, p, hd)).astype(BF16)
            d_in = d_in + dot(wu, dh_b[:, g], MT)
            d_out = d_out + dot(edy, h_b[:, g], MT)
            u32 = ub.astype(F32)
            t1_s[:, g] = dy * ys_in[:, g] - u32 * du
            t2_s[:, g] = du * acts[p]
            kept = dh_ref[:, g] * spread(total, p, hd)
            act_s[:, g] = colsum(u32 * late) + colsum(h_in[:, g] * kept)
            dh_ref[:, g] = kept + dot(out_map_t, edy)
            dx_s[:, g] = (spread(delta, p, hd) * du + lane_ref[0:1, g] * dy) * slopes[p]
        ds_b = ds_ref[...].astype(BF16)
        d_in = d_in + dot(ds_b, out_map)
        d_out = d_out + dot(ds_b, in_map, TM)

        hr = lax.broadcasted_iota(jnp.int32, (ip, LANES), 0)
        hc = lax.broadcasted_iota(jnp.int32, (ip, LANES), 1)
        pick = jnp.where(hr // hd == hc, 1.0, 0.0).astype(BF16)
        d_log = split_dot(t1_s[...], pick)
        last = split_dot(jnp.sum(act_s[...], axis=0, keepdims=True), pick)
        row = lax.broadcasted_iota(jnp.int32, (q, LANES), 0)
        d_log = d_log + jnp.where(row == q - 1, last, 0.0)
        d_step = dot_split(tri, d_log, TM)
        head_out[8:16, :] += colsum(d_step * delta)
        d_delta = hp_ref[1:2, :] * d_step + split_dot(t2_s[...], pick)
        d_raw = d_delta * sigmoid(raw + hp_ref[0:1, :])
        head_out[0:8, :] += colsum(d_raw)
        pj_s[:, vs:] = d_raw.astype(BF16)

        dbuf[q : q + 8, :] = dbuf[0:8, :]
        for c in range(vs // LANES):
            g = slice(c * LANES, (c + 1) * LANES)
            if c < dm.pairs:
                dbuf[0:q, g] = dx_s[:, g]
            else:
                k = (c - dm.pairs) * LANES
                source = d_in[:, k : k + LANES] if k < st else d_out[:, k - st : k - st + LANES]
                dbuf[0:q, g] = source * slopes[c]
        for c in range(vs // LANES):
            g = slice(c * LANES, (c + 1) * LANES)
            v = v_in[:, g].astype(F32)
            shifted = dbuf[0:q, g]
            tap_out[32:40, g] += colsum(shifted)
            tap_out[24:32, g] += colsum(shifted * v)
            dv = conv_ref[3:4, g] * shifted
            for lag in range(1, 4):
                shifted = dbuf[lag : lag + q, g] * cols[:, 3 + lag : 4 + lag]
                tap_out[24 - 8 * lag : 32 - 8 * lag, g] += colsum(shifted * v)
                dv = dv + conv_ref[3 - lag : 4 - lag, g] * shifted
            pj_s[:, g] = dv.astype(BF16)


    @pl.when(i == 0)
    def _():
        scan()

    @pl.when((i > 0) & (i < dm.blocks))
    def _():
        project()
        scan()

    @pl.when(i == dm.blocks)
    def _():
        project()

    before = jnp.minimum(blk + 1, dm.blocks - 1)
    before = jnp.where(i == dm.blocks, 0, before)
    for k in range(len(groups)):

        @pl.when((i > 0) & (scalars[dm.at_group + before] == k))
        def _():
            send(k, slot, scalars[dm.at_slot + before]).start()

    @pl.when(i == dm.blocks)
    def _():
        core, r = scalars[dm.at_core], dm.part_rows
        for h in range(dm.n_hi):
            at = pl.multiple_of((2 * h + core) * r, 8)
            mine_out[h * r : (h + 1) * r, :] = acc[pl.ds(at, r), :]
            at = pl.multiple_of((2 * h + 1 - core) * r, 8)
            theirs_out[h * r : (h + 1) * r, :] = acc[pl.ds(at, r), :].astype(BF16)
        small = []

        def put(v):
            for c in range(v.shape[1] // LANES):
                small.append(jnp.sum(v[:, c * LANES : (c + 1) * LANES], axis=0, keepdims=True))

        for k in range(5):
            put(tap_out[8 * k : 8 * k + 8, :ip])
        for k in range(2):
            put(lanes_ref[8 * k : 8 * k + 8, :])
        for k in range(2):
            put(head_out[8 * k : 8 * k + 8, :])
        zero = jnp.zeros((1, LANES), F32)
        small.extend([zero] * (dm.local_rows - len(small)))
        for k in range(5):
            put(tap_out[8 * k : 8 * k + 8, ip:])
        prod = acc[:, :LANES] * w_ref[:, ip : ip + LANES].astype(F32)
        for p in range(1, late_cols // LANES):
            g = slice(p * LANES, (p + 1) * LANES)
            o = slice(ip + p * LANES, ip + (p + 1) * LANES)
            prod = prod + acc[:, g] * w_ref[:, o].astype(F32)
        prod = gain_rows(prod)
        for c in range(dm.width // LANES):
            g = slice(c * LANES, (c + 1) * LANES)
            small.append(prod[0:1, g] + gain_ref[0:1, g])
        small.extend([zero] * (late_cols // 16 - len(small)))
        for c in range(late_cols // LANES):
            g = slice(c * LANES, (c + 1) * LANES)
            theirs_out[dm.n_hi * r :, g] = two_parts(jnp.concatenate(small[8 * c : 8 * c + 8], axis=0))
        send(0, 1 - slot, 0).wait()
        send(0, slot, 0).wait()


def two_parts(v):
    high = v.astype(BF16).astype(F32)
    return jnp.concatenate([high, v - high], axis=0).astype(BF16)


def one_part(v):
    return v[0:8, :].astype(F32) + v[8:16, :].astype(F32)


def gain_rows(acc):
    high = acc.astype(BF16)
    rest = acc - high.astype(F32)
    mid = rest.astype(BF16)
    low = (rest - mid.astype(F32)).astype(BF16)
    one = jnp.ones((8, LANES), BF16)
    return dot(one, high, MT) + dot(one, mid, MT) + dot(one, low, MT)


def pair_kernel(dm, scalars, mine_ref, kept_ref, theirs_ref, own_out, *outs):
    r = dm.part_rows
    tail = dm.n_hi * r
    small = one_part(kept_ref[...]) + one_part(theirs_ref[tail:, :])
    small = two_parts(small)
    for k in range(dm.n_hi):
        at = pl.multiple_of(scalars[dm.at_hi + k] * r, 8)
        both = mine_ref[pl.ds(at, r), :] + theirs_ref[pl.ds(at, r), :].astype(F32)
        if k == 0:
            own_out[...] = both
        else:
            outs[k][0:r, :] = both.astype(BF16)
        if k > 0:
            outs[k][r:, :] = small
        else:
            outs[0][...] = small


def early_kernel(dm, scalars, own_ref, *refs):
    parts, (mine_out, theirs_out, total) = refs[: dm.n_hi - 1], refs[dm.n_hi - 1 :]
    r = dm.part_rows
    both = own_ref[...]
    for part in parts:
        both = both + part[...].astype(F32)
    total[...] = both
    core = scalars[dm.at_core]
    mine_out[...] = total[pl.ds(pl.multiple_of(core * r, 8), r), :]
    theirs_out[...] = total[pl.ds(pl.multiple_of((1 - core) * r, 8), r), :].astype(BF16)


def grads_kernel(dm, scalars, hp_ref, own_ref, kept_ref, mine_ref, theirs_ref, *refs):
    n, r, st2 = dm.n_hi, dm.part_rows, 2 * dm.state
    parts = refs[: n - 1]
    (gate_out, value_out, step_out, outp_out, share_out) = refs[n - 1 : n + 4]
    (tap_out, tapb_out, gain_out, skip_out, sb_out, dl_out, hold) = refs[n + 4 :]
    total = own_ref[...]
    for part in parts:
        total = total + part[0:r, :].astype(F32)
    early = mine_ref[...] + theirs_ref[...].astype(F32)
    inner, heads = gate_out.shape[1], step_out.shape[0]
    gate_out[...] = early[:, :inner]
    outp_out[...] = early[:, dm.ip : dm.ip + inner]
    value_out[...] = total[:, :inner]
    share_out[0:r, :] = total[:, dm.ip : dm.vs].astype(BF16)
    step_out[...] = total[:, dm.vs :].T[0:heads, :]
    hold[0] = one_part(kept_ref[...])
    for k, part in enumerate(parts):
        hold[k + 1] = one_part(part[r:, :])
    small = hold[scalars[dm.at_from]]
    for k in range(1, n):
        small = small + hold[scalars[dm.at_from + k]]
    flat = [
        small[j : j + 1, c * LANES : (c + 1) * LANES]
        for c in range(dm.late // LANES)
        for j in range(8)
    ]

    def take(first, width):
        return jnp.concatenate(flat[first : first + dm.pairs], axis=1)[:, :width]

    for k in range(4):
        tap_out[k : k + 1, :] = take(k * dm.pairs, inner)
    tapb_out[...] = take(4 * dm.pairs, inner)
    gain_out[...] = take(5 * dm.pairs, inner)
    lane = lax.broadcasted_iota(jnp.int32, (1, LANES), 1)
    skip = jnp.zeros((1, LANES), F32)
    for h in range(heads):
        row = flat[6 * dm.pairs + h // dm.per]
        mine = lane // dm.hd == h % dm.per
        one = jnp.sum(jnp.where(mine, row, 0.0), axis=1, keepdims=True)
        skip = jnp.where(lane == h, one, skip)
    skip_out[...] = skip[:, :heads]
    sb_out[...] = flat[7 * dm.pairs][:, :heads]
    dl_out[...] = (flat[7 * dm.pairs + 1] * hp_ref[1:2, :])[:, :heads]
    first = dm.local_rows // 8
    for c in range(st2 // LANES):
        g = slice((first + c) * LANES, (first + c + 1) * LANES)
        share_out[r:, c * LANES : (c + 1) * LANES] = two_parts(small[:, g])


def share_kernel(dm, scalars, norm_ref, *refs):
    r, st2 = dm.part_rows, 2 * dm.state
    parts = refs[: dm.n_t]
    shared_out, tap_out, tapb_out, norm_out, hold = refs[dm.n_t :]
    for k, part in enumerate(parts):
        hold[k] = part[...]
    shared, common = None, None
    for k in range(dm.n_t):
        part = hold[scalars[dm.at_side + k]]
        share, small = part[0:r, :].astype(F32), one_part(part[r:, :])
        shared = share if shared is None else shared + share
        common = small if common is None else common + small
    shared_out[...] = shared
    flat = [
        common[j : j + 1, c * LANES : (c + 1) * LANES] for c in range(st2 // LANES) for j in range(8)
    ]
    per = st2 // LANES
    for k in range(4):
        tap_out[k : k + 1, :] = jnp.concatenate(flat[k * per : (k + 1) * per], axis=1)
    tapb_out[...] = jnp.concatenate(flat[4 * per : 5 * per], axis=1)
    rows = flat[5 * per : 5 * per + dm.width // LANES]
    norm_out[...] = jnp.concatenate(rows, axis=1) / norm_ref[...]


def input_kernel(sets, steps, x_ref, cot_ref, gain_ref, *refs):
    out = refs[-1]
    x = x_ref[...]
    root = lax.rsqrt(jnp.mean(x * x, axis=1, keepdims=True) + EPS)
    first = 0
    for k, count in enumerate(sets):
        parts = refs[first : first + count]
        first += count

        @pl.when(pl.program_id(0) // steps == k)
        def _():
            nc = parts[0][...].astype(F32)
            for part in parts[1:]:
                nc = nc + part[...].astype(F32)
            hat = nc * gain_ref[...]
            mean = jnp.mean(hat * x, axis=1, keepdims=True)
            out[...] = cot_ref[...].astype(F32) + root * hat - x * (root * root * root * mean)


def shift_hi(n, k):
    return [(i, ((i // 2 + k) % (n // 2)) * 2 + i % 2) for i in range(n)]


def swap(n, k):
    return [(i, i ^ k) for i in range(n)]


def pad_cols(v, to):
    return jnp.pad(v, ((0, 0), (0, to - v.shape[1])))


def pad_vec(v, to):
    return jnp.pad(v, (0, to - v.shape[0]))


def body(
    n_dp,
    n_t,
    block_input,
    segment_ids,
    norm_gain,
    gate_proj,
    value_proj,
    shared_proj,
    step_proj,
    conv_value_weight,
    conv_value_bias,
    conv_shared_weight,
    conv_shared_bias,
    step_bias,
    decay_log,
    skip_weight,
    gate_gain,
    output_proj,
    out_cotangent,
):
    q = BLOCK
    chunk_rows, width = block_input.shape
    length = segment_ids.shape[1]
    inner, heads = gate_proj.shape[1], step_proj.shape[1]
    part_rows = gate_proj.shape[0]
    state = shared_proj.shape[1] // 2
    hd = inner // heads
    dm = Dims(n_dp, n_t, length, width, inner, hd, state, part_rows, chunk_rows)
    ip, vs, nb, n_hi = dm.ip, dm.vs, dm.blocks, dm.n_hi
    me_t = lax.axis_index("tensor")
    me_dp = lax.axis_index("dp")
    hi, core = me_dp // 2, me_dp % 2

    def across(v, k):
        return lax.ppermute(v, "tensor", swap(n_t, k))

    def along(v, k):
        return lax.ppermute(v, "dp", shift_hi(n_dp, k))

    def partner(v):
        return lax.ppermute(v, "dp", swap(n_dp, 1))

    def vmem(shape, dtype):
        return pltpu.VMEM(shape, dtype)

    limit = 60 * 1024 * 1024
    params = pltpu.CompilerParams(dimension_semantics=("arbitrary",), vmem_limit_bytes=limit)
    hbm = pl.BlockSpec(memory_space=pl.ANY)

    def out(*shape, dtype=F32):
        return jax.ShapeDtypeStruct(shape, dtype)

    gain = norm_gain.reshape(1, width)
    part = min(LANES, dm.piece_rows)
    normed = pl.pallas_call(
        functools.partial(norm_kernel, part),
        out_shape=[out(dm.piece_rows, width, dtype=BF16)] * dm.halves,
        in_specs=[hbm, pl.BlockSpec(memory_space=pltpu.VMEM)],
        scratch_shapes=[
            vmem((chunk_rows, width), F32),
            pltpu.SemaphoreType.DMA((chunk_rows // part,)),
        ],
        compiler_params=pltpu.CompilerParams(vmem_limit_bytes=limit),
        name="normalize",
    )(block_input, gain)
    if dm.halves == 2:
        a, b = normed
        xa, yb = across(a, 1), across(b, 2)
        ya, xb = across(a, 2), across(b, 1)
        n_list = [a, b, xa, xb, ya, yb, across(xa, 2), across(yb, 1)]
        n_rows = jnp.concatenate(
            [(me_t ^ k) * chunk_rows + jnp.arange(2) * dm.piece_rows for k in range(4)]
        )
    else:
        n_list = [normed[0]] + [across(normed[0], k) for k in range(1, n_t)]
        n_rows = (me_t ^ jnp.arange(n_t)) * chunk_rows
    packed = pl.pallas_call(
        functools.partial(pack_kernel, dm),
        out_shape=out(part_rows, dm.np, dtype=BF16),
        name="pack_weights",
    )(gate_proj, value_proj, shared_proj, step_proj.T)
    w_list = [packed] + [along(packed, k) for k in range(1, n_hi)]
    w_list = w_list + [partner(v) for v in w_list]
    outp = pad_cols(output_proj.T, ip)
    o_list = [outp] + [along(outp, k) for k in range(1, n_hi)]
    o_list = o_list + [partner(v) for v in o_list]

    seg = segment_ids[0]
    segb = seg.reshape(nb, q)
    last = segb[:, -1]
    prev_last = jnp.concatenate([jnp.full((1,), -1, jnp.int32), last[:-1]])
    gap = jnp.full((3,), -1, jnp.int32)
    wide = jnp.concatenate([gap, seg, gap])
    rows = [seg.astype(F32)]
    rows += [(wide[3 - k : 3 - k + length] == seg).astype(F32) for k in range(1, 4)]
    rows += [(wide[3 + k : 3 + k + length] == seg).astype(F32) for k in range(1, 4)]
    rows += [
        (segb == prev_last[:, None]).astype(F32).reshape(-1),
        (segb == last[:, None]).astype(F32).reshape(-1),
    ]
    rows = jnp.concatenate([jnp.stack(rows), jnp.zeros((16 - len(rows), length), F32)], axis=0)
    keep = (last == prev_last).astype(jnp.int32)
    other = (hi - jnp.arange(n_hi)) % n_hi
    rel = (jnp.arange(nb) * q // chunk_rows) ^ me_t
    half = jnp.arange(nb) % (chunk_rows // q)
    if dm.halves == 2:
        group_of = jnp.array([[2, 2], [0, 2], [2, 1], [0, 1]])
        slot_of = jnp.array([[0, 2], [0, 3], [1, 0], [1, 1]])
        group, slot = group_of[rel, half], slot_of[rel, half]
        dm.group_sizes = (2, 2, 4)
    else:
        group, slot = rel, half
        dm.group_sizes = (chunk_rows // q,) * n_t
    scalars = jnp.concatenate(
        [
            (other * 2 + core) * part_rows,
            (other * 2 + 1 - core) * part_rows,
            n_rows,
            (me_t ^ jnp.arange(n_t)) * chunk_rows,
            keep,
            rel,
            group,
            slot,
            (hi + jnp.arange(n_hi)) % n_hi,
            core[None],
            (hi - jnp.arange(n_hi)) % n_hi,
            me_t ^ jnp.arange(n_t),
        ]
    ).astype(jnp.int32)

    conv = jnp.concatenate(
        [
            pad_cols(jnp.concatenate([conv_value_weight, conv_value_bias[None]]), ip),
            jnp.concatenate([conv_shared_weight, conv_shared_bias[None]]),
        ],
        axis=1,
    )
    conv = jnp.pad(conv, ((0, 3), (0, 0)))
    rate = -jnp.exp(decay_log)
    per_head = jnp.stack([pad_vec(step_bias, LANES), pad_vec(rate, LANES)])
    per_head = jnp.pad(per_head, ((0, 6), (0, 0)))
    per_lane = jnp.stack([pad_vec(jnp.repeat(skip_weight, hd), ip), pad_vec(gate_gain, ip)])
    per_lane = jnp.pad(per_lane, ((0, 6), (0, 0)))

    def const(*shape):
        return pl.BlockSpec(shape, lambda i, s: (0,) * len(shape))

    def fblock(cols):
        return pl.BlockSpec((q, cols), lambda i, s: (i, 0))

    def fsum(k):
        return pl.BlockSpec((None, k, q), lambda i, s: (i, 0, 0))

    def grid(steps, in_specs, out_specs, scratch):
        return pltpu.PrefetchScalarGridSpec(
            num_scalar_prefetch=1,
            grid=(steps,),
            in_specs=in_specs,
            out_specs=out_specs,
            scratch_shapes=scratch,
        )

    (gate, value, conved, scan, steps_raw, held, squares, normed_all, scaled, weights) = pl.pallas_call(
        functools.partial(forward_kernel, dm),
        out_shape=[
            out(length, ip, dtype=BF16),
            out(length, vs, dtype=BF16),
            out(length, vs, dtype=BF16),
            out(length, ip),
            out(length, LANES),
            out(nb * state, ip),
            out(nb, 1, q),
            out(length, width, dtype=BF16),
            out(length, ip, dtype=BF16),
            out(width, dm.np, dtype=BF16),
        ],
        grid_spec=grid(
            nb,
            [hbm] * (n_dp + dm.pieces)
            + [
                pl.BlockSpec((16, q), lambda i, s: (0, i)),
                const(8, vs),
                const(8, LANES),
                const(8, ip),
            ],
            [
                fblock(ip),
                fblock(vs),
                fblock(vs),
                fblock(ip),
                fblock(LANES),
                pl.BlockSpec((state, ip), lambda i, s: (i, 0)),
                fsum(1),
                fblock(width),
                fblock(ip),
                hbm,
            ],
            [
                vmem((width, dm.np), BF16),
                vmem((length, width), BF16),
                vmem((state, ip), F32),
                vmem((q + 8, vs), F32),
                vmem((q, q), BF16),
                vmem((q, q), F32),
                vmem((q, dm.np), F32),
                pltpu.SemaphoreType.DMA((n_dp,)),
                pltpu.SemaphoreType.DMA((dm.pieces,)),
                pltpu.SemaphoreType.DMA,
            ],
        ),
        compiler_params=params,
        cost_estimate=pl.CostEstimate(
            flops=30_000_000_000, bytes_accessed=30_000_000, transcendentals=0
        ),
        name="block_forward",
    )(scalars, *w_list, *n_list, rows, conv, per_head, per_lane)

    c_list = [out_cotangent] + [across(out_cotangent, k) for k in range(1, n_t)]
    in_vmem = pl.BlockSpec(memory_space=pltpu.VMEM)
    sc, sums, cot_all, w_back = pl.pallas_call(
        functools.partial(cotangent_kernel, dm),
        out_shape=[
            out(length, ip, dtype=BF16),
            out(nb, 2, q),
            out(length, width, dtype=BF16),
            out(width, ip, dtype=BF16),
        ],
        grid_spec=grid(
            1,
            [hbm] * (n_t + n_dp + 1) + [in_vmem],
            [hbm, in_vmem, hbm, in_vmem],
            [
                vmem((length, width), BF16),
                vmem((length, ip), BF16),
                vmem((length, ip), BF16),
                pltpu.SemaphoreType.DMA((n_t,)),
                pltpu.SemaphoreType.DMA((n_dp,)),
                pltpu.SemaphoreType.DMA,
                pltpu.SemaphoreType.DMA((n_t,)),
                pltpu.SemaphoreType.DMA((n_t,)),
            ],
        ),
        compiler_params=params,
        cost_estimate=pl.CostEstimate(
            flops=3_000_000_000, bytes_accessed=10_000_000, transcendentals=0
        ),
        name="branch_cotangent",
    )(scalars, *c_list, *o_list, scaled, squares)
    total = sums
    for k in range(1, n_t):
        total = total + across(sums, k)
    branch = pl.pallas_call(
        functools.partial(branch_kernel, dm),
        out_shape=[out(chunk_rows // q, q, width, dtype=BF16)] * n_t,
        grid_spec=grid(
            1,
            [in_vmem, in_vmem],
            [hbm] * n_t,
            [vmem((nb, q, width), BF16), pltpu.SemaphoreType.DMA((nb,))],
        ),
        compiler_params=params,
        cost_estimate=pl.CostEstimate(
            flops=3_000_000_000, bytes_accessed=10_000_000, transcendentals=0
        ),
        name="branch_output",
    )(scalars, w_back, scaled)
    root = lax.rsqrt(total[:, 0] / (inner * n_t) + EPS)
    pull = root * root * root * (total[:, 1] / (inner * n_t))
    rk = jnp.stack([root, pull], axis=1)
    branch_sum = branch[0].astype(F32)
    for k in range(1, n_t):
        branch_sum = branch_sum + across(branch[k], k).astype(F32)
    own_root = lax.dynamic_slice_in_dim(root.reshape(length), me_t * chunk_rows, chunk_rows)
    block_output = block_input + own_root[:, None] * branch_sum.reshape(chunk_rows, width)

    def bblock(cols):
        return pl.BlockSpec((q, cols), lambda i, s: (jnp.maximum(nb - 1 - i, 0), 0))

    def bago(cols):
        return pl.BlockSpec((q, cols), lambda i, s: (jnp.minimum(nb - i, nb - 1), 0))

    def now(cols):
        return pl.BlockSpec((q, cols), lambda i, s: (jnp.minimum(i, nb - 1), 0))

    def ago(cols):
        return pl.BlockSpec((q, cols), lambda i, s: (jnp.maximum(i - 1, 0), 0))

    dgate, dscan, lanes, gate_rows, own_early, *early = pl.pallas_call(
        functools.partial(gate_kernel, dm),
        out_shape=[
            out(length, ip, dtype=BF16),
            out(length, ip, dtype=BF16),
            out(16, ip),
            out(8, width),
            out(2 * part_rows, 2 * ip),
        ]
        + [out(2 * part_rows, 2 * ip, dtype=BF16)] * (n_hi - 1),
        grid_spec=grid(
            nb + 1,
            [
                const(width, ip),
                pl.BlockSpec((None, 2, q), lambda i, s: (jnp.minimum(i, nb - 1), 0, 0)),
                const(8, ip),
                now(ip),
                now(ip),
                now(ip),
                now(ip),
                ago(width),
                ago(width),
            ],
            [now(ip), now(ip), const(16, ip), const(8, width)]
            + [const(2 * part_rows, 2 * ip)] * n_hi,
            [vmem((width, 2 * ip), F32), vmem((q, ip), BF16), vmem((q, ip), BF16)],
        ),
        compiler_params=params,
        cost_estimate=pl.CostEstimate(
            flops=6_000_000_000, bytes_accessed=20_000_000, transcendentals=0
        ),
        name="gate_backward",
    )(scalars, weights, rk, per_lane, gate, conved, scan, sc, normed_all, cot_all)
    early = [along(v, k + 1) for k, v in enumerate(early)]

    r_all = n_hi * part_rows
    mine, theirs, *nc = pl.pallas_call(
        functools.partial(backward_kernel, dm),
        out_shape=[out(r_all, dm.late), out(r_all + 16, dm.late, dtype=BF16)]
        + [out(k, q, width, dtype=BF16) for k in dm.group_sizes],
        grid_spec=grid(
            nb + 1,
            [
                const(width, dm.np),
                pl.BlockSpec((16, q), lambda i, s: (0, jnp.maximum(nb - 1 - i, 0))),
                const(8, vs),
                const(8, LANES),
                const(8, ip),
                const(16, ip),
                const(8, width),
                bago(ip),
                bago(width),
                bblock(ip),
                bblock(vs),
                bblock(vs),
                bblock(ip),
                bblock(LANES),
                pl.BlockSpec((state, ip), lambda i, s: (jnp.maximum(nb - 1 - i, 0), 0)),
            ],
            [const(r_all, dm.late), const(r_all + 16, dm.late)] + [hbm] * len(dm.group_sizes),
            [
                vmem((state, ip), F32),
                vmem((q + 8, vs), F32),
                vmem((q, q), BF16),
                vmem((q, q), F32),
                vmem((q, q), F32),
                vmem((q, ip), F32),
                vmem((q, ip), F32),
                vmem((8, ip), F32),
                vmem((q, ip), F32),
                vmem((q, ip), F32),
                vmem((q, dm.late), BF16),
                vmem((width, dm.late), F32),
                vmem((40, vs), F32),
                vmem((16, LANES), F32),
                vmem((2, q, width), BF16),
                pltpu.SemaphoreType.DMA((2,)),
            ],
        ),
        compiler_params=params,
        cost_estimate=pl.CostEstimate(
            flops=40_000_000_000, bytes_accessed=30_000_000, transcendentals=0
        ),
        name="block_backward",
    )(
        scalars,
        weights,
        rows,
        conv,
        per_head,
        per_lane,
        lanes,
        gate_rows,
        dgate,
        normed_all,
        dscan,
        value,
        conved,
        scan,
        steps_raw,
        held,
    )

    part = min(q, dm.piece_rows)
    steps = dm.piece_rows // part

    def turn(k):
        return pl.BlockSpec((part, width), lambda i: (jnp.clip(i - k * steps, 0, steps - 1), 0))

    def slot_of_piece(k, at):
        return pl.BlockSpec(
            (None, part, width), lambda i: (at, jnp.clip(i - k * steps, 0, steps - 1), 0)
        )

    if dm.halves == 2:
        from_x, from_y, stay = across(nc[0], 1), across(nc[1], 2), nc[2]
        pass_y = (stay[1].astype(F32) + from_x[1].astype(F32)).astype(BF16)
        pass_x = (stay[3].astype(F32) + from_y[1].astype(F32)).astype(BF16)
        got_y, got_x = across(pass_y, 2), across(pass_x, 1)
        sets = (3, 3)
        terms = [stay, from_x, got_y, stay, from_y, got_x]
        specs = [slot_of_piece(0, 0), slot_of_piece(0, 0), turn(0)]
        specs += [slot_of_piece(1, 2), slot_of_piece(1, 0), turn(1)]
    else:
        sets = (n_t,)
        terms = [nc[0]] + [across(nc[k], k) for k in range(1, n_t)]
        terms = [v.reshape(chunk_rows, width) for v in terms]
        specs = [turn(0)] * n_t
    in_turn = pl.BlockSpec((part, width), lambda i: (i, 0))
    input_grad = pl.pallas_call(
        functools.partial(input_kernel, sets, steps),
        out_shape=out(chunk_rows, width),
        grid=(len(sets) * steps,),
        in_specs=[in_turn, in_turn, pl.BlockSpec((1, width), lambda i: (0, 0))] + specs,
        out_specs=in_turn,
        compiler_params=params,
        name="input_gradient",
    )(block_input, out_cotangent, gain, *terms)

    late = dm.late
    kept = theirs[r_all:]
    theirs = partner(theirs)
    own, own_small, *others = pl.pallas_call(
        functools.partial(pair_kernel, dm),
        out_shape=[out(part_rows, late), out(16, late, dtype=BF16)]
        + [out(part_rows + 16, late, dtype=BF16)] * (n_hi - 1),
        grid_spec=grid(1, [in_vmem] * 3, [in_vmem] * (n_hi + 1), []),
        compiler_params=params,
        name="core_sum",
    )(scalars, mine, kept, theirs)
    others = [along(v, k + 1) for k, v in enumerate(others)]
    early_mine, early_theirs = pl.pallas_call(
        functools.partial(early_kernel, dm),
        out_shape=[out(part_rows, 2 * ip), out(part_rows, 2 * ip, dtype=BF16)],
        grid_spec=grid(
            1, [in_vmem] * n_hi, [in_vmem] * 2, [vmem((2 * part_rows, 2 * ip), F32)]
        ),
        compiler_params=params,
        name="early_sum",
    )(scalars, own_early, *early)
    early_theirs = partner(early_theirs)
    (
        gate_proj_grad,
        value_proj_grad,
        step_t,
        outp_t,
        share,
        conv_value_weight_grad,
        conv_value_bias_grad,
        gate_gain_grad,
        skip_weight_grad,
        step_bias_grad,
        decay_log_grad,
    ) = pl.pallas_call(
        functools.partial(grads_kernel, dm),
        out_shape=[
            out(part_rows, inner),
            out(part_rows, inner),
            out(heads, part_rows),
            out(part_rows, inner),
            out(part_rows + 16, 2 * state, dtype=BF16),
            out(4, inner),
            out(1, inner),
            out(1, inner),
            out(1, heads),
            out(1, heads),
            out(1, heads),
        ],
        grid_spec=grid(1, [in_vmem] * (n_hi + 4), [in_vmem] * 11, [vmem((n_hi, 8, late), F32)]),
        compiler_params=params,
        name="gradient_sum",
    )(scalars, per_head, own, own_small, early_mine, early_theirs, *others)
    shares = [share] + [across(share, k) for k in range(1, n_t)]
    shared_proj_grad, conv_shared_weight_grad, conv_shared_bias_grad, norm_gain_grad = pl.pallas_call(
        functools.partial(share_kernel, dm),
        out_shape=[out(part_rows, 2 * state), out(4, 2 * state), out(1, 2 * state), out(1, width)],
        grid_spec=grid(
            1,
            [in_vmem] * (n_t + 1),
            [in_vmem] * 4,
            [vmem((n_t, part_rows + 16, 2 * state), BF16)],
        ),
        compiler_params=params,
        name="shared_sum",
    )(scalars, gain, *shares)
    return (
        block_output,
        input_grad,
        norm_gain_grad.reshape(width),
        gate_proj_grad,
        value_proj_grad,
        shared_proj_grad,
        step_t.T,
        conv_value_weight_grad,
        conv_value_bias_grad.reshape(inner),
        conv_shared_weight_grad,
        conv_shared_bias_grad.reshape(2 * state),
        step_bias_grad.reshape(heads),
        decay_log_grad.reshape(heads),
        skip_weight_grad.reshape(heads),
        gate_gain_grad.reshape(inner),
        outp_t.T,
    )


def solution(mesh):
    n_dp, n_t = mesh.shape["dp"], mesh.shape["tensor"]
    both = ("dp", "tensor")
    return jax.shard_map(
        functools.partial(body, n_dp, n_t),
        mesh=mesh,
        in_specs=(
            P(both, None),
            P("dp", None),
            P(),
            P("dp", "tensor"),
            P("dp", "tensor"),
            P("dp", None),
            P("dp", "tensor"),
            P(None, "tensor"),
            P("tensor"),
            P(),
            P(),
            P("tensor"),
            P("tensor"),
            P("tensor"),
            P("tensor"),
            P("tensor", "dp"),
            P(both, None),
        ),
        out_specs=(
            P(both, None),
            P(both, None),
            P(),
            P("dp", "tensor"),
            P("dp", "tensor"),
            P("dp", None),
            P("dp", "tensor"),
            P(None, "tensor"),
            P("tensor"),
            P(),
            P(),
            P("tensor"),
            P("tensor"),
            P("tensor"),
            P("tensor"),
            P("tensor", "dp"),
        ),
        check_vma=False,
    )
```

```python
import functools
import math

import jax
import jax.numpy as jnp
from jax import lax
from jax.experimental import pallas as pl
from jax.experimental.pallas import tpu as pltpu
from jax.sharding import PartitionSpec as P


BLOCK = 256
LANES = 128
EPS = 1e-05
LOG2E = math.log2(math.e)
FAR = -1e30
F32 = jnp.float32
BF16 = jnp.bfloat16

MM = (((1,), (0,)), ((), ()))
MT = (((1,), (1,)), ((), ()))
TM = (((0,), (0,)), ((), ()))


def dot(a, b, dims=MM):
    return lax.dot_general(a, b, dims, preferred_element_type=F32)


def dot_split(exact, values, dims=MM):
    high = values.astype(BF16)
    low = (values - high.astype(F32)).astype(BF16)
    return dot(exact, high, dims) + dot(exact, low, dims)


def split_dot(values, exact, dims=MM):
    high = values.astype(BF16)
    low = (values - high.astype(F32)).astype(BF16)
    return dot(high, exact, dims) + dot(low, exact, dims)


def up(n, to=LANES):
    return -(-n // to) * to


def softplus(v):
    return jnp.maximum(v, 0.0) + jnp.log1p(jnp.exp(-jnp.abs(v)))


def sigmoid(v):
    return 0.5 + 0.5 * jnp.tanh(0.5 * v)


def colsum(v):
    return jnp.sum(v.reshape(v.shape[0] // 8, 8, v.shape[1]), axis=0)


def spread(cols, pair, hd):
    per = LANES // hd
    lane = lax.broadcasted_iota(jnp.int32, (cols.shape[0], LANES), 1)
    out = jnp.broadcast_to(cols[:, pair * per : pair * per + 1], lane.shape)
    for j in range(1, per):
        col = cols[:, pair * per + j : pair * per + j + 1]
        out = jnp.where(lane >= j * hd, jnp.broadcast_to(col, lane.shape), out)
    return out


def columns_of(rows):
    pad = jnp.zeros((LANES - rows.shape[0], rows.shape[1]), F32)
    return jnp.concatenate([rows, pad], axis=0).T


class Dims:
    def __init__(self, n_dp, n_t, length, width, inner, hd, state, part_rows, chunk_rows):
        self.length, self.width, self.state, self.hd = length, width, state, hd
        self.n_dp, self.n_t, self.n_hi = n_dp, n_t, n_dp // 2
        self.ip = up(inner)
        self.vs = self.ip + 2 * state
        self.np = self.ip + self.vs + LANES
        self.blocks = length // BLOCK
        self.part_rows, self.chunk_rows = part_rows, chunk_rows
        self.pairs = self.ip // LANES
        self.per = LANES // hd
        self.halves = 2 if n_t == 4 and chunk_rows == 2 * BLOCK else 1
        self.piece_rows = chunk_rows // self.halves
        self.pieces = n_t * self.halves
        self.at_n = n_dp
        self.at_c = self.at_n + self.pieces
        self.at_keep = self.at_c + n_t
        self.at_rel = self.at_keep + self.blocks
        self.at_group = self.at_rel + self.blocks
        self.at_slot = self.at_group + self.blocks
        self.at_hi = self.at_slot + self.blocks
        self.at_core = self.at_hi + self.n_hi
        self.at_from = self.at_core + 1
        self.at_side = self.at_from + self.n_hi
        self.late = self.vs + LANES
        self.local_rows = up(7 * self.pairs + 2, 8)


def load_parts(refs, target, sems, scalars, first, rows):
    return [
        pltpu.make_async_copy(
            ref, target.at[pl.ds(pl.multiple_of(scalars[first + k], rows), rows), :], sems.at[k]
        )
        for k, ref in enumerate(refs)
    ]


def decay_parts(raw, hp_ref, cols, tri):
    delta = softplus(raw + hp_ref[0:1, :])
    logs = dot_split(tri, delta * (hp_ref[1:2, :] * LOG2E))
    enter = jnp.exp2(logs) * cols[:, 7:8]
    ending = jnp.exp2(logs[BLOCK - 1 :, :] - logs) * cols[:, 8:9]
    return delta, logs, enter, ending


def norm_kernel(part, x_hbm, gain_ref, *refs):
    outs, (x_v, sem) = refs[:-2], refs[-2:]
    count = x_v.shape[0] // part
    copies = [
        pltpu.make_async_copy(
            x_hbm.at[pl.ds(k * part, part), :], x_v.at[pl.ds(k * part, part), :], sem.at[k]
        )
        for k in range(count)
    ]
    for copy in copies:
        copy.start()
    rows = outs[0].shape[0]
    for k, copy in enumerate(copies):
        copy.wait()
        x = x_v[k * part : (k + 1) * part]
        root = lax.rsqrt(jnp.mean(x * x, axis=1, keepdims=True) + EPS)
        first = k * part % rows
        outs[k * part // rows][first : first + part] = (x * root * gain_ref[...][None]).astype(BF16)


def pack_kernel(dm, gate_ref, value_ref, shared_ref, step_ref, out_ref):
    inner, heads, r = gate_ref.shape[1], step_ref.shape[0], step_ref.shape[1]
    if inner != dm.ip:
        out_ref[...] = jnp.zeros_like(out_ref)
    row = lax.broadcasted_iota(jnp.int32, (r, r), 0)
    col = lax.broadcasted_iota(jnp.int32, (r, r), 1)
    eye = jnp.where(row == col, 1.0, 0.0).astype(BF16)
    out_ref[:, :inner] = gate_ref[...]
    out_ref[:, dm.ip : dm.ip + inner] = value_ref[...]
    out_ref[:, 2 * dm.ip : dm.ip + dm.vs] = shared_ref[...]
    out_ref[:, dm.ip + dm.vs :] = jnp.zeros((r, LANES), BF16)
    out_ref[:, dm.ip + dm.vs : dm.ip + dm.vs + heads] = dot(eye, step_ref[...], MT).astype(BF16)


def forward_kernel(dm, scalars, *refs):
    q, ip, vs, st, hd = BLOCK, dm.ip, dm.vs, dm.state, dm.hd
    w_parts = refs[: dm.n_dp]
    n_parts = refs[dm.n_dp : dm.n_dp + dm.pieces]
    rest = refs[dm.n_dp + dm.pieces :]
    rows_ref, conv_ref, hp_ref, lane_ref = rest[:4]
    (g_out, v_out, cv_out, ys_out, st_out, h_out, sum_out, nm_out, sg_out, w_out) = rest[4:14]
    (w_v, nm_v, h_ref, vbuf, tri_ref, bias_ref, pbuf, w_sem, n_sem, o_sem) = rest[14:]
    i = pl.program_id(0)
    save = pltpu.make_async_copy(w_v, w_out, o_sem)

    def rows_at(k):
        return nm_v[pl.ds(pl.multiple_of(k * q, q), q), :]

    @pl.when(i == 0)
    def _():
        copies = load_parts(w_parts, w_v, w_sem, scalars, 0, dm.part_rows)
        copies += load_parts(n_parts, nm_v, n_sem, scalars, dm.at_n, dm.piece_rows)
        for copy in copies:
            copy.start()
        h_ref[...] = jnp.zeros_like(h_ref)
        vbuf[...] = jnp.zeros_like(vbuf)
        r = lax.broadcasted_iota(jnp.int32, (q, q), 0)
        c = lax.broadcasted_iota(jnp.int32, (q, q), 1)
        tri_ref[...] = jnp.where(r >= c, 1.0, 0.0).astype(BF16)
        for copy in copies:
            copy.wait()
        save.start()
        pbuf[...] = dot(nm_v[0:q, :], w_v[...])

    rows = rows_ref[...]
    cols = columns_of(rows)
    nm_out[...] = rows_at(i)
    vbuf[0:8, :] = vbuf[q : q + 8, :]
    vbuf[8 : 8 + q, :] = pbuf[:, ip : ip + vs]
    v_out[...] = pbuf[:, ip : ip + vs].astype(BF16)
    raw = pbuf[:, ip + vs :]
    gates = pbuf[:, :ip].astype(BF16)
    g_out[...] = gates
    st_out[...] = raw
    pbuf[...] = dot(rows_at(jnp.minimum(i + 1, dm.blocks - 1)), w_v[...])

    acts = []
    for c in range(vs // LANES):
        g = slice(c * LANES, (c + 1) * LANES)
        acc = conv_ref[4:5, g] + conv_ref[3:4, g] * vbuf[8 : 8 + q, g]
        for lag in range(1, 4):
            acc = acc + conv_ref[3 - lag : 4 - lag, g] * (
                vbuf[8 - lag : 8 - lag + q, g] * cols[:, lag : lag + 1]
            )
        rounded = acc.astype(BF16)
        cv_out[:, g] = rounded
        acc = rounded.astype(F32)
        acts.append(acc * sigmoid(acc))
    in_map = jnp.concatenate(acts[dm.pairs : dm.pairs + st // LANES], axis=1).astype(BF16)
    out_map = jnp.concatenate(acts[dm.pairs + st // LANES :], axis=1).astype(BF16)

    delta, logs, enter, ending = decay_parts(raw, hp_ref, cols, tri_ref[...])
    logs_t = logs.T
    r = lax.broadcasted_iota(jnp.int32, (q, q), 0)
    c = lax.broadcasted_iota(jnp.int32, (q, q), 1)
    bias_ref[...] = jnp.where((r >= c) & (cols[:, 0:1] == rows[0:1, :]), 0.0, FAR)
    scores = dot(out_map, in_map, MT)
    keep = scalars[dm.at_keep + i].astype(F32)
    total = jnp.exp2(logs[q - 1 :, :]) * keep
    lane = lax.broadcasted_iota(jnp.int32, (q, LANES), 1)
    h_out[...] = h_ref[...]
    in_map_t = in_map.T
    squares = jnp.zeros((q, LANES), F32)
    for p in range(dm.pairs):
        g = slice(p * LANES, (p + 1) * LANES)
        x = acts[p]
        u = x * spread(delta, p, hd)
        ub = u.astype(BF16)
        y = None
        for j in range(dm.per):
            h = p * dm.per + j
            decay = jnp.exp2(logs[:, h : h + 1] - logs_t[h : h + 1, :] + bias_ref[...])
            part = dot((decay * scores).astype(BF16), ub)
            y = part if y is None else jnp.where(lane >= j * hd, part, y)
        held = h_ref[:, g]
        y = y + dot(out_map, held.astype(BF16)) * spread(enter, p, hd)
        wu = (u * spread(ending, p, hd)).astype(BF16)
        h_ref[:, g] = held * spread(total, p, hd) + dot(in_map_t, wu)
        ys_out[:, g] = y
        gate = gates[:, g].astype(F32)
        gated = (y + lane_ref[0:1, g] * x) * (gate * sigmoid(gate))
        sg_out[:, g] = (gated * lane_ref[1:2, g]).astype(BF16)
        squares = squares + gated * gated
    sum_out[...] = jnp.sum(squares.T, axis=0, keepdims=True)

    @pl.when(i == dm.blocks - 1)
    def _():
        save.wait()


def branch_kernel(dm, scalars, *refs):
    n_dp, n_t = dm.n_dp, dm.n_t
    w_parts, sg_hbm = refs[:n_dp], refs[n_dp]
    w_out, outs = refs[n_dp + 1], refs[n_dp + 2 : n_dp + 2 + n_t]
    sg_v, buf, w_sem, g_sem, sem = refs[n_dp + 2 + n_t :]
    per = dm.chunk_rows // BLOCK
    loads = load_parts(w_parts, w_out, w_sem, scalars, 0, dm.part_rows)
    whole = pltpu.make_async_copy(sg_hbm, sg_v, g_sem)
    for copy in loads:
        copy.start()
    whole.start()
    for copy in loads:
        copy.wait()
    whole.wait()
    for i in range(dm.blocks):
        at = slice(i * BLOCK, (i + 1) * BLOCK)
        buf[i] = dot(sg_v[at, :], w_out[...], MT).astype(BF16)
        for k in range(n_t):

            @pl.when(scalars[dm.at_rel + i] == k)
            def _():
                pltpu.make_async_copy(buf.at[i], outs[k].at[i % per], sem.at[i]).start()

    for i in range(dm.blocks):
        pltpu.make_async_copy(buf.at[i], outs[0].at[0], sem.at[i]).wait()


def dots_kernel(dm, scalars, *refs):
    q, n_t = BLOCK, dm.n_t
    c_parts, b_parts = refs[:n_t], refs[n_t : 2 * n_t]
    sq_ref, sum_out, ct_hbm = refs[2 * n_t : 2 * n_t + 3]
    ct_v, br_v, c_sem, b_sem, t_sem = refs[2 * n_t + 3 :]
    takes = [pltpu.make_async_copy(c_parts[k], ct_v.at[k], c_sem.at[k]) for k in range(n_t)]
    takes += [pltpu.make_async_copy(b_parts[k], br_v.at[k], b_sem.at[k]) for k in range(n_t)]
    for copy in takes:
        copy.start()
    gives = []
    for k in range(n_t):
        takes[k].wait()
        takes[n_t + k].wait()
        chunk = pl.multiple_of(scalars[dm.at_c + k], dm.chunk_rows)
        gives.append(
            pltpu.make_async_copy(ct_v.at[k], ct_hbm.at[pl.ds(chunk, dm.chunk_rows), :], t_sem.at[k])
        )
        gives[-1].start()
        for h in range(dm.chunk_rows // q):
            dots = None
            for c in range(dm.width // LANES):
                g = slice(c * LANES, (c + 1) * LANES)
                cot = ct_v[k, h * q : (h + 1) * q, g].astype(F32)
                prod = cot * br_v[k, h, :, g].astype(F32)
                dots = prod if dots is None else dots + prod
            blk = chunk // q + h
            sum_out[blk, 0:1, :] = sq_ref[blk]
            sum_out[blk, 1:2, :] = jnp.sum(dots.T, axis=0, keepdims=True)
    for copy in gives:
        copy.wait()


def gate_kernel(dm, scalars, *refs):
    q, ip, r = BLOCK, dm.ip, dm.part_rows
    (w_ref, wo_ref, rk_ref, lane_ref, g_in, cv_in, ys_in, cot_in, nm_in, ct_in) = refs[:10]
    dg_out, dy_out, lane_out, rows_out, own_out = refs[10:15]
    z_outs = refs[15 : 14 + dm.n_hi]
    acc, dg_s, both = refs[14 + dm.n_hi :]
    i = pl.program_id(0)

    @pl.when(i == 0)
    def _():
        lane_out[...] = jnp.zeros_like(lane_out)
        acc[...] = jnp.zeros_like(acc)

    def gather():
        acc[:, :ip] += dot(nm_in[...], dg_s[...], TM)
        acc[:, ip:] += dot(ct_in[...], both[...], TM)

    def gating():
        pad = jnp.zeros((LANES - 2, q), F32)
        cols = jnp.concatenate([rk_ref[...], pad], axis=0).T
        root, pull = cols[:, 0:1], cols[:, 1:2]
        scaled_cot = dot(cot_in[...], wo_ref[...])
        for p in range(dm.pairs):
            g = slice(p * LANES, (p + 1) * LANES)
            gate, sc = g_in[:, g].astype(F32), scaled_cot[:, g]
            cv = cv_in[:, g].astype(F32)
            x = cv * sigmoid(cv)
            sig = sigmoid(gate)
            z = gate * sig
            y = ys_in[:, g] + lane_ref[0:1, g] * x
            gated = y * z
            scaled = gated * root
            cot = root * (lane_ref[1:2, g] * sc) - pull * gated
            lane_out[0:8, g] += colsum(sc * scaled)
            dy = cot * z
            dy_out[:, g] = dy.astype(BF16)
            dg = (cot * y * (sig + z * (1.0 - sig))).astype(BF16)
            dg_out[:, g] = dg
            dg_s[:, g] = dg
            lane_out[8:16, g] += colsum(dy * x)
            both[:, g] = (scaled * lane_ref[1:2, g]).astype(BF16)

    @pl.when(i == 0)
    def _():
        gating()

    @pl.when((i > 0) & (i < dm.blocks))
    def _():
        gather()
        gating()

    @pl.when(i == dm.blocks)
    def _():
        gather()
        prod = acc[:, :LANES] * w_ref[:, :LANES].astype(F32)
        for p in range(1, dm.pairs):
            g = slice(p * LANES, (p + 1) * LANES)
            prod = prod + acc[:, g] * w_ref[:, g].astype(F32)
        rows_out[...] = gain_rows(prod)
        hi = scalars[dm.at_hi]
        own_out[...] = acc[pl.ds(pl.multiple_of(hi * 2 * r, 8), 2 * r), :]
        for k, z_out in enumerate(z_outs):
            at = pl.multiple_of(scalars[dm.at_hi + k + 1] * 2 * r, 8)
            z_out[...] = acc[pl.ds(at, 2 * r), :].astype(BF16)


def backward_kernel(dm, scalars, *refs):
    q, ip, vs, st, hd, late_cols = BLOCK, dm.ip, dm.vs, dm.state, dm.hd, dm.late
    groups = dm.group_sizes
    w_ref, rows_ref, conv_ref, hp_ref, lane_ref, lanes_ref, gain_ref = refs[:7]
    dg_in, nm_in, dy_in, v_in, cv_in, ys_in, st_in, h_in = refs[7:15]
    mine_out, theirs_out, kept_out = refs[15:18]
    nc_outs = refs[18 : 18 + len(groups)]
    (dh_ref, dbuf, tri_ref, bias_ref, ds_ref, u_s, dx_s, act_s, t1_s, t2_s) = refs[
        18 + len(groups) : 28 + len(groups)
    ]
    (pj_s, acc, tap_out, head_out, nc_buf, nc_sem) = refs[28 + len(groups) :]
    i = pl.program_id(0)
    blk = jnp.maximum(dm.blocks - 1 - i, 0)

    def send(k, at, row):
        return pltpu.make_async_copy(nc_buf.at[at], nc_outs[k].at[row], nc_sem.at[at])

    @pl.when(i == 0)
    def _():
        dh_ref[...] = jnp.zeros_like(dh_ref)
        dbuf[...] = jnp.zeros_like(dbuf)
        tap_out[...] = jnp.zeros_like(tap_out)
        head_out[...] = jnp.zeros_like(head_out)
        acc[...] = jnp.zeros_like(acc)
        r = lax.broadcasted_iota(jnp.int32, (q, q), 0)
        c = lax.broadcasted_iota(jnp.int32, (q, q), 1)
        tri_ref[...] = jnp.where(r >= c, 1.0, 0.0).astype(BF16)

    slot = lax.rem(i, 2)

    @pl.when(i >= 3)
    def _():
        send(0, slot, 0).wait()

    def project():
        nc = dot(dg_in[...], w_ref[:, :ip], MT) + dot(pj_s[...], w_ref[:, ip:], MT)
        nc_buf[slot] = nc.astype(BF16)
        acc[...] += dot(nm_in[...], pj_s[...], TM)

    def scan():
        rows = rows_ref[...]
        cols = columns_of(rows)
        raw = st_in[...]
        tri = tri_ref[...]
        delta, logs, enter, ending = decay_parts(raw, hp_ref, cols, tri)
        logs_t = logs.T
        lane = lax.broadcasted_iota(jnp.int32, (q, LANES), 1)

        acts, slopes = [], []
        for c in range(vs // LANES):
            g = slice(c * LANES, (c + 1) * LANES)
            cv = cv_in[:, g].astype(F32)
            sig = sigmoid(cv)
            act = cv * sig
            acts.append(act)
            slopes.append(sig + act * (1.0 - sig))
        in_map = jnp.concatenate(acts[dm.pairs : dm.pairs + st // LANES], axis=1).astype(BF16)
        out_map = jnp.concatenate(acts[dm.pairs + st // LANES :], axis=1).astype(BF16)

        for p in range(dm.pairs):
            g = slice(p * LANES, (p + 1) * LANES)
            u_s[:, g] = acts[p] * spread(delta, p, hd)

        r = lax.broadcasted_iota(jnp.int32, (q, q), 0)
        c = lax.broadcasted_iota(jnp.int32, (q, q), 1)
        bias_ref[...] = jnp.where((r <= c) & (cols[:, 0:1] == rows[0:1, :]), 0.0, FAR)
        scores = dot(in_map, out_map, MT)
        dh_b = dh_ref[...].astype(BF16)
        h_b = h_in[...].astype(BF16)
        out_map_t = out_map.T
        keep = scalars[dm.at_keep + blk].astype(F32)
        total = jnp.exp2(logs[q - 1 :, :]) * keep
        d_in = jnp.zeros((q, st), F32)
        d_out = jnp.zeros((q, st), F32)
        for p in range(dm.pairs):
            g = slice(p * LANES, (p + 1) * LANES)
            u, dyb = u_s[:, g], dy_in[:, g]
            ub, dy = u.astype(BF16), dyb.astype(F32)
            du = None
            for j in range(dm.per):
                h = p * dm.per + j
                mine = (lane >= j * hd) & (lane < (j + 1) * hd)
                decay = jnp.exp2(logs_t[h : h + 1, :] - logs[:, h : h + 1] + bias_ref[...])
                part = dot((decay * scores).astype(BF16), dyb)
                du = part if du is None else jnp.where(lane >= j * hd, part, du)
                dm_t = dot(jnp.where(mine, u, 0.0).astype(BF16), dyb, MT)
                if p == 0 and j == 0:
                    ds_ref[...] = dm_t * decay
                else:
                    ds_ref[...] += dm_t * decay
            end_e = spread(ending, p, hd)
            late = end_e * dot(in_map, dh_b[:, g])
            du = du + late
            wu = (u * end_e).astype(BF16)
            edy = (dy * spread(enter, p, hd)).astype(BF16)
            d_in = d_in + dot(wu, dh_b[:, g], MT)
            d_out = d_out + dot(edy, h_b[:, g], MT)
            u32 = ub.astype(F32)
            t1_s[:, g] = dy * ys_in[:, g] - u32 * du
            t2_s[:, g] = du * acts[p]
            kept = dh_ref[:, g] * spread(total, p, hd)
            act_s[:, g] = colsum(u32 * late) + colsum(h_in[:, g] * kept)
            dh_ref[:, g] = kept + dot(out_map_t, edy)
            dx_s[:, g] = (spread(delta, p, hd) * du + lane_ref[0:1, g] * dy) * slopes[p]
        ds_b = ds_ref[...].astype(BF16)
        d_in = d_in + dot(ds_b, out_map)
        d_out = d_out + dot(ds_b, in_map, TM)

        hr = lax.broadcasted_iota(jnp.int32, (ip, LANES), 0)
        hc = lax.broadcasted_iota(jnp.int32, (ip, LANES), 1)
        pick = jnp.where(hr // hd == hc, 1.0, 0.0).astype(BF16)
        d_log = split_dot(t1_s[...], pick)
        last = split_dot(jnp.sum(act_s[...], axis=0, keepdims=True), pick)
        row = lax.broadcasted_iota(jnp.int32, (q, LANES), 0)
        d_log = d_log + jnp.where(row == q - 1, last, 0.0)
        d_step = dot_split(tri, d_log, TM)
        head_out[8:16, :] += colsum(d_step * delta)
        d_delta = hp_ref[1:2, :] * d_step + split_dot(t2_s[...], pick)
        d_raw = d_delta * sigmoid(raw + hp_ref[0:1, :])
        head_out[0:8, :] += colsum(d_raw)
        pj_s[:, vs:] = d_raw.astype(BF16)

        dbuf[q : q + 8, :] = dbuf[0:8, :]
        for c in range(vs // LANES):
            g = slice(c * LANES, (c + 1) * LANES)
            if c < dm.pairs:
                dbuf[0:q, g] = dx_s[:, g]
            else:
                k = (c - dm.pairs) * LANES
                source = d_in[:, k : k + LANES] if k < st else d_out[:, k - st : k - st + LANES]
                dbuf[0:q, g] = source * slopes[c]
        for c in range(vs // LANES):
            g = slice(c * LANES, (c + 1) * LANES)
            v = v_in[:, g].astype(F32)
            shifted = dbuf[0:q, g]
            tap_out[32:40, g] += colsum(shifted)
            tap_out[24:32, g] += colsum(shifted * v)
            dv = conv_ref[3:4, g] * shifted
            for lag in range(1, 4):
                shifted = dbuf[lag : lag + q, g] * cols[:, 3 + lag : 4 + lag]
                tap_out[24 - 8 * lag : 32 - 8 * lag, g] += colsum(shifted * v)
                dv = dv + conv_ref[3 - lag : 4 - lag, g] * shifted
            pj_s[:, g] = dv.astype(BF16)


    @pl.when(i == 0)
    def _():
        scan()

    @pl.when((i > 0) & (i < dm.blocks))
    def _():
        project()
        scan()

    @pl.when(i == dm.blocks)
    def _():
        project()

    before = jnp.minimum(blk + 1, dm.blocks - 1)
    before = jnp.where(i == dm.blocks, 0, before)
    for k in range(len(groups)):

        @pl.when((i > 0) & (scalars[dm.at_group + before] == k))
        def _():
            send(k, slot, scalars[dm.at_slot + before]).start()

    @pl.when(i == dm.blocks)
    def _():
        core, r = scalars[dm.at_core], dm.part_rows
        for h in range(dm.n_hi):
            at = pl.multiple_of((2 * h + core) * r, 8)
            mine_out[h * r : (h + 1) * r, :] = acc[pl.ds(at, r), :]
            at = pl.multiple_of((2 * h + 1 - core) * r, 8)
            theirs_out[h * r : (h + 1) * r, :] = acc[pl.ds(at, r), :].astype(BF16)
        small = []

        def put(v):
            for c in range(v.shape[1] // LANES):
                small.append(jnp.sum(v[:, c * LANES : (c + 1) * LANES], axis=0, keepdims=True))

        for k in range(5):
            put(tap_out[8 * k : 8 * k + 8, :ip])
        for k in range(2):
            put(lanes_ref[8 * k : 8 * k + 8, :])
        for k in range(2):
            put(head_out[8 * k : 8 * k + 8, :])
        zero = jnp.zeros((1, LANES), F32)
        small.extend([zero] * (dm.local_rows - len(small)))
        for k in range(5):
            put(tap_out[8 * k : 8 * k + 8, ip:])
        prod = acc[:, :LANES] * w_ref[:, ip : ip + LANES].astype(F32)
        for p in range(1, late_cols // LANES):
            g = slice(p * LANES, (p + 1) * LANES)
            o = slice(ip + p * LANES, ip + (p + 1) * LANES)
            prod = prod + acc[:, g] * w_ref[:, o].astype(F32)
        prod = gain_rows(prod)
        for c in range(dm.width // LANES):
            g = slice(c * LANES, (c + 1) * LANES)
            small.append(prod[0:1, g] + gain_ref[0:1, g])
        small.extend([zero] * (late_cols // 16 - len(small)))
        for c in range(late_cols // LANES):
            g = slice(c * LANES, (c + 1) * LANES)
            parts = two_parts(jnp.concatenate(small[8 * c : 8 * c + 8], axis=0))
            theirs_out[dm.n_hi * r :, g] = parts
            kept_out[:, g] = parts
        send(0, 1 - slot, 0).wait()
        send(0, slot, 0).wait()


def two_parts(v):
    high = v.astype(BF16).astype(F32)
    return jnp.concatenate([high, v - high], axis=0).astype(BF16)


def one_part(v):
    return v[0:8, :].astype(F32) + v[8:16, :].astype(F32)


def gain_rows(acc):
    high = acc.astype(BF16)
    rest = acc - high.astype(F32)
    mid = rest.astype(BF16)
    low = (rest - mid.astype(F32)).astype(BF16)
    one = jnp.ones((8, LANES), BF16)
    return dot(one, high, MT) + dot(one, mid, MT) + dot(one, low, MT)


def pair_kernel(dm, scalars, mine_ref, kept_ref, theirs_ref, own_out, *outs):
    r = dm.part_rows
    tail = dm.n_hi * r
    small = one_part(kept_ref[...]) + one_part(theirs_ref[tail:, :])
    small = two_parts(small)
    for k in range(dm.n_hi):
        at = pl.multiple_of(scalars[dm.at_hi + k] * r, 8)
        both = mine_ref[pl.ds(at, r), :] + theirs_ref[pl.ds(at, r), :].astype(F32)
        if k == 0:
            own_out[...] = both
        else:
            outs[k][0:r, :] = both.astype(BF16)
        if k > 0:
            outs[k][r:, :] = small
        else:
            outs[0][...] = small


def early_kernel(dm, scalars, own_ref, *refs):
    parts, (mine_out, theirs_out, total) = refs[: dm.n_hi - 1], refs[dm.n_hi - 1 :]
    r = dm.part_rows
    both = own_ref[...]
    for part in parts:
        both = both + part[...].astype(F32)
    total[...] = both
    core = scalars[dm.at_core]
    mine_out[...] = total[pl.ds(pl.multiple_of(core * r, 8), r), :]
    theirs_out[...] = total[pl.ds(pl.multiple_of((1 - core) * r, 8), r), :].astype(BF16)


def grads_kernel(dm, scalars, hp_ref, own_ref, kept_ref, mine_ref, theirs_ref, *refs):
    n, r, st2 = dm.n_hi, dm.part_rows, 2 * dm.state
    parts = refs[: n - 1]
    (gate_out, value_out, step_out, outp_out, share_out) = refs[n - 1 : n + 4]
    (tap_out, tapb_out, gain_out, skip_out, sb_out, dl_out, hold) = refs[n + 4 :]
    total = own_ref[...]
    for part in parts:
        total = total + part[0:r, :].astype(F32)
    early = mine_ref[...] + theirs_ref[...].astype(F32)
    inner, heads = gate_out.shape[1], step_out.shape[0]
    gate_out[...] = early[:, :inner]
    outp_out[...] = early[:, dm.ip : dm.ip + inner]
    value_out[...] = total[:, :inner]
    share_out[0:r, :] = total[:, dm.ip : dm.vs].astype(BF16)
    step_out[...] = total[:, dm.vs :].T[0:heads, :]
    hold[0] = one_part(kept_ref[...])
    for k, part in enumerate(parts):
        hold[k + 1] = one_part(part[r:, :])
    small = hold[scalars[dm.at_from]]
    for k in range(1, n):
        small = small + hold[scalars[dm.at_from + k]]
    flat = [
        small[j : j + 1, c * LANES : (c + 1) * LANES]
        for c in range(dm.late // LANES)
        for j in range(8)
    ]

    def take(first, width):
        return jnp.concatenate(flat[first : first + dm.pairs], axis=1)[:, :width]

    for k in range(4):
        tap_out[k : k + 1, :] = take(k * dm.pairs, inner)
    tapb_out[...] = take(4 * dm.pairs, inner)[0]
    gain_out[...] = take(5 * dm.pairs, inner)[0]
    lane = lax.broadcasted_iota(jnp.int32, (1, LANES), 1)
    skip = jnp.zeros((1, LANES), F32)
    for h in range(heads):
        row = flat[6 * dm.pairs + h // dm.per]
        mine = lane // dm.hd == h % dm.per
        one = jnp.sum(jnp.where(mine, row, 0.0), axis=1, keepdims=True)
        skip = jnp.where(lane == h, one, skip)
    skip_out[...] = skip[0, :heads]
    sb_out[...] = flat[7 * dm.pairs][0, :heads]
    dl_out[...] = (flat[7 * dm.pairs + 1] * hp_ref[1:2, :])[0, :heads]
    first = dm.local_rows // 8
    for c in range(st2 // LANES):
        g = slice((first + c) * LANES, (first + c + 1) * LANES)
        share_out[r:, c * LANES : (c + 1) * LANES] = two_parts(small[:, g])


def share_kernel(dm, scalars, norm_ref, *refs):
    r, st2 = dm.part_rows, 2 * dm.state
    parts = refs[: dm.n_t]
    shared_out, tap_out, tapb_out, norm_out, hold = refs[dm.n_t :]
    for k, part in enumerate(parts):
        hold[k] = part[...]
    shared, common = None, None
    for k in range(dm.n_t):
        part = hold[scalars[dm.at_side + k]]
        share, small = part[0:r, :].astype(F32), one_part(part[r:, :])
        shared = share if shared is None else shared + share
        common = small if common is None else common + small
    shared_out[...] = shared
    flat = [
        common[j : j + 1, c * LANES : (c + 1) * LANES] for c in range(st2 // LANES) for j in range(8)
    ]
    per = st2 // LANES
    for k in range(4):
        tap_out[k : k + 1, :] = jnp.concatenate(flat[k * per : (k + 1) * per], axis=1)
    tapb_out[...] = jnp.concatenate(flat[4 * per : 5 * per], axis=1)[0]
    rows = flat[5 * per : 5 * per + dm.width // LANES]
    norm_out[...] = jnp.concatenate(rows, axis=1)[0] / norm_ref[...]


def input_kernel(sets, steps, x_ref, cot_ref, gain_ref, *refs):
    out = refs[-1]
    x = x_ref[...]
    root = lax.rsqrt(jnp.mean(x * x, axis=1, keepdims=True) + EPS)
    first = 0
    for k, count in enumerate(sets):
        parts = refs[first : first + count]
        first += count

        @pl.when(pl.program_id(0) // steps == k)
        def _():
            nc = parts[0][...].astype(F32)
            for part in parts[1:]:
                nc = nc + part[...].astype(F32)
            hat = nc * gain_ref[...][None]
            mean = jnp.mean(hat * x, axis=1, keepdims=True)
            out[...] = cot_ref[...].astype(F32) + root * hat - x * (root * root * root * mean)


def shift_hi(n, k):
    return [(i, ((i // 2 + k) % (n // 2)) * 2 + i % 2) for i in range(n)]


def swap(n, k):
    return [(i, i ^ k) for i in range(n)]


def pad_cols(v, to):
    return jnp.pad(v, ((0, 0), (0, to - v.shape[1])))


def pad_vec(v, to):
    return jnp.pad(v, (0, to - v.shape[0]))


def body(
    n_dp,
    n_t,
    block_input,
    segment_ids,
    norm_gain,
    gate_proj,
    value_proj,
    shared_proj,
    step_proj,
    conv_value_weight,
    conv_value_bias,
    conv_shared_weight,
    conv_shared_bias,
    step_bias,
    decay_log,
    skip_weight,
    gate_gain,
    output_proj,
    out_cotangent,
):
    q = BLOCK
    chunk_rows, width = block_input.shape
    length = segment_ids.shape[1]
    inner, heads = gate_proj.shape[1], step_proj.shape[1]
    part_rows = gate_proj.shape[0]
    state = shared_proj.shape[1] // 2
    hd = inner // heads
    dm = Dims(n_dp, n_t, length, width, inner, hd, state, part_rows, chunk_rows)
    ip, vs, nb, n_hi = dm.ip, dm.vs, dm.blocks, dm.n_hi
    me_t = lax.axis_index("tensor")
    me_dp = lax.axis_index("dp")
    hi, core = me_dp // 2, me_dp % 2

    def across(v, k):
        return lax.ppermute(v, "tensor", swap(n_t, k))

    def along(v, k):
        return lax.ppermute(v, "dp", shift_hi(n_dp, k))

    def partner(v):
        return lax.ppermute(v, "dp", swap(n_dp, 1))

    def vmem(shape, dtype):
        return pltpu.VMEM(shape, dtype)

    limit = 60 * 1024 * 1024
    params = pltpu.CompilerParams(dimension_semantics=("arbitrary",), vmem_limit_bytes=limit)
    hbm = pl.BlockSpec(memory_space=pl.ANY)

    def out(*shape, dtype=F32):
        return jax.ShapeDtypeStruct(shape, dtype)

    part = min(LANES, dm.piece_rows)
    normed = pl.pallas_call(
        functools.partial(norm_kernel, part),
        out_shape=[out(dm.piece_rows, width, dtype=BF16)] * dm.halves,
        in_specs=[hbm, pl.BlockSpec(memory_space=pltpu.VMEM)],
        scratch_shapes=[
            vmem((chunk_rows, width), F32),
            pltpu.SemaphoreType.DMA((chunk_rows // part,)),
        ],
        compiler_params=pltpu.CompilerParams(vmem_limit_bytes=limit),
        name="normalize",
    )(block_input, norm_gain)
    if dm.halves == 2:
        a, b = normed
        xa, yb = across(a, 1), across(b, 2)
        ya, xb = across(a, 2), across(b, 1)
        n_list = [a, b, xa, xb, ya, yb, across(xa, 2), across(yb, 1)]
        n_rows = jnp.concatenate(
            [(me_t ^ k) * chunk_rows + jnp.arange(2) * dm.piece_rows for k in range(4)]
        )
    else:
        n_list = [normed[0]] + [across(normed[0], k) for k in range(1, n_t)]
        n_rows = (me_t ^ jnp.arange(n_t)) * chunk_rows
    step_first, _ = lax.optimization_barrier((step_proj.T, normed[0]))
    packed = pl.pallas_call(
        functools.partial(pack_kernel, dm),
        out_shape=out(part_rows, dm.np, dtype=BF16),
        name="pack_weights",
    )(gate_proj, value_proj, shared_proj, step_first)
    w_list = [packed] + [along(packed, k) for k in range(1, n_hi)]
    w_list = w_list + [partner(v) for v in w_list]
    outp = pad_cols(output_proj.T, ip)
    o_list = [outp] + [along(outp, k) for k in range(1, n_hi)]
    o_list = o_list + [partner(v) for v in o_list]

    seg = segment_ids[0]
    segb = seg.reshape(nb, q)
    last = segb[:, -1]
    prev_last = jnp.concatenate([jnp.full((1,), -1, jnp.int32), last[:-1]])
    gap = jnp.full((3,), -1, jnp.int32)
    wide = jnp.concatenate([gap, seg, gap])
    rows = [seg.astype(F32)]
    rows += [(wide[3 - k : 3 - k + length] == seg).astype(F32) for k in range(1, 4)]
    rows += [(wide[3 + k : 3 + k + length] == seg).astype(F32) for k in range(1, 4)]
    rows += [
        (segb == prev_last[:, None]).astype(F32).reshape(-1),
        (segb == last[:, None]).astype(F32).reshape(-1),
    ]
    rows = jnp.concatenate([jnp.stack(rows), jnp.zeros((16 - len(rows), length), F32)], axis=0)
    keep = (last == prev_last).astype(jnp.int32)
    other = (hi - jnp.arange(n_hi)) % n_hi
    rel = (jnp.arange(nb) * q // chunk_rows) ^ me_t
    half = jnp.arange(nb) % (chunk_rows // q)
    if dm.halves == 2:
        group_of = jnp.array([[2, 2], [0, 2], [2, 1], [0, 1]])
        slot_of = jnp.array([[0, 2], [0, 3], [1, 0], [1, 1]])
        group, slot = group_of[rel, half], slot_of[rel, half]
        dm.group_sizes = (2, 2, 4)
    else:
        group, slot = rel, half
        dm.group_sizes = (chunk_rows // q,) * n_t
    scalars = jnp.concatenate(
        [
            (other * 2 + core) * part_rows,
            (other * 2 + 1 - core) * part_rows,
            n_rows,
            (me_t ^ jnp.arange(n_t)) * chunk_rows,
            keep,
            rel,
            group,
            slot,
            (hi + jnp.arange(n_hi)) % n_hi,
            core[None],
            (hi - jnp.arange(n_hi)) % n_hi,
            me_t ^ jnp.arange(n_t),
        ]
    ).astype(jnp.int32)

    conv = jnp.concatenate(
        [
            pad_cols(jnp.concatenate([conv_value_weight, conv_value_bias[None]]), ip),
            jnp.concatenate([conv_shared_weight, conv_shared_bias[None]]),
        ],
        axis=1,
    )
    conv = jnp.pad(conv, ((0, 3), (0, 0)))
    rate = -jnp.exp(decay_log)
    per_head = jnp.stack([pad_vec(step_bias, LANES), pad_vec(rate, LANES)])
    per_head = jnp.pad(per_head, ((0, 6), (0, 0)))
    per_lane = jnp.stack([pad_vec(jnp.repeat(skip_weight, hd), ip), pad_vec(gate_gain, ip)])
    per_lane = jnp.pad(per_lane, ((0, 6), (0, 0)))

    def const(*shape):
        return pl.BlockSpec(shape, lambda i, s: (0,) * len(shape))

    def fblock(cols):
        return pl.BlockSpec((q, cols), lambda i, s: (i, 0))

    def fsum(k):
        return pl.BlockSpec((None, k, q), lambda i, s: (i, 0, 0))

    def grid(steps, in_specs, out_specs, scratch):
        return pltpu.PrefetchScalarGridSpec(
            num_scalar_prefetch=1,
            grid=(steps,),
            in_specs=in_specs,
            out_specs=out_specs,
            scratch_shapes=scratch,
        )

    (gate, value, conved, scan, steps_raw, held, squares, normed_all, scaled, weights) = pl.pallas_call(
        functools.partial(forward_kernel, dm),
        out_shape=[
            out(length, ip, dtype=BF16),
            out(length, vs, dtype=BF16),
            out(length, vs, dtype=BF16),
            out(length, ip),
            out(length, LANES),
            out(nb * state, ip),
            out(nb, 1, q),
            out(length, width, dtype=BF16),
            out(length, ip, dtype=BF16),
            out(width, dm.np, dtype=BF16),
        ],
        grid_spec=grid(
            nb,
            [hbm] * (n_dp + dm.pieces)
            + [
                pl.BlockSpec((16, q), lambda i, s: (0, i)),
                const(8, vs),
                const(8, LANES),
                const(8, ip),
            ],
            [
                fblock(ip),
                fblock(vs),
                fblock(vs),
                fblock(ip),
                fblock(LANES),
                pl.BlockSpec((state, ip), lambda i, s: (i, 0)),
                fsum(1),
                fblock(width),
                fblock(ip),
                hbm,
            ],
            [
                vmem((width, dm.np), BF16),
                vmem((length, width), BF16),
                vmem((state, ip), F32),
                vmem((q + 8, vs), F32),
                vmem((q, q), BF16),
                vmem((q, q), F32),
                vmem((q, dm.np), F32),
                pltpu.SemaphoreType.DMA((n_dp,)),
                pltpu.SemaphoreType.DMA((dm.pieces,)),
                pltpu.SemaphoreType.DMA,
            ],
        ),
        compiler_params=params,
        cost_estimate=pl.CostEstimate(
            flops=30_000_000_000, bytes_accessed=30_000_000, transcendentals=0
        ),
        name="block_forward",
    )(scalars, *w_list, *n_list, rows, conv, per_head, per_lane)

    c_list = [out_cotangent] + [across(out_cotangent, k) for k in range(1, n_t)]
    in_vmem = pl.BlockSpec(memory_space=pltpu.VMEM)
    w_back, *branch = pl.pallas_call(
        functools.partial(branch_kernel, dm),
        out_shape=[out(width, ip, dtype=BF16)]
        + [out(chunk_rows // q, q, width, dtype=BF16)] * n_t,
        grid_spec=grid(
            1,
            [hbm] * (n_dp + 1),
            [in_vmem] + [hbm] * n_t,
            [
                vmem((length, ip), BF16),
                vmem((nb, q, width), BF16),
                pltpu.SemaphoreType.DMA((n_dp,)),
                pltpu.SemaphoreType.DMA,
                pltpu.SemaphoreType.DMA((nb,)),
            ],
        ),
        compiler_params=params,
        cost_estimate=pl.CostEstimate(
            flops=3_000_000_000, bytes_accessed=10_000_000, transcendentals=0
        ),
        name="branch_output",
    )(scalars, *o_list, scaled)
    sums, cot_all = pl.pallas_call(
        functools.partial(dots_kernel, dm),
        out_shape=[out(nb, 2, q), out(length, width, dtype=BF16)],
        grid_spec=grid(
            1,
            [hbm] * (2 * n_t) + [in_vmem],
            [in_vmem, hbm],
            [
                vmem((n_t, chunk_rows, width), BF16),
                vmem((n_t, chunk_rows // q, q, width), BF16),
                pltpu.SemaphoreType.DMA((n_t,)),
                pltpu.SemaphoreType.DMA((n_t,)),
                pltpu.SemaphoreType.DMA((n_t,)),
            ],
        ),
        compiler_params=params,
        cost_estimate=pl.CostEstimate(
            flops=3_000_000_000, bytes_accessed=10_000_000, transcendentals=0
        ),
        name="branch_dots",
    )(scalars, *c_list, *branch, squares)
    total = sums
    for k in range(1, n_t):
        total = total + across(sums, k)
    root = lax.rsqrt(total[:, 0] / (inner * n_t) + EPS)
    pull = root * root * root * (total[:, 1] / (inner * n_t))
    rk = jnp.stack([root, pull], axis=1)
    branch_sum = branch[0].astype(F32)
    for k in range(1, n_t):
        branch_sum = branch_sum + across(branch[k], k).astype(F32)
    own_root = lax.dynamic_slice_in_dim(root.reshape(length), me_t * chunk_rows, chunk_rows)
    block_output = block_input + own_root[:, None] * branch_sum.reshape(chunk_rows, width)

    def bblock(cols):
        return pl.BlockSpec((q, cols), lambda i, s: (jnp.maximum(nb - 1 - i, 0), 0))

    def bago(cols):
        return pl.BlockSpec((q, cols), lambda i, s: (jnp.minimum(nb - i, nb - 1), 0))

    def now(cols):
        return pl.BlockSpec((q, cols), lambda i, s: (jnp.minimum(i, nb - 1), 0))

    def ago(cols):
        return pl.BlockSpec((q, cols), lambda i, s: (jnp.maximum(i - 1, 0), 0))

    dgate, dscan, lanes, gate_rows, own_early, *early = pl.pallas_call(
        functools.partial(gate_kernel, dm),
        out_shape=[
            out(length, ip, dtype=BF16),
            out(length, ip, dtype=BF16),
            out(16, ip),
            out(8, width),
            out(2 * part_rows, 2 * ip),
        ]
        + [out(2 * part_rows, 2 * ip, dtype=BF16)] * (n_hi - 1),
        grid_spec=grid(
            nb + 1,
            [
                const(width, ip),
                const(width, ip),
                pl.BlockSpec((None, 2, q), lambda i, s: (jnp.minimum(i, nb - 1), 0, 0)),
                const(8, ip),
                now(ip),
                now(ip),
                now(ip),
                now(width),
                ago(width),
                ago(width),
            ],
            [now(ip), now(ip), const(16, ip), const(8, width)]
            + [const(2 * part_rows, 2 * ip)] * n_hi,
            [vmem((width, 2 * ip), F32), vmem((q, ip), BF16), vmem((q, ip), BF16)],
        ),
        compiler_params=params,
        cost_estimate=pl.CostEstimate(
            flops=6_000_000_000, bytes_accessed=20_000_000, transcendentals=0
        ),
        name="gate_backward",
    )(scalars, weights, w_back, rk, per_lane, gate, conved, scan, cot_all, normed_all, cot_all)
    early = [along(v, k + 1) for k, v in enumerate(early)]

    r_all = n_hi * part_rows
    mine, theirs, kept, *nc = pl.pallas_call(
        functools.partial(backward_kernel, dm),
        out_shape=[
            out(r_all, dm.late),
            out(r_all + 16, dm.late, dtype=BF16),
            out(16, dm.late, dtype=BF16),
        ]
        + [out(k, q, width, dtype=BF16) for k in dm.group_sizes],
        grid_spec=grid(
            nb + 1,
            [
                const(width, dm.np),
                pl.BlockSpec((16, q), lambda i, s: (0, jnp.maximum(nb - 1 - i, 0))),
                const(8, vs),
                const(8, LANES),
                const(8, ip),
                const(16, ip),
                const(8, width),
                bago(ip),
                bago(width),
                bblock(ip),
                bblock(vs),
                bblock(vs),
                bblock(ip),
                bblock(LANES),
                pl.BlockSpec((state, ip), lambda i, s: (jnp.maximum(nb - 1 - i, 0), 0)),
            ],
            [const(r_all, dm.late), const(r_all + 16, dm.late), const(16, dm.late)]
            + [hbm] * len(dm.group_sizes),
            [
                vmem((state, ip), F32),
                vmem((q + 8, vs), F32),
                vmem((q, q), BF16),
                vmem((q, q), F32),
                vmem((q, q), F32),
                vmem((q, ip), F32),
                vmem((q, ip), F32),
                vmem((8, ip), F32),
                vmem((q, ip), F32),
                vmem((q, ip), F32),
                vmem((q, dm.late), BF16),
                vmem((width, dm.late), F32),
                vmem((40, vs), F32),
                vmem((16, LANES), F32),
                vmem((2, q, width), BF16),
                pltpu.SemaphoreType.DMA((2,)),
            ],
        ),
        compiler_params=params,
        cost_estimate=pl.CostEstimate(
            flops=40_000_000_000, bytes_accessed=30_000_000, transcendentals=0
        ),
        name="block_backward",
    )(
        scalars,
        weights,
        rows,
        conv,
        per_head,
        per_lane,
        lanes,
        gate_rows,
        dgate,
        normed_all,
        dscan,
        value,
        conved,
        scan,
        steps_raw,
        held,
    )

    part = min(q, dm.piece_rows)
    steps = dm.piece_rows // part

    def turn(k):
        return pl.BlockSpec((part, width), lambda i: (jnp.clip(i - k * steps, 0, steps - 1), 0))

    def slot_of_piece(k, at):
        return pl.BlockSpec(
            (None, part, width), lambda i: (at, jnp.clip(i - k * steps, 0, steps - 1), 0)
        )

    if dm.halves == 2:
        from_x, from_y, stay = across(nc[0], 1), across(nc[1], 2), nc[2]
        pass_y = (stay[1].astype(F32) + from_x[1].astype(F32)).astype(BF16)
        pass_x = (stay[3].astype(F32) + from_y[1].astype(F32)).astype(BF16)
        got_y, got_x = across(pass_y, 2), across(pass_x, 1)
        sets = (3, 3)
        terms = [stay, from_x, got_y, stay, from_y, got_x]
        specs = [slot_of_piece(0, 0), slot_of_piece(0, 0), turn(0)]
        specs += [slot_of_piece(1, 2), slot_of_piece(1, 0), turn(1)]
    else:
        sets = (n_t,)
        terms = [nc[0]] + [across(nc[k], k) for k in range(1, n_t)]
        terms = [v.reshape(chunk_rows, width) for v in terms]
        specs = [turn(0)] * n_t
    in_turn = pl.BlockSpec((part, width), lambda i: (i, 0))
    input_grad = pl.pallas_call(
        functools.partial(input_kernel, sets, steps),
        out_shape=out(chunk_rows, width),
        grid=(len(sets) * steps,),
        in_specs=[in_turn, in_turn, pl.BlockSpec((width,), lambda i: (0,))] + specs,
        out_specs=in_turn,
        compiler_params=params,
        name="input_gradient",
    )(block_input, out_cotangent, norm_gain, *terms)

    late = dm.late
    theirs = partner(theirs)
    own, own_small, *others = pl.pallas_call(
        functools.partial(pair_kernel, dm),
        out_shape=[out(part_rows, late), out(16, late, dtype=BF16)]
        + [out(part_rows + 16, late, dtype=BF16)] * (n_hi - 1),
        grid_spec=grid(1, [in_vmem] * 3, [in_vmem] * (n_hi + 1), []),
        compiler_params=params,
        name="core_sum",
    )(scalars, mine, kept, theirs)
    others = [along(v, k + 1) for k, v in enumerate(others)]
    early_mine, early_theirs = pl.pallas_call(
        functools.partial(early_kernel, dm),
        out_shape=[out(part_rows, 2 * ip), out(part_rows, 2 * ip, dtype=BF16)],
        grid_spec=grid(
            1, [in_vmem] * n_hi, [in_vmem] * 2, [vmem((2 * part_rows, 2 * ip), F32)]
        ),
        compiler_params=params,
        name="early_sum",
    )(scalars, own_early, *early)
    early_theirs = partner(early_theirs)
    (
        gate_proj_grad,
        value_proj_grad,
        step_t,
        outp_t,
        share,
        conv_value_weight_grad,
        conv_value_bias_grad,
        gate_gain_grad,
        skip_weight_grad,
        step_bias_grad,
        decay_log_grad,
    ) = pl.pallas_call(
        functools.partial(grads_kernel, dm),
        out_shape=[
            out(part_rows, inner),
            out(part_rows, inner),
            out(heads, part_rows),
            out(part_rows, inner),
            out(part_rows + 16, 2 * state, dtype=BF16),
            out(4, inner),
            out(inner),
            out(inner),
            out(heads),
            out(heads),
            out(heads),
        ],
        grid_spec=grid(1, [in_vmem] * (n_hi + 4), [in_vmem] * 11, [vmem((n_hi, 8, late), F32)]),
        compiler_params=params,
        name="gradient_sum",
    )(scalars, per_head, own, own_small, early_mine, early_theirs, *others)
    shares = [share] + [across(share, k) for k in range(1, n_t)]
    shared_proj_grad, conv_shared_weight_grad, conv_shared_bias_grad, norm_gain_grad = pl.pallas_call(
        functools.partial(share_kernel, dm),
        out_shape=[out(part_rows, 2 * state), out(4, 2 * state), out(2 * state), out(width)],
        grid_spec=grid(
            1,
            [in_vmem] * (n_t + 1),
            [in_vmem] * 4,
            [vmem((n_t, part_rows + 16, 2 * state), BF16)],
        ),
        compiler_params=params,
        name="shared_sum",
    )(scalars, norm_gain, *shares)
    return (
        block_output,
        input_grad,
        norm_gain_grad,
        gate_proj_grad,
        value_proj_grad,
        shared_proj_grad,
        step_t.T,
        conv_value_weight_grad,
        conv_value_bias_grad,
        conv_shared_weight_grad,
        conv_shared_bias_grad,
        step_bias_grad,
        decay_log_grad,
        skip_weight_grad,
        gate_gain_grad,
        outp_t.T,
    )


def solution(mesh):
    n_dp, n_t = mesh.shape["dp"], mesh.shape["tensor"]
    both = ("dp", "tensor")
    return jax.shard_map(
        functools.partial(body, n_dp, n_t),
        mesh=mesh,
        in_specs=(
            P(both, None),
            P("dp", None),
            P(),
            P("dp", "tensor"),
            P("dp", "tensor"),
            P("dp", None),
            P("dp", "tensor"),
            P(None, "tensor"),
            P("tensor"),
            P(),
            P(),
            P("tensor"),
            P("tensor"),
            P("tensor"),
            P("tensor"),
            P("tensor", "dp"),
            P(both, None),
        ),
        out_specs=(
            P(both, None),
            P(both, None),
            P(),
            P("dp", "tensor"),
            P("dp", "tensor"),
            P("dp", None),
            P("dp", "tensor"),
            P(None, "tensor"),
            P("tensor"),
            P(),
            P(),
            P("tensor"),
            P("tensor"),
            P("tensor"),
            P("tensor"),
            P("tensor", "dp"),
        ),
        check_vma=False,
    )
```

```python
import functools
import math

import jax
import jax.numpy as jnp
from jax import lax
from jax.experimental import pallas as pl
from jax.experimental.pallas import tpu as pltpu
from jax.sharding import PartitionSpec as P


BLOCK = 256
SUB = 128
LANES = 128
EPS = 1e-05
LOG2E = math.log2(math.e)
FAR = -1e30
F32 = jnp.float32
BF16 = jnp.bfloat16

MM = (((1,), (0,)), ((), ()))
MT = (((1,), (1,)), ((), ()))
TM = (((0,), (0,)), ((), ()))


def dot(a, b, dims=MM):
    return lax.dot_general(a, b, dims, preferred_element_type=F32)


def dot_split(exact, values, dims=MM):
    high = values.astype(BF16)
    low = (values - high.astype(F32)).astype(BF16)
    return dot(exact, high, dims) + dot(exact, low, dims)


def split_dot(values, exact, dims=MM):
    high = values.astype(BF16)
    low = (values - high.astype(F32)).astype(BF16)
    return dot(high, exact, dims) + dot(low, exact, dims)


def up(n, to=LANES):
    return -(-n // to) * to


def softplus(v):
    return jnp.maximum(v, 0.0) + jnp.log1p(jnp.exp(-jnp.abs(v)))


def sigmoid(v):
    return 0.5 + 0.5 * jnp.tanh(0.5 * v)


def colsum(v):
    return jnp.sum(v.reshape(v.shape[0] // 8, 8, v.shape[1]), axis=0)


def spread(cols, pair, hd):
    per = LANES // hd
    lane = lax.broadcasted_iota(jnp.int32, (cols.shape[0], LANES), 1)
    out = jnp.broadcast_to(cols[:, pair * per : pair * per + 1], lane.shape)
    for j in range(1, per):
        col = cols[:, pair * per + j : pair * per + j + 1]
        out = jnp.where(lane >= j * hd, jnp.broadcast_to(col, lane.shape), out)
    return out


def columns_of(rows):
    pad = jnp.zeros((LANES - rows.shape[0], rows.shape[1]), F32)
    return jnp.concatenate([rows, pad], axis=0).T


class Dims:
    def __init__(self, n_dp, n_t, length, width, inner, hd, state, part_rows, chunk_rows):
        self.length, self.width, self.state, self.hd = length, width, state, hd
        self.n_dp, self.n_t, self.n_hi = n_dp, n_t, n_dp // 2
        self.ip = up(inner)
        self.vs = self.ip + 2 * state
        self.np = self.ip + self.vs + LANES
        self.blocks = length // BLOCK
        self.part_rows, self.chunk_rows = part_rows, chunk_rows
        self.pairs = self.ip // LANES
        self.per = LANES // hd
        self.halves = 2 if n_t == 4 and chunk_rows == 2 * BLOCK else 1
        self.piece_rows = chunk_rows // self.halves
        self.pieces = n_t * self.halves
        self.at_n = n_dp
        self.at_c = self.at_n + self.pieces
        self.at_keep = self.at_c + n_t
        self.at_rel = self.at_keep + length // SUB
        self.at_group = self.at_rel + self.blocks
        self.at_slot = self.at_group + self.blocks
        self.at_hi = self.at_slot + self.blocks
        self.at_core = self.at_hi + self.n_hi
        self.at_from = self.at_core + 1
        self.at_side = self.at_from + self.n_hi
        self.late = self.vs + LANES
        self.local_rows = up(7 * self.pairs + 2, 8)


def load_parts(refs, target, sems, scalars, first, rows):
    return [
        pltpu.make_async_copy(
            ref, target.at[pl.ds(pl.multiple_of(scalars[first + k], rows), rows), :], sems.at[k]
        )
        for k, ref in enumerate(refs)
    ]


def decay_parts(raw, hp_ref, cols, tri):
    delta = softplus(raw + hp_ref[0:1, :])
    logs = dot_split(tri, delta * (hp_ref[1:2, :] * LOG2E))
    enter = jnp.exp2(logs) * cols[:, 7:8]
    left = [logs[k + SUB - 1 : k + SUB, :] - logs[k : k + SUB, :] for k in range(0, BLOCK, SUB)]
    ending = jnp.exp2(jnp.concatenate(left, axis=0)) * cols[:, 8:9]
    return delta, logs, enter, ending


def lower_blocks():
    r = lax.broadcasted_iota(jnp.int32, (BLOCK, BLOCK), 0)
    c = lax.broadcasted_iota(jnp.int32, (BLOCK, BLOCK), 1)
    return jnp.where((r >= c) & (r // SUB == c // SUB), 1.0, 0.0).astype(BF16)


def head_masks(dm):
    lane = lax.broadcasted_iota(jnp.int32, (1, LANES), 1)
    return [jnp.where(lane // dm.hd == j, 1.0, 0.0).astype(BF16) for j in range(dm.per)]


def norm_kernel(part, x_hbm, gain_ref, *refs):
    outs, (x_v, sem) = refs[:-2], refs[-2:]
    count = x_v.shape[0] // part
    copies = [
        pltpu.make_async_copy(
            x_hbm.at[pl.ds(k * part, part), :], x_v.at[pl.ds(k * part, part), :], sem.at[k]
        )
        for k in range(count)
    ]
    for copy in copies:
        copy.start()
    rows = outs[0].shape[0]
    for k, copy in enumerate(copies):
        copy.wait()
        x = x_v[k * part : (k + 1) * part]
        root = lax.rsqrt(jnp.mean(x * x, axis=1, keepdims=True) + EPS)
        first = k * part % rows
        outs[k * part // rows][first : first + part] = (x * root * gain_ref[...][None]).astype(BF16)


def pack_kernel(dm, gate_ref, value_ref, shared_ref, step_ref, out_ref):
    inner, heads, r = gate_ref.shape[1], step_ref.shape[0], step_ref.shape[1]
    if inner != dm.ip:
        out_ref[...] = jnp.zeros_like(out_ref)
    row = lax.broadcasted_iota(jnp.int32, (r, r), 0)
    col = lax.broadcasted_iota(jnp.int32, (r, r), 1)
    eye = jnp.where(row == col, 1.0, 0.0).astype(BF16)
    out_ref[:, :inner] = gate_ref[...]
    out_ref[:, dm.ip : dm.ip + inner] = value_ref[...]
    out_ref[:, 2 * dm.ip : dm.ip + dm.vs] = shared_ref[...]
    out_ref[:, dm.ip + dm.vs :] = jnp.zeros((r, LANES), BF16)
    out_ref[:, dm.ip + dm.vs : dm.ip + dm.vs + heads] = dot(eye, step_ref[...], MT).astype(BF16)


def forward_kernel(dm, scalars, *refs):
    q, ip, vs, st, hd = BLOCK, dm.ip, dm.vs, dm.state, dm.hd
    w_parts = refs[: dm.n_dp]
    n_parts = refs[dm.n_dp : dm.n_dp + dm.pieces]
    rest = refs[dm.n_dp + dm.pieces :]
    rows_ref, conv_ref, hp_ref, lane_ref = rest[:4]
    (g_out, v_out, cv_out, ys_out, st_out, h_out, sum_out, nm_out, sg_out, w_out) = rest[4:14]
    (w_v, nm_v, h_ref, vbuf, tri_ref, pbuf, w_sem, n_sem, o_sem) = rest[14:]
    i = pl.program_id(0)
    save = pltpu.make_async_copy(w_v, w_out, o_sem)

    def rows_at(k):
        return nm_v[pl.ds(pl.multiple_of(k * q, q), q), :]

    @pl.when(i == 0)
    def _():
        copies = load_parts(w_parts, w_v, w_sem, scalars, 0, dm.part_rows)
        copies += load_parts(n_parts, nm_v, n_sem, scalars, dm.at_n, dm.piece_rows)
        for copy in copies:
            copy.start()
        h_ref[...] = jnp.zeros_like(h_ref)
        vbuf[...] = jnp.zeros_like(vbuf)
        tri_ref[...] = lower_blocks()
        for copy in copies:
            copy.wait()
        save.start()
        pbuf[...] = dot(nm_v[0:q, :], w_v[...])

    rows = rows_ref[...]
    cols = columns_of(rows)
    nm_out[...] = rows_at(i)
    for c in range(vs // LANES):
        vbuf[c, 0:8, :] = vbuf[c, q : q + 8, :]
        vbuf[c, 8 : 8 + q, :] = pbuf[:, ip + c * LANES : ip + (c + 1) * LANES]
    v_out[...] = pbuf[:, ip : ip + vs].astype(BF16)
    raw = pbuf[:, ip + vs :]
    g_out[...] = pbuf[:, :ip].astype(BF16)
    st_out[...] = raw

    acts = []
    count = vs // LANES
    edges = [k * dm.np // count // LANES * LANES for k in range(count)] + [dm.np]
    following = rows_at(jnp.minimum(i + 1, dm.blocks - 1))
    for c in range(count):
        g = slice(c * LANES, (c + 1) * LANES)
        acc = conv_ref[4:5, g] + conv_ref[3:4, g] * vbuf[c, 8 : 8 + q, :]
        for lag in range(1, 4):
            acc = acc + conv_ref[3 - lag : 4 - lag, g] * (
                vbuf[c, 8 - lag : 8 - lag + q, :] * cols[:, lag : lag + 1]
            )
        rounded = acc.astype(BF16)
        cv_out[:, g] = rounded
        acc = rounded.astype(F32)
        acts.append(acc * sigmoid(acc))
        n = slice(edges[c], edges[c + 1])
        pbuf[:, n] = dot(following, w_v[:, n])
    in_map = jnp.concatenate(acts[dm.pairs : dm.pairs + st // LANES], axis=1).astype(BF16)
    out_map = jnp.concatenate(acts[dm.pairs + st // LANES :], axis=1).astype(BF16)

    delta, logs, enter, ending = decay_parts(raw, hp_ref, cols, tri_ref[...])
    logs_t = logs.T
    r = lax.broadcasted_iota(jnp.int32, (SUB, SUB), 0)
    c = lax.broadcasted_iota(jnp.int32, (SUB, SUB), 1)
    masks = head_masks(dm)
    squares = []
    for k in range(q // SUB):
        a = slice(k * SUB, (k + 1) * SUB)
        bias = jnp.where((r >= c) & (cols[a, 0:1] == rows[0:1, a]), 0.0, FAR)
        source, target = in_map[a], out_map[a]
        scores = dot(target, source, MT)
        source_t = source.T
        keep = scalars[dm.at_keep + i * (q // SUB) + k].astype(F32)
        total = jnp.exp2(logs[a][SUB - 1 :, :]) * keep
        h_out[k * st : (k + 1) * st, :] = h_ref[...]
        square = None
        for p in range(dm.pairs):
            g = slice(p * LANES, (p + 1) * LANES)
            x = acts[p][a]
            u = x * spread(delta[a], p, hd)
            ub = u.astype(BF16)
            mixing = []
            for j in range(dm.per):
                h = p * dm.per + j
                decay = jnp.exp2(logs[a, h : h + 1] - logs_t[h : h + 1, a] + bias)
                mixing.append((decay * scores).astype(BF16))
            y = dot(
                jnp.concatenate(mixing, axis=1),
                jnp.concatenate([ub * mask for mask in masks], axis=0),
            )
            held = h_ref[:, g]
            y = y + dot(target, held.astype(BF16)) * spread(enter[a], p, hd)
            wu = (u * spread(ending[a], p, hd)).astype(BF16)
            h_ref[:, g] = held * spread(total, p, hd) + dot(source_t, wu)
            ys_out[a, g] = y
            gate = g_out[a, g].astype(F32)
            gated = (y + lane_ref[0:1, g] * x) * (gate * sigmoid(gate))
            sg_out[a, g] = (gated * lane_ref[1:2, g]).astype(BF16)
            square = gated * gated if square is None else square + gated * gated
        squares.append(square)
    sum_out[...] = jnp.sum(jnp.concatenate(squares, axis=0).T, axis=0, keepdims=True)

    @pl.when(i == dm.blocks - 1)
    def _():
        save.wait()


def branch_kernel(dm, scalars, *refs):
    n_dp, n_t = dm.n_dp, dm.n_t
    w_parts, sg_hbm = refs[:n_dp], refs[n_dp]
    w_out, outs = refs[n_dp + 1], refs[n_dp + 2 : n_dp + 2 + n_t]
    sg_v, buf, w_sem, g_sem, sem = refs[n_dp + 2 + n_t :]
    per = dm.chunk_rows // BLOCK
    loads = load_parts(w_parts, w_out, w_sem, scalars, 0, dm.part_rows)
    whole = pltpu.make_async_copy(sg_hbm, sg_v, g_sem)
    for copy in loads:
        copy.start()
    whole.start()
    for copy in loads:
        copy.wait()
    whole.wait()
    for i in range(dm.blocks):
        at = slice(i * BLOCK, (i + 1) * BLOCK)
        buf[i] = dot(sg_v[at, :], w_out[...], MT).astype(BF16)
        for k in range(n_t):

            @pl.when(scalars[dm.at_rel + i] == k)
            def _():
                pltpu.make_async_copy(buf.at[i], outs[k].at[i % per], sem.at[i]).start()

    for i in range(dm.blocks):
        pltpu.make_async_copy(buf.at[i], outs[0].at[0], sem.at[i]).wait()


def dots_kernel(dm, scalars, *refs):
    q, n_t = BLOCK, dm.n_t
    c_parts, b_parts = refs[:n_t], refs[n_t : 2 * n_t]
    sq_ref, sum_out, ct_hbm = refs[2 * n_t : 2 * n_t + 3]
    ct_v, br_v, c_sem, b_sem, t_sem = refs[2 * n_t + 3 :]
    takes = [pltpu.make_async_copy(c_parts[k], ct_v.at[k], c_sem.at[k]) for k in range(n_t)]
    takes += [pltpu.make_async_copy(b_parts[k], br_v.at[k], b_sem.at[k]) for k in range(n_t)]
    for copy in takes:
        copy.start()
    gives = []
    for k in range(n_t):
        takes[k].wait()
        takes[n_t + k].wait()
        chunk = pl.multiple_of(scalars[dm.at_c + k], dm.chunk_rows)
        gives.append(
            pltpu.make_async_copy(ct_v.at[k], ct_hbm.at[pl.ds(chunk, dm.chunk_rows), :], t_sem.at[k])
        )
        gives[-1].start()
        for h in range(dm.chunk_rows // q):
            dots = None
            for c in range(dm.width // LANES):
                g = slice(c * LANES, (c + 1) * LANES)
                cot = ct_v[k, h * q : (h + 1) * q, g].astype(F32)
                prod = cot * br_v[k, h, :, g].astype(F32)
                dots = prod if dots is None else dots + prod
            blk = chunk // q + h
            sum_out[blk, 0:1, :] = sq_ref[blk]
            sum_out[blk, 1:2, :] = jnp.sum(dots.T, axis=0, keepdims=True)
    for copy in gives:
        copy.wait()


def gate_kernel(dm, scalars, *refs):
    q, ip, r = BLOCK, dm.ip, dm.part_rows
    (w_ref, wo_ref, rk_ref, lane_ref, g_in, cv_in, ys_in, cot_in, nm_in, ct_in) = refs[:10]
    dg_out, dy_out, lane_out, rows_out, own_out = refs[10:15]
    z_outs = refs[15 : 14 + dm.n_hi]
    acc, dg_s, both = refs[14 + dm.n_hi :]
    i = pl.program_id(0)

    @pl.when(i == 0)
    def _():
        lane_out[...] = jnp.zeros_like(lane_out)
        acc[...] = jnp.zeros_like(acc)

    def gather():
        acc[:, :ip] += dot(nm_in[...], dg_s[...], TM)
        acc[:, ip:] += dot(ct_in[...], both[...], TM)

    def gating():
        pad = jnp.zeros((LANES - 2, q), F32)
        cols = jnp.concatenate([rk_ref[...], pad], axis=0).T
        root, pull = cols[:, 0:1], cols[:, 1:2]
        scaled_cot = dot(cot_in[...], wo_ref[...])
        for p in range(dm.pairs):
            g = slice(p * LANES, (p + 1) * LANES)
            gate, sc = g_in[:, g].astype(F32), scaled_cot[:, g]
            cv = cv_in[:, g].astype(F32)
            x = cv * sigmoid(cv)
            sig = sigmoid(gate)
            z = gate * sig
            y = ys_in[:, g] + lane_ref[0:1, g] * x
            gated = y * z
            scaled = gated * root
            cot = root * (lane_ref[1:2, g] * sc) - pull * gated
            lane_out[0:8, g] += colsum(sc * scaled)
            dy = cot * z
            dy_out[:, g] = dy.astype(BF16)
            dg = (cot * y * (sig + z * (1.0 - sig))).astype(BF16)
            dg_out[:, g] = dg
            dg_s[:, g] = dg
            lane_out[8:16, g] += colsum(dy * x)
            both[:, g] = (scaled * lane_ref[1:2, g]).astype(BF16)

    @pl.when(i == 0)
    def _():
        gating()

    @pl.when((i > 0) & (i < dm.blocks))
    def _():
        gather()
        gating()

    @pl.when(i == dm.blocks)
    def _():
        gather()
        prod = acc[:, :LANES] * w_ref[:, :LANES].astype(F32)
        for p in range(1, dm.pairs):
            g = slice(p * LANES, (p + 1) * LANES)
            prod = prod + acc[:, g] * w_ref[:, g].astype(F32)
        rows_out[...] = gain_rows(prod)
        hi = scalars[dm.at_hi]
        own_out[...] = acc[pl.ds(pl.multiple_of(hi * 2 * r, 8), 2 * r), :]
        for k, z_out in enumerate(z_outs):
            at = pl.multiple_of(scalars[dm.at_hi + k + 1] * 2 * r, 8)
            z_out[...] = acc[pl.ds(at, 2 * r), :].astype(BF16)


def backward_kernel(dm, scalars, *refs):
    q, ip, vs, st, hd, late_cols = BLOCK, dm.ip, dm.vs, dm.state, dm.hd, dm.late
    groups = dm.group_sizes
    w_ref, rows_ref, conv_ref, hp_ref, lane_ref, lanes_ref, gain_ref = refs[:7]
    dg_in, nm_in, dy_in, v_in, cv_in, ys_in, st_in, h_in = refs[7:15]
    mine_out, theirs_out, kept_out = refs[15:18]
    nc_outs = refs[18 : 18 + len(groups)]
    (dh_ref, dbuf, tri_ref, dx_s, act_s, t1_s, t2_s) = refs[18 + len(groups) : 25 + len(groups)]
    (pj_s, full, acc, tap_out, head_out, nc_buf, nc_sem) = refs[25 + len(groups) :]
    i = pl.program_id(0)
    blk = jnp.maximum(dm.blocks - 1 - i, 0)
    subs = q // SUB

    def send(k, at, row):
        return pltpu.make_async_copy(nc_buf.at[at], nc_outs[k].at[row], nc_sem.at[at])

    @pl.when(i == 0)
    def _():
        dh_ref[...] = jnp.zeros_like(dh_ref)
        dbuf[...] = jnp.zeros_like(dbuf)
        tap_out[...] = jnp.zeros_like(tap_out)
        head_out[...] = jnp.zeros_like(head_out)
        acc[...] = jnp.zeros_like(acc)
        tri_ref[...] = lower_blocks()

    slot = lax.rem(i, 2)

    @pl.when(i >= 3)
    def _():
        send(0, slot, 0).wait()

    third = dm.width // 3

    def cotangent_piece(n):
        def run():
            g = slice(n * third, (n + 1) * third)
            nc_buf[slot, :, g] = dot(full[...], w_ref[g, :], MT).astype(BF16)

        return run

    def gradient_piece(n):
        def run():
            g = slice(n * third, (n + 1) * third)
            acc[g, :] += dot(nm_in[:, g], full[:, ip:], TM)

        return run

    pieces = [make(n) for n in range(3) for make in (cotangent_piece, gradient_piece)]

    def take_over():
        full[:, :ip] = dg_in[...]
        full[:, ip:] = pj_s[...]

    def scan(between):
        rows = rows_ref[...]
        cols = columns_of(rows)
        raw = st_in[...]
        tri = tri_ref[...]
        delta, logs, enter, ending = decay_parts(raw, hp_ref, cols, tri)
        logs_t = logs.T

        acts, slopes = [], []
        for c in range(vs // LANES):
            g = slice(c * LANES, (c + 1) * LANES)
            cv = cv_in[:, g].astype(F32)
            sig = sigmoid(cv)
            act = cv * sig
            acts.append(act)
            slopes.append(sig + act * (1.0 - sig))
        in_map = jnp.concatenate(acts[dm.pairs : dm.pairs + st // LANES], axis=1).astype(BF16)
        out_map = jnp.concatenate(acts[dm.pairs + st // LANES :], axis=1).astype(BF16)

        r = lax.broadcasted_iota(jnp.int32, (SUB, SUB), 0)
        c = lax.broadcasted_iota(jnp.int32, (SUB, SUB), 1)
        masks = head_masks(dm)
        d_in, d_out = [None] * subs, [None] * subs
        for k in reversed(range(subs)):
            a = slice(k * SUB, (k + 1) * SUB)
            bias = jnp.where((r <= c) & (cols[a, 0:1] == rows[0:1, a]), 0.0, FAR)
            source, target = in_map[a], out_map[a]
            scores = dot(source, target, MT)
            target_t = target.T
            keep = scalars[dm.at_keep + blk * subs + k].astype(F32)
            total = jnp.exp2(logs[a][SUB - 1 :, :]) * keep
            ds = None
            for p in range(dm.pairs):
                g = slice(p * LANES, (p + 1) * LANES)
                x, dyb = acts[p][a], dy_in[a, g]
                delta_e = spread(delta[a], p, hd)
                u = x * delta_e
                ub, dy = u.astype(BF16), dyb.astype(F32)
                decays = []
                for j in range(dm.per):
                    h = p * dm.per + j
                    decays.append(jnp.exp2(logs_t[h : h + 1, a] - logs[a, h : h + 1] + bias))
                du = dot(
                    jnp.concatenate([(d * scores).astype(BF16) for d in decays], axis=1),
                    jnp.concatenate([dyb * mask for mask in masks], axis=0),
                )
                dm_t = dot(jnp.concatenate([ub * mask for mask in masks], axis=0), dyb, MT)
                for j, d in enumerate(decays):
                    part = dm_t[j * SUB : (j + 1) * SUB] * d
                    ds = part if ds is None else ds + part
                dh, h_rows = dh_ref[:, g], h_in[k * st : (k + 1) * st, g]
                dh_b = dh.astype(BF16)
                end_e = spread(ending[a], p, hd)
                late = end_e * dot(source, dh_b)
                du = du + late
                wu = (u * end_e).astype(BF16)
                edy = (dy * spread(enter[a], p, hd)).astype(BF16)
                from_wu, from_dy = dot(wu, dh_b, MT), dot(edy, h_rows.astype(BF16), MT)
                d_in[k] = from_wu if p == 0 else d_in[k] + from_wu
                d_out[k] = from_dy if p == 0 else d_out[k] + from_dy
                u32 = ub.astype(F32)
                t1_s[a, g] = dy * ys_in[a, g] - u32 * du
                t2_s[a, g] = du * x
                kept = dh * spread(total, p, hd)
                act_s[8 * k : 8 * k + 8, g] = colsum(u32 * late) + colsum(h_rows * kept)
                dh_ref[:, g] = kept + dot(target_t, edy)
                dx_s[a, g] = (delta_e * du + lane_ref[0:1, g] * dy) * slopes[p][a]
            ds_b = ds.astype(BF16)
            d_in[k] = d_in[k] + dot(ds_b, target)
            d_out[k] = d_out[k] + dot(ds_b, source, TM)

        hr = lax.broadcasted_iota(jnp.int32, (ip, LANES), 0)
        hc = lax.broadcasted_iota(jnp.int32, (ip, LANES), 1)
        pick = jnp.where(hr // hd == hc, 1.0, 0.0).astype(BF16)
        d_log = split_dot(t1_s[...], pick)
        last = split_dot(act_s[...], pick)
        row = lax.broadcasted_iota(jnp.int32, (q, LANES), 0)
        for k in range(subs):
            end = jnp.sum(last[8 * k : 8 * k + 8, :], axis=0, keepdims=True)
            d_log = d_log + jnp.where(row == (k + 1) * SUB - 1, end, 0.0)
        d_step = dot_split(tri, d_log, TM)
        head_out[8:16, :] += colsum(d_step * delta)
        d_delta = hp_ref[1:2, :] * d_step + split_dot(t2_s[...], pick)
        d_raw = d_delta * sigmoid(raw + hp_ref[0:1, :])
        head_out[0:8, :] += colsum(d_raw)
        pj_s[:, vs:] = d_raw.astype(BF16)

        count = vs // LANES
        for c in range(count):
            dbuf[c, q : q + 8, :] = dbuf[c, 0:8, :]
            for k in range(subs):
                a = slice(k * SUB, (k + 1) * SUB)
                if c < dm.pairs:
                    dbuf[c, a, :] = dx_s[a, c * LANES : (c + 1) * LANES]
                else:
                    n = (c - dm.pairs) * LANES
                    part = d_in[k][:, n : n + LANES] if n < st else d_out[k][:, n - st : n - st + LANES]
                    dbuf[c, a, :] = part * slopes[c][a]
        for c in range(count):
            g = slice(c * LANES, (c + 1) * LANES)
            v = v_in[:, g].astype(F32)
            shifted = dbuf[c, 0:q, :]
            tap_out[32:40, g] += colsum(shifted)
            tap_out[24:32, g] += colsum(shifted * v)
            dv = conv_ref[3:4, g] * shifted
            for lag in range(1, 4):
                shifted = dbuf[c, lag : lag + q, :] * cols[:, 3 + lag : 4 + lag]
                tap_out[24 - 8 * lag : 32 - 8 * lag, g] += colsum(shifted * v)
                dv = dv + conv_ref[3 - lag : 4 - lag, g] * shifted
            pj_s[:, g] = dv.astype(BF16)
            first, stop = c * len(between) // count, (c + 1) * len(between) // count
            for run in between[first:stop]:
                run()

    @pl.when(i == 0)
    def _():
        scan([])

    @pl.when((i > 0) & (i < dm.blocks))
    def _():
        take_over()
        scan(pieces)

    @pl.when(i == dm.blocks)
    def _():
        take_over()
        for run in pieces:
            run()

    before = jnp.minimum(blk + 1, dm.blocks - 1)
    before = jnp.where(i == dm.blocks, 0, before)
    for k in range(len(groups)):

        @pl.when((i > 0) & (scalars[dm.at_group + before] == k))
        def _():
            send(k, slot, scalars[dm.at_slot + before]).start()

    @pl.when(i == dm.blocks)
    def _():
        core, r = scalars[dm.at_core], dm.part_rows
        for h in range(dm.n_hi):
            at = pl.multiple_of((2 * h + core) * r, 8)
            mine_out[h * r : (h + 1) * r, :] = acc[pl.ds(at, r), :]
            at = pl.multiple_of((2 * h + 1 - core) * r, 8)
            theirs_out[h * r : (h + 1) * r, :] = acc[pl.ds(at, r), :].astype(BF16)
        small = []

        def put(v):
            for c in range(v.shape[1] // LANES):
                small.append(jnp.sum(v[:, c * LANES : (c + 1) * LANES], axis=0, keepdims=True))

        for k in range(5):
            put(tap_out[8 * k : 8 * k + 8, :ip])
        for k in range(2):
            put(lanes_ref[8 * k : 8 * k + 8, :])
        for k in range(2):
            put(head_out[8 * k : 8 * k + 8, :])
        zero = jnp.zeros((1, LANES), F32)
        small.extend([zero] * (dm.local_rows - len(small)))
        for k in range(5):
            put(tap_out[8 * k : 8 * k + 8, ip:])
        prod = acc[:, :LANES] * w_ref[:, ip : ip + LANES].astype(F32)
        for p in range(1, late_cols // LANES):
            g = slice(p * LANES, (p + 1) * LANES)
            o = slice(ip + p * LANES, ip + (p + 1) * LANES)
            prod = prod + acc[:, g] * w_ref[:, o].astype(F32)
        prod = gain_rows(prod)
        for c in range(dm.width // LANES):
            g = slice(c * LANES, (c + 1) * LANES)
            small.append(prod[0:1, g] + gain_ref[0:1, g])
        small.extend([zero] * (late_cols // 16 - len(small)))
        for c in range(late_cols // LANES):
            g = slice(c * LANES, (c + 1) * LANES)
            parts = two_parts(jnp.concatenate(small[8 * c : 8 * c + 8], axis=0))
            theirs_out[dm.n_hi * r :, g] = parts
            kept_out[:, g] = parts
        send(0, 1 - slot, 0).wait()
        send(0, slot, 0).wait()


def two_parts(v):
    high = v.astype(BF16).astype(F32)
    return jnp.concatenate([high, v - high], axis=0).astype(BF16)


def one_part(v):
    return v[0:8, :].astype(F32) + v[8:16, :].astype(F32)


def gain_rows(acc):
    high = acc.astype(BF16)
    rest = acc - high.astype(F32)
    mid = rest.astype(BF16)
    low = (rest - mid.astype(F32)).astype(BF16)
    one = jnp.ones((8, LANES), BF16)
    return dot(one, high, MT) + dot(one, mid, MT) + dot(one, low, MT)


def pair_kernel(dm, scalars, mine_ref, kept_ref, theirs_ref, own_out, *outs):
    r = dm.part_rows
    tail = dm.n_hi * r
    small = one_part(kept_ref[...]) + one_part(theirs_ref[tail:, :])
    small = two_parts(small)
    for k in range(dm.n_hi):
        at = pl.multiple_of(scalars[dm.at_hi + k] * r, 8)
        both = mine_ref[pl.ds(at, r), :] + theirs_ref[pl.ds(at, r), :].astype(F32)
        if k == 0:
            own_out[...] = both
        else:
            outs[k][0:r, :] = both.astype(BF16)
        if k > 0:
            outs[k][r:, :] = small
        else:
            outs[0][...] = small


def early_kernel(dm, scalars, own_ref, *refs):
    parts, (mine_out, theirs_out, total) = refs[: dm.n_hi - 1], refs[dm.n_hi - 1 :]
    r = dm.part_rows
    both = own_ref[...]
    for part in parts:
        both = both + part[...].astype(F32)
    total[...] = both
    core = scalars[dm.at_core]
    mine_out[...] = total[pl.ds(pl.multiple_of(core * r, 8), r), :]
    theirs_out[...] = total[pl.ds(pl.multiple_of((1 - core) * r, 8), r), :].astype(BF16)


def grads_kernel(dm, scalars, hp_ref, own_ref, kept_ref, mine_ref, theirs_ref, *refs):
    n, r, st2 = dm.n_hi, dm.part_rows, 2 * dm.state
    parts = refs[: n - 1]
    (gate_out, value_out, step_out, outp_out, share_out) = refs[n - 1 : n + 4]
    (tap_out, tapb_out, gain_out, skip_out, sb_out, dl_out, hold) = refs[n + 4 :]
    total = own_ref[...]
    for part in parts:
        total = total + part[0:r, :].astype(F32)
    early = mine_ref[...] + theirs_ref[...].astype(F32)
    inner, heads = gate_out.shape[1], step_out.shape[0]
    gate_out[...] = early[:, :inner]
    outp_out[...] = early[:, dm.ip : dm.ip + inner]
    value_out[...] = total[:, :inner]
    share_out[0:r, :] = total[:, dm.ip : dm.vs].astype(BF16)
    step_out[...] = total[:, dm.vs :].T[0:heads, :]
    hold[0] = one_part(kept_ref[...])
    for k, part in enumerate(parts):
        hold[k + 1] = one_part(part[r:, :])
    small = hold[scalars[dm.at_from]]
    for k in range(1, n):
        small = small + hold[scalars[dm.at_from + k]]
    flat = [
        small[j : j + 1, c * LANES : (c + 1) * LANES]
        for c in range(dm.late // LANES)
        for j in range(8)
    ]

    def take(first, width):
        return jnp.concatenate(flat[first : first + dm.pairs], axis=1)[:, :width]

    for k in range(4):
        tap_out[k : k + 1, :] = take(k * dm.pairs, inner)
    tapb_out[...] = take(4 * dm.pairs, inner)[0]
    gain_out[...] = take(5 * dm.pairs, inner)[0]
    lane = lax.broadcasted_iota(jnp.int32, (1, LANES), 1)
    skip = jnp.zeros((1, LANES), F32)
    for h in range(heads):
        row = flat[6 * dm.pairs + h // dm.per]
        mine = lane // dm.hd == h % dm.per
        one = jnp.sum(jnp.where(mine, row, 0.0), axis=1, keepdims=True)
        skip = jnp.where(lane == h, one, skip)
    skip_out[...] = skip[0, :heads]
    sb_out[...] = flat[7 * dm.pairs][0, :heads]
    dl_out[...] = (flat[7 * dm.pairs + 1] * hp_ref[1:2, :])[0, :heads]
    first = dm.local_rows // 8
    for c in range(st2 // LANES):
        g = slice((first + c) * LANES, (first + c + 1) * LANES)
        share_out[r:, c * LANES : (c + 1) * LANES] = two_parts(small[:, g])


def share_kernel(dm, scalars, norm_ref, *refs):
    r, st2 = dm.part_rows, 2 * dm.state
    parts = refs[: dm.n_t]
    shared_out, tap_out, tapb_out, norm_out, hold = refs[dm.n_t :]
    for k, part in enumerate(parts):
        hold[k] = part[...]
    shared, common = None, None
    for k in range(dm.n_t):
        part = hold[scalars[dm.at_side + k]]
        share, small = part[0:r, :].astype(F32), one_part(part[r:, :])
        shared = share if shared is None else shared + share
        common = small if common is None else common + small
    shared_out[...] = shared
    flat = [
        common[j : j + 1, c * LANES : (c + 1) * LANES] for c in range(st2 // LANES) for j in range(8)
    ]
    per = st2 // LANES
    for k in range(4):
        tap_out[k : k + 1, :] = jnp.concatenate(flat[k * per : (k + 1) * per], axis=1)
    tapb_out[...] = jnp.concatenate(flat[4 * per : 5 * per], axis=1)[0]
    rows = flat[5 * per : 5 * per + dm.width // LANES]
    norm_out[...] = jnp.concatenate(rows, axis=1)[0] / norm_ref[...]


def input_kernel(sets, steps, x_ref, cot_ref, gain_ref, *refs):
    out = refs[-1]
    x = x_ref[...]
    root = lax.rsqrt(jnp.mean(x * x, axis=1, keepdims=True) + EPS)
    first = 0
    for k, count in enumerate(sets):
        parts = refs[first : first + count]
        first += count

        @pl.when(pl.program_id(0) // steps == k)
        def _():
            nc = parts[0][...].astype(F32)
            for part in parts[1:]:
                nc = nc + part[...].astype(F32)
            hat = nc * gain_ref[...][None]
            mean = jnp.mean(hat * x, axis=1, keepdims=True)
            out[...] = cot_ref[...].astype(F32) + root * hat - x * (root * root * root * mean)


def shift_hi(n, k):
    return [(i, ((i // 2 + k) % (n // 2)) * 2 + i % 2) for i in range(n)]


def swap(n, k):
    return [(i, i ^ k) for i in range(n)]


def pad_cols(v, to):
    return jnp.pad(v, ((0, 0), (0, to - v.shape[1])))


def pad_vec(v, to):
    return jnp.pad(v, (0, to - v.shape[0]))


def body(
    n_dp,
    n_t,
    block_input,
    segment_ids,
    norm_gain,
    gate_proj,
    value_proj,
    shared_proj,
    step_proj,
    conv_value_weight,
    conv_value_bias,
    conv_shared_weight,
    conv_shared_bias,
    step_bias,
    decay_log,
    skip_weight,
    gate_gain,
    output_proj,
    out_cotangent,
):
    q = BLOCK
    chunk_rows, width = block_input.shape
    length = segment_ids.shape[1]
    inner, heads = gate_proj.shape[1], step_proj.shape[1]
    part_rows = gate_proj.shape[0]
    state = shared_proj.shape[1] // 2
    hd = inner // heads
    dm = Dims(n_dp, n_t, length, width, inner, hd, state, part_rows, chunk_rows)
    ip, vs, nb, n_hi = dm.ip, dm.vs, dm.blocks, dm.n_hi
    me_t = lax.axis_index("tensor")
    me_dp = lax.axis_index("dp")
    hi, core = me_dp // 2, me_dp % 2

    def across(v, k):
        return lax.ppermute(v, "tensor", swap(n_t, k))

    def along(v, k):
        return lax.ppermute(v, "dp", shift_hi(n_dp, k))

    def partner(v):
        return lax.ppermute(v, "dp", swap(n_dp, 1))

    def vmem(shape, dtype):
        return pltpu.VMEM(shape, dtype)

    limit = 20 * 1024 * 1024
    params = pltpu.CompilerParams(dimension_semantics=("arbitrary",), vmem_limit_bytes=limit)
    hbm = pl.BlockSpec(memory_space=pl.ANY)

    def out(*shape, dtype=F32):
        return jax.ShapeDtypeStruct(shape, dtype)

    part = min(LANES, dm.piece_rows)
    normed = pl.pallas_call(
        functools.partial(norm_kernel, part),
        out_shape=[out(dm.piece_rows, width, dtype=BF16)] * dm.halves,
        in_specs=[hbm, pl.BlockSpec(memory_space=pltpu.VMEM)],
        scratch_shapes=[
            vmem((chunk_rows, width), F32),
            pltpu.SemaphoreType.DMA((chunk_rows // part,)),
        ],
        compiler_params=pltpu.CompilerParams(vmem_limit_bytes=limit),
        name="normalize",
    )(block_input, norm_gain)
    if dm.halves == 2:
        a, b = normed
        xa, yb = across(a, 1), across(b, 2)
        ya, xb = across(a, 2), across(b, 1)
        n_list = [a, b, xa, xb, ya, yb, across(xa, 2), across(yb, 1)]
        n_rows = jnp.concatenate(
            [(me_t ^ k) * chunk_rows + jnp.arange(2) * dm.piece_rows for k in range(4)]
        )
    else:
        n_list = [normed[0]] + [across(normed[0], k) for k in range(1, n_t)]
        n_rows = (me_t ^ jnp.arange(n_t)) * chunk_rows
    step_first, _ = lax.optimization_barrier((step_proj.T, normed[0]))
    packed = pl.pallas_call(
        functools.partial(pack_kernel, dm),
        out_shape=out(part_rows, dm.np, dtype=BF16),
        name="pack_weights",
    )(gate_proj, value_proj, shared_proj, step_first)
    w_list = [packed] + [along(packed, k) for k in range(1, n_hi)]
    w_list = w_list + [partner(v) for v in w_list]
    outp = pad_cols(output_proj.T, ip)
    o_list = [outp] + [along(outp, k) for k in range(1, n_hi)]
    o_list = o_list + [partner(v) for v in o_list]

    seg = segment_ids[0]
    subs = q // SUB
    segb = seg.reshape(nb * subs, SUB)
    last = segb[:, -1]
    prev_last = jnp.concatenate([jnp.full((1,), -1, jnp.int32), last[:-1]])
    gap = jnp.full((3,), -1, jnp.int32)
    wide = jnp.concatenate([gap, seg, gap])
    rows = [seg.astype(F32)]
    rows += [(wide[3 - k : 3 - k + length] == seg).astype(F32) for k in range(1, 4)]
    rows += [(wide[3 + k : 3 + k + length] == seg).astype(F32) for k in range(1, 4)]
    rows += [
        (segb == prev_last[:, None]).astype(F32).reshape(-1),
        (segb == last[:, None]).astype(F32).reshape(-1),
    ]
    rows = jnp.concatenate([jnp.stack(rows), jnp.zeros((16 - len(rows), length), F32)], axis=0)
    keep = (last == prev_last).astype(jnp.int32)
    other = (hi - jnp.arange(n_hi)) % n_hi
    rel = (jnp.arange(nb) * q // chunk_rows) ^ me_t
    half = jnp.arange(nb) % (chunk_rows // q)
    if dm.halves == 2:
        group_of = jnp.array([[2, 2], [0, 2], [2, 1], [0, 1]])
        slot_of = jnp.array([[0, 2], [0, 3], [1, 0], [1, 1]])
        group, slot = group_of[rel, half], slot_of[rel, half]
        dm.group_sizes = (2, 2, 4)
    else:
        group, slot = rel, half
        dm.group_sizes = (chunk_rows // q,) * n_t
    scalars = jnp.concatenate(
        [
            (other * 2 + core) * part_rows,
            (other * 2 + 1 - core) * part_rows,
            n_rows,
            (me_t ^ jnp.arange(n_t)) * chunk_rows,
            keep,
            rel,
            group,
            slot,
            (hi + jnp.arange(n_hi)) % n_hi,
            core[None],
            (hi - jnp.arange(n_hi)) % n_hi,
            me_t ^ jnp.arange(n_t),
        ]
    ).astype(jnp.int32)

    conv = jnp.concatenate(
        [
            pad_cols(jnp.concatenate([conv_value_weight, conv_value_bias[None]]), ip),
            jnp.concatenate([conv_shared_weight, conv_shared_bias[None]]),
        ],
        axis=1,
    )
    conv = jnp.pad(conv, ((0, 3), (0, 0)))
    rate = -jnp.exp(decay_log)
    per_head = jnp.stack([pad_vec(step_bias, LANES), pad_vec(rate, LANES)])
    per_head = jnp.pad(per_head, ((0, 6), (0, 0)))
    per_lane = jnp.stack([pad_vec(jnp.repeat(skip_weight, hd), ip), pad_vec(gate_gain, ip)])
    per_lane = jnp.pad(per_lane, ((0, 6), (0, 0)))

    def const(*shape):
        return pl.BlockSpec(shape, lambda i, s: (0,) * len(shape))

    def fblock(cols):
        return pl.BlockSpec((q, cols), lambda i, s: (i, 0))

    def fsum(k):
        return pl.BlockSpec((None, k, q), lambda i, s: (i, 0, 0))

    def grid(steps, in_specs, out_specs, scratch):
        return pltpu.PrefetchScalarGridSpec(
            num_scalar_prefetch=1,
            grid=(steps,),
            in_specs=in_specs,
            out_specs=out_specs,
            scratch_shapes=scratch,
        )

    (gate, value, conved, scan, steps_raw, held, squares, normed_all, scaled, weights) = pl.pallas_call(
        functools.partial(forward_kernel, dm),
        out_shape=[
            out(length, ip, dtype=BF16),
            out(length, vs, dtype=BF16),
            out(length, vs, dtype=BF16),
            out(length, ip),
            out(length, LANES),
            out(nb * subs * state, ip),
            out(nb, 1, q),
            out(length, width, dtype=BF16),
            out(length, ip, dtype=BF16),
            out(width, dm.np, dtype=BF16),
        ],
        grid_spec=grid(
            nb,
            [hbm] * (n_dp + dm.pieces)
            + [
                pl.BlockSpec((16, q), lambda i, s: (0, i)),
                const(8, vs),
                const(8, LANES),
                const(8, ip),
            ],
            [
                fblock(ip),
                fblock(vs),
                fblock(vs),
                fblock(ip),
                fblock(LANES),
                pl.BlockSpec((subs * state, ip), lambda i, s: (i, 0)),
                fsum(1),
                fblock(width),
                fblock(ip),
                hbm,
            ],
            [
                vmem((width, dm.np), BF16),
                vmem((length, width), BF16),
                vmem((state, ip), F32),
                vmem((vs // LANES, q + 8, LANES), F32),
                vmem((q, q), BF16),
                vmem((q, dm.np), F32),
                pltpu.SemaphoreType.DMA((n_dp,)),
                pltpu.SemaphoreType.DMA((dm.pieces,)),
                pltpu.SemaphoreType.DMA,
            ],
        ),
        compiler_params=params,
        cost_estimate=pl.CostEstimate(
            flops=30_000_000_000, bytes_accessed=30_000_000, transcendentals=0
        ),
        name="block_forward",
    )(scalars, *w_list, *n_list, rows, conv, per_head, per_lane)

    c_list = [out_cotangent] + [across(out_cotangent, k) for k in range(1, n_t)]
    in_vmem = pl.BlockSpec(memory_space=pltpu.VMEM)
    w_back, *branch = pl.pallas_call(
        functools.partial(branch_kernel, dm),
        out_shape=[out(width, ip, dtype=BF16)]
        + [out(chunk_rows // q, q, width, dtype=BF16)] * n_t,
        grid_spec=grid(
            1,
            [hbm] * (n_dp + 1),
            [in_vmem] + [hbm] * n_t,
            [
                vmem((length, ip), BF16),
                vmem((nb, q, width), BF16),
                pltpu.SemaphoreType.DMA((n_dp,)),
                pltpu.SemaphoreType.DMA,
                pltpu.SemaphoreType.DMA((nb,)),
            ],
        ),
        compiler_params=params,
        cost_estimate=pl.CostEstimate(
            flops=3_000_000_000, bytes_accessed=10_000_000, transcendentals=0
        ),
        name="branch_output",
    )(scalars, *o_list, scaled)
    sums, cot_all = pl.pallas_call(
        functools.partial(dots_kernel, dm),
        out_shape=[out(nb, 2, q), out(length, width, dtype=BF16)],
        grid_spec=grid(
            1,
            [hbm] * (2 * n_t) + [in_vmem],
            [in_vmem, hbm],
            [
                vmem((n_t, chunk_rows, width), BF16),
                vmem((n_t, chunk_rows // q, q, width), BF16),
                pltpu.SemaphoreType.DMA((n_t,)),
                pltpu.SemaphoreType.DMA((n_t,)),
                pltpu.SemaphoreType.DMA((n_t,)),
            ],
        ),
        compiler_params=params,
        cost_estimate=pl.CostEstimate(
            flops=3_000_000_000, bytes_accessed=10_000_000, transcendentals=0
        ),
        name="branch_dots",
    )(scalars, *c_list, *branch, squares)
    total = sums
    for k in range(1, n_t):
        total = total + across(sums, k)
    root = lax.rsqrt(total[:, 0] / (inner * n_t) + EPS)
    pull = root * root * root * (total[:, 1] / (inner * n_t))
    rk = jnp.stack([root, pull], axis=1)
    branch_sum = branch[0].astype(F32)
    for k in range(1, n_t):
        branch_sum = branch_sum + across(branch[k], k).astype(F32)
    own_root = lax.dynamic_slice_in_dim(root.reshape(length), me_t * chunk_rows, chunk_rows)
    block_output = block_input + own_root[:, None] * branch_sum.reshape(chunk_rows, width)

    def bblock(cols):
        return pl.BlockSpec((q, cols), lambda i, s: (jnp.maximum(nb - 1 - i, 0), 0))

    def bago(cols):
        return pl.BlockSpec((q, cols), lambda i, s: (jnp.minimum(nb - i, nb - 1), 0))

    def now(cols):
        return pl.BlockSpec((q, cols), lambda i, s: (jnp.minimum(i, nb - 1), 0))

    def ago(cols):
        return pl.BlockSpec((q, cols), lambda i, s: (jnp.maximum(i - 1, 0), 0))

    dgate, dscan, lanes, gate_rows, own_early, *early = pl.pallas_call(
        functools.partial(gate_kernel, dm),
        out_shape=[
            out(length, ip, dtype=BF16),
            out(length, ip, dtype=BF16),
            out(16, ip),
            out(8, width),
            out(2 * part_rows, 2 * ip),
        ]
        + [out(2 * part_rows, 2 * ip, dtype=BF16)] * (n_hi - 1),
        grid_spec=grid(
            nb + 1,
            [
                const(width, ip),
                const(width, ip),
                pl.BlockSpec((None, 2, q), lambda i, s: (jnp.minimum(i, nb - 1), 0, 0)),
                const(8, ip),
                now(ip),
                now(ip),
                now(ip),
                now(width),
                ago(width),
                ago(width),
            ],
            [now(ip), now(ip), const(16, ip), const(8, width)]
            + [const(2 * part_rows, 2 * ip)] * n_hi,
            [vmem((width, 2 * ip), F32), vmem((q, ip), BF16), vmem((q, ip), BF16)],
        ),
        compiler_params=params,
        cost_estimate=pl.CostEstimate(
            flops=6_000_000_000, bytes_accessed=20_000_000, transcendentals=0
        ),
        name="gate_backward",
    )(scalars, weights, w_back, rk, per_lane, gate, conved, scan, cot_all, normed_all, cot_all)
    early = [along(v, k + 1) for k, v in enumerate(early)]

    r_all = n_hi * part_rows
    mine, theirs, kept, *nc = pl.pallas_call(
        functools.partial(backward_kernel, dm),
        out_shape=[
            out(r_all, dm.late),
            out(r_all + 16, dm.late, dtype=BF16),
            out(16, dm.late, dtype=BF16),
        ]
        + [out(k, q, width, dtype=BF16) for k in dm.group_sizes],
        grid_spec=grid(
            nb + 1,
            [
                const(width, dm.np),
                pl.BlockSpec((16, q), lambda i, s: (0, jnp.maximum(nb - 1 - i, 0))),
                const(8, vs),
                const(8, LANES),
                const(8, ip),
                const(16, ip),
                const(8, width),
                bago(ip),
                bago(width),
                bblock(ip),
                bblock(vs),
                bblock(vs),
                bblock(ip),
                bblock(LANES),
                pl.BlockSpec((subs * state, ip), lambda i, s: (jnp.maximum(nb - 1 - i, 0), 0)),
            ],
            [const(r_all, dm.late), const(r_all + 16, dm.late), const(16, dm.late)]
            + [hbm] * len(dm.group_sizes),
            [
                vmem((state, ip), F32),
                vmem((vs // LANES, q + 8, LANES), F32),
                vmem((q, q), BF16),
                vmem((q, ip), F32),
                vmem((8 * subs, ip), F32),
                vmem((q, ip), F32),
                vmem((q, ip), F32),
                vmem((q, dm.late), BF16),
                vmem((q, dm.np), BF16),
                vmem((width, dm.late), F32),
                vmem((40, vs), F32),
                vmem((16, LANES), F32),
                vmem((2, q, width), BF16),
                pltpu.SemaphoreType.DMA((2,)),
            ],
        ),
        compiler_params=params,
        cost_estimate=pl.CostEstimate(
            flops=40_000_000_000, bytes_accessed=30_000_000, transcendentals=0
        ),
        name="block_backward",
    )(
        scalars,
        weights,
        rows,
        conv,
        per_head,
        per_lane,
        lanes,
        gate_rows,
        dgate,
        normed_all,
        dscan,
        value,
        conved,
        scan,
        steps_raw,
        held,
    )

    part = min(q, dm.piece_rows)
    steps = dm.piece_rows // part

    def turn(k):
        return pl.BlockSpec((part, width), lambda i: (jnp.clip(i - k * steps, 0, steps - 1), 0))

    def slot_of_piece(k, at):
        return pl.BlockSpec(
            (None, part, width), lambda i: (at, jnp.clip(i - k * steps, 0, steps - 1), 0)
        )

    if dm.halves == 2:
        from_x, from_y, stay = across(nc[0], 1), across(nc[1], 2), nc[2]
        pass_y = (stay[1].astype(F32) + from_x[1].astype(F32)).astype(BF16)
        pass_x = (stay[3].astype(F32) + from_y[1].astype(F32)).astype(BF16)
        got_y, got_x = across(pass_y, 2), across(pass_x, 1)
        sets = (3, 3)
        terms = [stay, from_x, got_y, stay, from_y, got_x]
        specs = [slot_of_piece(0, 0), slot_of_piece(0, 0), turn(0)]
        specs += [slot_of_piece(1, 2), slot_of_piece(1, 0), turn(1)]
    else:
        sets = (n_t,)
        terms = [nc[0]] + [across(nc[k], k) for k in range(1, n_t)]
        terms = [v.reshape(chunk_rows, width) for v in terms]
        specs = [turn(0)] * n_t
    in_turn = pl.BlockSpec((part, width), lambda i: (i, 0))
    input_grad = pl.pallas_call(
        functools.partial(input_kernel, sets, steps),
        out_shape=out(chunk_rows, width),
        grid=(len(sets) * steps,),
        in_specs=[in_turn, in_turn, pl.BlockSpec((width,), lambda i: (0,))] + specs,
        out_specs=in_turn,
        compiler_params=params,
        name="input_gradient",
    )(block_input, out_cotangent, norm_gain, *terms)

    late = dm.late
    theirs = partner(theirs)
    own, own_small, *others = pl.pallas_call(
        functools.partial(pair_kernel, dm),
        out_shape=[out(part_rows, late), out(16, late, dtype=BF16)]
        + [out(part_rows + 16, late, dtype=BF16)] * (n_hi - 1),
        grid_spec=grid(1, [in_vmem] * 3, [in_vmem] * (n_hi + 1), []),
        compiler_params=params,
        name="core_sum",
    )(scalars, mine, kept, theirs)
    others = [along(v, k + 1) for k, v in enumerate(others)]
    early_mine, early_theirs = pl.pallas_call(
        functools.partial(early_kernel, dm),
        out_shape=[out(part_rows, 2 * ip), out(part_rows, 2 * ip, dtype=BF16)],
        grid_spec=grid(
            1, [in_vmem] * n_hi, [in_vmem] * 2, [vmem((2 * part_rows, 2 * ip), F32)]
        ),
        compiler_params=params,
        name="early_sum",
    )(scalars, own_early, *early)
    early_theirs = partner(early_theirs)
    (
        gate_proj_grad,
        value_proj_grad,
        step_t,
        outp_t,
        share,
        conv_value_weight_grad,
        conv_value_bias_grad,
        gate_gain_grad,
        skip_weight_grad,
        step_bias_grad,
        decay_log_grad,
    ) = pl.pallas_call(
        functools.partial(grads_kernel, dm),
        out_shape=[
            out(part_rows, inner),
            out(part_rows, inner),
            out(heads, part_rows),
            out(part_rows, inner),
            out(part_rows + 16, 2 * state, dtype=BF16),
            out(4, inner),
            out(inner),
            out(inner),
            out(heads),
            out(heads),
            out(heads),
        ],
        grid_spec=grid(1, [in_vmem] * (n_hi + 4), [in_vmem] * 11, [vmem((n_hi, 8, late), F32)]),
        compiler_params=params,
        name="gradient_sum",
    )(scalars, per_head, own, own_small, early_mine, early_theirs, *others)
    shares = [share] + [across(share, k) for k in range(1, n_t)]
    shared_proj_grad, conv_shared_weight_grad, conv_shared_bias_grad, norm_gain_grad = pl.pallas_call(
        functools.partial(share_kernel, dm),
        out_shape=[out(part_rows, 2 * state), out(4, 2 * state), out(2 * state), out(width)],
        grid_spec=grid(
            1,
            [in_vmem] * (n_t + 1),
            [in_vmem] * 4,
            [vmem((n_t, part_rows + 16, 2 * state), BF16)],
        ),
        compiler_params=params,
        name="shared_sum",
    )(scalars, norm_gain, *shares)
    return (
        block_output,
        input_grad,
        norm_gain_grad,
        gate_proj_grad,
        value_proj_grad,
        shared_proj_grad,
        step_t.T,
        conv_value_weight_grad,
        conv_value_bias_grad,
        conv_shared_weight_grad,
        conv_shared_bias_grad,
        step_bias_grad,
        decay_log_grad,
        skip_weight_grad,
        gate_gain_grad,
        outp_t.T,
    )


def solution(mesh):
    n_dp, n_t = mesh.shape["dp"], mesh.shape["tensor"]
    both = ("dp", "tensor")
    return jax.shard_map(
        functools.partial(body, n_dp, n_t),
        mesh=mesh,
        in_specs=(
            P(both, None),
            P("dp", None),
            P(),
            P("dp", "tensor"),
            P("dp", "tensor"),
            P("dp", None),
            P("dp", "tensor"),
            P(None, "tensor"),
            P("tensor"),
            P(),
            P(),
            P("tensor"),
            P("tensor"),
            P("tensor"),
            P("tensor"),
            P("tensor", "dp"),
            P(both, None),
        ),
        out_specs=(
            P(both, None),
            P(both, None),
            P(),
            P("dp", "tensor"),
            P("dp", "tensor"),
            P("dp", None),
            P("dp", "tensor"),
            P(None, "tensor"),
            P("tensor"),
            P(),
            P(),
            P("tensor"),
            P("tensor"),
            P("tensor"),
            P("tensor"),
            P("tensor", "dp"),
        ),
        check_vma=False,
    )
```

```python
import functools
import math

import jax
import jax.numpy as jnp
from jax import lax
from jax.experimental import pallas as pl
from jax.experimental.pallas import tpu as pltpu
from jax.sharding import PartitionSpec as P


BLOCK = 256
SUB = 128
LANES = 128
EPS = 1e-05
LOG2E = math.log2(math.e)
FAR = -1e30
F32 = jnp.float32
BF16 = jnp.bfloat16

MM = (((1,), (0,)), ((), ()))
MT = (((1,), (1,)), ((), ()))
TM = (((0,), (0,)), ((), ()))


def dot(a, b, dims=MM):
    return lax.dot_general(a, b, dims, preferred_element_type=F32)


def dot_split(exact, values, dims=MM):
    high = values.astype(BF16)
    low = (values - high.astype(F32)).astype(BF16)
    return dot(exact, high, dims) + dot(exact, low, dims)


def split_dot(values, exact, dims=MM):
    high = values.astype(BF16)
    low = (values - high.astype(F32)).astype(BF16)
    return dot(high, exact, dims) + dot(low, exact, dims)


def up(n, to=LANES):
    return -(-n // to) * to


def softplus(v):
    return jnp.maximum(v, 0.0) + jnp.log1p(jnp.exp(-jnp.abs(v)))


def sigmoid(v):
    return 0.5 + 0.5 * jnp.tanh(0.5 * v)


def colsum(v):
    return jnp.sum(v.reshape(v.shape[0] // 8, 8, v.shape[1]), axis=0)


def spread(cols, pair, hd):
    per = LANES // hd
    lane = lax.broadcasted_iota(jnp.int32, (cols.shape[0], LANES), 1)
    out = jnp.broadcast_to(cols[:, pair * per : pair * per + 1], lane.shape)
    for j in range(1, per):
        col = cols[:, pair * per + j : pair * per + j + 1]
        out = jnp.where(lane >= j * hd, jnp.broadcast_to(col, lane.shape), out)
    return out


def columns_of(rows):
    pad = jnp.zeros((LANES - rows.shape[0], rows.shape[1]), F32)
    return jnp.concatenate([rows, pad], axis=0).T


class Dims:
    def __init__(self, n_dp, n_t, length, width, inner, hd, state, part_rows, chunk_rows):
        self.length, self.width, self.state, self.hd = length, width, state, hd
        self.n_dp, self.n_t, self.n_hi = n_dp, n_t, n_dp // 2
        self.ip = up(inner)
        self.vs = self.ip + 2 * state
        self.np = self.ip + self.vs + LANES
        self.blocks = length // BLOCK
        self.part_rows, self.chunk_rows = part_rows, chunk_rows
        self.pairs = self.ip // LANES
        self.per = LANES // hd
        self.halves = 2 if n_t == 4 and chunk_rows == 2 * BLOCK else 1
        self.piece_rows = chunk_rows // self.halves
        self.pieces = n_t * self.halves
        self.at_n = n_dp
        self.at_c = self.at_n + self.pieces
        self.at_keep = self.at_c + n_t
        self.at_rel = self.at_keep + length // SUB
        self.at_group = self.at_rel + self.blocks
        self.at_slot = self.at_group + self.blocks
        self.at_hi = self.at_slot + self.blocks
        self.at_core = self.at_hi + self.n_hi
        self.at_from = self.at_core + 1
        self.at_side = self.at_from + self.n_hi
        self.late = self.vs + LANES
        self.local_rows = up(7 * self.pairs + 2, 8)


def load_parts(refs, target, sems, scalars, first, rows):
    return [
        pltpu.make_async_copy(
            ref, target.at[pl.ds(pl.multiple_of(scalars[first + k], rows), rows), :], sems.at[k]
        )
        for k, ref in enumerate(refs)
    ]


def decay_parts(raw, hp_ref, cols, tri):
    delta = softplus(raw + hp_ref[0:1, :])
    logs = dot_split(tri, delta * (hp_ref[1:2, :] * LOG2E))
    enter = jnp.exp2(logs) * cols[:, 7:8]
    left = [logs[k + SUB - 1 : k + SUB, :] - logs[k : k + SUB, :] for k in range(0, BLOCK, SUB)]
    ending = jnp.exp2(jnp.concatenate(left, axis=0)) * cols[:, 8:9]
    return delta, logs, enter, ending


def lower_blocks():
    r = lax.broadcasted_iota(jnp.int32, (BLOCK, BLOCK), 0)
    c = lax.broadcasted_iota(jnp.int32, (BLOCK, BLOCK), 1)
    return jnp.where((r >= c) & (r // SUB == c // SUB), 1.0, 0.0).astype(BF16)


def lane_pick(dm):
    r = lax.broadcasted_iota(jnp.int32, (2 * LANES, dm.ip), 0)
    c = lax.broadcasted_iota(jnp.int32, (2 * LANES, dm.ip), 1)
    return jnp.where(r % LANES == c // dm.hd, 1.0, 0.0).astype(BF16)


def to_lanes(cols, pick):
    high = cols.astype(BF16)
    low = (cols - high.astype(F32)).astype(BF16)
    return dot(jnp.concatenate([high, low], axis=1), pick)


def head_masks(dm):
    lane = lax.broadcasted_iota(jnp.int32, (1, LANES), 1)
    return [jnp.where(lane // dm.hd == j, 1.0, 0.0).astype(BF16) for j in range(dm.per)]


def norm_kernel(part, x_hbm, gain_ref, *refs):
    outs, (x_v, sem) = refs[:-2], refs[-2:]
    count = x_v.shape[0] // part
    copies = [
        pltpu.make_async_copy(
            x_hbm.at[pl.ds(k * part, part), :], x_v.at[pl.ds(k * part, part), :], sem.at[k]
        )
        for k in range(count)
    ]
    for copy in copies:
        copy.start()
    rows = outs[0].shape[0]
    for k, copy in enumerate(copies):
        copy.wait()
        x = x_v[k * part : (k + 1) * part]
        root = lax.rsqrt(jnp.mean(x * x, axis=1, keepdims=True) + EPS)
        first = k * part % rows
        outs[k * part // rows][first : first + part] = (x * root * gain_ref[...][None]).astype(BF16)


def pack_kernel(dm, gate_ref, value_ref, shared_ref, step_ref, out_ref):
    inner, heads, r = gate_ref.shape[1], step_ref.shape[0], step_ref.shape[1]
    if inner != dm.ip:
        out_ref[...] = jnp.zeros_like(out_ref)
    row = lax.broadcasted_iota(jnp.int32, (r, r), 0)
    col = lax.broadcasted_iota(jnp.int32, (r, r), 1)
    eye = jnp.where(row == col, 1.0, 0.0).astype(BF16)
    out_ref[:, :inner] = gate_ref[...]
    out_ref[:, dm.ip : dm.ip + inner] = value_ref[...]
    out_ref[:, 2 * dm.ip : dm.ip + dm.vs] = shared_ref[...]
    out_ref[:, dm.ip + dm.vs :] = jnp.zeros((r, LANES), BF16)
    out_ref[:, dm.ip + dm.vs : dm.ip + dm.vs + heads] = dot(eye, step_ref[...], MT).astype(BF16)


def forward_kernel(dm, scalars, *refs):
    q, ip, vs, st, hd = BLOCK, dm.ip, dm.vs, dm.state, dm.hd
    w_parts = refs[: dm.n_dp]
    n_parts = refs[dm.n_dp : dm.n_dp + dm.pieces]
    rest = refs[dm.n_dp + dm.pieces :]
    rows_ref, conv_ref, hp_ref, lane_ref = rest[:4]
    (z_out, e_out, gd_out, v_out, cv_out, ys_out, st_out, h_out, sum_out, nm_out, sg_out, w_out) = rest[
        4:16
    ]
    (w_v, nm_v, h_ref, vbuf, tri_ref, pick_ref, pbuf, gate_s, w_sem, n_sem, o_sem) = rest[16:]
    i = pl.program_id(0)
    save = pltpu.make_async_copy(w_v, w_out, o_sem)

    def rows_at(k):
        return nm_v[pl.ds(pl.multiple_of(k * q, q), q), :]

    @pl.when(i == 0)
    def _():
        copies = load_parts(w_parts, w_v, w_sem, scalars, 0, dm.part_rows)
        copies += load_parts(n_parts, nm_v, n_sem, scalars, dm.at_n, dm.piece_rows)
        for copy in copies:
            copy.start()
        h_ref[...] = jnp.zeros_like(h_ref)
        vbuf[...] = jnp.zeros_like(vbuf)
        tri_ref[...] = lower_blocks()
        pick_ref[...] = lane_pick(dm)
        for copy in copies:
            copy.wait()
        save.start()
        pbuf[...] = dot(nm_v[0:q, :], w_v[...])

    rows = rows_ref[...]
    cols = columns_of(rows)
    nm_out[...] = rows_at(i)
    for c in range(vs // LANES):
        vbuf[c, 0:8, :] = vbuf[c, q : q + 8, :]
        vbuf[c, 8 : 8 + q, :] = pbuf[:, ip + c * LANES : ip + (c + 1) * LANES]
    v_out[...] = pbuf[:, ip : ip + vs].astype(BF16)
    raw = pbuf[:, ip + vs :]
    gate_s[...] = pbuf[:, :ip]
    st_out[...] = raw

    acts = []
    count = vs // LANES
    edges = [k * dm.np // count // LANES * LANES for k in range(count)] + [dm.np]
    following = rows_at(jnp.minimum(i + 1, dm.blocks - 1))
    for c in range(count):
        g = slice(c * LANES, (c + 1) * LANES)
        acc = conv_ref[4:5, g] + conv_ref[3:4, g] * vbuf[c, 8 : 8 + q, :]
        for lag in range(1, 4):
            acc = acc + conv_ref[3 - lag : 4 - lag, g] * (
                vbuf[c, 8 - lag : 8 - lag + q, :] * cols[:, lag : lag + 1]
            )
        rounded = acc.astype(BF16)
        cv_out[:, g] = rounded
        acc = rounded.astype(F32)
        acts.append(acc * sigmoid(acc))
        n = slice(edges[c], edges[c + 1])
        pbuf[:, n] = dot(following, w_v[:, n])
    in_map = jnp.concatenate(acts[dm.pairs : dm.pairs + st // LANES], axis=1).astype(BF16)
    out_map = jnp.concatenate(acts[dm.pairs + st // LANES :], axis=1).astype(BF16)

    delta, logs, enter, ending = decay_parts(raw, hp_ref, cols, tri_ref[...])
    logs_t = logs.T
    delta_e, enter_e, ending_e = [to_lanes(v, pick_ref[...]) for v in (delta, enter, ending)]
    r = lax.broadcasted_iota(jnp.int32, (SUB, SUB), 0)
    c = lax.broadcasted_iota(jnp.int32, (SUB, SUB), 1)
    masks = head_masks(dm)
    squares = []
    for k in range(q // SUB):
        a = slice(k * SUB, (k + 1) * SUB)
        bias = jnp.where((r >= c) & (cols[a, 0:1] == rows[0:1, a]), 0.0, FAR)
        source, target = in_map[a], out_map[a]
        scores = dot(target, source, MT)
        source_t = source.T
        keep = scalars[dm.at_keep + i * (q // SUB) + k].astype(F32)
        total = jnp.exp2(logs[a][SUB - 1 :, :]) * keep
        h_out[k * st : (k + 1) * st, :] = h_ref[...].astype(BF16)
        square = None
        for p in range(dm.pairs):
            g = slice(p * LANES, (p + 1) * LANES)
            x = acts[p][a]
            u = x * delta_e[a, g]
            ub = u.astype(BF16)
            mixing = []
            for j in range(dm.per):
                h = p * dm.per + j
                decay = jnp.exp2(logs[a, h : h + 1] - logs_t[h : h + 1, a] + bias)
                mixing.append((decay * scores).astype(BF16))
            y = dot(
                jnp.concatenate(mixing, axis=1),
                jnp.concatenate([ub * mask for mask in masks], axis=0),
            )
            held = h_ref[:, g]
            y = y + dot(target, held.astype(BF16)) * enter_e[a, g]
            wu = (u * ending_e[a, g]).astype(BF16)
            h_ref[:, g] = held * spread(total, p, hd) + dot(source_t, wu)
            ys_out[a, g] = y
            gate = gate_s[a, g]
            sig = sigmoid(gate)
            z = gate * sig
            y = y + lane_ref[0:1, g] * x
            gated = y * z
            z_out[a, g] = z
            gd_out[a, g] = gated
            e_out[a, g] = (y * (sig + z * (1.0 - sig))).astype(BF16)
            sg_out[a, g] = (gated * lane_ref[1:2, g]).astype(BF16)
            square = gated * gated if square is None else square + gated * gated
        squares.append(square)
    sum_out[...] = jnp.sum(jnp.concatenate(squares, axis=0).T, axis=0, keepdims=True)

    @pl.when(i == dm.blocks - 1)
    def _():
        save.wait()


def branch_kernel(dm, scalars, *refs):
    n_dp, n_t, q = dm.n_dp, dm.n_t, BLOCK
    w_parts, sg_ref = refs[:n_dp], refs[n_dp]
    w_out, outs, (w_sem,) = refs[n_dp + 1], refs[n_dp + 2 : n_dp + 2 + n_t], refs[n_dp + 2 + n_t :]
    loads = load_parts(w_parts, w_out, w_sem, scalars, 0, dm.part_rows)
    for copy in loads:
        copy.start()
    for copy in loads:
        copy.wait()
    for k in range(n_t):
        chunk = pl.multiple_of(scalars[dm.at_c + k], dm.chunk_rows)
        for h in range(dm.chunk_rows // q):
            at = pl.ds(pl.multiple_of(chunk + h * q, q), q)
            outs[k][h] = dot(sg_ref[at, :], w_out[...], MT).astype(BF16)


def scaled_kernel(dm, scalars, *refs):
    q, n_t = BLOCK, dm.n_t
    c_parts = refs[:n_t]
    w_ref, lane_ref, gd_ref, sq_ref, sc_out, sum_out, ct_out = refs[n_t:]
    for k in range(n_t):
        chunk = pl.multiple_of(scalars[dm.at_c + k], dm.chunk_rows)
        for h in range(dm.chunk_rows // q):
            at = pl.ds(pl.multiple_of(chunk + h * q, q), q)
            cot = c_parts[k][h * q : (h + 1) * q, :]
            ct_out[at, :] = cot
            sc = (dot(cot, w_ref[...]) * lane_ref[1:2, :]).astype(BF16)
            sc_out[at, :] = sc
            prod = sc.astype(F32) * gd_ref[at, :]
            dots = prod[:, :LANES]
            for p in range(1, dm.pairs):
                dots = dots + prod[:, p * LANES : (p + 1) * LANES]
            blk = chunk // q + h
            sum_out[blk, 0:1, :] = sq_ref[blk]
            sum_out[blk, 1:2, :] = jnp.sum(dots.T, axis=0, keepdims=True)


def gate_kernel(dm, scalars, *refs):
    q, ip, r = BLOCK, dm.ip, dm.part_rows
    (w_ref, rk_ref, lane_ref, z_in, e_in, gd_in, sc_in, nm_in, ct_in) = refs[:9]
    dg_out, dy_out, lane_out, rows_out, own_out = refs[9:14]
    z_outs = refs[14 : 13 + dm.n_hi]
    acc, dg_s, both = refs[13 + dm.n_hi :]
    i = pl.program_id(0)

    @pl.when(i == 0)
    def _():
        lane_out[...] = jnp.zeros_like(lane_out)
        acc[...] = jnp.zeros_like(acc)

    def gather():
        acc[:, :ip] += dot(nm_in[...], dg_s[...], TM)
        acc[:, ip:] += dot(ct_in[...], both[...], TM)

    def gating():
        pad = jnp.zeros((LANES - 2, q), F32)
        cols = jnp.concatenate([rk_ref[...], pad], axis=0).T
        root, pull = [jnp.broadcast_to(cols[:, k : k + 1], (q, LANES)) for k in range(2)]
        for p in range(dm.pairs):
            g = slice(p * LANES, (p + 1) * LANES)
            sc, gated = sc_in[:, g].astype(F32), gd_in[:, g]
            scaled = gated * root
            cot = root * sc - pull * gated
            lane_out[:, g] += colsum(sc * scaled)
            dy = cot * z_in[:, g]
            dy_out[:, g] = dy.astype(BF16)
            dg = (cot * e_in[:, g].astype(F32)).astype(BF16)
            dg_out[:, g] = dg
            dg_s[:, g] = dg
            both[:, g] = (scaled * lane_ref[1:2, g]).astype(BF16)

    @pl.when(i == 0)
    def _():
        gating()

    @pl.when((i > 0) & (i < dm.blocks))
    def _():
        gather()
        gating()

    @pl.when(i == dm.blocks)
    def _():
        gather()
        lane_out[...] = lane_out[...] / lane_ref[1:2, :]
        prod = acc[:, :LANES] * w_ref[:, :LANES].astype(F32)
        for p in range(1, dm.pairs):
            g = slice(p * LANES, (p + 1) * LANES)
            prod = prod + acc[:, g] * w_ref[:, g].astype(F32)
        rows_out[...] = gain_rows(prod)
        hi = scalars[dm.at_hi]
        own_out[...] = acc[pl.ds(pl.multiple_of(hi * 2 * r, 8), 2 * r), :]
        for k, z_out in enumerate(z_outs):
            at = pl.multiple_of(scalars[dm.at_hi + k + 1] * 2 * r, 8)
            z_out[...] = acc[pl.ds(at, 2 * r), :].astype(BF16)


def backward_kernel(dm, scalars, *refs):
    q, ip, vs, st, hd, late_cols = BLOCK, dm.ip, dm.vs, dm.state, dm.hd, dm.late
    groups = dm.group_sizes
    w_ref, rows_ref, conv_ref, hp_ref, lane_ref, lanes_ref, gain_ref = refs[:7]
    dg_in, nm_in, dy_in, v_in, cv_in, ys_in, st_in, h_in = refs[7:15]
    mine_out, theirs_out, kept_out = refs[15:18]
    nc_outs = refs[18 : 18 + len(groups)]
    (dh_ref, dbuf, tri_ref, dx_s, act_s, t1_s, t2_s) = refs[18 + len(groups) : 25 + len(groups)]
    (pick_ref, skip_s, pj_s, full, acc, tap_out, head_out, nc_buf, nc_sem) = refs[25 + len(groups) :]
    i = pl.program_id(0)
    blk = jnp.maximum(dm.blocks - 1 - i, 0)
    subs = q // SUB

    def send(k, at, row):
        return pltpu.make_async_copy(nc_buf.at[at], nc_outs[k].at[row], nc_sem.at[at])

    @pl.when(i == 0)
    def _():
        dh_ref[...] = jnp.zeros_like(dh_ref)
        dbuf[...] = jnp.zeros_like(dbuf)
        tap_out[...] = jnp.zeros_like(tap_out)
        head_out[...] = jnp.zeros_like(head_out)
        skip_s[...] = jnp.zeros_like(skip_s)
        acc[...] = jnp.zeros_like(acc)
        tri_ref[...] = lower_blocks()
        pick_ref[...] = lane_pick(dm)

    slot = lax.rem(i, 2)

    @pl.when(i >= 3)
    def _():
        send(0, slot, 0).wait()

    third = dm.width // 3

    def cotangent_piece(n):
        def run():
            g = slice(n * third, (n + 1) * third)
            nc_buf[slot, :, g] = dot(full[...], w_ref[g, :], MT).astype(BF16)

        return run

    def gradient_piece(n):
        def run():
            g = slice(n * third, (n + 1) * third)
            acc[g, :] += dot(nm_in[:, g], full[:, ip:], TM)

        return run

    pieces = [make(n) for n in range(3) for make in (cotangent_piece, gradient_piece)]

    def take_over():
        full[:, :ip] = dg_in[...]
        full[:, ip:] = pj_s[...]

    def scan(between):
        rows = rows_ref[...]
        cols = columns_of(rows)
        raw = st_in[...]
        tri = tri_ref[...]
        delta, logs, enter, ending = decay_parts(raw, hp_ref, cols, tri)
        logs_t = logs.T
        deltas, enters, endings = [to_lanes(v, pick_ref[...]) for v in (delta, enter, ending)]

        acts, slopes = [], []
        for c in range(vs // LANES):
            g = slice(c * LANES, (c + 1) * LANES)
            cv = cv_in[:, g].astype(F32)
            sig = sigmoid(cv)
            act = cv * sig
            acts.append(act)
            slopes.append(sig + act * (1.0 - sig))
        in_map = jnp.concatenate(acts[dm.pairs : dm.pairs + st // LANES], axis=1).astype(BF16)
        out_map = jnp.concatenate(acts[dm.pairs + st // LANES :], axis=1).astype(BF16)

        r = lax.broadcasted_iota(jnp.int32, (SUB, SUB), 0)
        c = lax.broadcasted_iota(jnp.int32, (SUB, SUB), 1)
        masks = head_masks(dm)
        d_in, d_out = [None] * subs, [None] * subs
        for k in reversed(range(subs)):
            a = slice(k * SUB, (k + 1) * SUB)
            bias = jnp.where((r <= c) & (cols[a, 0:1] == rows[0:1, a]), 0.0, FAR)
            source, target = in_map[a], out_map[a]
            scores = dot(source, target, MT)
            target_t = target.T
            keep = scalars[dm.at_keep + blk * subs + k].astype(F32)
            total = jnp.exp2(logs[a][SUB - 1 :, :]) * keep
            ds = None
            for p in range(dm.pairs):
                g = slice(p * LANES, (p + 1) * LANES)
                x, dyb = acts[p][a], dy_in[a, g]
                delta_e = deltas[a, g]
                u = x * delta_e
                ub, dy = u.astype(BF16), dyb.astype(F32)
                decays = []
                for j in range(dm.per):
                    h = p * dm.per + j
                    decays.append(jnp.exp2(logs_t[h : h + 1, a] - logs[a, h : h + 1] + bias))
                du = dot(
                    jnp.concatenate([(d * scores).astype(BF16) for d in decays], axis=1),
                    jnp.concatenate([dyb * mask for mask in masks], axis=0),
                )
                dm_t = dot(jnp.concatenate([ub * mask for mask in masks], axis=0), dyb, MT)
                for j, d in enumerate(decays):
                    part = dm_t[j * SUB : (j + 1) * SUB] * d
                    ds = part if ds is None else ds + part
                dh, h_rows = dh_ref[:, g], h_in[k * st : (k + 1) * st, g]
                dh_b = dh.astype(BF16)
                end_e = endings[a, g]
                late = end_e * dot(source, dh_b)
                du = du + late
                wu = (u * end_e).astype(BF16)
                edy = (dy * enters[a, g]).astype(BF16)
                from_wu, from_dy = dot(wu, dh_b, MT), dot(edy, h_rows, MT)
                d_in[k] = from_wu if p == 0 else d_in[k] + from_wu
                d_out[k] = from_dy if p == 0 else d_out[k] + from_dy
                u32 = ub.astype(F32)
                t1_s[a, g] = dy * ys_in[a, g] - u32 * du
                t2_s[a, g] = du * x
                skip_s[:, g] += colsum(dy * x)
                kept = dh * spread(total, p, hd)
                act_s[8 * k : 8 * k + 8, g] = colsum(u32 * late) + colsum(h_rows.astype(F32) * kept)
                dh_ref[:, g] = kept + dot(target_t, edy)
                dx_s[a, g] = (delta_e * du + lane_ref[0:1, g] * dy) * slopes[p][a]
            ds_b = ds.astype(BF16)
            d_in[k] = d_in[k] + dot(ds_b, target)
            d_out[k] = d_out[k] + dot(ds_b, source, TM)

        hr = lax.broadcasted_iota(jnp.int32, (ip, LANES), 0)
        hc = lax.broadcasted_iota(jnp.int32, (ip, LANES), 1)
        pick = jnp.where(hr // hd == hc, 1.0, 0.0).astype(BF16)
        d_log = split_dot(t1_s[...], pick)
        last = split_dot(act_s[...], pick)
        row = lax.broadcasted_iota(jnp.int32, (q, LANES), 0)
        for k in range(subs):
            end = jnp.sum(last[8 * k : 8 * k + 8, :], axis=0, keepdims=True)
            d_log = d_log + jnp.where(row == (k + 1) * SUB - 1, end, 0.0)
        d_step = dot_split(tri, d_log, TM)
        head_out[8:16, :] += colsum(d_step * delta)
        d_delta = hp_ref[1:2, :] * d_step + dot(t2_s[...].astype(BF16), pick)
        d_raw = d_delta * sigmoid(raw + hp_ref[0:1, :])
        head_out[0:8, :] += colsum(d_raw)
        pj_s[:, vs:] = d_raw.astype(BF16)

        count = vs // LANES
        for c in range(count):
            dbuf[c, q : q + 8, :] = dbuf[c, 0:8, :]
            for k in range(subs):
                a = slice(k * SUB, (k + 1) * SUB)
                if c < dm.pairs:
                    dbuf[c, a, :] = dx_s[a, c * LANES : (c + 1) * LANES]
                else:
                    n = (c - dm.pairs) * LANES
                    part = d_in[k][:, n : n + LANES] if n < st else d_out[k][:, n - st : n - st + LANES]
                    dbuf[c, a, :] = part * slopes[c][a]
        for c in range(count):
            g = slice(c * LANES, (c + 1) * LANES)
            v = v_in[:, g].astype(F32)
            shifted = dbuf[c, 0:q, :]
            tap_out[32:40, g] += colsum(shifted)
            tap_out[24:32, g] += colsum(shifted * v)
            dv = conv_ref[3:4, g] * shifted
            for lag in range(1, 4):
                shifted = dbuf[c, lag : lag + q, :] * cols[:, 3 + lag : 4 + lag]
                tap_out[24 - 8 * lag : 32 - 8 * lag, g] += colsum(shifted * v)
                dv = dv + conv_ref[3 - lag : 4 - lag, g] * shifted
            pj_s[:, g] = dv.astype(BF16)
            first, stop = c * len(between) // count, (c + 1) * len(between) // count
            for run in between[first:stop]:
                run()

    @pl.when(i == 0)
    def _():
        scan([])

    @pl.when((i > 0) & (i < dm.blocks))
    def _():
        take_over()
        scan(pieces)

    @pl.when(i == dm.blocks)
    def _():
        take_over()
        for run in pieces:
            run()

    before = jnp.minimum(blk + 1, dm.blocks - 1)
    before = jnp.where(i == dm.blocks, 0, before)
    for k in range(len(groups)):

        @pl.when((i > 0) & (scalars[dm.at_group + before] == k))
        def _():
            send(k, slot, scalars[dm.at_slot + before]).start()

    @pl.when(i == dm.blocks)
    def _():
        core, r = scalars[dm.at_core], dm.part_rows
        for h in range(dm.n_hi):
            at = pl.multiple_of((2 * h + core) * r, 8)
            mine_out[h * r : (h + 1) * r, :] = acc[pl.ds(at, r), :]
            at = pl.multiple_of((2 * h + 1 - core) * r, 8)
            theirs_out[h * r : (h + 1) * r, :] = acc[pl.ds(at, r), :].astype(BF16)
        small = []

        def put(v):
            for c in range(v.shape[1] // LANES):
                small.append(jnp.sum(v[:, c * LANES : (c + 1) * LANES], axis=0, keepdims=True))

        for k in range(5):
            put(tap_out[8 * k : 8 * k + 8, :ip])
        put(lanes_ref[...])
        put(skip_s[...])
        for k in range(2):
            put(head_out[8 * k : 8 * k + 8, :])
        zero = jnp.zeros((1, LANES), F32)
        small.extend([zero] * (dm.local_rows - len(small)))
        for k in range(5):
            put(tap_out[8 * k : 8 * k + 8, ip:])
        prod = acc[:, :LANES] * w_ref[:, ip : ip + LANES].astype(F32)
        for p in range(1, late_cols // LANES):
            g = slice(p * LANES, (p + 1) * LANES)
            o = slice(ip + p * LANES, ip + (p + 1) * LANES)
            prod = prod + acc[:, g] * w_ref[:, o].astype(F32)
        prod = gain_rows(prod)
        for c in range(dm.width // LANES):
            g = slice(c * LANES, (c + 1) * LANES)
            small.append(prod[0:1, g] + gain_ref[0:1, g])
        small.extend([zero] * (late_cols // 16 - len(small)))
        for c in range(late_cols // LANES):
            g = slice(c * LANES, (c + 1) * LANES)
            parts = two_parts(jnp.concatenate(small[8 * c : 8 * c + 8], axis=0))
            theirs_out[dm.n_hi * r :, g] = parts
            kept_out[:, g] = parts
        send(0, 1 - slot, 0).wait()
        send(0, slot, 0).wait()


def two_parts(v):
    high = v.astype(BF16).astype(F32)
    return jnp.concatenate([high, v - high], axis=0).astype(BF16)


def one_part(v):
    return v[0:8, :].astype(F32) + v[8:16, :].astype(F32)


def gain_rows(acc):
    high = acc.astype(BF16)
    rest = acc - high.astype(F32)
    mid = rest.astype(BF16)
    low = (rest - mid.astype(F32)).astype(BF16)
    one = jnp.ones((8, LANES), BF16)
    return dot(one, high, MT) + dot(one, mid, MT) + dot(one, low, MT)


def pair_kernel(dm, scalars, mine_ref, kept_ref, theirs_ref, own_out, *outs):
    r = dm.part_rows
    tail = dm.n_hi * r
    small = one_part(kept_ref[...]) + one_part(theirs_ref[tail:, :])
    small = two_parts(small)
    for k in range(dm.n_hi):
        at = pl.multiple_of(scalars[dm.at_hi + k] * r, 8)
        both = mine_ref[pl.ds(at, r), :] + theirs_ref[pl.ds(at, r), :].astype(F32)
        if k == 0:
            own_out[...] = both
        else:
            outs[k][0:r, :] = both.astype(BF16)
        if k > 0:
            outs[k][r:, :] = small
        else:
            outs[0][...] = small


def early_kernel(dm, scalars, own_ref, *refs):
    parts, (mine_out, theirs_out, total) = refs[: dm.n_hi - 1], refs[dm.n_hi - 1 :]
    r = dm.part_rows
    both = own_ref[...]
    for part in parts:
        both = both + part[...].astype(F32)
    total[...] = both
    core = scalars[dm.at_core]
    mine_out[...] = total[pl.ds(pl.multiple_of(core * r, 8), r), :]
    theirs_out[...] = total[pl.ds(pl.multiple_of((1 - core) * r, 8), r), :].astype(BF16)


def grads_kernel(dm, scalars, hp_ref, own_ref, kept_ref, mine_ref, theirs_ref, *refs):
    n, r, st2 = dm.n_hi, dm.part_rows, 2 * dm.state
    parts = refs[: n - 1]
    (gate_out, value_out, step_out, outp_out, share_out) = refs[n - 1 : n + 4]
    (tap_out, tapb_out, gain_out, skip_out, sb_out, dl_out, hold) = refs[n + 4 :]
    total = own_ref[...]
    for part in parts:
        total = total + part[0:r, :].astype(F32)
    early = mine_ref[...] + theirs_ref[...].astype(F32)
    inner, heads = gate_out.shape[1], step_out.shape[0]
    gate_out[...] = early[:, :inner]
    outp_out[...] = early[:, dm.ip : dm.ip + inner]
    value_out[...] = total[:, :inner]
    share_out[0:r, :] = total[:, dm.ip : dm.vs].astype(BF16)
    step_out[...] = total[:, dm.vs :].T[0:heads, :]
    hold[0] = one_part(kept_ref[...])
    for k, part in enumerate(parts):
        hold[k + 1] = one_part(part[r:, :])
    small = hold[scalars[dm.at_from]]
    for k in range(1, n):
        small = small + hold[scalars[dm.at_from + k]]
    flat = [
        small[j : j + 1, c * LANES : (c + 1) * LANES]
        for c in range(dm.late // LANES)
        for j in range(8)
    ]

    def take(first, width):
        return jnp.concatenate(flat[first : first + dm.pairs], axis=1)[:, :width]

    for k in range(4):
        tap_out[k : k + 1, :] = take(k * dm.pairs, inner)
    tapb_out[...] = take(4 * dm.pairs, inner)[0]
    gain_out[...] = take(5 * dm.pairs, inner)[0]
    lane = lax.broadcasted_iota(jnp.int32, (1, LANES), 1)
    skip = jnp.zeros((1, LANES), F32)
    for h in range(heads):
        row = flat[6 * dm.pairs + h // dm.per]
        mine = lane // dm.hd == h % dm.per
        one = jnp.sum(jnp.where(mine, row, 0.0), axis=1, keepdims=True)
        skip = jnp.where(lane == h, one, skip)
    skip_out[...] = skip[0, :heads]
    sb_out[...] = flat[7 * dm.pairs][0, :heads]
    dl_out[...] = (flat[7 * dm.pairs + 1] * hp_ref[1:2, :])[0, :heads]
    first = dm.local_rows // 8
    for c in range(st2 // LANES):
        g = slice((first + c) * LANES, (first + c + 1) * LANES)
        share_out[r:, c * LANES : (c + 1) * LANES] = two_parts(small[:, g])


def share_kernel(dm, scalars, norm_ref, *refs):
    r, st2 = dm.part_rows, 2 * dm.state
    parts = refs[: dm.n_t]
    shared_out, tap_out, tapb_out, norm_out, hold = refs[dm.n_t :]
    for k, part in enumerate(parts):
        hold[k] = part[...]
    shared, common = None, None
    for k in range(dm.n_t):
        part = hold[scalars[dm.at_side + k]]
        share, small = part[0:r, :].astype(F32), one_part(part[r:, :])
        shared = share if shared is None else shared + share
        common = small if common is None else common + small
    shared_out[...] = shared
    flat = [
        common[j : j + 1, c * LANES : (c + 1) * LANES] for c in range(st2 // LANES) for j in range(8)
    ]
    per = st2 // LANES
    for k in range(4):
        tap_out[k : k + 1, :] = jnp.concatenate(flat[k * per : (k + 1) * per], axis=1)
    tapb_out[...] = jnp.concatenate(flat[4 * per : 5 * per], axis=1)[0]
    rows = flat[5 * per : 5 * per + dm.width // LANES]
    norm_out[...] = jnp.concatenate(rows, axis=1)[0] / norm_ref[...]


def input_kernel(sets, steps, x_ref, cot_ref, gain_ref, *refs):
    out = refs[-1]
    x = x_ref[...]
    root = lax.rsqrt(jnp.mean(x * x, axis=1, keepdims=True) + EPS)
    first = 0
    for k, count in enumerate(sets):
        parts = refs[first : first + count]
        first += count

        @pl.when(pl.program_id(0) // steps == k)
        def _():
            nc = parts[0][...].astype(F32)
            for part in parts[1:]:
                nc = nc + part[...].astype(F32)
            hat = nc * gain_ref[...][None]
            mean = jnp.mean(hat * x, axis=1, keepdims=True)
            out[...] = cot_ref[...].astype(F32) + root * hat - x * (root * root * root * mean)


def shift_hi(n, k):
    return [(i, ((i // 2 + k) % (n // 2)) * 2 + i % 2) for i in range(n)]


def swap(n, k):
    return [(i, i ^ k) for i in range(n)]


def pad_cols(v, to):
    return jnp.pad(v, ((0, 0), (0, to - v.shape[1])))


def pad_vec(v, to):
    return jnp.pad(v, (0, to - v.shape[0]))


def body(
    n_dp,
    n_t,
    block_input,
    segment_ids,
    norm_gain,
    gate_proj,
    value_proj,
    shared_proj,
    step_proj,
    conv_value_weight,
    conv_value_bias,
    conv_shared_weight,
    conv_shared_bias,
    step_bias,
    decay_log,
    skip_weight,
    gate_gain,
    output_proj,
    out_cotangent,
):
    q = BLOCK
    chunk_rows, width = block_input.shape
    length = segment_ids.shape[1]
    inner, heads = gate_proj.shape[1], step_proj.shape[1]
    part_rows = gate_proj.shape[0]
    state = shared_proj.shape[1] // 2
    hd = inner // heads
    dm = Dims(n_dp, n_t, length, width, inner, hd, state, part_rows, chunk_rows)
    ip, vs, nb, n_hi = dm.ip, dm.vs, dm.blocks, dm.n_hi
    me_t = lax.axis_index("tensor")
    me_dp = lax.axis_index("dp")
    hi, core = me_dp // 2, me_dp % 2

    def across(v, k):
        return lax.ppermute(v, "tensor", swap(n_t, k))

    def along(v, k):
        return lax.ppermute(v, "dp", shift_hi(n_dp, k))

    def partner(v):
        return lax.ppermute(v, "dp", swap(n_dp, 1))

    def vmem(shape, dtype):
        return pltpu.VMEM(shape, dtype)

    limit = 16 * 1024 * 1024
    params = pltpu.CompilerParams(dimension_semantics=("arbitrary",), vmem_limit_bytes=limit)
    hbm = pl.BlockSpec(memory_space=pl.ANY)

    def out(*shape, dtype=F32):
        return jax.ShapeDtypeStruct(shape, dtype)

    part = min(LANES, dm.piece_rows)
    normed = pl.pallas_call(
        functools.partial(norm_kernel, part),
        out_shape=[out(dm.piece_rows, width, dtype=BF16)] * dm.halves,
        in_specs=[hbm, pl.BlockSpec(memory_space=pltpu.VMEM)],
        scratch_shapes=[
            vmem((chunk_rows, width), F32),
            pltpu.SemaphoreType.DMA((chunk_rows // part,)),
        ],
        compiler_params=pltpu.CompilerParams(vmem_limit_bytes=limit),
        name="normalize",
    )(block_input, norm_gain)
    if dm.halves == 2:
        a, b = normed
        xa, yb = across(a, 1), across(b, 2)
        ya, xb = across(a, 2), across(b, 1)
        n_list = [a, b, xa, xb, ya, yb, across(xa, 2), across(yb, 1)]
        n_rows = jnp.concatenate(
            [(me_t ^ k) * chunk_rows + jnp.arange(2) * dm.piece_rows for k in range(4)]
        )
    else:
        n_list = [normed[0]] + [across(normed[0], k) for k in range(1, n_t)]
        n_rows = (me_t ^ jnp.arange(n_t)) * chunk_rows
    packed = pl.pallas_call(
        functools.partial(pack_kernel, dm),
        out_shape=out(part_rows, dm.np, dtype=BF16),
        name="pack_weights",
    )(gate_proj, value_proj, shared_proj, step_proj.T)
    w_list = [packed] + [along(packed, k) for k in range(1, n_hi)]
    w_list = w_list + [partner(v) for v in w_list]
    outp = pad_cols(output_proj.T, ip)
    o_list = [outp] + [along(outp, k) for k in range(1, n_hi)]
    o_list = o_list + [partner(v) for v in o_list]

    seg = segment_ids[0]
    subs = q // SUB
    segb = seg.reshape(nb * subs, SUB)
    last = segb[:, -1]
    prev_last = jnp.concatenate([jnp.full((1,), -1, jnp.int32), last[:-1]])
    gap = jnp.full((3,), -1, jnp.int32)
    wide = jnp.concatenate([gap, seg, gap])
    rows = [seg.astype(F32)]
    rows += [(wide[3 - k : 3 - k + length] == seg).astype(F32) for k in range(1, 4)]
    rows += [(wide[3 + k : 3 + k + length] == seg).astype(F32) for k in range(1, 4)]
    rows += [
        (segb == prev_last[:, None]).astype(F32).reshape(-1),
        (segb == last[:, None]).astype(F32).reshape(-1),
    ]
    rows = jnp.concatenate([jnp.stack(rows), jnp.zeros((16 - len(rows), length), F32)], axis=0)
    keep = (last == prev_last).astype(jnp.int32)
    other = (hi - jnp.arange(n_hi)) % n_hi
    rel = (jnp.arange(nb) * q // chunk_rows) ^ me_t
    half = jnp.arange(nb) % (chunk_rows // q)
    if dm.halves == 2:
        group_of = jnp.array([[2, 2], [0, 2], [2, 1], [0, 1]])
        slot_of = jnp.array([[0, 2], [0, 3], [1, 0], [1, 1]])
        group, slot = group_of[rel, half], slot_of[rel, half]
        dm.group_sizes = (2, 2, 4)
    else:
        group, slot = rel, half
        dm.group_sizes = (chunk_rows // q,) * n_t
    scalars = jnp.concatenate(
        [
            (other * 2 + core) * part_rows,
            (other * 2 + 1 - core) * part_rows,
            n_rows,
            (me_t ^ jnp.arange(n_t)) * chunk_rows,
            keep,
            rel,
            group,
            slot,
            (hi + jnp.arange(n_hi)) % n_hi,
            core[None],
            (hi - jnp.arange(n_hi)) % n_hi,
            me_t ^ jnp.arange(n_t),
        ]
    ).astype(jnp.int32)

    conv = jnp.concatenate(
        [
            pad_cols(jnp.concatenate([conv_value_weight, conv_value_bias[None]]), ip),
            jnp.concatenate([conv_shared_weight, conv_shared_bias[None]]),
        ],
        axis=1,
    )
    conv = jnp.pad(conv, ((0, 3), (0, 0)))
    rate = -jnp.exp(decay_log)
    per_head = jnp.stack([pad_vec(step_bias, LANES), pad_vec(rate, LANES)])
    per_head = jnp.pad(per_head, ((0, 6), (0, 0)))
    per_lane = jnp.stack([pad_vec(jnp.repeat(skip_weight, hd), ip), jnp.pad(gate_gain, (0, ip - inner), constant_values=1.0)])
    per_lane = jnp.pad(per_lane, ((0, 6), (0, 0)))

    def const(*shape):
        return pl.BlockSpec(shape, lambda i, s: (0,) * len(shape))

    def fblock(cols):
        return pl.BlockSpec((q, cols), lambda i, s: (i, 0))

    def fsum(k):
        return pl.BlockSpec((None, k, q), lambda i, s: (i, 0, 0))

    def grid(steps, in_specs, out_specs, scratch):
        return pltpu.PrefetchScalarGridSpec(
            num_scalar_prefetch=1,
            grid=(steps,),
            in_specs=in_specs,
            out_specs=out_specs,
            scratch_shapes=scratch,
        )

    (gate, slope, gated, value, conved, scan, steps_raw, held, squares, normed_all, scaled, weights) = pl.pallas_call(
        functools.partial(forward_kernel, dm),
        out_shape=[
            out(length, ip),
            out(length, ip, dtype=BF16),
            out(length, ip),
            out(length, vs, dtype=BF16),
            out(length, vs, dtype=BF16),
            out(length, ip),
            out(length, LANES),
            out(nb * subs * state, ip, dtype=BF16),
            out(nb, 1, q),
            out(length, width, dtype=BF16),
            out(length, ip, dtype=BF16),
            out(width, dm.np, dtype=BF16),
        ],
        grid_spec=grid(
            nb,
            [hbm] * (n_dp + dm.pieces)
            + [
                pl.BlockSpec((16, q), lambda i, s: (0, i)),
                const(8, vs),
                const(8, LANES),
                const(8, ip),
            ],
            [
                fblock(ip),
                fblock(ip),
                fblock(ip),
                fblock(vs),
                fblock(vs),
                fblock(ip),
                fblock(LANES),
                pl.BlockSpec((subs * state, ip), lambda i, s: (i, 0)),
                fsum(1),
                fblock(width),
                fblock(ip),
                hbm,
            ],
            [
                vmem((width, dm.np), BF16),
                vmem((length, width), BF16),
                vmem((state, ip), F32),
                vmem((vs // LANES, q + 8, LANES), F32),
                vmem((q, q), BF16),
                vmem((2 * LANES, ip), BF16),
                vmem((q, dm.np), F32),
                vmem((q, ip), F32),
                pltpu.SemaphoreType.DMA((n_dp,)),
                pltpu.SemaphoreType.DMA((dm.pieces,)),
                pltpu.SemaphoreType.DMA,
            ],
        ),
        compiler_params=params,
        cost_estimate=pl.CostEstimate(
            flops=30_000_000_000, bytes_accessed=30_000_000, transcendentals=0
        ),
        name="block_forward",
    )(scalars, *w_list, *n_list, rows, conv, per_head, per_lane)

    c_list = [out_cotangent] + [across(out_cotangent, k) for k in range(1, n_t)]
    in_vmem = pl.BlockSpec(memory_space=pltpu.VMEM)
    w_back, *branch = pl.pallas_call(
        functools.partial(branch_kernel, dm),
        out_shape=[out(width, ip, dtype=BF16)]
        + [out(chunk_rows // q, q, width, dtype=BF16)] * n_t,
        grid_spec=grid(
            1,
            [hbm] * n_dp + [in_vmem],
            [in_vmem] * (n_t + 1),
            [pltpu.SemaphoreType.DMA((n_dp,))],
        ),
        compiler_params=params,
        cost_estimate=pl.CostEstimate(
            flops=3_000_000_000, bytes_accessed=10_000_000, transcendentals=0
        ),
        name="branch_output",
    )(scalars, *o_list, scaled)
    sc, sums, cot_all = pl.pallas_call(
        functools.partial(scaled_kernel, dm),
        out_shape=[
            out(length, ip, dtype=BF16),
            out(nb, 2, q),
            out(length, width, dtype=BF16),
        ],
        grid_spec=grid(1, [in_vmem] * (n_t + 4), [in_vmem] * 3, []),
        compiler_params=params,
        cost_estimate=pl.CostEstimate(
            flops=3_000_000_000, bytes_accessed=10_000_000, transcendentals=0
        ),
        name="scaled_cotangent",
    )(scalars, *c_list, w_back, per_lane, gated, squares)
    total = sums
    for k in range(1, n_t):
        total = total + across(sums, k)
    root = lax.rsqrt(total[:, 0] / (inner * n_t) + EPS)
    pull = root * root * root * (total[:, 1] / (inner * n_t))
    rk = jnp.stack([root, pull], axis=1)
    branch_sum = branch[0].astype(F32)
    for k in range(1, n_t):
        branch_sum = branch_sum + across(branch[k], k).astype(F32)
    own_root = lax.dynamic_slice_in_dim(root.reshape(length), me_t * chunk_rows, chunk_rows)
    block_output = block_input + own_root[:, None] * branch_sum.reshape(chunk_rows, width)

    def bblock(cols):
        return pl.BlockSpec((q, cols), lambda i, s: (jnp.maximum(nb - 1 - i, 0), 0))

    def bago(cols):
        return pl.BlockSpec((q, cols), lambda i, s: (jnp.minimum(nb - i, nb - 1), 0))

    def now(cols):
        return pl.BlockSpec((q, cols), lambda i, s: (jnp.minimum(i, nb - 1), 0))

    def ago(cols):
        return pl.BlockSpec((q, cols), lambda i, s: (jnp.maximum(i - 1, 0), 0))

    dgate, dscan, lanes, gate_rows, own_early, *early = pl.pallas_call(
        functools.partial(gate_kernel, dm),
        out_shape=[
            out(length, ip, dtype=BF16),
            out(length, ip, dtype=BF16),
            out(8, ip),
            out(8, width),
            out(2 * part_rows, 2 * ip),
        ]
        + [out(2 * part_rows, 2 * ip, dtype=BF16)] * (n_hi - 1),
        grid_spec=grid(
            nb + 1,
            [
                const(width, ip),
                pl.BlockSpec((None, 2, q), lambda i, s: (jnp.minimum(i, nb - 1), 0, 0)),
                const(8, ip),
                now(ip),
                now(ip),
                now(ip),
                now(ip),
                ago(width),
                ago(width),
            ],
            [now(ip), now(ip), const(8, ip), const(8, width)]
            + [const(2 * part_rows, 2 * ip)] * n_hi,
            [vmem((width, 2 * ip), F32), vmem((q, ip), BF16), vmem((q, ip), BF16)],
        ),
        compiler_params=params,
        cost_estimate=pl.CostEstimate(
            flops=6_000_000_000, bytes_accessed=20_000_000, transcendentals=0
        ),
        name="gate_backward",
    )(scalars, weights, rk, per_lane, gate, slope, gated, sc, normed_all, cot_all)
    early = [along(v, k + 1) for k, v in enumerate(early)]

    r_all = n_hi * part_rows
    mine, theirs, kept, *nc = pl.pallas_call(
        functools.partial(backward_kernel, dm),
        out_shape=[
            out(r_all, dm.late),
            out(r_all + 16, dm.late, dtype=BF16),
            out(16, dm.late, dtype=BF16),
        ]
        + [out(k, q, width, dtype=BF16) for k in dm.group_sizes],
        grid_spec=grid(
            nb + 1,
            [
                const(width, dm.np),
                pl.BlockSpec((16, q), lambda i, s: (0, jnp.maximum(nb - 1 - i, 0))),
                const(8, vs),
                const(8, LANES),
                const(8, ip),
                const(8, ip),
                const(8, width),
                bago(ip),
                bago(width),
                bblock(ip),
                bblock(vs),
                bblock(vs),
                bblock(ip),
                bblock(LANES),
                pl.BlockSpec((subs * state, ip), lambda i, s: (jnp.maximum(nb - 1 - i, 0), 0)),
            ],
            [const(r_all, dm.late), const(r_all + 16, dm.late), const(16, dm.late)]
            + [hbm] * len(dm.group_sizes),
            [
                vmem((state, ip), F32),
                vmem((vs // LANES, q + 8, LANES), F32),
                vmem((q, q), BF16),
                vmem((q, ip), F32),
                vmem((8 * subs, ip), F32),
                vmem((q, ip), F32),
                vmem((q, ip), F32),
                vmem((2 * LANES, ip), BF16),
                vmem((8, ip), F32),
                vmem((q, dm.late), BF16),
                vmem((q, dm.np), BF16),
                vmem((width, dm.late), F32),
                vmem((40, vs), F32),
                vmem((16, LANES), F32),
                vmem((2, q, width), BF16),
                pltpu.SemaphoreType.DMA((2,)),
            ],
        ),
        compiler_params=params,
        cost_estimate=pl.CostEstimate(
            flops=40_000_000_000, bytes_accessed=30_000_000, transcendentals=0
        ),
        name="block_backward",
    )(
        scalars,
        weights,
        rows,
        conv,
        per_head,
        per_lane,
        lanes,
        gate_rows,
        dgate,
        normed_all,
        dscan,
        value,
        conved,
        scan,
        steps_raw,
        held,
    )

    part = min(q, dm.piece_rows)
    steps = dm.piece_rows // part

    def turn(k):
        return pl.BlockSpec((part, width), lambda i: (jnp.clip(i - k * steps, 0, steps - 1), 0))

    def slot_of_piece(k, at):
        return pl.BlockSpec(
            (None, part, width), lambda i: (at, jnp.clip(i - k * steps, 0, steps - 1), 0)
        )

    if dm.halves == 2:
        from_x, from_y, stay = across(nc[0], 1), across(nc[1], 2), nc[2]
        pass_y = (stay[1].astype(F32) + from_x[1].astype(F32)).astype(BF16)
        pass_x = (stay[3].astype(F32) + from_y[1].astype(F32)).astype(BF16)
        got_y, got_x = across(pass_y, 2), across(pass_x, 1)
        sets = (3, 3)
        terms = [stay, from_x, got_y, stay, from_y, got_x]
        specs = [slot_of_piece(0, 0), slot_of_piece(0, 0), turn(0)]
        specs += [slot_of_piece(1, 2), slot_of_piece(1, 0), turn(1)]
    else:
        sets = (n_t,)
        terms = [nc[0]] + [across(nc[k], k) for k in range(1, n_t)]
        terms = [v.reshape(chunk_rows, width) for v in terms]
        specs = [turn(0)] * n_t
    in_turn = pl.BlockSpec((part, width), lambda i: (i, 0))
    input_grad = pl.pallas_call(
        functools.partial(input_kernel, sets, steps),
        out_shape=out(chunk_rows, width),
        grid=(len(sets) * steps,),
        in_specs=[in_turn, in_turn, pl.BlockSpec((width,), lambda i: (0,))] + specs,
        out_specs=in_turn,
        compiler_params=params,
        name="input_gradient",
    )(block_input, out_cotangent, norm_gain, *terms)

    late = dm.late
    theirs = partner(theirs)
    own, own_small, *others = pl.pallas_call(
        functools.partial(pair_kernel, dm),
        out_shape=[out(part_rows, late), out(16, late, dtype=BF16)]
        + [out(part_rows + 16, late, dtype=BF16)] * (n_hi - 1),
        grid_spec=grid(1, [in_vmem] * 3, [in_vmem] * (n_hi + 1), []),
        compiler_params=params,
        name="core_sum",
    )(scalars, mine, kept, theirs)
    others = [along(v, k + 1) for k, v in enumerate(others)]
    early_mine, early_theirs = pl.pallas_call(
        functools.partial(early_kernel, dm),
        out_shape=[out(part_rows, 2 * ip), out(part_rows, 2 * ip, dtype=BF16)],
        grid_spec=grid(
            1, [in_vmem] * n_hi, [in_vmem] * 2, [vmem((2 * part_rows, 2 * ip), F32)]
        ),
        compiler_params=params,
        name="early_sum",
    )(scalars, own_early, *early)
    early_theirs = partner(early_theirs)
    (
        gate_proj_grad,
        value_proj_grad,
        step_t,
        outp_t,
        share,
        conv_value_weight_grad,
        conv_value_bias_grad,
        gate_gain_grad,
        skip_weight_grad,
        step_bias_grad,
        decay_log_grad,
    ) = pl.pallas_call(
        functools.partial(grads_kernel, dm),
        out_shape=[
            out(part_rows, inner),
            out(part_rows, inner),
            out(heads, part_rows),
            out(part_rows, inner),
            out(part_rows + 16, 2 * state, dtype=BF16),
            out(4, inner),
            out(inner),
            out(inner),
            out(heads),
            out(heads),
            out(heads),
        ],
        grid_spec=grid(1, [in_vmem] * (n_hi + 4), [in_vmem] * 11, [vmem((n_hi, 8, late), F32)]),
        compiler_params=params,
        name="gradient_sum",
    )(scalars, per_head, own, own_small, early_mine, early_theirs, *others)
    shares = [share] + [across(share, k) for k in range(1, n_t)]
    shared_proj_grad, conv_shared_weight_grad, conv_shared_bias_grad, norm_gain_grad = pl.pallas_call(
        functools.partial(share_kernel, dm),
        out_shape=[out(part_rows, 2 * state), out(4, 2 * state), out(2 * state), out(width)],
        grid_spec=grid(
            1,
            [in_vmem] * (n_t + 1),
            [in_vmem] * 4,
            [vmem((n_t, part_rows + 16, 2 * state), BF16)],
        ),
        compiler_params=params,
        name="shared_sum",
    )(scalars, norm_gain, *shares)
    return (
        block_output,
        input_grad,
        norm_gain_grad,
        gate_proj_grad,
        value_proj_grad,
        shared_proj_grad,
        step_t.T,
        conv_value_weight_grad,
        conv_value_bias_grad,
        conv_shared_weight_grad,
        conv_shared_bias_grad,
        step_bias_grad,
        decay_log_grad,
        skip_weight_grad,
        gate_gain_grad,
        outp_t.T,
    )


def solution(mesh):
    n_dp, n_t = mesh.shape["dp"], mesh.shape["tensor"]
    both = ("dp", "tensor")
    return jax.shard_map(
        functools.partial(body, n_dp, n_t),
        mesh=mesh,
        in_specs=(
            P(both, None),
            P("dp", None),
            P(),
            P("dp", "tensor"),
            P("dp", "tensor"),
            P("dp", None),
            P("dp", "tensor"),
            P(None, "tensor"),
            P("tensor"),
            P(),
            P(),
            P("tensor"),
            P("tensor"),
            P("tensor"),
            P("tensor"),
            P("tensor", "dp"),
            P(both, None),
        ),
        out_specs=(
            P(both, None),
            P(both, None),
            P(),
            P("dp", "tensor"),
            P("dp", "tensor"),
            P("dp", None),
            P("dp", "tensor"),
            P(None, "tensor"),
            P("tensor"),
            P(),
            P(),
            P("tensor"),
            P("tensor"),
            P("tensor"),
            P("tensor"),
            P("tensor", "dp"),
        ),
        check_vma=False,
    )
```

```python
import functools
import math

import jax
import jax.numpy as jnp
from jax import lax
from jax.experimental import pallas as pl
from jax.experimental.pallas import tpu as pltpu
from jax.sharding import PartitionSpec as P


BLOCK = 256
SUB = 128
LANES = 128
EPS = 1e-05
LOG2E = math.log2(math.e)
FAR = -1e30
F32 = jnp.float32
BF16 = jnp.bfloat16

MM = (((1,), (0,)), ((), ()))
MT = (((1,), (1,)), ((), ()))
TM = (((0,), (0,)), ((), ()))


def dot(a, b, dims=MM):
    return lax.dot_general(a, b, dims, preferred_element_type=F32)


def dot_split(exact, values, dims=MM):
    high = values.astype(BF16)
    low = (values - high.astype(F32)).astype(BF16)
    return dot(exact, high, dims) + dot(exact, low, dims)


def split_dot(values, exact, dims=MM):
    high = values.astype(BF16)
    low = (values - high.astype(F32)).astype(BF16)
    return dot(high, exact, dims) + dot(low, exact, dims)


def up(n, to=LANES):
    return -(-n // to) * to


def softplus(v):
    return jnp.maximum(v, 0.0) + jnp.log1p(jnp.exp(-jnp.abs(v)))


def sigmoid(v):
    return 0.5 + 0.5 * jnp.tanh(0.5 * v)


def colsum(v):
    return jnp.sum(v.reshape(v.shape[0] // 8, 8, v.shape[1]), axis=0)


def spread(cols, pair, hd):
    per = LANES // hd
    lane = lax.broadcasted_iota(jnp.int32, (cols.shape[0], LANES), 1)
    out = jnp.broadcast_to(cols[:, pair * per : pair * per + 1], lane.shape)
    for j in range(1, per):
        col = cols[:, pair * per + j : pair * per + j + 1]
        out = jnp.where(lane >= j * hd, jnp.broadcast_to(col, lane.shape), out)
    return out


def columns_of(rows):
    pad = jnp.zeros((LANES - rows.shape[0], rows.shape[1]), F32)
    return jnp.concatenate([rows, pad], axis=0).T


class Dims:
    def __init__(self, n_dp, n_t, length, width, inner, hd, state, part_rows, chunk_rows):
        self.length, self.width, self.state, self.hd = length, width, state, hd
        self.n_dp, self.n_t, self.n_hi = n_dp, n_t, n_dp // 2
        self.ip = up(inner)
        self.vs = self.ip + 2 * state
        self.np = self.ip + self.vs + LANES
        self.blocks = length // BLOCK
        self.part_rows, self.chunk_rows = part_rows, chunk_rows
        self.pairs = self.ip // LANES
        self.per = LANES // hd
        self.halves = 2 if n_t == 4 and chunk_rows == 2 * BLOCK else 1
        self.piece_rows = chunk_rows // self.halves
        self.pieces = n_t * self.halves
        self.at_n = n_dp
        self.at_c = self.at_n + self.pieces
        self.at_keep = self.at_c + n_t
        self.at_rel = self.at_keep + length // SUB
        self.at_group = self.at_rel + self.blocks
        self.at_slot = self.at_group + self.blocks
        self.at_hi = self.at_slot + self.blocks
        self.at_core = self.at_hi + self.n_hi
        self.at_from = self.at_core + 1
        self.at_side = self.at_from + self.n_hi
        self.late = self.vs + LANES
        self.local_rows = up(7 * self.pairs + 2, 8)


def load_parts(refs, target, sems, scalars, first, rows):
    return [
        pltpu.make_async_copy(
            ref, target.at[pl.ds(pl.multiple_of(scalars[first + k], rows), rows), :], sems.at[k]
        )
        for k, ref in enumerate(refs)
    ]


def decay_parts(raw, hp_ref, cols, tri):
    delta = softplus(raw + hp_ref[0:1, :])
    logs = dot_split(tri, delta * (hp_ref[1:2, :] * LOG2E))
    enter = jnp.exp2(logs) * cols[:, 7:8]
    left = [logs[k + SUB - 1 : k + SUB, :] - logs[k : k + SUB, :] for k in range(0, BLOCK, SUB)]
    ending = jnp.exp2(jnp.concatenate(left, axis=0)) * cols[:, 8:9]
    return delta, logs, enter, ending


def lower_blocks():
    r = lax.broadcasted_iota(jnp.int32, (BLOCK, BLOCK), 0)
    c = lax.broadcasted_iota(jnp.int32, (BLOCK, BLOCK), 1)
    return jnp.where((r >= c) & (r // SUB == c // SUB), 1.0, 0.0).astype(BF16)


def lane_pick(dm):
    r = lax.broadcasted_iota(jnp.int32, (2 * LANES, dm.ip), 0)
    c = lax.broadcasted_iota(jnp.int32, (2 * LANES, dm.ip), 1)
    return jnp.where(r % LANES == c // dm.hd, 1.0, 0.0).astype(BF16)


def to_lanes(cols, pick):
    high = cols.astype(BF16)
    low = (cols - high.astype(F32)).astype(BF16)
    return dot(jnp.concatenate([high, low], axis=1), pick)


def head_masks(dm):
    lane = lax.broadcasted_iota(jnp.int32, (1, LANES), 1)
    return [jnp.where(lane // dm.hd == j, 1.0, 0.0).astype(BF16) for j in range(dm.per)]


def norm_kernel(x_ref, gain_ref, *outs):
    rows = outs[0].shape[0]
    part = min(LANES, rows)
    for k in range(x_ref.shape[0] // part):
        x = x_ref[k * part : (k + 1) * part]
        root = lax.rsqrt(jnp.mean(x * x, axis=1, keepdims=True) + EPS)
        first = k * part % rows
        outs[k * part // rows][first : first + part] = (x * root * gain_ref[...][None]).astype(BF16)


def pack_kernel(dm, gate_ref, value_ref, shared_ref, step_ref, out_ref):
    inner, heads, r = gate_ref.shape[1], step_ref.shape[0], step_ref.shape[1]
    if inner != dm.ip:
        out_ref[...] = jnp.zeros_like(out_ref)
    row = lax.broadcasted_iota(jnp.int32, (r, r), 0)
    col = lax.broadcasted_iota(jnp.int32, (r, r), 1)
    eye = jnp.where(row == col, 1.0, 0.0).astype(BF16)
    out_ref[:, :inner] = gate_ref[...]
    out_ref[:, dm.ip : dm.ip + inner] = value_ref[...]
    out_ref[:, 2 * dm.ip : dm.ip + dm.vs] = shared_ref[...]
    out_ref[:, dm.ip + dm.vs :] = jnp.zeros((r, LANES), BF16)
    out_ref[:, dm.ip + dm.vs : dm.ip + dm.vs + heads] = dot(eye, step_ref[...], MT).astype(BF16)


def forward_kernel(dm, scalars, *refs):
    q, ip, vs, st, hd = BLOCK, dm.ip, dm.vs, dm.state, dm.hd
    w_parts = refs[: dm.n_dp]
    n_parts = refs[dm.n_dp : dm.n_dp + dm.pieces]
    rest = refs[dm.n_dp + dm.pieces :]
    rows_ref, conv_ref, hp_ref, lane_ref = rest[:4]
    (z_out, e_out, gd_out, v_out, cv_out, ys_out, st_out, h_out, sum_out, nm_out, sg_out, w_out) = rest[
        4:16
    ]
    (w_v, nm_v, h_ref, vbuf, tri_ref, pick_ref, pbuf, gate_s, w_sem, n_sem, o_sem) = rest[16:]
    i = pl.program_id(0)
    save = pltpu.make_async_copy(w_v, w_out, o_sem)

    def rows_at(k):
        return nm_v[pl.ds(pl.multiple_of(k * q, q), q), :]

    @pl.when(i == 0)
    def _():
        copies = load_parts(w_parts, w_v, w_sem, scalars, 0, dm.part_rows)
        copies += load_parts(n_parts, nm_v, n_sem, scalars, dm.at_n, dm.piece_rows)
        for copy in copies:
            copy.start()
        h_ref[...] = jnp.zeros_like(h_ref)
        vbuf[...] = jnp.zeros_like(vbuf)
        tri_ref[...] = lower_blocks()
        pick_ref[...] = lane_pick(dm)
        for copy in copies:
            copy.wait()
        save.start()
        pbuf[...] = dot(nm_v[0:q, :], w_v[...])

    rows = rows_ref[...]
    cols = columns_of(rows)
    nm_out[...] = rows_at(i)
    for c in range(vs // LANES):
        vbuf[c, 0:8, :] = vbuf[c, q : q + 8, :]
        vbuf[c, 8 : 8 + q, :] = pbuf[:, ip + c * LANES : ip + (c + 1) * LANES]
    v_out[...] = pbuf[:, ip : ip + vs].astype(BF16)
    raw = pbuf[:, ip + vs :]
    gate_s[...] = pbuf[:, :ip]
    st_out[...] = raw

    acts = []
    count = vs // LANES
    edges = [k * dm.np // count // LANES * LANES for k in range(count)] + [dm.np]
    following = rows_at(jnp.minimum(i + 1, dm.blocks - 1))
    for c in range(count):
        g = slice(c * LANES, (c + 1) * LANES)
        acc = conv_ref[4:5, g] + conv_ref[3:4, g] * vbuf[c, 8 : 8 + q, :]
        for lag in range(1, 4):
            acc = acc + conv_ref[3 - lag : 4 - lag, g] * (
                vbuf[c, 8 - lag : 8 - lag + q, :] * cols[:, lag : lag + 1]
            )
        rounded = acc.astype(BF16)
        cv_out[:, g] = rounded
        acc = rounded.astype(F32)
        acts.append(acc * sigmoid(acc))
        n = slice(edges[c], edges[c + 1])
        pbuf[:, n] = dot(following, w_v[:, n])
    in_map = jnp.concatenate(acts[dm.pairs : dm.pairs + st // LANES], axis=1).astype(BF16)
    out_map = jnp.concatenate(acts[dm.pairs + st // LANES :], axis=1).astype(BF16)

    delta, logs, enter, ending = decay_parts(raw, hp_ref, cols, tri_ref[...])
    logs_t = logs.T
    delta_e, enter_e, ending_e = [to_lanes(v, pick_ref[...]) for v in (delta, enter, ending)]
    r = lax.broadcasted_iota(jnp.int32, (SUB, SUB), 0)
    c = lax.broadcasted_iota(jnp.int32, (SUB, SUB), 1)
    masks = head_masks(dm)
    squares = []
    for k in range(q // SUB):
        a = slice(k * SUB, (k + 1) * SUB)
        bias = jnp.where((r >= c) & (cols[a, 0:1] == rows[0:1, a]), 0.0, FAR)
        source, target = in_map[a], out_map[a]
        scores = dot(target, source, MT)
        source_t = source.T
        keep = scalars[dm.at_keep + i * (q // SUB) + k].astype(F32)
        total = jnp.exp2(logs[a][SUB - 1 :, :]) * keep
        h_out[k * st : (k + 1) * st, :] = h_ref[...].astype(BF16)
        square = None
        for p in range(dm.pairs):
            g = slice(p * LANES, (p + 1) * LANES)
            x = acts[p][a]
            u = x * delta_e[a, g]
            ub = u.astype(BF16)
            mixing = []
            for j in range(dm.per):
                h = p * dm.per + j
                decay = jnp.exp2(logs[a, h : h + 1] - logs_t[h : h + 1, a] + bias)
                mixing.append((decay * scores).astype(BF16))
            y = dot(
                jnp.concatenate(mixing, axis=1),
                jnp.concatenate([ub * mask for mask in masks], axis=0),
            )
            held = h_ref[:, g]
            y = y + dot(target, held.astype(BF16)) * enter_e[a, g]
            wu = (u * ending_e[a, g]).astype(BF16)
            h_ref[:, g] = held * spread(total, p, hd) + dot(source_t, wu)
            ys_out[a, g] = y
            gate = gate_s[a, g]
            sig = sigmoid(gate)
            z = gate * sig
            y = y + lane_ref[0:1, g] * x
            gated = y * z
            z_out[a, g] = z
            gd_out[a, g] = gated
            e_out[a, g] = (y * (sig + z * (1.0 - sig))).astype(BF16)
            sg_out[a, g] = (gated * lane_ref[1:2, g]).astype(BF16)
            square = gated * gated if square is None else square + gated * gated
        squares.append(square)
    sum_out[...] = jnp.sum(jnp.concatenate(squares, axis=0).T, axis=0, keepdims=True)

    @pl.when(i == dm.blocks - 1)
    def _():
        save.wait()


def branch_kernel(dm, scalars, *refs):
    n_dp, n_t, q = dm.n_dp, dm.n_t, BLOCK
    w_parts, sg_ref = refs[:n_dp], refs[n_dp]
    w_out, outs, (w_sem,) = refs[n_dp + 1], refs[n_dp + 2 : n_dp + 2 + n_t], refs[n_dp + 2 + n_t :]
    loads = load_parts(w_parts, w_out, w_sem, scalars, 0, dm.part_rows)
    for copy in loads:
        copy.start()
    for copy in loads:
        copy.wait()
    for k in range(n_t):
        chunk = pl.multiple_of(scalars[dm.at_c + k], dm.chunk_rows)
        for h in range(dm.chunk_rows // q):
            at = pl.ds(pl.multiple_of(chunk + h * q, q), q)
            outs[k][h] = dot(sg_ref[at, :], w_out[...], MT).astype(BF16)


def scaled_kernel(dm, scalars, *refs):
    q, n_t = BLOCK, dm.n_t
    c_parts = refs[:n_t]
    w_ref, lane_ref, gd_ref, sq_ref, sc_out, sum_out, ct_out = refs[n_t:]
    for k in range(n_t):
        chunk = pl.multiple_of(scalars[dm.at_c + k], dm.chunk_rows)
        for h in range(dm.chunk_rows // q):
            at = pl.ds(pl.multiple_of(chunk + h * q, q), q)
            cot = c_parts[k][h * q : (h + 1) * q, :]
            ct_out[at, :] = cot
            sc = (dot(cot, w_ref[...]) * lane_ref[1:2, :]).astype(BF16)
            sc_out[at, :] = sc
            prod = sc.astype(F32) * gd_ref[at, :]
            dots = prod[:, :LANES]
            for p in range(1, dm.pairs):
                dots = dots + prod[:, p * LANES : (p + 1) * LANES]
            blk = chunk // q + h
            sum_out[blk, 0:1, :] = sq_ref[blk]
            sum_out[blk, 1:2, :] = jnp.sum(dots.T, axis=0, keepdims=True)


def gate_kernel(dm, scalars, *refs):
    q, ip, r = BLOCK, dm.ip, dm.part_rows
    (w_ref, rk_ref, lane_ref, z_in, e_in, gd_in, sc_in, nm_in, ct_in) = refs[:9]
    dg_out, dy_out, lane_out, rows_out, own_out = refs[9:14]
    z_outs = refs[14 : 13 + dm.n_hi]
    acc, dg_s, both = refs[13 + dm.n_hi :]
    i = pl.program_id(0)

    @pl.when(i == 0)
    def _():
        lane_out[...] = jnp.zeros_like(lane_out)
        acc[...] = jnp.zeros_like(acc)

    def gather():
        acc[:, :ip] += dot(nm_in[...], dg_s[...], TM)
        acc[:, ip:] += dot(ct_in[...], both[...], TM)

    def gating():
        pad = jnp.zeros((LANES - 2, q), F32)
        cols = jnp.concatenate([rk_ref[...], pad], axis=0).T
        root, pull = [jnp.broadcast_to(cols[:, k : k + 1], (q, LANES)) for k in range(2)]
        for p in range(dm.pairs):
            g = slice(p * LANES, (p + 1) * LANES)
            sc, gated = sc_in[:, g].astype(F32), gd_in[:, g]
            scaled = gated * root
            cot = root * sc - pull * gated
            lane_out[:, g] += colsum(sc * scaled)
            dy = cot * z_in[:, g]
            dy_out[:, g] = dy.astype(BF16)
            dg = (cot * e_in[:, g].astype(F32)).astype(BF16)
            dg_out[:, g] = dg
            dg_s[:, g] = dg
            both[:, g] = (scaled * lane_ref[1:2, g]).astype(BF16)

    @pl.when(i == 0)
    def _():
        gating()

    @pl.when((i > 0) & (i < dm.blocks))
    def _():
        gather()
        gating()

    @pl.when(i == dm.blocks)
    def _():
        gather()
        lane_out[...] = lane_out[...] / lane_ref[1:2, :]
        prod = acc[:, :LANES] * w_ref[:, :LANES].astype(F32)
        for p in range(1, dm.pairs):
            g = slice(p * LANES, (p + 1) * LANES)
            prod = prod + acc[:, g] * w_ref[:, g].astype(F32)
        rows_out[...] = gain_rows(prod)
        hi = scalars[dm.at_hi]
        own_out[...] = acc[pl.ds(pl.multiple_of(hi * 2 * r, 8), 2 * r), :]
        for k, z_out in enumerate(z_outs):
            at = pl.multiple_of(scalars[dm.at_hi + k + 1] * 2 * r, 8)
            z_out[...] = acc[pl.ds(at, 2 * r), :].astype(BF16)


def backward_kernel(dm, scalars, *refs):
    q, ip, vs, st, hd, late_cols = BLOCK, dm.ip, dm.vs, dm.state, dm.hd, dm.late
    groups = dm.group_sizes
    w_ref, rows_ref, conv_ref, hp_ref, lane_ref, lanes_ref, gain_ref = refs[:7]
    dg_in, nm_in, dy_in, v_in, cv_in, ys_in, st_in, h_in = refs[7:15]
    mine_out, theirs_out, kept_out = refs[15:18]
    nc_outs = refs[18 : 18 + len(groups)]
    (dh_ref, dbuf, tri_ref, dx_s, act_s, t1_s, t2_s) = refs[18 + len(groups) : 25 + len(groups)]
    (pick_ref, skip_s, pj_s, full, acc, tap_out, head_out, nc_buf, nc_sem, own_sem) = refs[25 + len(groups) :]
    i = pl.program_id(0)
    blk = jnp.maximum(dm.blocks - 1 - i, 0)
    subs = q // SUB

    def send(k, at, row):
        return pltpu.make_async_copy(nc_buf.at[at], nc_outs[k].at[row], nc_sem.at[at])

    @pl.when(i == 0)
    def _():
        dh_ref[...] = jnp.zeros_like(dh_ref)
        dbuf[...] = jnp.zeros_like(dbuf)
        tap_out[...] = jnp.zeros_like(tap_out)
        head_out[...] = jnp.zeros_like(head_out)
        skip_s[...] = jnp.zeros_like(skip_s)
        acc[...] = jnp.zeros_like(acc)
        tri_ref[...] = lower_blocks()
        pick_ref[...] = lane_pick(dm)

    slot = lax.rem(i, 2)

    @pl.when(i >= 3)
    def _():
        send(0, slot, 0).wait()

    third = dm.width // 3

    def cotangent_piece(n):
        def run():
            g = slice(n * third, (n + 1) * third)
            nc_buf[slot, :, g] = dot(full[...], w_ref[g, :], MT).astype(BF16)

        return run

    def gradient_piece(n):
        def run():
            g = slice(n * third, (n + 1) * third)
            acc[g, :] += dot(nm_in[:, g], full[:, ip:], TM)

        return run

    pieces = [make(n) for n in range(3) for make in (cotangent_piece, gradient_piece)]

    def take_over():
        full[:, :ip] = dg_in[...]
        full[:, ip:] = pj_s[...]

    def scan(between):
        rows = rows_ref[...]
        cols = columns_of(rows)
        raw = st_in[...]
        tri = tri_ref[...]
        delta, logs, enter, ending = decay_parts(raw, hp_ref, cols, tri)
        logs_t = logs.T
        deltas, enters, endings = [to_lanes(v, pick_ref[...]) for v in (delta, enter, ending)]

        acts, slopes = [], []
        for c in range(vs // LANES):
            g = slice(c * LANES, (c + 1) * LANES)
            cv = cv_in[:, g].astype(F32)
            sig = sigmoid(cv)
            act = cv * sig
            acts.append(act)
            slopes.append(sig + act * (1.0 - sig))
        in_map = jnp.concatenate(acts[dm.pairs : dm.pairs + st // LANES], axis=1).astype(BF16)
        out_map = jnp.concatenate(acts[dm.pairs + st // LANES :], axis=1).astype(BF16)

        r = lax.broadcasted_iota(jnp.int32, (SUB, SUB), 0)
        c = lax.broadcasted_iota(jnp.int32, (SUB, SUB), 1)
        masks = head_masks(dm)
        d_in, d_out = [None] * subs, [None] * subs
        for k in reversed(range(subs)):
            a = slice(k * SUB, (k + 1) * SUB)
            bias = jnp.where((r <= c) & (cols[a, 0:1] == rows[0:1, a]), 0.0, FAR)
            source, target = in_map[a], out_map[a]
            scores = dot(source, target, MT)
            target_t = target.T
            keep = scalars[dm.at_keep + blk * subs + k].astype(F32)
            total = jnp.exp2(logs[a][SUB - 1 :, :]) * keep
            ds = None
            for p in range(dm.pairs):
                g = slice(p * LANES, (p + 1) * LANES)
                x, dyb = acts[p][a], dy_in[a, g]
                delta_e = deltas[a, g]
                u = x * delta_e
                ub, dy = u.astype(BF16), dyb.astype(F32)
                decays = []
                for j in range(dm.per):
                    h = p * dm.per + j
                    decays.append(jnp.exp2(logs_t[h : h + 1, a] - logs[a, h : h + 1] + bias))
                du = dot(
                    jnp.concatenate([(d * scores).astype(BF16) for d in decays], axis=1),
                    jnp.concatenate([dyb * mask for mask in masks], axis=0),
                )
                dm_t = dot(jnp.concatenate([ub * mask for mask in masks], axis=0), dyb, MT)
                for j, d in enumerate(decays):
                    part = dm_t[j * SUB : (j + 1) * SUB] * d
                    ds = part if ds is None else ds + part
                dh, h_rows = dh_ref[:, g], h_in[k * st : (k + 1) * st, g]
                dh_b = dh.astype(BF16)
                end_e = endings[a, g]
                late = end_e * dot(source, dh_b)
                du = du + late
                wu = (u * end_e).astype(BF16)
                edy = (dy * enters[a, g]).astype(BF16)
                from_wu, from_dy = dot(wu, dh_b, MT), dot(edy, h_rows, MT)
                d_in[k] = from_wu if p == 0 else d_in[k] + from_wu
                d_out[k] = from_dy if p == 0 else d_out[k] + from_dy
                u32 = ub.astype(F32)
                t1_s[a, g] = dy * ys_in[a, g] - u32 * du
                t2_s[a, g] = du * x
                skip_s[:, g] += colsum(dy * x)
                kept = dh * spread(total, p, hd)
                act_s[8 * k : 8 * k + 8, g] = colsum(u32 * late) + colsum(h_rows.astype(F32) * kept)
                dh_ref[:, g] = kept + dot(target_t, edy)
                dx_s[a, g] = (delta_e * du + lane_ref[0:1, g] * dy) * slopes[p][a]
            ds_b = ds.astype(BF16)
            d_in[k] = d_in[k] + dot(ds_b, target)
            d_out[k] = d_out[k] + dot(ds_b, source, TM)

        hr = lax.broadcasted_iota(jnp.int32, (ip, LANES), 0)
        hc = lax.broadcasted_iota(jnp.int32, (ip, LANES), 1)
        pick = jnp.where(hr // hd == hc, 1.0, 0.0).astype(BF16)
        d_log = split_dot(t1_s[...], pick)
        last = split_dot(act_s[...], pick)
        row = lax.broadcasted_iota(jnp.int32, (q, LANES), 0)
        for k in range(subs):
            end = jnp.sum(last[8 * k : 8 * k + 8, :], axis=0, keepdims=True)
            d_log = d_log + jnp.where(row == (k + 1) * SUB - 1, end, 0.0)
        d_step = dot_split(tri, d_log, TM)
        head_out[8:16, :] += colsum(d_step * delta)
        d_delta = hp_ref[1:2, :] * d_step + dot(t2_s[...].astype(BF16), pick)
        d_raw = d_delta * sigmoid(raw + hp_ref[0:1, :])
        head_out[0:8, :] += colsum(d_raw)
        pj_s[:, vs:] = d_raw.astype(BF16)

        count = vs // LANES
        for c in range(count):
            dbuf[c, q : q + 8, :] = dbuf[c, 0:8, :]
            for k in range(subs):
                a = slice(k * SUB, (k + 1) * SUB)
                if c < dm.pairs:
                    dbuf[c, a, :] = dx_s[a, c * LANES : (c + 1) * LANES]
                else:
                    n = (c - dm.pairs) * LANES
                    part = d_in[k][:, n : n + LANES] if n < st else d_out[k][:, n - st : n - st + LANES]
                    dbuf[c, a, :] = part * slopes[c][a]
        for c in range(count):
            g = slice(c * LANES, (c + 1) * LANES)
            v = v_in[:, g].astype(F32)
            shifted = dbuf[c, 0:q, :]
            tap_out[32:40, g] += colsum(shifted)
            tap_out[24:32, g] += colsum(shifted * v)
            dv = conv_ref[3:4, g] * shifted
            for lag in range(1, 4):
                shifted = dbuf[c, lag : lag + q, :] * cols[:, 3 + lag : 4 + lag]
                tap_out[24 - 8 * lag : 32 - 8 * lag, g] += colsum(shifted * v)
                dv = dv + conv_ref[3 - lag : 4 - lag, g] * shifted
            pj_s[:, g] = dv.astype(BF16)
            first, stop = c * len(between) // count, (c + 1) * len(between) // count
            for run in between[first:stop]:
                run()

    @pl.when(i == 0)
    def _():
        scan([])

    @pl.when((i > 0) & (i < dm.blocks))
    def _():
        take_over()
        scan(pieces)

    @pl.when(i == dm.blocks)
    def _():
        take_over()
        for run in pieces:
            run()

    before = jnp.minimum(blk + 1, dm.blocks - 1)
    before = jnp.where(i == dm.blocks, 0, before)
    for k in range(len(groups)):

        @pl.when((i > 0) & (scalars[dm.at_group + before] == k))
        def _():
            send(k, slot, scalars[dm.at_slot + before]).start()

    @pl.when(i == dm.blocks)
    def _():
        core, r = scalars[dm.at_core], dm.part_rows
        owns = []
        for h in range(dm.n_hi):
            at = pl.multiple_of((2 * h + core) * r, 8)
            own = pltpu.make_async_copy(
                acc.at[pl.ds(at, r), :], mine_out.at[h * r : (h + 1) * r, :], own_sem.at[h]
            )
            own.start()
            owns.append(own)
            at = pl.multiple_of((2 * h + 1 - core) * r, 8)
            theirs_out[h * r : (h + 1) * r, :] = acc[pl.ds(at, r), :].astype(BF16)
        small = []

        def put(v):
            for c in range(v.shape[1] // LANES):
                small.append(jnp.sum(v[:, c * LANES : (c + 1) * LANES], axis=0, keepdims=True))

        for k in range(5):
            put(tap_out[8 * k : 8 * k + 8, :ip])
        put(lanes_ref[...])
        put(skip_s[...])
        for k in range(2):
            put(head_out[8 * k : 8 * k + 8, :])
        zero = jnp.zeros((1, LANES), F32)
        small.extend([zero] * (dm.local_rows - len(small)))
        for k in range(5):
            put(tap_out[8 * k : 8 * k + 8, ip:])
        prod = acc[:, :LANES] * w_ref[:, ip : ip + LANES].astype(F32)
        for p in range(1, late_cols // LANES):
            g = slice(p * LANES, (p + 1) * LANES)
            o = slice(ip + p * LANES, ip + (p + 1) * LANES)
            prod = prod + acc[:, g] * w_ref[:, o].astype(F32)
        prod = gain_rows(prod)
        for c in range(dm.width // LANES):
            g = slice(c * LANES, (c + 1) * LANES)
            small.append(prod[0:1, g] + gain_ref[0:1, g])
        small.extend([zero] * (late_cols // 16 - len(small)))
        for c in range(late_cols // LANES):
            g = slice(c * LANES, (c + 1) * LANES)
            parts = two_parts(jnp.concatenate(small[8 * c : 8 * c + 8], axis=0))
            theirs_out[dm.n_hi * r :, g] = parts
            kept_out[:, g] = parts
        for own in owns:
            own.wait()
        send(0, 1 - slot, 0).wait()
        send(0, slot, 0).wait()


def two_parts(v):
    high = v.astype(BF16).astype(F32)
    return jnp.concatenate([high, v - high], axis=0).astype(BF16)


def one_part(v):
    return v[0:8, :].astype(F32) + v[8:16, :].astype(F32)


def gain_rows(acc):
    high = acc.astype(BF16)
    rest = acc - high.astype(F32)
    mid = rest.astype(BF16)
    low = (rest - mid.astype(F32)).astype(BF16)
    one = jnp.ones((8, LANES), BF16)
    return dot(one, high, MT) + dot(one, mid, MT) + dot(one, low, MT)


def pair_kernel(dm, scalars, mine_ref, kept_ref, theirs_ref, own_out, *outs):
    r = dm.part_rows
    tail = dm.n_hi * r
    small = one_part(kept_ref[...]) + one_part(theirs_ref[tail:, :])
    small = two_parts(small)
    for k in range(dm.n_hi):
        at = pl.multiple_of(scalars[dm.at_hi + k] * r, 8)
        both = mine_ref[pl.ds(at, r), :] + theirs_ref[pl.ds(at, r), :].astype(F32)
        if k == 0:
            own_out[...] = both
        else:
            outs[k][0:r, :] = both.astype(BF16)
        if k > 0:
            outs[k][r:, :] = small
        else:
            outs[0][...] = small


def early_kernel(dm, scalars, own_ref, *refs):
    parts, (mine_out, theirs_out, total) = refs[: dm.n_hi - 1], refs[dm.n_hi - 1 :]
    r = dm.part_rows
    both = own_ref[...]
    for part in parts:
        both = both + part[...].astype(F32)
    total[...] = both
    core = scalars[dm.at_core]
    mine_out[...] = total[pl.ds(pl.multiple_of(core * r, 8), r), :]
    theirs_out[...] = total[pl.ds(pl.multiple_of((1 - core) * r, 8), r), :].astype(BF16)


def grads_kernel(dm, scalars, hp_ref, own_ref, kept_ref, mine_ref, theirs_ref, *refs):
    n, r, st2 = dm.n_hi, dm.part_rows, 2 * dm.state
    parts = refs[: n - 1]
    (gate_out, value_out, step_out, outp_out, share_out) = refs[n - 1 : n + 4]
    (tap_out, tapb_out, gain_out, skip_out, sb_out, dl_out, hold) = refs[n + 4 :]
    total = own_ref[...]
    for part in parts:
        total = total + part[0:r, :].astype(F32)
    early = mine_ref[...] + theirs_ref[...].astype(F32)
    inner, heads = gate_out.shape[1], step_out.shape[0]
    gate_out[...] = early[:, :inner]
    outp_out[...] = early[:, dm.ip : dm.ip + inner]
    value_out[...] = total[:, :inner]
    share_out[0:r, :] = total[:, dm.ip : dm.vs].astype(BF16)
    step_out[...] = total[:, dm.vs :].T[0:heads, :]
    hold[0] = one_part(kept_ref[...])
    for k, part in enumerate(parts):
        hold[k + 1] = one_part(part[r:, :])
    small = hold[scalars[dm.at_from]]
    for k in range(1, n):
        small = small + hold[scalars[dm.at_from + k]]
    flat = [
        small[j : j + 1, c * LANES : (c + 1) * LANES]
        for c in range(dm.late // LANES)
        for j in range(8)
    ]

    def take(first, width):
        return jnp.concatenate(flat[first : first + dm.pairs], axis=1)[:, :width]

    for k in range(4):
        tap_out[k : k + 1, :] = take(k * dm.pairs, inner)
    tapb_out[...] = take(4 * dm.pairs, inner)[0]
    gain_out[...] = take(5 * dm.pairs, inner)[0]
    lane = lax.broadcasted_iota(jnp.int32, (1, LANES), 1)
    skip = jnp.zeros((1, LANES), F32)
    for h in range(heads):
        row = flat[6 * dm.pairs + h // dm.per]
        mine = lane // dm.hd == h % dm.per
        one = jnp.sum(jnp.where(mine, row, 0.0), axis=1, keepdims=True)
        skip = jnp.where(lane == h, one, skip)
    skip_out[...] = skip[0, :heads]
    sb_out[...] = flat[7 * dm.pairs][0, :heads]
    dl_out[...] = (flat[7 * dm.pairs + 1] * hp_ref[1:2, :])[0, :heads]
    first = dm.local_rows // 8
    for c in range(st2 // LANES):
        g = slice((first + c) * LANES, (first + c + 1) * LANES)
        share_out[r:, c * LANES : (c + 1) * LANES] = two_parts(small[:, g])


def share_kernel(dm, scalars, norm_ref, *refs):
    r, st2 = dm.part_rows, 2 * dm.state
    parts = refs[: dm.n_t]
    shared_out, tap_out, tapb_out, norm_out, hold = refs[dm.n_t :]
    for k, part in enumerate(parts):
        hold[k] = part[...]
    shared, common = None, None
    for k in range(dm.n_t):
        part = hold[scalars[dm.at_side + k]]
        share, small = part[0:r, :].astype(F32), one_part(part[r:, :])
        shared = share if shared is None else shared + share
        common = small if common is None else common + small
    shared_out[...] = shared
    flat = [
        common[j : j + 1, c * LANES : (c + 1) * LANES] for c in range(st2 // LANES) for j in range(8)
    ]
    per = st2 // LANES
    for k in range(4):
        tap_out[k : k + 1, :] = jnp.concatenate(flat[k * per : (k + 1) * per], axis=1)
    tapb_out[...] = jnp.concatenate(flat[4 * per : 5 * per], axis=1)[0]
    rows = flat[5 * per : 5 * per + dm.width // LANES]
    norm_out[...] = jnp.concatenate(rows, axis=1)[0] / norm_ref[...]


def input_kernel(sets, steps, x_ref, cot_ref, gain_ref, *refs):
    out = refs[-1]
    x = x_ref[...]
    root = lax.rsqrt(jnp.mean(x * x, axis=1, keepdims=True) + EPS)
    first = 0
    for k, count in enumerate(sets):
        parts = refs[first : first + count]
        first += count

        @pl.when(pl.program_id(0) // steps == k)
        def _():
            nc = parts[0][...].astype(F32)
            for part in parts[1:]:
                nc = nc + part[...].astype(F32)
            hat = nc * gain_ref[...][None]
            mean = jnp.mean(hat * x, axis=1, keepdims=True)
            out[...] = cot_ref[...].astype(F32) + root * hat - x * (root * root * root * mean)


def shift_hi(n, k):
    return [(i, ((i // 2 + k) % (n // 2)) * 2 + i % 2) for i in range(n)]


def swap(n, k):
    return [(i, i ^ k) for i in range(n)]


def pad_cols(v, to):
    return jnp.pad(v, ((0, 0), (0, to - v.shape[1])))


def pad_vec(v, to):
    return jnp.pad(v, (0, to - v.shape[0]))


def body(
    n_dp,
    n_t,
    block_input,
    segment_ids,
    norm_gain,
    gate_proj,
    value_proj,
    shared_proj,
    step_proj,
    conv_value_weight,
    conv_value_bias,
    conv_shared_weight,
    conv_shared_bias,
    step_bias,
    decay_log,
    skip_weight,
    gate_gain,
    output_proj,
    out_cotangent,
):
    q = BLOCK
    chunk_rows, width = block_input.shape
    length = segment_ids.shape[1]
    inner, heads = gate_proj.shape[1], step_proj.shape[1]
    part_rows = gate_proj.shape[0]
    state = shared_proj.shape[1] // 2
    hd = inner // heads
    dm = Dims(n_dp, n_t, length, width, inner, hd, state, part_rows, chunk_rows)
    ip, vs, nb, n_hi = dm.ip, dm.vs, dm.blocks, dm.n_hi
    me_t = lax.axis_index("tensor")
    me_dp = lax.axis_index("dp")
    hi, core = me_dp // 2, me_dp % 2

    def across(v, k):
        return lax.ppermute(v, "tensor", swap(n_t, k))

    def along(v, k):
        return lax.ppermute(v, "dp", shift_hi(n_dp, k))

    def partner(v):
        return lax.ppermute(v, "dp", swap(n_dp, 1))

    def vmem(shape, dtype):
        return pltpu.VMEM(shape, dtype)

    limit = 16 * 1024 * 1024
    params = pltpu.CompilerParams(dimension_semantics=("arbitrary",), vmem_limit_bytes=limit)
    hbm = pl.BlockSpec(memory_space=pl.ANY)
    in_hbm = pl.BlockSpec(memory_space=pltpu.HBM)

    def out(*shape, dtype=F32):
        return jax.ShapeDtypeStruct(shape, dtype)

    normed = pl.pallas_call(
        norm_kernel,
        out_shape=[out(dm.piece_rows, width, dtype=BF16)] * dm.halves,
        compiler_params=pltpu.CompilerParams(vmem_limit_bytes=limit),
        name="normalize",
    )(block_input, norm_gain)
    if dm.halves == 2:
        a, b = normed
        xa, yb = across(a, 1), across(b, 2)
        ya, xb = across(a, 2), across(b, 1)
        n_list = [a, b, xa, xb, ya, yb, across(xa, 2), across(yb, 1)]
        n_rows = jnp.concatenate(
            [(me_t ^ k) * chunk_rows + jnp.arange(2) * dm.piece_rows for k in range(4)]
        )
    else:
        n_list = [normed[0]] + [across(normed[0], k) for k in range(1, n_t)]
        n_rows = (me_t ^ jnp.arange(n_t)) * chunk_rows
    packed = pl.pallas_call(
        functools.partial(pack_kernel, dm),
        out_shape=out(part_rows, dm.np, dtype=BF16),
        name="pack_weights",
    )(gate_proj, value_proj, shared_proj, step_proj.T)
    w_list = [packed] + [along(packed, k) for k in range(1, n_hi)]
    w_list = w_list + [partner(v) for v in w_list]
    outp = pad_cols(output_proj.T, ip)
    o_list = [outp] + [along(outp, k) for k in range(1, n_hi)]
    o_list = o_list + [partner(v) for v in o_list]

    seg = segment_ids[0]
    subs = q // SUB
    segb = seg.reshape(nb * subs, SUB)
    last = segb[:, -1]
    prev_last = jnp.concatenate([jnp.full((1,), -1, jnp.int32), last[:-1]])
    gap = jnp.full((3,), -1, jnp.int32)
    wide = jnp.concatenate([gap, seg, gap])
    rows = [seg.astype(F32)]
    rows += [(wide[3 - k : 3 - k + length] == seg).astype(F32) for k in range(1, 4)]
    rows += [(wide[3 + k : 3 + k + length] == seg).astype(F32) for k in range(1, 4)]
    rows += [
        (segb == prev_last[:, None]).astype(F32).reshape(-1),
        (segb == last[:, None]).astype(F32).reshape(-1),
    ]
    rows = jnp.concatenate([jnp.stack(rows), jnp.zeros((16 - len(rows), length), F32)], axis=0)
    keep = (last == prev_last).astype(jnp.int32)
    other = (hi - jnp.arange(n_hi)) % n_hi
    rel = (jnp.arange(nb) * q // chunk_rows) ^ me_t
    half = jnp.arange(nb) % (chunk_rows // q)
    if dm.halves == 2:
        group_of = jnp.array([[2, 2], [0, 2], [2, 1], [0, 1]])
        slot_of = jnp.array([[0, 2], [0, 3], [1, 0], [1, 1]])
        group, slot = group_of[rel, half], slot_of[rel, half]
        dm.group_sizes = (2, 2, 4)
    else:
        group, slot = rel, half
        dm.group_sizes = (chunk_rows // q,) * n_t
    scalars = jnp.concatenate(
        [
            (other * 2 + core) * part_rows,
            (other * 2 + 1 - core) * part_rows,
            n_rows,
            (me_t ^ jnp.arange(n_t)) * chunk_rows,
            keep,
            rel,
            group,
            slot,
            (hi + jnp.arange(n_hi)) % n_hi,
            core[None],
            (hi - jnp.arange(n_hi)) % n_hi,
            me_t ^ jnp.arange(n_t),
        ]
    ).astype(jnp.int32)

    conv = jnp.concatenate(
        [
            pad_cols(jnp.concatenate([conv_value_weight, conv_value_bias[None]]), ip),
            jnp.concatenate([conv_shared_weight, conv_shared_bias[None]]),
        ],
        axis=1,
    )
    conv = jnp.pad(conv, ((0, 3), (0, 0)))
    rate = -jnp.exp(decay_log)
    per_head = jnp.stack([pad_vec(step_bias, LANES), pad_vec(rate, LANES)])
    per_head = jnp.pad(per_head, ((0, 6), (0, 0)))
    per_lane = jnp.stack([pad_vec(jnp.repeat(skip_weight, hd), ip), jnp.pad(gate_gain, (0, ip - inner), constant_values=1.0)])
    per_lane = jnp.pad(per_lane, ((0, 6), (0, 0)))

    def const(*shape):
        return pl.BlockSpec(shape, lambda i, s: (0,) * len(shape))

    def fblock(cols):
        return pl.BlockSpec((q, cols), lambda i, s: (i, 0))

    def fsum(k):
        return pl.BlockSpec((None, k, q), lambda i, s: (i, 0, 0))

    def grid(steps, in_specs, out_specs, scratch):
        return pltpu.PrefetchScalarGridSpec(
            num_scalar_prefetch=1,
            grid=(steps,),
            in_specs=in_specs,
            out_specs=out_specs,
            scratch_shapes=scratch,
        )

    (gate, slope, gated, value, conved, scan, steps_raw, held, squares, normed_all, scaled, weights) = pl.pallas_call(
        functools.partial(forward_kernel, dm),
        out_shape=[
            out(length, ip),
            out(length, ip, dtype=BF16),
            out(length, ip),
            out(length, vs, dtype=BF16),
            out(length, vs, dtype=BF16),
            out(length, ip),
            out(length, LANES),
            out(nb * subs * state, ip, dtype=BF16),
            out(nb, 1, q),
            out(length, width, dtype=BF16),
            out(length, ip, dtype=BF16),
            out(width, dm.np, dtype=BF16),
        ],
        grid_spec=grid(
            nb,
            [in_hbm] * (n_dp + dm.pieces)
            + [
                pl.BlockSpec((16, q), lambda i, s: (0, i)),
                const(8, vs),
                const(8, LANES),
                const(8, ip),
            ],
            [
                fblock(ip),
                fblock(ip),
                fblock(ip),
                fblock(vs),
                fblock(vs),
                fblock(ip),
                fblock(LANES),
                pl.BlockSpec((subs * state, ip), lambda i, s: (i, 0)),
                fsum(1),
                fblock(width),
                fblock(ip),
                hbm,
            ],
            [
                vmem((width, dm.np), BF16),
                vmem((length, width), BF16),
                vmem((state, ip), F32),
                vmem((vs // LANES, q + 8, LANES), F32),
                vmem((q, q), BF16),
                vmem((2 * LANES, ip), BF16),
                vmem((q, dm.np), F32),
                vmem((q, ip), F32),
                pltpu.SemaphoreType.DMA((n_dp,)),
                pltpu.SemaphoreType.DMA((dm.pieces,)),
                pltpu.SemaphoreType.DMA,
            ],
        ),
        compiler_params=params,
        cost_estimate=pl.CostEstimate(
            flops=30_000_000_000, bytes_accessed=30_000_000, transcendentals=0
        ),
        name="block_forward",
    )(scalars, *w_list, *n_list, rows, conv, per_head, per_lane)

    c_list = [out_cotangent] + [across(out_cotangent, k) for k in range(1, n_t)]
    in_vmem = pl.BlockSpec(memory_space=pltpu.VMEM)
    w_back, *branch = pl.pallas_call(
        functools.partial(branch_kernel, dm),
        out_shape=[out(width, ip, dtype=BF16)]
        + [out(chunk_rows // q, q, width, dtype=BF16)] * n_t,
        grid_spec=grid(
            1,
            [hbm] * n_dp + [in_vmem],
            [in_vmem] * (n_t + 1),
            [pltpu.SemaphoreType.DMA((n_dp,))],
        ),
        compiler_params=params,
        cost_estimate=pl.CostEstimate(
            flops=3_000_000_000, bytes_accessed=10_000_000, transcendentals=0
        ),
        name="branch_output",
    )(scalars, *o_list, scaled)
    sc, sums, cot_all = pl.pallas_call(
        functools.partial(scaled_kernel, dm),
        out_shape=[
            out(length, ip, dtype=BF16),
            out(nb, 2, q),
            out(length, width, dtype=BF16),
        ],
        grid_spec=grid(1, [in_vmem] * (n_t + 4), [in_vmem] * 3, []),
        compiler_params=params,
        cost_estimate=pl.CostEstimate(
            flops=3_000_000_000, bytes_accessed=10_000_000, transcendentals=0
        ),
        name="scaled_cotangent",
    )(scalars, *c_list, w_back, per_lane, gated, squares)
    total = sums
    for k in range(1, n_t):
        total = total + across(sums, k)
    root = lax.rsqrt(total[:, 0] / (inner * n_t) + EPS)
    pull = root * root * root * (total[:, 1] / (inner * n_t))
    rk = jnp.stack([root, pull], axis=1)
    branch_sum = branch[0].astype(F32)
    for k in range(1, n_t):
        branch_sum = branch_sum + across(branch[k], k).astype(F32)
    own_root = lax.dynamic_slice_in_dim(root.reshape(length), me_t * chunk_rows, chunk_rows)
    block_output = block_input + own_root[:, None] * branch_sum.reshape(chunk_rows, width)

    def bblock(cols):
        return pl.BlockSpec((q, cols), lambda i, s: (jnp.maximum(nb - 1 - i, 0), 0))

    def bago(cols):
        return pl.BlockSpec((q, cols), lambda i, s: (jnp.minimum(nb - i, nb - 1), 0))

    def now(cols):
        return pl.BlockSpec((q, cols), lambda i, s: (jnp.minimum(i, nb - 1), 0))

    def ago(cols):
        return pl.BlockSpec((q, cols), lambda i, s: (jnp.maximum(i - 1, 0), 0))

    dgate, dscan, lanes, gate_rows, own_early, *early = pl.pallas_call(
        functools.partial(gate_kernel, dm),
        out_shape=[
            out(length, ip, dtype=BF16),
            out(length, ip, dtype=BF16),
            out(8, ip),
            out(8, width),
            out(2 * part_rows, 2 * ip),
        ]
        + [out(2 * part_rows, 2 * ip, dtype=BF16)] * (n_hi - 1),
        grid_spec=grid(
            nb + 1,
            [
                const(width, ip),
                pl.BlockSpec((None, 2, q), lambda i, s: (jnp.minimum(i, nb - 1), 0, 0)),
                const(8, ip),
                now(ip),
                now(ip),
                now(ip),
                now(ip),
                ago(width),
                ago(width),
            ],
            [now(ip), now(ip), const(8, ip), const(8, width)]
            + [const(2 * part_rows, 2 * ip)] * n_hi,
            [vmem((width, 2 * ip), F32), vmem((q, ip), BF16), vmem((q, ip), BF16)],
        ),
        compiler_params=params,
        cost_estimate=pl.CostEstimate(
            flops=6_000_000_000, bytes_accessed=20_000_000, transcendentals=0
        ),
        name="gate_backward",
    )(scalars, weights, rk, per_lane, gate, slope, gated, sc, normed_all, cot_all)
    early = [along(v, k + 1) for k, v in enumerate(early)]

    r_all = n_hi * part_rows
    mine, theirs, kept, *nc = pl.pallas_call(
        functools.partial(backward_kernel, dm),
        out_shape=[
            out(r_all, dm.late),
            out(r_all + 16, dm.late, dtype=BF16),
            out(16, dm.late, dtype=BF16),
        ]
        + [out(k, q, width, dtype=BF16) for k in dm.group_sizes],
        grid_spec=grid(
            nb + 1,
            [
                const(width, dm.np),
                pl.BlockSpec((16, q), lambda i, s: (0, jnp.maximum(nb - 1 - i, 0))),
                const(8, vs),
                const(8, LANES),
                const(8, ip),
                const(8, ip),
                const(8, width),
                bago(ip),
                bago(width),
                bblock(ip),
                bblock(vs),
                bblock(vs),
                bblock(ip),
                bblock(LANES),
                pl.BlockSpec((subs * state, ip), lambda i, s: (jnp.maximum(nb - 1 - i, 0), 0)),
            ],
            [in_hbm, const(r_all + 16, dm.late), const(16, dm.late)]
            + [in_hbm] * len(dm.group_sizes),
            [
                vmem((state, ip), F32),
                vmem((vs // LANES, q + 8, LANES), F32),
                vmem((q, q), BF16),
                vmem((q, ip), F32),
                vmem((8 * subs, ip), F32),
                vmem((q, ip), F32),
                vmem((q, ip), F32),
                vmem((2 * LANES, ip), BF16),
                vmem((8, ip), F32),
                vmem((q, dm.late), BF16),
                vmem((q, dm.np), BF16),
                vmem((width, dm.late), F32),
                vmem((40, vs), F32),
                vmem((16, LANES), F32),
                vmem((2, q, width), BF16),
                pltpu.SemaphoreType.DMA((2,)),
                pltpu.SemaphoreType.DMA((n_hi,)),
            ],
        ),
        compiler_params=params,
        cost_estimate=pl.CostEstimate(
            flops=40_000_000_000, bytes_accessed=30_000_000, transcendentals=0
        ),
        name="block_backward",
    )(
        scalars,
        weights,
        rows,
        conv,
        per_head,
        per_lane,
        lanes,
        gate_rows,
        dgate,
        normed_all,
        dscan,
        value,
        conved,
        scan,
        steps_raw,
        held,
    )

    part = min(q, dm.piece_rows)
    steps = dm.piece_rows // part

    def turn(k):
        return pl.BlockSpec((part, width), lambda i: (jnp.clip(i - k * steps, 0, steps - 1), 0))

    def slot_of_piece(k, at):
        return pl.BlockSpec(
            (None, part, width), lambda i: (at, jnp.clip(i - k * steps, 0, steps - 1), 0)
        )

    if dm.halves == 2:
        from_x, from_y, stay = across(nc[0], 1), across(nc[1], 2), nc[2]
        pass_y = (stay[1].astype(F32) + from_x[1].astype(F32)).astype(BF16)
        pass_x = (stay[3].astype(F32) + from_y[1].astype(F32)).astype(BF16)
        got_y, got_x = across(pass_y, 2), across(pass_x, 1)
        sets = (3, 3)
        terms = [stay, from_x, got_y, stay, from_y, got_x]
        specs = [slot_of_piece(0, 0), slot_of_piece(0, 0), turn(0)]
        specs += [slot_of_piece(1, 2), slot_of_piece(1, 0), turn(1)]
    else:
        sets = (n_t,)
        terms = [nc[0]] + [across(nc[k], k) for k in range(1, n_t)]
        terms = [v.reshape(chunk_rows, width) for v in terms]
        specs = [turn(0)] * n_t
    in_turn = pl.BlockSpec((part, width), lambda i: (i, 0))
    input_grad = pl.pallas_call(
        functools.partial(input_kernel, sets, steps),
        out_shape=out(chunk_rows, width),
        grid=(len(sets) * steps,),
        in_specs=[in_turn, in_turn, pl.BlockSpec((width,), lambda i: (0,))] + specs,
        out_specs=in_turn,
        compiler_params=params,
        name="input_gradient",
    )(block_input, out_cotangent, norm_gain, *terms)

    late = dm.late
    theirs = partner(theirs)
    own, own_small, *others = pl.pallas_call(
        functools.partial(pair_kernel, dm),
        out_shape=[out(part_rows, late), out(16, late, dtype=BF16)]
        + [out(part_rows + 16, late, dtype=BF16)] * (n_hi - 1),
        grid_spec=grid(1, [in_vmem] * 3, [in_vmem] * (n_hi + 1), []),
        compiler_params=params,
        name="core_sum",
    )(scalars, mine, kept, theirs)
    others = [along(v, k + 1) for k, v in enumerate(others)]
    early_mine, early_theirs = pl.pallas_call(
        functools.partial(early_kernel, dm),
        out_shape=[out(part_rows, 2 * ip), out(part_rows, 2 * ip, dtype=BF16)],
        grid_spec=grid(
            1, [in_vmem] * n_hi, [in_vmem] * 2, [vmem((2 * part_rows, 2 * ip), F32)]
        ),
        compiler_params=params,
        name="early_sum",
    )(scalars, own_early, *early)
    early_theirs = partner(early_theirs)
    (
        gate_proj_grad,
        value_proj_grad,
        step_t,
        outp_t,
        share,
        conv_value_weight_grad,
        conv_value_bias_grad,
        gate_gain_grad,
        skip_weight_grad,
        step_bias_grad,
        decay_log_grad,
    ) = pl.pallas_call(
        functools.partial(grads_kernel, dm),
        out_shape=[
            out(part_rows, inner),
            out(part_rows, inner),
            out(heads, part_rows),
            out(part_rows, inner),
            out(part_rows + 16, 2 * state, dtype=BF16),
            out(4, inner),
            out(inner),
            out(inner),
            out(heads),
            out(heads),
            out(heads),
        ],
        grid_spec=grid(1, [in_vmem] * (n_hi + 4), [in_vmem] * 11, [vmem((n_hi, 8, late), F32)]),
        compiler_params=params,
        name="gradient_sum",
    )(scalars, per_head, own, own_small, early_mine, early_theirs, *others)
    shares = [share] + [across(share, k) for k in range(1, n_t)]
    shared_proj_grad, conv_shared_weight_grad, conv_shared_bias_grad, norm_gain_grad = pl.pallas_call(
        functools.partial(share_kernel, dm),
        out_shape=[out(part_rows, 2 * state), out(4, 2 * state), out(2 * state), out(width)],
        grid_spec=grid(
            1,
            [in_vmem] * (n_t + 1),
            [in_vmem] * 4,
            [vmem((n_t, part_rows + 16, 2 * state), BF16)],
        ),
        compiler_params=params,
        name="shared_sum",
    )(scalars, norm_gain, *shares)
    return (
        block_output,
        input_grad,
        norm_gain_grad,
        gate_proj_grad,
        value_proj_grad,
        shared_proj_grad,
        step_t.T,
        conv_value_weight_grad,
        conv_value_bias_grad,
        conv_shared_weight_grad,
        conv_shared_bias_grad,
        step_bias_grad,
        decay_log_grad,
        skip_weight_grad,
        gate_gain_grad,
        outp_t.T,
    )


def solution(mesh):
    n_dp, n_t = mesh.shape["dp"], mesh.shape["tensor"]
    both = ("dp", "tensor")
    return jax.shard_map(
        functools.partial(body, n_dp, n_t),
        mesh=mesh,
        in_specs=(
            P(both, None),
            P("dp", None),
            P(),
            P("dp", "tensor"),
            P("dp", "tensor"),
            P("dp", None),
            P("dp", "tensor"),
            P(None, "tensor"),
            P("tensor"),
            P(),
            P(),
            P("tensor"),
            P("tensor"),
            P("tensor"),
            P("tensor"),
            P("tensor", "dp"),
            P(both, None),
        ),
        out_specs=(
            P(both, None),
            P(both, None),
            P(),
            P("dp", "tensor"),
            P("dp", "tensor"),
            P("dp", None),
            P("dp", "tensor"),
            P(None, "tensor"),
            P("tensor"),
            P(),
            P(),
            P("tensor"),
            P("tensor"),
            P("tensor"),
            P("tensor"),
            P("tensor", "dp"),
        ),
        check_vma=False,
    )
```

```python
import functools
import math

import jax
import jax.numpy as jnp
from jax import lax
from jax.experimental import pallas as pl
from jax.experimental.pallas import tpu as pltpu
from jax.sharding import PartitionSpec as P


BLOCK = 256
SUB = 128
LANES = 128
EPS = 1e-05
LOG2E = math.log2(math.e)
FAR = -1e30
F32 = jnp.float32
BF16 = jnp.bfloat16

MM = (((1,), (0,)), ((), ()))
MT = (((1,), (1,)), ((), ()))
TM = (((0,), (0,)), ((), ()))


def dot(a, b, dims=MM):
    return lax.dot_general(a, b, dims, preferred_element_type=F32)


def dot_split(exact, values, dims=MM):
    high = values.astype(BF16)
    low = (values - high.astype(F32)).astype(BF16)
    return dot(exact, high, dims) + dot(exact, low, dims)


def split_dot(values, exact, dims=MM):
    high = values.astype(BF16)
    low = (values - high.astype(F32)).astype(BF16)
    return dot(high, exact, dims) + dot(low, exact, dims)


def up(n, to=LANES):
    return -(-n // to) * to


def softplus(v):
    return jnp.maximum(v, 0.0) + jnp.log1p(jnp.exp(-jnp.abs(v)))


def sigmoid(v):
    return 0.5 + 0.5 * jnp.tanh(0.5 * v)


def colsum(v):
    return jnp.sum(v.reshape(v.shape[0] // 8, 8, v.shape[1]), axis=0)


def spread(cols, pair, hd):
    per = LANES // hd
    lane = lax.broadcasted_iota(jnp.int32, (cols.shape[0], LANES), 1)
    out = jnp.broadcast_to(cols[:, pair * per : pair * per + 1], lane.shape)
    for j in range(1, per):
        col = cols[:, pair * per + j : pair * per + j + 1]
        out = jnp.where(lane >= j * hd, jnp.broadcast_to(col, lane.shape), out)
    return out


def columns_of(rows):
    pad = jnp.zeros((LANES - rows.shape[0], rows.shape[1]), F32)
    return jnp.concatenate([rows, pad], axis=0).T


class Dims:
    def __init__(self, n_dp, n_t, length, width, inner, hd, state, part_rows, chunk_rows):
        self.length, self.width, self.state, self.hd = length, width, state, hd
        self.n_dp, self.n_t, self.n_hi = n_dp, n_t, n_dp // 2
        self.ip = up(inner)
        self.vs = self.ip + 2 * state
        self.np = self.ip + self.vs + LANES
        self.blocks = length // BLOCK
        self.part_rows, self.chunk_rows = part_rows, chunk_rows
        self.pairs = self.ip // LANES
        self.per = LANES // hd
        self.halves = 2 if n_t == 4 and chunk_rows == 2 * BLOCK else 1
        self.piece_rows = chunk_rows // self.halves
        self.pieces = n_t * self.halves
        self.at_n = n_dp
        self.at_c = self.at_n + self.pieces
        self.at_keep = self.at_c + n_t
        self.at_rel = self.at_keep + length // SUB
        self.at_group = self.at_rel + self.blocks
        self.at_slot = self.at_group + self.blocks
        self.at_hi = self.at_slot + self.blocks
        self.at_core = self.at_hi + self.n_hi
        self.at_from = self.at_core + 1
        self.at_side = self.at_from + self.n_hi
        self.late = self.vs + LANES
        self.local_rows = up(7 * self.pairs + 2, 8)


def load_parts(refs, target, sems, scalars, first, rows):
    return [
        pltpu.make_async_copy(
            ref, target.at[pl.ds(pl.multiple_of(scalars[first + k], rows), rows), :], sems.at[k]
        )
        for k, ref in enumerate(refs)
    ]


def decay_parts(raw, hp_ref, cols, tri):
    delta = softplus(raw + hp_ref[0:1, :])
    logs = dot_split(tri, delta * (hp_ref[1:2, :] * LOG2E))
    enter = jnp.exp2(logs) * cols[:, 7:8]
    left = [logs[k + SUB - 1 : k + SUB, :] - logs[k : k + SUB, :] for k in range(0, BLOCK, SUB)]
    ending = jnp.exp2(jnp.concatenate(left, axis=0)) * cols[:, 8:9]
    return delta, logs, enter, ending


def lower_blocks():
    r = lax.broadcasted_iota(jnp.int32, (BLOCK, BLOCK), 0)
    c = lax.broadcasted_iota(jnp.int32, (BLOCK, BLOCK), 1)
    return jnp.where((r >= c) & (r // SUB == c // SUB), 1.0, 0.0).astype(BF16)


def lane_pick(dm):
    r = lax.broadcasted_iota(jnp.int32, (2 * LANES, dm.ip), 0)
    c = lax.broadcasted_iota(jnp.int32, (2 * LANES, dm.ip), 1)
    return jnp.where(r % LANES == c // dm.hd, 1.0, 0.0).astype(BF16)


def to_lanes(cols, pick):
    high = cols.astype(BF16)
    low = (cols - high.astype(F32)).astype(BF16)
    return dot(jnp.concatenate([high, low], axis=1), pick)


def head_masks(dm):
    lane = lax.broadcasted_iota(jnp.int32, (1, LANES), 1)
    return [jnp.where(lane // dm.hd == j, 1.0, 0.0).astype(BF16) for j in range(dm.per)]


def norm_kernel(x_ref, gain_ref, *outs):
    rows = outs[0].shape[0]
    part = min(LANES, rows)
    for k in range(x_ref.shape[0] // part):
        x = x_ref[k * part : (k + 1) * part]
        root = lax.rsqrt(jnp.mean(x * x, axis=1, keepdims=True) + EPS)
        first = k * part % rows
        outs[k * part // rows][first : first + part] = (x * root * gain_ref[...][None]).astype(BF16)


def pack_kernel(dm, gate_ref, value_ref, shared_ref, step_ref, out_ref):
    inner, heads, r = gate_ref.shape[1], step_ref.shape[0], step_ref.shape[1]
    if inner != dm.ip:
        out_ref[...] = jnp.zeros_like(out_ref)
    row = lax.broadcasted_iota(jnp.int32, (r, r), 0)
    col = lax.broadcasted_iota(jnp.int32, (r, r), 1)
    eye = jnp.where(row == col, 1.0, 0.0).astype(BF16)
    out_ref[:, :inner] = gate_ref[...]
    out_ref[:, dm.ip : dm.ip + inner] = value_ref[...]
    out_ref[:, 2 * dm.ip : dm.ip + dm.vs] = shared_ref[...]
    out_ref[:, dm.ip + dm.vs :] = jnp.zeros((r, LANES), BF16)
    out_ref[:, dm.ip + dm.vs : dm.ip + dm.vs + heads] = dot(eye, step_ref[...], MT).astype(BF16)


def forward_kernel(dm, scalars, *refs):
    q, ip, vs, st, hd = BLOCK, dm.ip, dm.vs, dm.state, dm.hd
    w_parts = refs[: dm.n_dp]
    n_parts = refs[dm.n_dp : dm.n_dp + dm.pieces]
    rest = refs[dm.n_dp + dm.pieces :]
    rows_ref, conv_ref, hp_ref, lane_ref = rest[:4]
    (z_out, e_out, gd_out, v_out, cv_out, ys_out, st_out, h_out, sum_out, nm_out, sg_out, w_out) = rest[
        4:16
    ]
    (w_v, nm_v, h_ref, vbuf, tri_ref, pick_ref, pbuf, gate_s, w_sem, n_sem, o_sem) = rest[16:]
    i = pl.program_id(0)
    save = pltpu.make_async_copy(w_v, w_out, o_sem)

    def rows_at(k):
        return nm_v[pl.ds(pl.multiple_of(k * q, q), q), :]

    @pl.when(i == 0)
    def _():
        copies = load_parts(w_parts, w_v, w_sem, scalars, 0, dm.part_rows)
        copies += load_parts(n_parts, nm_v, n_sem, scalars, dm.at_n, dm.piece_rows)
        for copy in copies:
            copy.start()
        h_ref[...] = jnp.zeros_like(h_ref)
        vbuf[...] = jnp.zeros_like(vbuf)
        tri_ref[...] = lower_blocks()
        pick_ref[...] = lane_pick(dm)
        for copy in copies:
            copy.wait()
        save.start()
        pbuf[...] = dot(nm_v[0:q, :], w_v[...])

    rows = rows_ref[...]
    cols = columns_of(rows)
    nm_out[...] = rows_at(i)
    for c in range(vs // LANES):
        vbuf[c, 0:8, :] = vbuf[c, q : q + 8, :]
        vbuf[c, 8 : 8 + q, :] = pbuf[:, ip + c * LANES : ip + (c + 1) * LANES]
    v_out[...] = pbuf[:, ip : ip + vs].astype(BF16)
    raw = pbuf[:, ip + vs :]
    gate_s[...] = pbuf[:, :ip]
    st_out[...] = raw

    acts = []
    count = vs // LANES
    edges = [k * dm.np // count // LANES * LANES for k in range(count)] + [dm.np]
    following = rows_at(jnp.minimum(i + 1, dm.blocks - 1))
    for c in range(count):
        g = slice(c * LANES, (c + 1) * LANES)
        acc = conv_ref[4:5, g] + conv_ref[3:4, g] * vbuf[c, 8 : 8 + q, :]
        for lag in range(1, 4):
            acc = acc + conv_ref[3 - lag : 4 - lag, g] * (
                vbuf[c, 8 - lag : 8 - lag + q, :] * cols[:, lag : lag + 1]
            )
        rounded = acc.astype(BF16)
        cv_out[:, g] = rounded
        acc = rounded.astype(F32)
        acts.append(acc * sigmoid(acc))
        n = slice(edges[c], edges[c + 1])
        pbuf[:, n] = dot(following, w_v[:, n])
    in_map = jnp.concatenate(acts[dm.pairs : dm.pairs + st // LANES], axis=1).astype(BF16)
    out_map = jnp.concatenate(acts[dm.pairs + st // LANES :], axis=1).astype(BF16)

    delta, logs, enter, ending = decay_parts(raw, hp_ref, cols, tri_ref[...])
    logs_t = logs.T
    delta_e, enter_e, ending_e = [to_lanes(v, pick_ref[...]) for v in (delta, enter, ending)]
    r = lax.broadcasted_iota(jnp.int32, (SUB, SUB), 0)
    c = lax.broadcasted_iota(jnp.int32, (SUB, SUB), 1)
    masks = head_masks(dm)
    squares = []
    for k in range(q // SUB):
        a = slice(k * SUB, (k + 1) * SUB)
        bias = jnp.where((r >= c) & (cols[a, 0:1] == rows[0:1, a]), 0.0, FAR)
        source, target = in_map[a], out_map[a]
        scores = dot(target, source, MT)
        source_t = source.T
        keep = scalars[dm.at_keep + i * (q // SUB) + k].astype(F32)
        total = jnp.exp2(logs[a][SUB - 1 :, :]) * keep
        h_out[k * st : (k + 1) * st, :] = h_ref[...].astype(BF16)
        square = None
        for p in range(dm.pairs):
            g = slice(p * LANES, (p + 1) * LANES)
            x = acts[p][a]
            u = x * delta_e[a, g]
            ub = u.astype(BF16)
            mixing = []
            for j in range(dm.per):
                h = p * dm.per + j
                decay = jnp.exp2(logs[a, h : h + 1] - logs_t[h : h + 1, a] + bias)
                mixing.append((decay * scores).astype(BF16))
            y = dot(
                jnp.concatenate(mixing, axis=1),
                jnp.concatenate([ub * mask for mask in masks], axis=0),
            )
            held = h_ref[:, g]
            y = y + dot(target, held.astype(BF16)) * enter_e[a, g]
            wu = (u * ending_e[a, g]).astype(BF16)
            h_ref[:, g] = held * spread(total, p, hd) + dot(source_t, wu)
            ys_out[a, g] = y
            gate = gate_s[a, g]
            sig = sigmoid(gate)
            z = gate * sig
            y = y + lane_ref[0:1, g] * x
            gated = y * z
            z_out[a, g] = z
            gd_out[a, g] = gated
            e_out[a, g] = (y * (sig + z * (1.0 - sig))).astype(BF16)
            sg_out[a, g] = (gated * lane_ref[1:2, g]).astype(BF16)
            square = gated * gated if square is None else square + gated * gated
        squares.append(square)
    sum_out[...] = jnp.sum(jnp.concatenate(squares, axis=0).T, axis=0, keepdims=True)

    @pl.when(i == dm.blocks - 1)
    def _():
        save.wait()


def branch_kernel(dm, scalars, *refs):
    n_dp, n_t, q = dm.n_dp, dm.n_t, BLOCK
    w_parts, sg_ref = refs[:n_dp], refs[n_dp]
    w_out, outs, (w_sem,) = refs[n_dp + 1], refs[n_dp + 2 : n_dp + 2 + n_t], refs[n_dp + 2 + n_t :]
    loads = load_parts(w_parts, w_out, w_sem, scalars, 0, dm.part_rows)
    for copy in loads:
        copy.start()
    for copy in loads:
        copy.wait()
    for k in range(n_t):
        chunk = pl.multiple_of(scalars[dm.at_c + k], dm.chunk_rows)
        for h in range(dm.chunk_rows // q):
            at = pl.ds(pl.multiple_of(chunk + h * q, q), q)
            outs[k][h] = dot(sg_ref[at, :], w_out[...], MT).astype(BF16)


def scaled_kernel(dm, scalars, *refs):
    q, n_t = BLOCK, dm.n_t
    c_parts = refs[:n_t]
    w_ref, lane_ref, gd_ref, sq_ref, sc_out, sum_out, ct_out = refs[n_t:]
    for k in range(n_t):
        chunk = pl.multiple_of(scalars[dm.at_c + k], dm.chunk_rows)
        for h in range(dm.chunk_rows // q):
            at = pl.ds(pl.multiple_of(chunk + h * q, q), q)
            cot = c_parts[k][h * q : (h + 1) * q, :]
            ct_out[at, :] = cot
            sc = (dot(cot, w_ref[...]) * lane_ref[1:2, :]).astype(BF16)
            sc_out[at, :] = sc
            prod = sc.astype(F32) * gd_ref[at, :]
            dots = prod[:, :LANES]
            for p in range(1, dm.pairs):
                dots = dots + prod[:, p * LANES : (p + 1) * LANES]
            blk = chunk // q + h
            sum_out[blk, 0:1, :] = sq_ref[blk]
            sum_out[blk, 1:2, :] = jnp.sum(dots.T, axis=0, keepdims=True)


def gate_kernel(dm, scalars, *refs):
    q, ip, r = BLOCK, dm.ip, dm.part_rows
    (w_ref, rk_ref, lane_ref, z_in, e_in, gd_in, sc_in, nm_in, ct_in) = refs[:9]
    dg_out, dy_out, lane_out, rows_out, own_out = refs[9:14]
    z_outs = refs[14 : 13 + dm.n_hi]
    acc, dg_s, both = refs[13 + dm.n_hi :]
    i = pl.program_id(0)

    @pl.when(i == 0)
    def _():
        lane_out[...] = jnp.zeros_like(lane_out)
        acc[...] = jnp.zeros_like(acc)

    def gather():
        acc[:, :ip] += dot(nm_in[...], dg_s[...], TM)
        acc[:, ip:] += dot(ct_in[...], both[...], TM)

    def gating():
        pad = jnp.zeros((LANES - 2, q), F32)
        cols = jnp.concatenate([rk_ref[...], pad], axis=0).T
        root, pull = [jnp.broadcast_to(cols[:, k : k + 1], (q, LANES)) for k in range(2)]
        for p in range(dm.pairs):
            g = slice(p * LANES, (p + 1) * LANES)
            sc, gated = sc_in[:, g].astype(F32), gd_in[:, g]
            scaled = gated * root
            cot = root * sc - pull * gated
            lane_out[:, g] += colsum(sc * scaled)
            dy = cot * z_in[:, g]
            dy_out[:, g] = dy.astype(BF16)
            dg = (cot * e_in[:, g].astype(F32)).astype(BF16)
            dg_out[:, g] = dg
            dg_s[:, g] = dg
            both[:, g] = (scaled * lane_ref[1:2, g]).astype(BF16)

    @pl.when(i == 0)
    def _():
        gating()

    @pl.when((i > 0) & (i < dm.blocks))
    def _():
        gather()
        gating()

    @pl.when(i == dm.blocks)
    def _():
        gather()
        lane_out[...] = lane_out[...] / lane_ref[1:2, :]
        prod = acc[:, :LANES] * w_ref[:, :LANES].astype(F32)
        for p in range(1, dm.pairs):
            g = slice(p * LANES, (p + 1) * LANES)
            prod = prod + acc[:, g] * w_ref[:, g].astype(F32)
        rows_out[...] = gain_rows(prod)
        hi = scalars[dm.at_hi]
        own_out[...] = acc[pl.ds(pl.multiple_of(hi * 2 * r, 8), 2 * r), :]
        for k, z_out in enumerate(z_outs):
            at = pl.multiple_of(scalars[dm.at_hi + k + 1] * 2 * r, 8)
            z_out[...] = acc[pl.ds(at, 2 * r), :].astype(BF16)


def backward_kernel(dm, scalars, *refs):
    q, ip, vs, st, hd, late_cols = BLOCK, dm.ip, dm.vs, dm.state, dm.hd, dm.late
    groups = dm.group_sizes
    w_ref, rows_ref, conv_ref, hp_ref, lane_ref, lanes_ref, gain_ref = refs[:7]
    dg_in, nm_in, dy_in, v_in, cv_in, ys_in, st_in, h_in = refs[7:15]
    mine_out, theirs_out, kept_out = refs[15:18]
    nc_outs = refs[18 : 18 + len(groups)]
    (dh_ref, dbuf, tri_ref, dx_s, act_s, t1_s, t2_s) = refs[18 + len(groups) : 25 + len(groups)]
    (pick_ref, skip_s, pj_s, full, acc, tap_out, head_out, nc_buf, nc_sem, own_sem) = refs[25 + len(groups) :]
    i = pl.program_id(0)
    blk = jnp.maximum(dm.blocks - 1 - i, 0)
    subs = q // SUB

    def send(k, at, row):
        return pltpu.make_async_copy(nc_buf.at[at], nc_outs[k].at[row], nc_sem.at[at])

    @pl.when(i == 0)
    def _():
        dh_ref[...] = jnp.zeros_like(dh_ref)
        dbuf[...] = jnp.zeros_like(dbuf)
        tap_out[...] = jnp.zeros_like(tap_out)
        head_out[...] = jnp.zeros_like(head_out)
        skip_s[...] = jnp.zeros_like(skip_s)
        acc[...] = jnp.zeros_like(acc)
        tri_ref[...] = lower_blocks()
        pick_ref[...] = lane_pick(dm)

    slot = lax.rem(i, 2)

    @pl.when(i >= 3)
    def _():
        send(0, slot, 0).wait()

    third = dm.width // 3

    def cotangent_piece(n):
        def run():
            g = slice(n * third, (n + 1) * third)
            nc_buf[slot, :, g] = dot(full[...], w_ref[g, :], MT).astype(BF16)

        return run

    def gradient_piece(n):
        def run():
            g = slice(n * third, (n + 1) * third)
            acc[g, :] += dot(nm_in[:, g], full[:, ip:], TM)

        return run

    pieces = [make(n) for n in range(3) for make in (cotangent_piece, gradient_piece)]

    def take_over():
        full[:, :ip] = dg_in[...]
        full[:, ip:] = pj_s[...]

    def scan(between):
        rows = rows_ref[...]
        cols = columns_of(rows)
        raw = st_in[...]
        tri = tri_ref[...]
        delta, logs, enter, ending = decay_parts(raw, hp_ref, cols, tri)
        logs_t = logs.T
        deltas, enters, endings = [to_lanes(v, pick_ref[...]) for v in (delta, enter, ending)]

        acts, slopes = [], []
        for c in range(vs // LANES):
            g = slice(c * LANES, (c + 1) * LANES)
            cv = cv_in[:, g].astype(F32)
            sig = sigmoid(cv)
            act = cv * sig
            acts.append(act)
            slopes.append(sig + act * (1.0 - sig))
        in_map = jnp.concatenate(acts[dm.pairs : dm.pairs + st // LANES], axis=1).astype(BF16)
        out_map = jnp.concatenate(acts[dm.pairs + st // LANES :], axis=1).astype(BF16)

        r = lax.broadcasted_iota(jnp.int32, (SUB, SUB), 0)
        c = lax.broadcasted_iota(jnp.int32, (SUB, SUB), 1)
        masks = head_masks(dm)
        d_in, d_out = [None] * subs, [None] * subs
        for k in reversed(range(subs)):
            a = slice(k * SUB, (k + 1) * SUB)
            bias = jnp.where((r <= c) & (cols[a, 0:1] == rows[0:1, a]), 0.0, FAR)
            source, target = in_map[a], out_map[a]
            scores = dot(source, target, MT)
            target_t = target.T
            keep = scalars[dm.at_keep + blk * subs + k].astype(F32)
            total = jnp.exp2(logs[a][SUB - 1 :, :]) * keep
            ds = None
            for p in range(dm.pairs):
                g = slice(p * LANES, (p + 1) * LANES)
                x, dyb = acts[p][a], dy_in[a, g]
                delta_e = deltas[a, g]
                u = x * delta_e
                ub, dy = u.astype(BF16), dyb.astype(F32)
                decays = []
                for j in range(dm.per):
                    h = p * dm.per + j
                    decays.append(jnp.exp2(logs_t[h : h + 1, a] - logs[a, h : h + 1] + bias))
                du = dot(
                    jnp.concatenate([(d * scores).astype(BF16) for d in decays], axis=1),
                    jnp.concatenate([dyb * mask for mask in masks], axis=0),
                )
                dm_t = dot(jnp.concatenate([ub * mask for mask in masks], axis=0), dyb, MT)
                for j, d in enumerate(decays):
                    part = dm_t[j * SUB : (j + 1) * SUB] * d
                    ds = part if ds is None else ds + part
                dh, h_rows = dh_ref[:, g], h_in[k * st : (k + 1) * st, g]
                dh_b = dh.astype(BF16)
                end_e = endings[a, g]
                late = end_e * dot(source, dh_b)
                du = du + late
                wu = (u * end_e).astype(BF16)
                edy = (dy * enters[a, g]).astype(BF16)
                from_wu, from_dy = dot(wu, dh_b, MT), dot(edy, h_rows, MT)
                d_in[k] = from_wu if p == 0 else d_in[k] + from_wu
                d_out[k] = from_dy if p == 0 else d_out[k] + from_dy
                u32 = ub.astype(F32)
                t1_s[a, g] = dy * ys_in[a, g] - u32 * du
                t2_s[a, g] = du * x
                skip_s[:, g] += colsum(dy * x)
                kept = dh * spread(total, p, hd)
                act_s[8 * k : 8 * k + 8, g] = colsum(u32 * late) + colsum(h_rows.astype(F32) * kept)
                dh_ref[:, g] = kept + dot(target_t, edy)
                dx_s[a, g] = (delta_e * du + lane_ref[0:1, g] * dy) * slopes[p][a]
            ds_b = ds.astype(BF16)
            d_in[k] = d_in[k] + dot(ds_b, target)
            d_out[k] = d_out[k] + dot(ds_b, source, TM)

        hr = lax.broadcasted_iota(jnp.int32, (ip, LANES), 0)
        hc = lax.broadcasted_iota(jnp.int32, (ip, LANES), 1)
        pick = jnp.where(hr // hd == hc, 1.0, 0.0).astype(BF16)
        d_log = split_dot(t1_s[...], pick)
        last = split_dot(act_s[...], pick)
        row = lax.broadcasted_iota(jnp.int32, (q, LANES), 0)
        for k in range(subs):
            end = jnp.sum(last[8 * k : 8 * k + 8, :], axis=0, keepdims=True)
            d_log = d_log + jnp.where(row == (k + 1) * SUB - 1, end, 0.0)
        d_step = dot_split(tri, d_log, TM)
        head_out[8:16, :] += colsum(d_step * delta)
        d_delta = hp_ref[1:2, :] * d_step + dot(t2_s[...].astype(BF16), pick)
        d_raw = d_delta * sigmoid(raw + hp_ref[0:1, :])
        head_out[0:8, :] += colsum(d_raw)
        pj_s[:, vs:] = d_raw.astype(BF16)

        count = vs // LANES
        for c in range(count):
            dbuf[c, q : q + 8, :] = dbuf[c, 0:8, :]
            for k in range(subs):
                a = slice(k * SUB, (k + 1) * SUB)
                if c < dm.pairs:
                    dbuf[c, a, :] = dx_s[a, c * LANES : (c + 1) * LANES]
                else:
                    n = (c - dm.pairs) * LANES
                    part = d_in[k][:, n : n + LANES] if n < st else d_out[k][:, n - st : n - st + LANES]
                    dbuf[c, a, :] = part * slopes[c][a]
        for c in range(count):
            g = slice(c * LANES, (c + 1) * LANES)
            v = v_in[:, g].astype(F32)
            shifted = dbuf[c, 0:q, :]
            tap_out[32:40, g] += colsum(shifted)
            tap_out[24:32, g] += colsum(shifted * v)
            dv = conv_ref[3:4, g] * shifted
            for lag in range(1, 4):
                shifted = dbuf[c, lag : lag + q, :] * cols[:, 3 + lag : 4 + lag]
                tap_out[24 - 8 * lag : 32 - 8 * lag, g] += colsum(shifted * v)
                dv = dv + conv_ref[3 - lag : 4 - lag, g] * shifted
            pj_s[:, g] = dv.astype(BF16)
            first, stop = c * len(between) // count, (c + 1) * len(between) // count
            for run in between[first:stop]:
                run()

    @pl.when(i == 0)
    def _():
        scan([])

    @pl.when((i > 0) & (i < dm.blocks))
    def _():
        take_over()
        scan(pieces)

    @pl.when(i == dm.blocks)
    def _():
        take_over()
        for run in pieces:
            run()

    before = jnp.minimum(blk + 1, dm.blocks - 1)
    before = jnp.where(i == dm.blocks, 0, before)
    for k in range(len(groups)):

        @pl.when((i > 0) & (scalars[dm.at_group + before] == k))
        def _():
            send(k, slot, scalars[dm.at_slot + before]).start()

    @pl.when(i == dm.blocks)
    def _():
        core, r = scalars[dm.at_core], dm.part_rows
        owns = []
        for h in range(dm.n_hi):
            at = pl.multiple_of((2 * h + core) * r, 8)
            own = pltpu.make_async_copy(
                acc.at[pl.ds(at, r), :], mine_out.at[h * r : (h + 1) * r, :], own_sem.at[h]
            )
            own.start()
            owns.append(own)
            at = pl.multiple_of((2 * h + 1 - core) * r, 8)
            theirs_out[h * r : (h + 1) * r, :] = acc[pl.ds(at, r), :].astype(BF16)
        small = []

        def put(v):
            for c in range(v.shape[1] // LANES):
                small.append(jnp.sum(v[:, c * LANES : (c + 1) * LANES], axis=0, keepdims=True))

        for k in range(5):
            put(tap_out[8 * k : 8 * k + 8, :ip])
        put(lanes_ref[...])
        put(skip_s[...])
        for k in range(2):
            put(head_out[8 * k : 8 * k + 8, :])
        zero = jnp.zeros((1, LANES), F32)
        small.extend([zero] * (dm.local_rows - len(small)))
        for k in range(5):
            put(tap_out[8 * k : 8 * k + 8, ip:])
        prod = acc[:, :LANES] * w_ref[:, ip : ip + LANES].astype(F32)
        for p in range(1, late_cols // LANES):
            g = slice(p * LANES, (p + 1) * LANES)
            o = slice(ip + p * LANES, ip + (p + 1) * LANES)
            prod = prod + acc[:, g] * w_ref[:, o].astype(F32)
        prod = gain_rows(prod)
        for c in range(dm.width // LANES):
            g = slice(c * LANES, (c + 1) * LANES)
            small.append(prod[0:1, g] + gain_ref[0:1, g])
        small.extend([zero] * (late_cols // 16 - len(small)))
        for c in range(late_cols // LANES):
            g = slice(c * LANES, (c + 1) * LANES)
            parts = two_parts(jnp.concatenate(small[8 * c : 8 * c + 8], axis=0))
            theirs_out[dm.n_hi * r :, g] = parts
            kept_out[:, g] = parts
        for own in owns:
            own.wait()
        send(0, 1 - slot, 0).wait()
        send(0, slot, 0).wait()


def two_parts(v):
    high = v.astype(BF16).astype(F32)
    return jnp.concatenate([high, v - high], axis=0).astype(BF16)


def one_part(v):
    return v[0:8, :].astype(F32) + v[8:16, :].astype(F32)


def gain_rows(acc):
    high = acc.astype(BF16)
    rest = acc - high.astype(F32)
    mid = rest.astype(BF16)
    low = (rest - mid.astype(F32)).astype(BF16)
    one = jnp.ones((8, LANES), BF16)
    return dot(one, high, MT) + dot(one, mid, MT) + dot(one, low, MT)


def pair_kernel(dm, scalars, mine_ref, kept_ref, theirs_ref, own_out, *outs):
    r = dm.part_rows
    tail = dm.n_hi * r
    small = one_part(kept_ref[...]) + one_part(theirs_ref[tail:, :])
    small = two_parts(small)
    for k in range(dm.n_hi):
        at = pl.multiple_of(scalars[dm.at_hi + k] * r, 8)
        both = mine_ref[pl.ds(at, r), :] + theirs_ref[pl.ds(at, r), :].astype(F32)
        if k == 0:
            own_out[...] = both
        else:
            outs[k][0:r, :] = both.astype(BF16)
        if k > 0:
            outs[k][r:, :] = small
        else:
            outs[0][...] = small


def early_kernel(dm, scalars, own_ref, *refs):
    parts, (mine_out, theirs_out, total) = refs[: dm.n_hi - 1], refs[dm.n_hi - 1 :]
    r = dm.part_rows
    both = own_ref[...]
    for part in parts:
        both = both + part[...].astype(F32)
    total[...] = both
    core = scalars[dm.at_core]
    mine_out[...] = total[pl.ds(pl.multiple_of(core * r, 8), r), :]
    theirs_out[...] = total[pl.ds(pl.multiple_of((1 - core) * r, 8), r), :].astype(BF16)


def grads_kernel(dm, scalars, hp_ref, own_ref, kept_ref, mine_ref, theirs_ref, *refs):
    n, r, st2 = dm.n_hi, dm.part_rows, 2 * dm.state
    parts = refs[: n - 1]
    (gate_out, value_out, step_out, outp_out, share_out) = refs[n - 1 : n + 4]
    (tap_out, tapb_out, gain_out, skip_out, sb_out, dl_out, hold) = refs[n + 4 :]
    total = own_ref[...]
    for part in parts:
        total = total + part[0:r, :].astype(F32)
    early = mine_ref[...] + theirs_ref[...].astype(F32)
    inner, heads = gate_out.shape[1], step_out.shape[0]
    gate_out[...] = early[:, :inner]
    outp_out[...] = early[:, dm.ip : dm.ip + inner]
    value_out[...] = total[:, :inner]
    share_out[0:r, :] = total[:, dm.ip : dm.vs].astype(BF16)
    step_out[...] = total[:, dm.vs :].T[0:heads, :]
    hold[0] = one_part(kept_ref[...])
    for k, part in enumerate(parts):
        hold[k + 1] = one_part(part[r:, :])
    small = hold[scalars[dm.at_from]]
    for k in range(1, n):
        small = small + hold[scalars[dm.at_from + k]]
    flat = [
        small[j : j + 1, c * LANES : (c + 1) * LANES]
        for c in range(dm.late // LANES)
        for j in range(8)
    ]

    def take(first, width):
        return jnp.concatenate(flat[first : first + dm.pairs], axis=1)[:, :width]

    for k in range(4):
        tap_out[k : k + 1, :] = take(k * dm.pairs, inner)
    tapb_out[...] = take(4 * dm.pairs, inner)[0]
    gain_out[...] = take(5 * dm.pairs, inner)[0]
    lane = lax.broadcasted_iota(jnp.int32, (1, LANES), 1)
    skip = jnp.zeros((1, LANES), F32)
    for h in range(heads):
        row = flat[6 * dm.pairs + h // dm.per]
        mine = lane // dm.hd == h % dm.per
        one = jnp.sum(jnp.where(mine, row, 0.0), axis=1, keepdims=True)
        skip = jnp.where(lane == h, one, skip)
    skip_out[...] = skip[0, :heads]
    sb_out[...] = flat[7 * dm.pairs][0, :heads]
    dl_out[...] = (flat[7 * dm.pairs + 1] * hp_ref[1:2, :])[0, :heads]
    first = dm.local_rows // 8
    for c in range(st2 // LANES):
        g = slice((first + c) * LANES, (first + c + 1) * LANES)
        share_out[r:, c * LANES : (c + 1) * LANES] = two_parts(small[:, g])


def share_kernel(dm, scalars, norm_ref, *refs):
    r, st2 = dm.part_rows, 2 * dm.state
    parts = refs[: dm.n_t]
    shared_out, tap_out, tapb_out, norm_out, hold = refs[dm.n_t :]
    for k, part in enumerate(parts):
        hold[k] = part[...]
    shared, common = None, None
    for k in range(dm.n_t):
        part = hold[scalars[dm.at_side + k]]
        share, small = part[0:r, :].astype(F32), one_part(part[r:, :])
        shared = share if shared is None else shared + share
        common = small if common is None else common + small
    shared_out[...] = shared
    flat = [
        common[j : j + 1, c * LANES : (c + 1) * LANES] for c in range(st2 // LANES) for j in range(8)
    ]
    per = st2 // LANES
    for k in range(4):
        tap_out[k : k + 1, :] = jnp.concatenate(flat[k * per : (k + 1) * per], axis=1)
    tapb_out[...] = jnp.concatenate(flat[4 * per : 5 * per], axis=1)[0]
    rows = flat[5 * per : 5 * per + dm.width // LANES]
    norm_out[...] = jnp.concatenate(rows, axis=1)[0] / norm_ref[...]


def input_kernel(sets, steps, x_ref, cot_ref, gain_ref, *refs):
    out = refs[-1]
    x = x_ref[...]
    root = lax.rsqrt(jnp.mean(x * x, axis=1, keepdims=True) + EPS)
    first = 0
    for k, count in enumerate(sets):
        parts = refs[first : first + count]
        first += count

        @pl.when(pl.program_id(0) // steps == k)
        def _():
            nc = parts[0][...].astype(F32)
            for part in parts[1:]:
                nc = nc + part[...].astype(F32)
            hat = nc * gain_ref[...][None]
            mean = jnp.mean(hat * x, axis=1, keepdims=True)
            out[...] = cot_ref[...].astype(F32) + root * hat - x * (root * root * root * mean)


def shift_hi(n, k):
    return [(i, ((i // 2 + k) % (n // 2)) * 2 + i % 2) for i in range(n)]


def swap(n, k):
    return [(i, i ^ k) for i in range(n)]


def pad_cols(v, to):
    return jnp.pad(v, ((0, 0), (0, to - v.shape[1])))


def pad_vec(v, to):
    return jnp.pad(v, (0, to - v.shape[0]))


def body(
    n_dp,
    n_t,
    block_input,
    segment_ids,
    norm_gain,
    gate_proj,
    value_proj,
    shared_proj,
    step_proj,
    conv_value_weight,
    conv_value_bias,
    conv_shared_weight,
    conv_shared_bias,
    step_bias,
    decay_log,
    skip_weight,
    gate_gain,
    output_proj,
    out_cotangent,
):
    q = BLOCK
    chunk_rows, width = block_input.shape
    length = segment_ids.shape[1]
    inner, heads = gate_proj.shape[1], step_proj.shape[1]
    part_rows = gate_proj.shape[0]
    state = shared_proj.shape[1] // 2
    hd = inner // heads
    dm = Dims(n_dp, n_t, length, width, inner, hd, state, part_rows, chunk_rows)
    ip, vs, nb, n_hi = dm.ip, dm.vs, dm.blocks, dm.n_hi
    me_t = lax.axis_index("tensor")
    me_dp = lax.axis_index("dp")
    hi, core = me_dp // 2, me_dp % 2

    def across(v, k):
        return lax.ppermute(v, "tensor", swap(n_t, k))

    def along(v, k):
        return lax.ppermute(v, "dp", shift_hi(n_dp, k))

    def partner(v):
        return lax.ppermute(v, "dp", swap(n_dp, 1))

    def vmem(shape, dtype):
        return pltpu.VMEM(shape, dtype)

    limit = 16 * 1024 * 1024
    params = pltpu.CompilerParams(dimension_semantics=("arbitrary",), vmem_limit_bytes=limit)
    hbm = pl.BlockSpec(memory_space=pl.ANY)
    in_hbm = pl.BlockSpec(memory_space=pltpu.HBM)

    def out(*shape, dtype=F32):
        return jax.ShapeDtypeStruct(shape, dtype)

    normed = pl.pallas_call(
        norm_kernel,
        out_shape=[out(dm.piece_rows, width, dtype=BF16)] * dm.halves,
        compiler_params=pltpu.CompilerParams(vmem_limit_bytes=limit),
        name="normalize",
    )(block_input, norm_gain)
    if dm.halves == 2:
        a, b = normed
        xa, yb = across(a, 1), across(b, 2)
        ya, xb = across(a, 2), across(b, 1)
        n_list = [a, b, xa, xb, ya, yb, across(xa, 2), across(yb, 1)]
        n_rows = jnp.concatenate(
            [(me_t ^ k) * chunk_rows + jnp.arange(2) * dm.piece_rows for k in range(4)]
        )
    else:
        n_list = [normed[0]] + [across(normed[0], k) for k in range(1, n_t)]
        n_rows = (me_t ^ jnp.arange(n_t)) * chunk_rows
    packed = pl.pallas_call(
        functools.partial(pack_kernel, dm),
        out_shape=out(part_rows, dm.np, dtype=BF16),
        name="pack_weights",
    )(gate_proj, value_proj, shared_proj, step_proj.T)
    w_list = [packed] + [along(packed, k) for k in range(1, n_hi)]
    w_list = w_list + [partner(v) for v in w_list]
    outp = pad_cols(output_proj.T, ip)
    o_list = [outp] + [along(outp, k) for k in range(1, n_hi)]
    o_list = o_list + [partner(v) for v in o_list]

    seg = segment_ids[0]
    subs = q // SUB
    segb = seg.reshape(nb * subs, SUB)
    last = segb[:, -1]
    prev_last = jnp.concatenate([jnp.full((1,), -1, jnp.int32), last[:-1]])
    gap = jnp.full((3,), -1, jnp.int32)
    wide = jnp.concatenate([gap, seg, gap])
    rows = [seg.astype(F32)]
    rows += [(wide[3 - k : 3 - k + length] == seg).astype(F32) for k in range(1, 4)]
    rows += [(wide[3 + k : 3 + k + length] == seg).astype(F32) for k in range(1, 4)]
    rows += [
        (segb == prev_last[:, None]).astype(F32).reshape(-1),
        (segb == last[:, None]).astype(F32).reshape(-1),
    ]
    rows = jnp.concatenate([jnp.stack(rows), jnp.zeros((16 - len(rows), length), F32)], axis=0)
    keep = (last == prev_last).astype(jnp.int32)
    other = (hi - jnp.arange(n_hi)) % n_hi
    rel = (jnp.arange(nb) * q // chunk_rows) ^ me_t
    half = jnp.arange(nb) % (chunk_rows // q)
    if dm.halves == 2:
        group_of = jnp.array([[2, 2], [0, 2], [2, 1], [0, 1]])
        slot_of = jnp.array([[0, 2], [0, 3], [1, 0], [1, 1]])
        group, slot = group_of[rel, half], slot_of[rel, half]
        dm.group_sizes = (2, 2, 4)
    else:
        group, slot = rel, half
        dm.group_sizes = (chunk_rows // q,) * n_t
    scalars = jnp.concatenate(
        [
            (other * 2 + core) * part_rows,
            (other * 2 + 1 - core) * part_rows,
            n_rows,
            (me_t ^ jnp.arange(n_t)) * chunk_rows,
            keep,
            rel,
            group,
            slot,
            (hi + jnp.arange(n_hi)) % n_hi,
            core[None],
            (hi - jnp.arange(n_hi)) % n_hi,
            me_t ^ jnp.arange(n_t),
        ]
    ).astype(jnp.int32)

    conv = jnp.concatenate(
        [
            pad_cols(jnp.concatenate([conv_value_weight, conv_value_bias[None]]), ip),
            jnp.concatenate([conv_shared_weight, conv_shared_bias[None]]),
        ],
        axis=1,
    )
    conv = jnp.pad(conv, ((0, 3), (0, 0)))
    rate = -jnp.exp(decay_log)
    per_head = jnp.stack([pad_vec(step_bias, LANES), pad_vec(rate, LANES)])
    per_head = jnp.pad(per_head, ((0, 6), (0, 0)))
    per_lane = jnp.stack([pad_vec(jnp.repeat(skip_weight, hd), ip), jnp.pad(gate_gain, (0, ip - inner), constant_values=1.0)])
    per_lane = jnp.pad(per_lane, ((0, 6), (0, 0)))

    def const(*shape):
        return pl.BlockSpec(shape, lambda i, s: (0,) * len(shape))

    def fblock(cols):
        return pl.BlockSpec((q, cols), lambda i, s: (i, 0))

    def fsum(k):
        return pl.BlockSpec((None, k, q), lambda i, s: (i, 0, 0))

    def grid(steps, in_specs, out_specs, scratch):
        return pltpu.PrefetchScalarGridSpec(
            num_scalar_prefetch=1,
            grid=(steps,),
            in_specs=in_specs,
            out_specs=out_specs,
            scratch_shapes=scratch,
        )

    (gate, slope, gated, value, conved, scan, steps_raw, held, squares, normed_all, scaled, weights) = pl.pallas_call(
        functools.partial(forward_kernel, dm),
        out_shape=[
            out(length, ip),
            out(length, ip, dtype=BF16),
            out(length, ip),
            out(length, vs, dtype=BF16),
            out(length, vs, dtype=BF16),
            out(length, ip),
            out(length, LANES),
            out(nb * subs * state, ip, dtype=BF16),
            out(nb, 1, q),
            out(length, width, dtype=BF16),
            out(length, ip, dtype=BF16),
            out(width, dm.np, dtype=BF16),
        ],
        grid_spec=grid(
            nb,
            [in_hbm] * (n_dp + dm.pieces)
            + [
                pl.BlockSpec((16, q), lambda i, s: (0, i)),
                const(8, vs),
                const(8, LANES),
                const(8, ip),
            ],
            [
                fblock(ip),
                fblock(ip),
                fblock(ip),
                fblock(vs),
                fblock(vs),
                fblock(ip),
                fblock(LANES),
                pl.BlockSpec((subs * state, ip), lambda i, s: (i, 0)),
                fsum(1),
                fblock(width),
                fblock(ip),
                hbm,
            ],
            [
                vmem((width, dm.np), BF16),
                vmem((length, width), BF16),
                vmem((state, ip), F32),
                vmem((vs // LANES, q + 8, LANES), F32),
                vmem((q, q), BF16),
                vmem((2 * LANES, ip), BF16),
                vmem((q, dm.np), F32),
                vmem((q, ip), F32),
                pltpu.SemaphoreType.DMA((n_dp,)),
                pltpu.SemaphoreType.DMA((dm.pieces,)),
                pltpu.SemaphoreType.DMA,
            ],
        ),
        compiler_params=params,
        cost_estimate=pl.CostEstimate(
            flops=30_000_000_000, bytes_accessed=30_000_000, transcendentals=0
        ),
        name="block_forward",
    )(scalars, *w_list, *n_list, rows, conv, per_head, per_lane)

    c_list = [out_cotangent] + [across(out_cotangent, k) for k in range(1, n_t)]
    in_vmem = pl.BlockSpec(memory_space=pltpu.VMEM)
    w_back, *branch = pl.pallas_call(
        functools.partial(branch_kernel, dm),
        out_shape=[out(width, ip, dtype=BF16)]
        + [out(chunk_rows // q, q, width, dtype=BF16)] * n_t,
        grid_spec=grid(
            1,
            [hbm] * n_dp + [in_vmem],
            [in_vmem] * (n_t + 1),
            [pltpu.SemaphoreType.DMA((n_dp,))],
        ),
        compiler_params=params,
        cost_estimate=pl.CostEstimate(
            flops=3_000_000_000, bytes_accessed=10_000_000, transcendentals=0
        ),
        name="branch_output",
    )(scalars, *o_list, scaled)
    sc, sums, cot_all = pl.pallas_call(
        functools.partial(scaled_kernel, dm),
        out_shape=[
            out(length, ip, dtype=BF16),
            out(nb, 2, q),
            out(length, width, dtype=BF16),
        ],
        grid_spec=grid(1, [in_vmem] * (n_t + 4), [in_vmem] * 3, []),
        compiler_params=params,
        cost_estimate=pl.CostEstimate(
            flops=3_000_000_000, bytes_accessed=10_000_000, transcendentals=0
        ),
        name="scaled_cotangent",
    )(scalars, *c_list, w_back, per_lane, gated, squares)
    total = sums
    for k in range(1, n_t):
        total = total + across(sums, k)
    root = lax.rsqrt(total[:, 0] / (inner * n_t) + EPS)
    pull = root * root * root * (total[:, 1] / (inner * n_t))
    rk = jnp.stack([root, pull], axis=1)
    branch = branch[:1] + [across(branch[k], k) for k in range(1, n_t)]
    branch_sum = branch[0].astype(F32)
    for piece in branch[1:]:
        branch_sum = branch_sum + piece.astype(F32)
    own_root = lax.dynamic_slice_in_dim(root.reshape(length), me_t * chunk_rows, chunk_rows)
    block_output = block_input + own_root[:, None] * branch_sum.reshape(chunk_rows, width)

    def bblock(cols):
        return pl.BlockSpec((q, cols), lambda i, s: (jnp.maximum(nb - 1 - i, 0), 0))

    def bago(cols):
        return pl.BlockSpec((q, cols), lambda i, s: (jnp.minimum(nb - i, nb - 1), 0))

    def now(cols):
        return pl.BlockSpec((q, cols), lambda i, s: (jnp.minimum(i, nb - 1), 0))

    def ago(cols):
        return pl.BlockSpec((q, cols), lambda i, s: (jnp.maximum(i - 1, 0), 0))

    dgate, dscan, lanes, gate_rows, own_early, *early = pl.pallas_call(
        functools.partial(gate_kernel, dm),
        out_shape=[
            out(length, ip, dtype=BF16),
            out(length, ip, dtype=BF16),
            out(8, ip),
            out(8, width),
            out(2 * part_rows, 2 * ip),
        ]
        + [out(2 * part_rows, 2 * ip, dtype=BF16)] * (n_hi - 1),
        grid_spec=grid(
            nb + 1,
            [
                const(width, ip),
                pl.BlockSpec((None, 2, q), lambda i, s: (jnp.minimum(i, nb - 1), 0, 0)),
                const(8, ip),
                now(ip),
                now(ip),
                now(ip),
                now(ip),
                ago(width),
                ago(width),
            ],
            [now(ip), now(ip), const(8, ip), const(8, width)]
            + [const(2 * part_rows, 2 * ip)] * n_hi,
            [vmem((width, 2 * ip), F32), vmem((q, ip), BF16), vmem((q, ip), BF16)],
        ),
        compiler_params=params,
        cost_estimate=pl.CostEstimate(
            flops=6_000_000_000, bytes_accessed=20_000_000, transcendentals=0
        ),
        name="gate_backward",
    )(scalars, weights, rk, per_lane, gate, slope, gated, sc, normed_all, cot_all)
    early = [along(v, k + 1) for k, v in enumerate(early)]

    r_all = n_hi * part_rows
    mine, theirs, kept, *nc = pl.pallas_call(
        functools.partial(backward_kernel, dm),
        out_shape=[
            out(r_all, dm.late),
            out(r_all + 16, dm.late, dtype=BF16),
            out(16, dm.late, dtype=BF16),
        ]
        + [out(k, q, width, dtype=BF16) for k in dm.group_sizes],
        grid_spec=grid(
            nb + 1,
            [
                const(width, dm.np),
                pl.BlockSpec((16, q), lambda i, s: (0, jnp.maximum(nb - 1 - i, 0))),
                const(8, vs),
                const(8, LANES),
                const(8, ip),
                const(8, ip),
                const(8, width),
                bago(ip),
                bago(width),
                bblock(ip),
                bblock(vs),
                bblock(vs),
                bblock(ip),
                bblock(LANES),
                pl.BlockSpec((subs * state, ip), lambda i, s: (jnp.maximum(nb - 1 - i, 0), 0)),
            ],
            [in_hbm, const(r_all + 16, dm.late), const(16, dm.late)]
            + [in_hbm] * len(dm.group_sizes),
            [
                vmem((state, ip), F32),
                vmem((vs // LANES, q + 8, LANES), F32),
                vmem((q, q), BF16),
                vmem((q, ip), F32),
                vmem((8 * subs, ip), F32),
                vmem((q, ip), F32),
                vmem((q, ip), F32),
                vmem((2 * LANES, ip), BF16),
                vmem((8, ip), F32),
                vmem((q, dm.late), BF16),
                vmem((q, dm.np), BF16),
                vmem((width, dm.late), F32),
                vmem((40, vs), F32),
                vmem((16, LANES), F32),
                vmem((2, q, width), BF16),
                pltpu.SemaphoreType.DMA((2,)),
                pltpu.SemaphoreType.DMA((n_hi,)),
            ],
        ),
        compiler_params=params,
        cost_estimate=pl.CostEstimate(
            flops=40_000_000_000, bytes_accessed=30_000_000, transcendentals=0
        ),
        name="block_backward",
    )(
        scalars,
        weights,
        rows,
        conv,
        per_head,
        per_lane,
        lanes,
        gate_rows,
        dgate,
        normed_all,
        dscan,
        value,
        conved,
        scan,
        steps_raw,
        held,
    )

    part = min(q, dm.piece_rows)
    steps = dm.piece_rows // part

    def turn(k):
        return pl.BlockSpec((part, width), lambda i: (jnp.clip(i - k * steps, 0, steps - 1), 0))

    def slot_of_piece(k, at):
        return pl.BlockSpec(
            (None, part, width), lambda i: (at, jnp.clip(i - k * steps, 0, steps - 1), 0)
        )

    if dm.halves == 2:
        from_x, from_y, stay = across(nc[0], 1), across(nc[1], 2), nc[2]
        pass_y = (stay[1].astype(F32) + from_x[1].astype(F32)).astype(BF16)
        pass_x = (stay[3].astype(F32) + from_y[1].astype(F32)).astype(BF16)
        got_y, got_x = across(pass_y, 2), across(pass_x, 1)
        sets = (3, 3)
        terms = [stay, from_x, got_y, stay, from_y, got_x]
        specs = [slot_of_piece(0, 0), slot_of_piece(0, 0), turn(0)]
        specs += [slot_of_piece(1, 2), slot_of_piece(1, 0), turn(1)]
    else:
        sets = (n_t,)
        terms = [nc[0]] + [across(nc[k], k) for k in range(1, n_t)]
        terms = [v.reshape(chunk_rows, width) for v in terms]
        specs = [turn(0)] * n_t
    in_turn = pl.BlockSpec((part, width), lambda i: (i, 0))
    input_grad = pl.pallas_call(
        functools.partial(input_kernel, sets, steps),
        out_shape=out(chunk_rows, width),
        grid=(len(sets) * steps,),
        in_specs=[in_turn, in_turn, pl.BlockSpec((width,), lambda i: (0,))] + specs,
        out_specs=in_turn,
        compiler_params=params,
        name="input_gradient",
    )(block_input, out_cotangent, norm_gain, *terms)

    late = dm.late
    theirs = partner(theirs)
    own, own_small, *others = pl.pallas_call(
        functools.partial(pair_kernel, dm),
        out_shape=[out(part_rows, late), out(16, late, dtype=BF16)]
        + [out(part_rows + 16, late, dtype=BF16)] * (n_hi - 1),
        grid_spec=grid(1, [in_vmem] * 3, [in_vmem] * (n_hi + 1), []),
        compiler_params=params,
        name="core_sum",
    )(scalars, mine, kept, theirs)
    others = [along(v, k + 1) for k, v in enumerate(others)]
    early_mine, early_theirs = pl.pallas_call(
        functools.partial(early_kernel, dm),
        out_shape=[out(part_rows, 2 * ip), out(part_rows, 2 * ip, dtype=BF16)],
        grid_spec=grid(
            1, [in_vmem] * n_hi, [in_vmem] * 2, [vmem((2 * part_rows, 2 * ip), F32)]
        ),
        compiler_params=params,
        name="early_sum",
    )(scalars, own_early, *early)
    early_theirs = partner(early_theirs)
    (
        gate_proj_grad,
        value_proj_grad,
        step_t,
        outp_t,
        share,
        conv_value_weight_grad,
        conv_value_bias_grad,
        gate_gain_grad,
        skip_weight_grad,
        step_bias_grad,
        decay_log_grad,
    ) = pl.pallas_call(
        functools.partial(grads_kernel, dm),
        out_shape=[
            out(part_rows, inner),
            out(part_rows, inner),
            out(heads, part_rows),
            out(part_rows, inner),
            out(part_rows + 16, 2 * state, dtype=BF16),
            out(4, inner),
            out(inner),
            out(inner),
            out(heads),
            out(heads),
            out(heads),
        ],
        grid_spec=grid(1, [in_vmem] * (n_hi + 4), [in_vmem] * 11, [vmem((n_hi, 8, late), F32)]),
        compiler_params=params,
        name="gradient_sum",
    )(scalars, per_head, own, own_small, early_mine, early_theirs, *others)
    shares = [share] + [across(share, k) for k in range(1, n_t)]
    shared_proj_grad, conv_shared_weight_grad, conv_shared_bias_grad, norm_gain_grad = pl.pallas_call(
        functools.partial(share_kernel, dm),
        out_shape=[out(part_rows, 2 * state), out(4, 2 * state), out(2 * state), out(width)],
        grid_spec=grid(
            1,
            [in_vmem] * (n_t + 1),
            [in_vmem] * 4,
            [vmem((n_t, part_rows + 16, 2 * state), BF16)],
        ),
        compiler_params=params,
        name="shared_sum",
    )(scalars, norm_gain, *shares)
    return (
        block_output,
        input_grad,
        norm_gain_grad,
        gate_proj_grad,
        value_proj_grad,
        shared_proj_grad,
        step_t.T,
        conv_value_weight_grad,
        conv_value_bias_grad,
        conv_shared_weight_grad,
        conv_shared_bias_grad,
        step_bias_grad,
        decay_log_grad,
        skip_weight_grad,
        gate_gain_grad,
        outp_t.T,
    )


def solution(mesh):
    n_dp, n_t = mesh.shape["dp"], mesh.shape["tensor"]
    both = ("dp", "tensor")
    return jax.shard_map(
        functools.partial(body, n_dp, n_t),
        mesh=mesh,
        in_specs=(
            P(both, None),
            P("dp", None),
            P(),
            P("dp", "tensor"),
            P("dp", "tensor"),
            P("dp", None),
            P("dp", "tensor"),
            P(None, "tensor"),
            P("tensor"),
            P(),
            P(),
            P("tensor"),
            P("tensor"),
            P("tensor"),
            P("tensor"),
            P("tensor", "dp"),
            P(both, None),
        ),
        out_specs=(
            P(both, None),
            P(both, None),
            P(),
            P("dp", "tensor"),
            P("dp", "tensor"),
            P("dp", None),
            P("dp", "tensor"),
            P(None, "tensor"),
            P("tensor"),
            P(),
            P(),
            P("tensor"),
            P("tensor"),
            P("tensor"),
            P("tensor"),
            P("tensor", "dp"),
        ),
        check_vma=False,
    )
```
